32 devices in a mesh: dp: 4 (over y, x), vocab: 8 (over z, core).
Axes of the slice: x: 2, y: 2, z: 4, core: 2. Of those that a mesh axis runs over, the one named last changes fastest.
Arguments:
- token_ids: int32 [64, 512], P(('dp', 'vocab')), may hold values from 0 to 30719, as said below
- type_ids: int32 [64, 512], P(('dp', 'vocab')), may hold values from 0 to 1
- lengths: int32 [64], P(('dp', 'vocab')), may hold values from 20 to 512, as said below
- word_table: bfloat16 [30720, 768], P('vocab'), may hold values from -6 to 6
- pos_table: bfloat16 [512, 768], replicated, may hold values from -4 to 4
- token_type_embeddings: bfloat16 [2, 768], replicated, may hold values from -4 to 4
- emb_gain: float32 [768], replicated, may hold values from 0.25 to 1.75
- emb_bias: float32 [768], replicated, may hold values from -3 to 3
- query_weight: bfloat16 [768, 768], replicated, may hold values from -0.21875 to 0.21875
- query_bias: float32 [768], replicated, may hold values from -3 to 3
- key_weight: bfloat16 [768, 768], replicated, may hold values from -0.21875 to 0.21875
- value_weight: bfloat16 [768, 768], replicated, may hold values from -0.21875 to 0.21875
- value_bias: float32 [768], replicated, may hold values from -3 to 3
- out_weight: bfloat16 [768, 768], replicated, may hold values from -0.875 to 0.875
- out_bias: float32 [768], replicated, may hold values from -3 to 3
- attn_gain: float32 [768], replicated, may hold values from 0.25 to 1.75
- attn_bias: float32 [768], replicated, may hold values from -3 to 3
- up_weight: bfloat16 [768, 3072], replicated, may hold values from -0.21875 to 0.21875
- up_bias: float32 [3072], replicated, may hold values from -3 to 3
- down_weight: bfloat16 [3072, 768], replicated, may hold values from -0.109375 to 0.109375
- down_bias: float32 [768], replicated, may hold values from -3 to 3
- final_gain: float32 [768], replicated, may hold values from 0.25 to 1.75
- final_bias: float32 [768], replicated, may hold values from -3 to 3
- cotangent: bfloat16 [64, 512, 768], P(('dp', 'vocab')), may hold values from -6 to 6
Outputs:
- encoded: float32 [64, 512, 768], P(('dp', 'vocab'))
- word_grad: float32 [30720, 768], P('vocab')
- pos_grad: float32 [512, 768], P('vocab')
- type_grad: float32 [2, 768], P(None, 'vocab')
- emb_gain_grad: float32 [768], P('vocab')
- emb_bias_grad: float32 [768], P('vocab')
- query_weight_grad: float32 [768, 768], P('vocab')
- query_bias_grad: float32 [768], P('vocab')
- key_weight_grad: float32 [768, 768], P('vocab')
- value_weight_grad: float32 [768, 768], P('vocab')
- value_bias_grad: float32 [768], P('vocab')
- out_weight_grad: float32 [768, 768], P('vocab')
- out_bias_grad: float32 [768], P('vocab')
- attn_gain_grad: float32 [768], P('vocab')
- attn_bias_grad: float32 [768], P('vocab')
- up_weight_grad: float32 [768, 3072], P('vocab')
- up_bias_grad: float32 [3072], P('vocab')
- down_weight_grad: float32 [3072, 768], P('vocab')
- down_bias_grad: float32 [768], P('vocab')
- final_gain_grad: float32 [768], P('vocab')
- final_bias_grad: float32 [768], P('vocab')
The draws below stay inside these ranges and needn't reach their ends.
Inputs may be any that keep to these rules, and one draw needn't show every extreme that they name: `token_ids`: among the tokens of one device, at most 256 ids fall into the 3840 rows of word_table that one index of vocab holds; for one such block of rows, the same on every device, exactly 256 do. `lengths`: the tokens at positions from a sequence's length on are padding; some sequence has length 512 and some 20.
All inputs are finite; a program needn't handle non-finite values.
Results may differ from the reference program's by a relative error of at most 0.017.
Values may be sent and summed in bfloat16 or wider, within the bound.
A program may use at most 192 MiB of HBM per device.

```python
from functools import partial
import jax
import jax.numpy as jnp
from jax import lax

D = 768
HEADS = 12
HEAD = 64
FF = 3072
L = 512
TYPES = 2
V = 30720
QLEN = 20
SEQ_DEV = 2
TOK_DEV = 1024
SEQS = 64
ROWS_DEV = 3840
CAP = 256


def draw_token_ids(key, part):
    blocks = SEQS // SEQ_DEV
    owners = V // ROWS_DEV
    hottest = jax.random.randint(jax.random.fold_in(key, 11), (), 0, owners)

    def one_block(block_key):
        block_keys = jax.random.split(block_key, 3)
        slot_holder_index = (jnp.arange(owners * CAP) // CAP + hottest) % owners
        others = jax.random.permutation(block_keys[0], owners * CAP - CAP)[:TOK_DEV - CAP] + CAP
        chosen = jnp.concatenate([jnp.arange(CAP), others])
        picked = jax.random.permutation(block_keys[1], slot_holder_index[chosen])
        offsets = jax.random.randint(block_keys[2], (TOK_DEV,), 0, ROWS_DEV)
        return picked * ROWS_DEV + offsets
    all_keys = jax.random.split(jax.random.fold_in(key, 12), blocks)
    return jax.vmap(one_block)(all_keys).reshape(SEQS, L).astype(jnp.int32)


def draw_lengths(key, part):
    coins = jax.random.randint(jax.random.fold_in(key, 21), (SEQS,), 0, 2)
    longer = jax.random.randint(jax.random.fold_in(key, 22), (SEQS,), QLEN + 1, L + 1)
    drawn = jnp.where(coins == 1, QLEN, longer)
    return drawn.at[0].set(L).at[1].set(QLEN).astype(jnp.int32)


def touch_ends(entries, own_key, low, top_value):
    extent = entries.shape
    spot = [jax.random.randint(jax.random.fold_in(own_key, axis), (), 0, extent[axis]) for axis in range(len(extent))]
    entries = entries.at[tuple(spot)].set(low)
    longest = extent.index(max(extent))
    spot[longest] = (spot[longest] + 1) % extent[longest]
    return entries.at[tuple(spot)].set(top_value)


def strengthened(entries, rng, source, target, shards_of, factor):
    owner, partner = [(jnp.arange(entries.shape[axis_at]) // (entries.shape[axis_at] // shards_of)).reshape([-1 if axis == axis_at else 1 for axis in range(entries.ndim)]) for axis_at in (source, target)]
    chosen = jax.random.permutation(rng, shards_of)[partner]
    strong = (owner == chosen) | (owner == (partner + shards_of // 2) % shards_of)
    return jnp.where(strong, factor * entries, entries)


def steps_of(rng, dims, shards, smallest, largest):
    level = 1.0
    for dim, shards_of in shards:
        steps = jax.random.uniform(jax.random.fold_in(jax.random.fold_in(rng, 6), dim), (shards_of,), jnp.float32, smallest / len(shards), largest / len(shards))
        level = level * jnp.repeat(jnp.exp(steps), dims[dim] // shards_of).reshape((-1,) + (1,) * (len(dims) - 1 - dim))
    return level


def gaussian(own_key, extent, scale, reach, cuts=(), held_as=jnp.bfloat16):
    values = jax.random.normal(own_key, extent, jnp.float32) * scale
    if len(cuts) > 0:
        values = steps_of(own_key, extent, cuts, -0.22, 0.18) * values
    return jnp.clip(values, min=-reach, max=reach).astype(held_as)


def gaussian_with(rng, extent, width, limit, pieces, heavy, kind=jnp.bfloat16):
    values = width * jax.random.normal(rng, extent, jnp.float32)
    if pieces:
        values = values * steps_of(rng, extent, pieces, -0.22, 0.18)
    return jnp.clip(strengthened(values, jax.random.fold_in(rng, 3), *heavy), -limit, limit).astype(kind)


def setup_inputs(seed: int = 0) -> dict:
    arg_keys = jax.random.split(jax.random.key(seed), 25)
    return {
        "token_ids": draw_token_ids(jax.random.fold_in(arg_keys[24], 71), 0),
        "type_ids": touch_ends(jax.random.randint(arg_keys[1], (SEQS, L), 0, TYPES), jax.random.fold_in(arg_keys[1], 1), 0, TYPES - 1).astype(jnp.int32),
        "lengths": draw_lengths(jax.random.fold_in(arg_keys[24], 71), 0),
        "word_table": gaussian(arg_keys[3], (V, D), 1.0, 6.0, ((0, 8),)),
        "pos_table": gaussian(arg_keys[4], (L, D), 0.5, 4.0),
        "token_type_embeddings": gaussian(arg_keys[5], (TYPES, D), 0.5, 4.0),
        "emb_gain": jnp.clip(1.0 + 0.15 * jax.random.normal(arg_keys[6], (D,), jnp.float32), 0.25, 1.75),
        "emb_bias": gaussian(arg_keys[7], (D,), 0.5, 3.0, (), jnp.float32),
        "query_weight": gaussian(arg_keys[8], (D, D), D ** -0.5, 0.21875),
        "query_bias": gaussian(arg_keys[9], (D,), 0.5, 3.0, (), jnp.float32),
        "key_weight": gaussian(arg_keys[10], (D, D), D ** -0.5, 0.21875),
        "value_weight": gaussian(arg_keys[11], (D, D), D ** -0.5, 0.21875),
        "value_bias": gaussian(arg_keys[12], (D,), 0.5, 3.0, (), jnp.float32),
        "out_weight": gaussian(arg_keys[13], (D, D), (D // 16) ** -0.5, 0.875),
        "out_bias": gaussian(arg_keys[14], (D,), 0.5, 3.0, (), jnp.float32),
        "attn_gain": jnp.clip(1.0 + 0.15 * jax.random.normal(arg_keys[15], (D,), jnp.float32), 0.25, 1.75),
        "attn_bias": gaussian(arg_keys[16], (D,), 0.5, 3.0, (), jnp.float32),
        "up_weight": gaussian(arg_keys[17], (D, FF), D ** -0.5, 0.21875),
        "up_bias": gaussian(arg_keys[18], (FF,), 0.5, 3.0, (), jnp.float32),
        "down_weight": gaussian(arg_keys[19], (FF, D), FF ** -0.5, 0.109375),
        "down_bias": gaussian(arg_keys[20], (D,), 0.5, 3.0, (), jnp.float32),
        "final_gain": jnp.clip(1.0 + 0.15 * jax.random.normal(arg_keys[21], (D,), jnp.float32), 0.25, 1.75),
        "final_bias": gaussian(arg_keys[22], (D,), 0.5, 3.0, (), jnp.float32),
        "cotangent": gaussian_with(arg_keys[23], (SEQS, L, D), 1.0, 6.0, ((0, 32),), (0, 2, 32, 2.75)),
    }


@jax.custom_vjp
def low(v):
    return lax.optimization_barrier(v.astype(jnp.bfloat16)).astype(jnp.float32)

@jax.custom_vjp
def reduced_precision_backward(v):
    return v

def low_keep(v):
    return (low(v), None)

def low_pass(kept, grad):
    return (grad,)

def back_keep(v):
    return (v, None)

def back_low(kept, grad):
    return (low(grad),)
low.defvjp(low_keep, low_pass)
reduced_precision_backward.defvjp(back_keep, back_low)
EPSILON = 1e-12

def matmul(left, right):
    return jnp.dot(left, right, precision=lax.Precision.HIGHEST, preferred_element_type=jnp.float32)

def layer_norm(values, gain, bias):
    center = values - lax.optimization_barrier(jnp.mean(values, -1, keepdims=True))
    spread = lax.optimization_barrier(jnp.mean(center * center, -1, keepdims=True))
    return center * lax.rsqrt(spread + EPSILON) * gain + bias

def attend(block):
    query, keys, values, length = block
    scores = jnp.einsum('qhd,khd->hqk', query, keys, precision=lax.Precision.HIGHEST) * HEAD ** (-0.5)
    scores = reduced_precision_backward(scores)
    visible = jnp.arange(L) < length
    scores = jnp.where(visible[None, None, :], scores, -1000000000.0)
    probs = low(jax.nn.softmax(scores, axis=-1))
    return jnp.einsum('hqk,khd->qhd', probs, values, precision=lax.Precision.HIGHEST)

def forward(word_table, pos_table, token_type_embeddings, emb_gain, emb_bias, query_weight, query_bias, key_weight, value_weight, value_bias, out_weight, out_bias, attn_gain, attn_bias, up_weight, up_bias, down_weight, down_bias, final_gain, final_bias, token_ids, type_ids, lengths):
    embedded = word_table[token_ids] + pos_table[None, :, :] + token_type_embeddings[type_ids]
    normed = layer_norm(embedded, emb_gain, emb_bias).reshape(SEQS * L, D)
    normed_low = low(normed)
    query = low(reduced_precision_backward(matmul(normed_low, query_weight)) + query_bias)
    keys = low(reduced_precision_backward(matmul(normed_low, key_weight)))
    values = low(reduced_precision_backward(matmul(normed_low, value_weight)) + value_bias)
    split_shape = (SEQS, L, HEADS, HEAD)
    mixed = lax.map(jax.checkpoint(attend), (query.reshape(split_shape), keys.reshape(split_shape), values.reshape(split_shape), lengths))
    mixed_low = reduced_precision_backward(low(mixed.reshape(SEQS * L, D)))
    first = normed + (reduced_precision_backward(matmul(mixed_low, out_weight)) + out_bias)
    hidden = layer_norm(first, attn_gain, attn_bias)
    upper = reduced_precision_backward(matmul(low(hidden), up_weight)) + up_bias
    active = low(jax.nn.gelu(upper, approximate=False))
    second = hidden + (reduced_precision_backward(matmul(active, down_weight)) + down_bias)
    return layer_norm(second, final_gain, final_bias).reshape(SEQS, L, D)

def reference(token_ids, type_ids, lengths, word_table, pos_table, token_type_embeddings, emb_gain, emb_bias, query_weight, query_bias, key_weight, value_weight, value_bias, out_weight, out_bias, attn_gain, attn_bias, up_weight, up_bias, down_weight, down_bias, final_gain, final_bias, cotangent):
    floats = (word_table, pos_table, token_type_embeddings, emb_gain, emb_bias, query_weight, query_bias, key_weight, value_weight, value_bias, out_weight, out_bias, attn_gain, attn_bias, up_weight, up_bias, down_weight, down_bias, final_gain, final_bias)
    floats = tuple((item.astype(jnp.float32) for item in floats))
    encoded, pull = jax.vjp(partial(forward, token_ids=token_ids, type_ids=type_ids, lengths=lengths), *floats)
    grads = pull(cotangent.astype(jnp.float32))
    word_grad, pos_grad, type_grad, emb_gain_grad, emb_bias_grad, query_weight_grad, query_bias_grad, key_weight_grad, value_weight_grad, value_bias_grad, out_weight_grad, out_bias_grad, attn_gain_grad, attn_bias_grad, up_weight_grad, up_bias_grad, down_weight_grad, down_bias_grad, final_gain_grad, final_bias_grad = grads
    return (encoded, word_grad, pos_grad, type_grad, emb_gain_grad, emb_bias_grad, query_weight_grad, query_bias_grad, key_weight_grad, value_weight_grad, value_bias_grad, out_weight_grad, out_bias_grad, attn_gain_grad, attn_bias_grad, up_weight_grad, up_bias_grad, down_weight_grad, down_bias_grad, final_gain_grad, final_bias_grad)
```

```python
from functools import partial

import jax
import jax.numpy as jnp
from jax import lax
from jax.sharding import PartitionSpec as P

HEADS = 12
HEAD = 64
L = 512


EPSILON = 1e-12


def layer_norm(values, gain, bias):
    center = values - jnp.mean(values, -1, keepdims=True)
    spread = jnp.mean(center * center, -1, keepdims=True)
    return center * lax.rsqrt(spread + EPSILON) * gain + bias


def matmul(left, right):
    return jnp.dot(left, right, preferred_element_type=jnp.float32)


def matmul_tn(left, right):
    return lax.dot_general(
        left, right, (((0,), (0,)), ((), ())), preferred_element_type=jnp.float32
    )


def matmul_nt(left, right):
    return lax.dot_general(
        left, right, (((1,), (1,)), ((), ())), preferred_element_type=jnp.float32
    )


def masked_scores(query, keys, length):
    scores = jnp.einsum("qhd,khd->hqk", query, keys, preferred_element_type=jnp.float32) * HEAD ** (
        -0.5
    )
    visible = jnp.arange(L) < length
    return jnp.where(visible[None, None, :], scores, -1000000000.0)


def attend_forward(block):
    query, keys, values, length = block
    scores = masked_scores(query, keys, length)
    highest = jnp.max(scores, -1, keepdims=True)
    expd = jnp.exp(scores - highest)
    totals = jnp.sum(expd, -1, keepdims=True)
    probs_low = (expd / totals).astype(jnp.bfloat16)
    mixed = jnp.einsum("hqk,khd->qhd", probs_low, values, preferred_element_type=jnp.float32)
    return (mixed.astype(jnp.bfloat16), highest + jnp.log(totals))


def attend_backward(block):
    query, keys, values, grad_mixed, logsum, length = block
    probs = jnp.exp(masked_scores(query, keys, length) - logsum)
    probs_low = probs.astype(jnp.bfloat16)
    grad_values = jnp.einsum(
        "hqk,qhd->khd", probs_low, grad_mixed, preferred_element_type=jnp.float32
    )
    grad_probs = jnp.einsum("qhd,khd->hqk", grad_mixed, values, preferred_element_type=jnp.float32)
    inner = jnp.sum(grad_probs * probs, -1, keepdims=True)
    grad_scores = (probs * (grad_probs - inner)).astype(jnp.bfloat16)
    scale = HEAD ** (-0.5)
    grad_query = (
        jnp.einsum("hqk,khd->qhd", grad_scores, keys, preferred_element_type=jnp.float32) * scale
    )
    grad_keys = (
        jnp.einsum("hqk,qhd->khd", grad_scores, query, preferred_element_type=jnp.float32) * scale
    )
    return (grad_query, grad_keys, grad_values)


def swap(value, axis_name, bit):
    size = lax.axis_size(axis_name)
    return lax.ppermute(value, axis_name, [(i, i ^ bit) for i in range(size)])


def pick(value, index, axis):
    return lax.dynamic_index_in_dim(value, index, axis, keepdims=False)


def plus(left, right):
    return (left.astype(jnp.float32) + right.astype(jnp.float32)).astype(jnp.bfloat16)


def dp_bits():
    index = lax.axis_index("dp")
    return lax.rem(index, 2), index // 2


def reorder(own, across_x, across_y, across_both):
    xb, yb = dp_bits()
    flip_x, flip_y = xb == 1, yb == 1
    rows = [[own, across_y], [across_x, across_both]]
    rows = [
        [jnp.where(flip_x, rows[1 - i][j], rows[i][j]) for j in range(2)] for i in range(2)
    ]
    rows = [
        [jnp.where(flip_y, rows[i][1 - j], rows[i][j]) for j in range(2)] for i in range(2)
    ]
    return rows


def sum_over_all(grad):
    size = lax.axis_size("vocab")
    me = lax.axis_index("vocab")
    core = lax.rem(me, 2)
    place = me // 2
    places = size // 2
    total, n = grad.shape
    r = total // size
    xb, yb = dp_bits()
    grad = grad.reshape(places, 2, r, n)
    other = swap(pick(grad, 1 - core, 1), "vocab", 1)
    held = plus(pick(grad, core, 1), other).reshape(places, 2, 2, r // 4, n)
    first, last = held[: places // 2], held[places // 2 :]
    first_in = swap(pick(first, 1 - xb, 1), "dp", 1)
    last_in = swap(pick(last, 1 - yb, 2), "dp", 2)
    first = plus(pick(first, xb, 1), first_in)
    last = plus(pick(last, yb, 2), last_in)
    first_in = swap(pick(first, 1 - yb, 1), "dp", 2)
    last_in = swap(pick(last, 1 - xb, 1), "dp", 1)
    first = plus(pick(first, yb, 1), first_in)
    last = plus(pick(last, xb, 1), last_in)
    held = jnp.concatenate([first, last], 0)
    summed = pick(held, place, 0).astype(jnp.float32)
    for step in range(1, places):
        block = pick(held, lax.rem(place + step, places), 0)
        block = lax.ppermute(
            block, "vocab", [(i, (i + 2 * step) % size) for i in range(size)]
        )
        summed = summed + block.astype(jnp.float32)
    own = summed.astype(jnp.bfloat16)
    across_x = swap(own, "dp", 1)
    across_y = swap(own, "dp", 2)
    half = n // 2
    both = jnp.concatenate(
        [swap(across_x[:, :half], "dp", 2), swap(across_y[:, half:], "dp", 1)], 1
    )
    rows = reorder(own, across_x, across_y, both)
    return jnp.stack([rows[0][0], rows[0][1], rows[1][0], rows[1][1]]).reshape(r, n).astype(jnp.float32)


def sum_over_dp(grad):
    rows, n = grad.shape
    xb, yb = dp_bits()
    held = grad.reshape(2, 2, 2, rows // 8, n)
    first, last = held[0], held[1]
    first_in = swap(pick(first, 1 - xb, 0), "dp", 1)
    last_in = swap(pick(last, 1 - yb, 1), "dp", 2)
    first = plus(pick(first, xb, 0), first_in)
    last = plus(pick(last, yb, 1), last_in)
    first_in = swap(pick(first, 1 - yb, 0), "dp", 2)
    last_in = swap(pick(last, 1 - xb, 0), "dp", 1)
    first = plus(pick(first, yb, 0), first_in)
    last = plus(pick(last, xb, 0), last_in)
    first_x = swap(first, "dp", 1)
    last_y = swap(last, "dp", 2)
    first_y = swap(jnp.stack([first, first_x]), "dp", 2)
    last_x = swap(jnp.stack([last, last_y]), "dp", 1)
    a = reorder(first, first_x, first_y[0], first_y[1])
    b = reorder(last, last_x[0], last_y, last_x[1])
    parts = [p for group in (a, b) for line in group for p in line]
    return jnp.concatenate(parts, 0).astype(jnp.float32)


def local(
    token_ids,
    type_ids,
    lengths,
    word_table,
    pos_table,
    token_type_embeddings,
    emb_gain,
    emb_bias,
    query_weight,
    query_bias,
    key_weight,
    value_weight,
    value_bias,
    out_weight,
    out_bias,
    attn_gain,
    attn_bias,
    up_weight,
    up_bias,
    down_weight,
    down_bias,
    final_gain,
    final_bias,
    cotangent,
):
    seq_count, seq_len = token_ids.shape
    tokens = seq_count * seq_len
    width = word_table.shape[1]
    rows_local = word_table.shape[0]
    owners = lax.axis_size("vocab")
    capacity = max(2, 2 * tokens // owners)
    flat_ids = token_ids.reshape(tokens)
    owner = flat_ids // rows_local
    member = (owner[:, None] == jnp.arange(owners)[None, :]).astype(jnp.int32)
    earlier = jnp.cumsum(member, 0) - member
    rank = jnp.sum(earlier * member, 1)
    slot = owner * capacity + rank
    requests = (
        jnp.full((owners * capacity,), -1, jnp.int32).at[slot].set(flat_ids - owner * rows_local)
    )
    requests = requests.reshape(owners, capacity)
    asked = lax.all_to_all(requests, "vocab", split_axis=0, concat_axis=0, tiled=True)
    valid = asked >= 0
    found = word_table[jnp.maximum(asked, 0)]
    found = jnp.where(valid[..., None], found, jnp.zeros((), jnp.bfloat16))
    returned = lax.all_to_all(found, "vocab", split_axis=0, concat_axis=0, tiled=True)
    word_rows = returned.reshape(owners * capacity, width)[slot]
    kinds = token_type_embeddings.shape[0]
    selection_matrix = (type_ids[..., None] == jnp.arange(kinds)[None, None, :]).astype(jnp.float32)
    type_rows = jnp.einsum(
        "tcr,rb->tcb",
        selection_matrix,
        token_type_embeddings.astype(jnp.float32),
        precision=lax.Precision.HIGHEST,
    )
    embedded = (
        word_rows.reshape(seq_count, seq_len, width).astype(jnp.float32)
        + pos_table.astype(jnp.float32)[None]
        + type_rows
    )
    normed = layer_norm(embedded, emb_gain, emb_bias).reshape(tokens, width)
    normed_low = normed.astype(jnp.bfloat16)
    query = (matmul(normed_low, query_weight) + query_bias).astype(jnp.bfloat16)
    keys = matmul(normed_low, key_weight).astype(jnp.bfloat16)
    values = (matmul(normed_low, value_weight) + value_bias).astype(jnp.bfloat16)
    split_shape = (seq_count, seq_len, HEADS, HEAD)
    query_split = query.reshape(split_shape)
    keys_split = keys.reshape(split_shape)
    values_split = values.reshape(split_shape)
    mixed, logsum = lax.map(attend_forward, (query_split, keys_split, values_split, lengths))
    mixed_low = mixed.reshape(tokens, width)
    first = normed + matmul(mixed_low, out_weight) + out_bias
    hidden = layer_norm(first, attn_gain, attn_bias)
    hidden_reduced_precision = hidden.astype(jnp.bfloat16)
    upper = matmul(hidden_reduced_precision, up_weight) + up_bias
    active_low = jax.nn.gelu(upper, approximate=False).astype(jnp.bfloat16)
    second = hidden + matmul(active_low, down_weight) + down_bias
    encoded = layer_norm(second, final_gain, final_bias)
    grad_out = cotangent.reshape(tokens, width).astype(jnp.float32)
    _, final_pull = jax.vjp(layer_norm, second, final_gain, final_bias)
    grad_second, grad_final_gain, grad_final_bias = final_pull(grad_out)
    grad_down_bias = jnp.sum(grad_second, 0)
    second_matmul_gradient_reduced = grad_second.astype(jnp.bfloat16)
    grad_down = matmul_tn(active_low, second_matmul_gradient_reduced)
    grad_active = matmul_nt(second_matmul_gradient_reduced, down_weight)
    _, gelu_pull = jax.vjp(partial(jax.nn.gelu, approximate=False), upper)
    (grad_upper,) = gelu_pull(grad_active)
    grad_up_bias = jnp.sum(grad_upper, 0)
    grad_upper_low = grad_upper.astype(jnp.bfloat16)
    grad_up = matmul_tn(hidden_reduced_precision, grad_upper_low)
    grad_hidden = grad_second + matmul_nt(grad_upper_low, up_weight)
    _, attn_pull = jax.vjp(layer_norm, first, attn_gain, attn_bias)
    grad_first, grad_attn_gain, grad_attn_bias = attn_pull(grad_hidden)
    grad_out_bias = jnp.sum(grad_first, 0)
    grad_first_low = grad_first.astype(jnp.bfloat16)
    grad_out_weight = matmul_tn(mixed_low, grad_first_low)
    grad_mixed = matmul_nt(grad_first_low, out_weight).astype(jnp.bfloat16)
    grad_query, grad_keys, grad_values = lax.map(
        attend_backward,
        (query_split, keys_split, values_split, grad_mixed.reshape(split_shape), logsum, lengths),
    )
    grad_query = grad_query.reshape(tokens, width)
    grad_keys = grad_keys.reshape(tokens, width)
    grad_values = grad_values.reshape(tokens, width)
    grad_query_bias = jnp.sum(grad_query, 0)
    grad_value_bias = jnp.sum(grad_values, 0)
    grad_query_low = grad_query.astype(jnp.bfloat16)
    grad_keys_low = grad_keys.astype(jnp.bfloat16)
    grad_values_low = grad_values.astype(jnp.bfloat16)
    grad_query_weight = matmul_tn(normed_low, grad_query_low)
    grad_key_weight = matmul_tn(normed_low, grad_keys_low)
    grad_value_weight = matmul_tn(normed_low, grad_values_low)
    grad_normed = (
        grad_first
        + matmul_nt(grad_query_low, query_weight)
        + matmul_nt(grad_keys_low, key_weight)
        + matmul_nt(grad_values_low, value_weight)
    )
    _, emb_pull = jax.vjp(layer_norm, embedded, emb_gain, emb_bias)
    embedding_output_gradient, grad_emb_gain, grad_emb_bias = emb_pull(
        grad_normed.reshape(seq_count, seq_len, width)
    )
    grad_pos = jnp.sum(embedding_output_gradient, 0)
    token_type_gradient = jnp.einsum(
        "nox,noh->xh", selection_matrix, embedding_output_gradient, precision=lax.Precision.HIGHEST
    )
    bf = jnp.bfloat16
    per = width // owners
    grad_down_all = sum_over_all(grad_down.astype(bf))
    grad_up_all = sum_over_all(grad_up.astype(bf))
    places = slot[None, :] == jnp.arange(owners * capacity)[:, None]
    outgoing = matmul(
        places.astype(bf), embedding_output_gradient.reshape(tokens, width).astype(bf)
    ).astype(bf)
    hits = (jnp.arange(rows_local)[:, None] == asked.reshape(-1)[None, :]).astype(bf)
    pieces = []
    step = 256
    for start in range(0, width, step):
        incoming = lax.all_to_all(
            outgoing[:, start : start + step].reshape(owners, capacity, step),
            "vocab",
            split_axis=0,
            concat_axis=0,
            tiled=True,
        )
        dense = matmul(hits, incoming.reshape(owners * capacity, step)).astype(bf)
        pieces.append(sum_over_dp(dense))
    grad_word = jnp.concatenate(pieces, 1)
    small = jnp.stack(
        [
            grad_query_bias,
            grad_value_bias,
            grad_out_bias,
            grad_attn_gain,
            grad_attn_bias,
            grad_emb_gain,
            grad_emb_bias,
            grad_down_bias,
            grad_final_gain,
            grad_final_bias,
            token_type_gradient[0],
            token_type_gradient[1],
        ]
    )
    small = small.reshape(12, owners, per).transpose(1, 0, 2).reshape(owners, 12 * per)
    small = jnp.concatenate([small, grad_up_bias.reshape(owners, 4 * per)], 1)
    wide = 4 * width
    lines = (seq_len // owners) * width // wide
    rest = per // 3 - lines
    small_lines = jnp.pad(small, ((0, 0), (0, rest * wide - 16 * per))).reshape(owners, rest, wide)
    mixed_grads = jnp.concatenate(
        [grad_query_weight, grad_key_weight, grad_value_weight, grad_out_weight], 1
    ).astype(bf)
    packed = jnp.concatenate(
        [
            mixed_grads.reshape(owners, per, wide),
            grad_pos.astype(bf).reshape(owners, lines, wide),
            small_lines.astype(bf),
        ],
        1,
    )
    packed = sum_over_all(packed.reshape(-1, wide))
    weights = packed[:per]
    grad_query_weight = weights[:, :width]
    grad_key_weight = weights[:, width : 2 * width]
    grad_value_weight = weights[:, 2 * width : 3 * width]
    grad_out_weight = weights[:, 3 * width :]
    grad_pos = packed[per : per + lines].reshape(seq_len // owners, width)
    small = packed[per + lines :].reshape(-1)[: 16 * per].reshape(16, per)
    (
        grad_query_bias,
        grad_value_bias,
        grad_out_bias,
        grad_attn_gain,
        grad_attn_bias,
        grad_emb_gain,
        grad_emb_bias,
        grad_down_bias,
        grad_final_gain,
        grad_final_bias,
    ) = [small[i] for i in range(10)]
    token_type_gradient = small[10:12]
    grad_up_bias = small[12:].reshape(-1)
    grad_up, grad_down = grad_up_all, grad_down_all
    return (
        encoded.reshape(seq_count, seq_len, width),
        grad_word,
        grad_pos,
        token_type_gradient,
        grad_emb_gain,
        grad_emb_bias,
        grad_query_weight,
        grad_query_bias,
        grad_key_weight,
        grad_value_weight,
        grad_value_bias,
        grad_out_weight,
        grad_out_bias,
        grad_attn_gain,
        grad_attn_bias,
        grad_up,
        grad_up_bias,
        grad_down,
        grad_down_bias,
        grad_final_gain,
        grad_final_bias,
    )


def solution(mesh):
    placed = (
        P(("dp", "vocab"), None),
        P(("dp", "vocab"), None),
        P(("dp", "vocab")),
        P("vocab", None),
        P(),
        P(),
        P(),
        P(),
        P(),
        P(),
        P(),
        P(),
        P(),
        P(),
        P(),
        P(),
        P(),
        P(),
        P(),
        P(),
        P(),
        P(),
        P(),
        P(("dp", "vocab"), None, None),
    )
    return jax.shard_map(
        local,
        mesh=mesh,
        in_specs=placed,
        out_specs=(
            P(("dp", "vocab"), None, None),
            P("vocab", None),
            P("vocab", None),
            P(None, "vocab"),
            P("vocab"),
            P("vocab"),
            P("vocab", None),
            P("vocab"),
            P("vocab", None),
            P("vocab", None),
            P("vocab"),
            P("vocab", None),
            P("vocab"),
            P("vocab"),
            P("vocab"),
            P("vocab", None),
            P("vocab"),
            P("vocab", None),
            P("vocab"),
            P("vocab"),
            P("vocab"),
        ),
        check_vma=False,
    )
```

```python
from functools import partial

import jax
import jax.numpy as jnp
from jax import lax
from jax.experimental import pallas as pl
from jax.experimental.pallas import tpu as pltpu
from jax.sharding import PartitionSpec as P

HEADS = 12
HEAD = 64
L = 512


EPSILON = 1e-12


def layer_norm(values, gain, bias):
    center = values - jnp.mean(values, -1, keepdims=True)
    spread = jnp.mean(center * center, -1, keepdims=True)
    return center * lax.rsqrt(spread + EPSILON) * gain + bias


def matmul(left, right):
    return jnp.dot(left, right, preferred_element_type=jnp.float32)


def matmul_tn(left, right):
    return lax.dot_general(
        left, right, (((0,), (0,)), ((), ())), preferred_element_type=jnp.float32
    )


def matmul_nt(left, right):
    return lax.dot_general(
        left, right, (((1,), (1,)), ((), ())), preferred_element_type=jnp.float32
    )


def masked_scores(query, keys, length):
    scores = jnp.einsum("qhd,khd->hqk", query, keys, preferred_element_type=jnp.float32) * HEAD ** (
        -0.5
    )
    visible = jnp.arange(L) < length
    return jnp.where(visible[None, None, :], scores, -1000000000.0)


def attend_forward(block):
    query, keys, values, length = block
    scores = masked_scores(query, keys, length)
    highest = jnp.max(scores, -1, keepdims=True)
    expd = jnp.exp(scores - highest)
    totals = jnp.sum(expd, -1, keepdims=True)
    probs_low = (expd / totals).astype(jnp.bfloat16)
    mixed = jnp.einsum("hqk,khd->qhd", probs_low, values, preferred_element_type=jnp.float32)
    return (mixed.astype(jnp.bfloat16), highest + jnp.log(totals))


def attend_backward(block):
    query, keys, values, grad_mixed, logsum, length = block
    probs = jnp.exp(masked_scores(query, keys, length) - logsum)
    probs_low = probs.astype(jnp.bfloat16)
    grad_values = jnp.einsum(
        "hqk,qhd->khd", probs_low, grad_mixed, preferred_element_type=jnp.float32
    )
    grad_probs = jnp.einsum("qhd,khd->hqk", grad_mixed, values, preferred_element_type=jnp.float32)
    inner = jnp.sum(grad_probs * probs, -1, keepdims=True)
    grad_scores = (probs * (grad_probs - inner)).astype(jnp.bfloat16)
    scale = HEAD ** (-0.5)
    grad_query = (
        jnp.einsum("hqk,khd->qhd", grad_scores, keys, preferred_element_type=jnp.float32) * scale
    )
    grad_keys = (
        jnp.einsum("hqk,qhd->khd", grad_scores, query, preferred_element_type=jnp.float32) * scale
    )
    return (grad_query, grad_keys, grad_values)


def swap(value, axis_name, bit):
    size = lax.axis_size(axis_name)
    return lax.ppermute(value, axis_name, [(i, i ^ bit) for i in range(size)])


def pick(value, index, axis):
    return lax.dynamic_index_in_dim(value, index, axis, keepdims=False)


def plus(left, right):
    return (left.astype(jnp.float32) + right.astype(jnp.float32)).astype(jnp.bfloat16)


def dp_bits():
    index = lax.axis_index("dp")
    return lax.rem(index, 2), index // 2


def reorder(own, across_x, across_y, across_both):
    xb, yb = dp_bits()
    flip_x, flip_y = xb == 1, yb == 1
    rows = [[own, across_y], [across_x, across_both]]
    rows = [
        [jnp.where(flip_x, rows[1 - i][j], rows[i][j]) for j in range(2)] for i in range(2)
    ]
    rows = [
        [jnp.where(flip_y, rows[i][1 - j], rows[i][j]) for j in range(2)] for i in range(2)
    ]
    return rows


def sum_over_all(grad):
    size = lax.axis_size("vocab")
    me = lax.axis_index("vocab")
    core = lax.rem(me, 2)
    place = me // 2
    places = size // 2
    total, n = grad.shape
    r = total // size
    xb, yb = dp_bits()
    grad = grad.reshape(places, 2, r, n)
    other = swap(pick(grad, 1 - core, 1), "vocab", 1)
    held = plus(pick(grad, core, 1), other).reshape(places, 2, 2, r // 4, n)
    first, last = held[: places // 2], held[places // 2 :]
    first_in = swap(pick(first, 1 - xb, 1), "dp", 1)
    last_in = swap(pick(last, 1 - yb, 2), "dp", 2)
    first = plus(pick(first, xb, 1), first_in)
    last = plus(pick(last, yb, 2), last_in)
    first_in = swap(pick(first, 1 - yb, 1), "dp", 2)
    last_in = swap(pick(last, 1 - xb, 1), "dp", 1)
    first = plus(pick(first, yb, 1), first_in)
    last = plus(pick(last, xb, 1), last_in)
    held = jnp.concatenate([first, last], 0)
    summed = pick(held, place, 0).astype(jnp.float32)
    for step in range(1, places):
        block = pick(held, lax.rem(place + step, places), 0)
        block = lax.ppermute(
            block, "vocab", [(i, (i + 2 * step) % size) for i in range(size)]
        )
        summed = summed + block.astype(jnp.float32)
    own = summed.astype(jnp.bfloat16)
    across_x = swap(own, "dp", 1)
    across_y = swap(own, "dp", 2)
    half = n // 2
    both = jnp.concatenate(
        [swap(across_x[:, :half], "dp", 2), swap(across_y[:, half:], "dp", 1)], 1
    )
    rows = reorder(own, across_x, across_y, both)
    return jnp.stack([rows[0][0], rows[0][1], rows[1][0], rows[1][1]]).reshape(r, n).astype(jnp.float32)


def sum_over_dp(grad):
    rows, n = grad.shape
    xb, yb = dp_bits()
    held = grad.reshape(2, 2, 2, rows // 8, n)
    first, last = held[0], held[1]
    first_in = swap(pick(first, 1 - xb, 0), "dp", 1)
    last_in = swap(pick(last, 1 - yb, 1), "dp", 2)
    first = plus(pick(first, xb, 0), first_in)
    last = plus(pick(last, yb, 1), last_in)
    first_in = swap(pick(first, 1 - yb, 0), "dp", 2)
    last_in = swap(pick(last, 1 - xb, 0), "dp", 1)
    first = plus(pick(first, yb, 0), first_in)
    last = plus(pick(last, xb, 0), last_in)
    first_x = swap(first, "dp", 1)
    last_y = swap(last, "dp", 2)
    first_y = swap(jnp.stack([first, first_x]), "dp", 2)
    last_x = swap(jnp.stack([last, last_y]), "dp", 1)
    a = reorder(first, first_x, first_y[0], first_y[1])
    b = reorder(last, last_x[0], last_y, last_x[1])
    parts = [p for group in (a, b) for line in group for p in line]
    return jnp.concatenate(parts, 0).astype(jnp.float32)


MESH = pl.DeviceIdType.MESH
BF = jnp.bfloat16
F32 = jnp.float32


def flipped(index, bits):
    out = 0
    for place in range(3):
        bit = lax.rem(lax.div(index, 1 << place), 2)
        out = out + (1 << place) * (1 - bit if (bits >> place) & 1 else bit)
    return out


ORDER = (6, 7, 4, 5, 2, 3, 1)


def tail_kernel(
    demb, slot, asked, small, normed, mixed, gfirst, dq, dk, dv,
    word, packed,
    og, inc, hits, dense, r1a, r1b, r2a, r2b,
    ops, turned, wbuf, wcore, w1a, w1b, w2a, w2b, wz, wown,
    load_sem, z_send, z_recv, d_send, d_recv, w_send, w_recv, own_sem,
):
    owners, cap = og.shape[1], og.shape[2]
    chunks, cols = og.shape[0], og.shape[3]
    tokens = demb.shape[0]
    part = dense.shape[4]
    me = lax.axis_index("vocab")
    spot = lax.axis_index("dp")
    core, place = lax.rem(me, 2), lax.div(me, 2)
    xb, yb = lax.rem(spot, 2), lax.div(spot, 2)
    across_x = {"dp": spot + 1 - 2 * xb}
    across_y = {"dp": spot + 2 - 4 * yb}

    loads = [
        pltpu.make_async_copy(ref, ops.at[i], load_sem.at[i])
        for i, ref in enumerate((normed, dq, dk, dv, mixed, gfirst))
    ]
    for load in loads:
        load.start()
    barrier = pltpu.get_barrier_semaphore()
    for k in ORDER:
        pl.semaphore_signal(barrier, inc=1, device_id={"vocab": flipped(me, k)}, device_id_type=MESH)
    for peer in (across_x, across_y):
        pl.semaphore_signal(barrier, inc=1, device_id=peer, device_id_type=MESH)
    pl.semaphore_wait(barrier, len(ORDER) + 2)

    def remote(src, dst, send, recv, peer):
        return pltpu.make_async_remote_copy(
            src_ref=src, dst_ref=dst, send_sem=send, recv_sem=recv, device_id=peer, device_id_type=MESH
        )

    def row_copy(c, k):
        peer = flipped(me, k)
        return remote(
            og.at[c, peer], inc.at[c, me], z_send.at[c, k], z_recv.at[c, k], {"vocab": peer}
        )

    def slots_of(peer):
        wanted = lax.broadcasted_iota(jnp.int32, (cap, tokens), 0) + peer * cap
        hot = jnp.where(wanted == slot[...], 1.0, 0.0).astype(BF)
        return jnp.dot(hot, demb[...], preferred_element_type=F32).astype(BF)

    for k in ORDER:
        peer = flipped(me, k)
        rows = slots_of(peer)
        for c in range(chunks):
            og[c, peer] = rows[:, c * cols : (c + 1) * cols]
        row_copy(0, k).start()
    rows = slots_of(me)
    for c in range(chunks):
        inc[c, me] = rows[:, c * cols : (c + 1) * cols]

    width = demb.shape[1]
    per = width // owners
    block = 256

    def turn(which):
        for i in range(tokens // block):
            for j in range(width // block):
                turned[pl.ds(j * block, block), pl.ds(i * block, block)] = ops[
                    which, pl.ds(i * block, block), pl.ds(j * block, block)
                ].T

    def weight(which, at):
        def one(n, carry):
            there = pl.multiple_of(n * block, block)
            out = jnp.dot(turned[...], ops[which, :, pl.ds(there, block)], preferred_element_type=F32).astype(BF)
            there = pl.multiple_of(at * width + n * block, block)
            for v in range(owners):
                wbuf[v // 2, v % 2, pl.ds(0, per), pl.ds(there, block)] = out[v * per : (v + 1) * per]
            return carry

        lax.fori_loop(0, width // block, one, 0)

    loads[0].wait()
    turn(0)
    for i in range(3):
        loads[1 + i].wait()
        weight(1 + i, i)
    loads[4].wait()
    turn(4)
    loads[5].wait()
    weight(5, 3)
    half = tokens // 2
    lines = half // owners // 4
    for v in range(owners):
        for j in range(4):
            at = v * (half // owners) + j * lines
            total = demb[pl.ds(at, lines), :].astype(F32) + demb[pl.ds(half + at, lines), :].astype(F32)
            wbuf[v // 2, v % 2, pl.ds(per, lines), pl.ds(j * width, width)] = total.astype(BF)
        wbuf[v // 2, v % 2, pl.ds(per + lines, 16), :] = jnp.zeros((16, 4 * width), BF)
        wbuf[v // 2, v % 2, pl.ds(per + lines, 16), pl.ds(0, 128)] = jnp.pad(
            small[:, v * per : (v + 1) * per], ((0, 0), (0, 128 - per))
        ).astype(BF)
    partner = {"vocab": flipped(me, 1)}
    core_copy = remote(wbuf.at[:, 1 - core], wcore, w_send.at[0], w_recv.at[0], partner)
    core_copy.start()

    tile = 240
    rows_local = 8 * part

    def match(t, carry):
        at = pl.multiple_of(t * tile, tile)
        row = lax.broadcasted_iota(jnp.int32, (tile, owners * cap), 0) + at
        hits[pl.ds(at, tile), :] = jnp.where(row == asked[...], 1.0, 0.0).astype(BF)
        return carry

    lax.fori_loop(0, rows_local // tile, match, 0)

    quarter = wown.shape[0]
    def w_view(z, x, y):
        return wbuf.at[z, core, pl.ds(pl.multiple_of((2 * x + y) * quarter, quarter), quarter), :]

    def w_half(z, x):
        return wbuf.at[z, core, pl.ds(pl.multiple_of(2 * x * quarter, quarter), 2 * quarter), :]

    def core_sum(i, carry):
        z = lax.div(i, 4)
        at = pl.multiple_of(lax.rem(i, 4) * quarter, quarter)
        mine = wbuf[z, core, pl.ds(at, quarter), :].astype(F32)
        wbuf[z, core, pl.ds(at, quarter), :] = (mine + wcore[z, pl.ds(at, quarter), :].astype(F32)).astype(BF)
        return carry

    def first_weights():
        copies = []
        for z in range(2):
            copies.append(remote(w_half(z, 1 - xb), w1a.at[z], w_send.at[1 + z], w_recv.at[1 + z], across_x))
            for x in range(2):
                at = 2 * z + x
                copies.append(
                    remote(w_view(2 + z, x, 1 - yb), w1b.at[z, x], w_send.at[3 + at], w_recv.at[3 + at], across_y)
                )
        return copies

    def add_to(z, x, y, value):
        view = w_view(z, x, y)
        view[...] = (view[...].astype(F32) + value.astype(F32)).astype(BF)

    def second_weights():
        copies = []
        for z in range(2):
            copies.append(remote(w_view(z, xb, 1 - yb), w2a.at[z], w_send.at[7 + z], w_recv.at[7 + z], across_y))
            copies.append(remote(w_view(2 + z, 1 - xb, yb), w2b.at[z], w_send.at[9 + z], w_recv.at[9 + z], across_x))
        return copies

    def place_copy(k):
        to = flipped(place, k)
        return remote(
            w_view(to, xb, yb), wz.at[k - 1], w_send.at[10 + k], w_recv.at[10 + k], {"vocab": 2 * to + core}
        )

    def third_weights():
        return [place_copy(k) for k in (3, 2, 1)]

    def own_weights():
        return pltpu.make_async_copy(wown, packed.at[xb, yb], own_sem.at[0])

    def fourth_weights():
        return [
            remote(wown, packed.at[xb, yb], w_send.at[14], w_recv.at[14], across_x),
            remote(wown, packed.at[xb, yb], w_send.at[15], w_recv.at[15], across_y),
        ]

    wide = 2 * width

    def fifth_weights():
        left, right = pl.ds(0, wide), pl.ds(wide, wide)
        return [
            remote(
                packed.at[1 - xb, yb, :, left], packed.at[1 - xb, yb, :, left], w_send.at[16], w_recv.at[16], across_y
            ),
            remote(
                packed.at[xb, 1 - yb, :, right], packed.at[xb, 1 - yb, :, right], w_send.at[17], w_recv.at[17], across_x
            ),
        ]

    def first_rows(c):
        return [
            remote(dense.at[c, 0, 1 - xb], r1a.at[c], d_send.at[c, 0], d_recv.at[c, 0], across_x),
            remote(dense.at[c, 1, :, 1 - yb], r1b.at[c], d_send.at[c, 1], d_recv.at[c, 1], across_y),
        ]

    def second_rows(c):
        return [
            remote(dense.at[c, 0, xb, 1 - yb], r2a.at[c], d_send.at[c, 2], d_recv.at[c, 2], across_y),
            remote(dense.at[c, 1, 1 - xb, yb], r2b.at[c], d_send.at[c, 3], d_recv.at[c, 3], across_x),
        ]

    def spread(c):
        return pl.ds(c * cols, cols)

    def own_rows(c):
        return [
            pltpu.make_async_copy(dense.at[c, h, xb, yb], word.at[h, xb, yb, :, spread(c)], own_sem.at[1 + 2 * c + h])
            for h in range(2)
        ]

    def third_rows(c):
        return [
            remote(dense.at[c, 0, xb, yb], word.at[0, xb, yb, :, spread(c)], d_send.at[c, 4], d_recv.at[c, 4], across_x),
            remote(dense.at[c, 1, xb, yb], word.at[1, xb, yb, :, spread(c)], d_send.at[c, 5], d_recv.at[c, 5], across_y),
        ]

    def fourth_rows(c):
        return [
            remote(
                word.at[0, :, yb, :, spread(c)], word.at[0, :, yb, :, spread(c)], d_send.at[c, 6], d_recv.at[c, 6], across_y
            ),
            remote(
                word.at[1, xb, :, :, spread(c)], word.at[1, xb, :, :, spread(c)], d_send.at[c, 7], d_recv.at[c, 7], across_x
            ),
        ]

    def start(copies):
        for copy in copies:
            copy.start()

    def arrived(copies):
        for copy in copies:
            copy.wait_recv()

    def gone(copies):
        for copy in copies:
            copy.wait_send()

    def arrive_slots(c):
        for k in ORDER:
            row_copy(c, k).wait_recv()

    def sum_slots(c):
        def one(t, carry):
            h, x, y = lax.div(t, 4), lax.rem(lax.div(t, 2), 2), lax.rem(t, 2)
            at = pl.multiple_of(t * part, part)
            total = jnp.zeros((part, cols), F32)
            for p in range(owners):
                total = total + jnp.dot(
                    hits[pl.ds(at, part), pl.ds(p * cap, cap)], inc[c, p], preferred_element_type=F32
                )
            dense[c, h, x, y] = total.astype(BF)
            return carry

        lax.fori_loop(0, 8, one, 0)

    def add_rows(c, h, x, y, value):
        dense[c, h, x, y] = (dense[c, h, x, y].astype(F32) + value.astype(F32)).astype(BF)

    def add_first(c):
        arrived(first_rows(c))
        for i in range(2):
            add_rows(c, 0, xb, i, r1a[c, i])
            add_rows(c, 1, i, yb, r1b[c, i])
        start(second_rows(c))

    def add_second(c):
        arrived(second_rows(c))
        add_rows(c, 0, xb, yb, r2a[c])
        add_rows(c, 1, xb, yb, r2b[c])
        start(third_rows(c))
        start(own_rows(c))

    def pass_on(c):
        for copy in own_rows(c):
            copy.wait()
        arrived(third_rows(c))
        start(fourth_rows(c))

    core_copy.wait_recv()
    core_copy.wait_send()
    lax.fori_loop(0, 16, core_sum, 0)
    start(first_weights())

    arrive_slots(0)
    for k in ORDER:
        row_copy(1, k).start()
    sum_slots(0)
    start(first_rows(0))

    arrived(first_weights())
    for z in range(2):
        for i in range(2):
            add_to(z, xb, i, w1a[z, pl.ds(i * quarter, quarter), :])
            add_to(2 + z, i, yb, w1b[z, i])
    start(second_weights())

    add_first(0)
    arrive_slots(1)
    for k in ORDER:
        row_copy(2, k).start()
    sum_slots(1)
    start(first_rows(1))
    add_second(0)

    arrived(second_weights())
    for z in range(2):
        add_to(z, xb, yb, w2a[z])
        add_to(2 + z, xb, yb, w2b[z])
    start(third_weights())

    pass_on(0)
    add_first(1)
    arrive_slots(2)
    sum_slots(2)
    start(first_rows(2))
    add_second(1)

    arrived(third_weights())
    mine = w_view(place, xb, yb)[...].astype(F32)
    for k in range(3):
        mine = mine + wz[k].astype(F32)
    wown[...] = mine.astype(BF)
    start(fourth_weights())
    own_weights().start()

    add_first(2)
    pass_on(1)
    own_weights().wait()
    arrived(fourth_weights())
    start(fifth_weights())
    add_second(2)
    pass_on(2)

    for c in range(chunks):
        arrived(fourth_rows(c))
    arrived(fifth_weights())
    for c in range(chunks):
        for k in ORDER:
            row_copy(c, k).wait_send()
        for step in (first_rows, second_rows, third_rows, fourth_rows):
            gone(step(c))
    for step in (first_weights, second_weights, third_weights, fourth_weights, fifth_weights):
        gone(step())


def tail(demb, slot, asked, small, normed, mixed, gfirst, dq, dk, dv, rows_local, owners):
    tokens, width = demb.shape
    cap = asked.size // owners
    chunks = 3
    cols = width // chunks
    part = rows_local // 8
    lines = 128
    wide = 4 * width
    vmem = pl.BlockSpec(memory_space=pltpu.VMEM)
    hbm = pl.BlockSpec(memory_space=pl.ANY)
    word, packed = pl.pallas_call(
        tail_kernel,
        out_shape=(
            jax.ShapeDtypeStruct((2, 2, 2, part, width), BF),
            jax.ShapeDtypeStruct((2, 2, lines // 4, wide), BF),
        ),
        in_specs=[vmem] * 4 + [hbm] * 6,
        out_specs=(hbm, hbm),
        scratch_shapes=[
            pltpu.VMEM((chunks, owners, cap, cols), BF),
            pltpu.VMEM((chunks, owners, cap, cols), BF),
            pltpu.VMEM((rows_local, owners * cap), BF),
            pltpu.VMEM((chunks, 2, 2, 2, part, cols), BF),
            pltpu.VMEM((chunks, 2, part, cols), BF),
            pltpu.VMEM((chunks, 2, part, cols), BF),
            pltpu.VMEM((chunks, part, cols), BF),
            pltpu.VMEM((chunks, part, cols), BF),
            pltpu.VMEM((6, tokens, width), BF),
            pltpu.VMEM((width, tokens), BF),
            pltpu.VMEM((4, 2, lines, wide), BF),
            pltpu.VMEM((4, lines, wide), BF),
            pltpu.VMEM((2, lines // 2, wide), BF),
            pltpu.VMEM((2, 2, lines // 4, wide), BF),
            pltpu.VMEM((2, lines // 4, wide), BF),
            pltpu.VMEM((2, lines // 4, wide), BF),
            pltpu.VMEM((3, lines // 4, wide), BF),
            pltpu.VMEM((lines // 4, wide), BF),
            pltpu.SemaphoreType.DMA((6,)),
            pltpu.SemaphoreType.DMA((chunks, owners)),
            pltpu.SemaphoreType.DMA((chunks, owners)),
            pltpu.SemaphoreType.DMA((chunks, 8)),
            pltpu.SemaphoreType.DMA((chunks, 8)),
            pltpu.SemaphoreType.DMA((18,)),
            pltpu.SemaphoreType.DMA((18,)),
            pltpu.SemaphoreType.DMA((7,)),
        ],
        compiler_params=pltpu.CompilerParams(
            collective_id=1, has_side_effects=True, vmem_limit_bytes=62 * 1024 * 1024
        ),
        name="tail",
    )(demb, slot.reshape(1, tokens), asked.reshape(1, owners * cap), small, normed, mixed, gfirst, dq, dk, dv)
    return word.reshape(rows_local, width), packed.reshape(lines, wide)


def local(
    token_ids,
    type_ids,
    lengths,
    word_table,
    pos_table,
    token_type_embeddings,
    emb_gain,
    emb_bias,
    query_weight,
    query_bias,
    key_weight,
    value_weight,
    value_bias,
    out_weight,
    out_bias,
    attn_gain,
    attn_bias,
    up_weight,
    up_bias,
    down_weight,
    down_bias,
    final_gain,
    final_bias,
    cotangent,
):
    seq_count, seq_len = token_ids.shape
    tokens = seq_count * seq_len
    width = word_table.shape[1]
    rows_local = word_table.shape[0]
    owners = lax.axis_size("vocab")
    capacity = max(2, 2 * tokens // owners)
    flat_ids = token_ids.reshape(tokens)
    owner = flat_ids // rows_local
    member = (owner[:, None] == jnp.arange(owners)[None, :]).astype(jnp.int32)
    earlier = jnp.cumsum(member, 0) - member
    rank = jnp.sum(earlier * member, 1)
    slot = owner * capacity + rank
    requests = (
        jnp.full((owners * capacity,), -1, jnp.int32).at[slot].set(flat_ids - owner * rows_local)
    )
    requests = requests.reshape(owners, capacity)
    asked = lax.all_to_all(requests, "vocab", split_axis=0, concat_axis=0, tiled=True)
    valid = asked >= 0
    found = word_table[jnp.maximum(asked, 0)]
    found = jnp.where(valid[..., None], found, jnp.zeros((), jnp.bfloat16))
    returned = lax.all_to_all(found, "vocab", split_axis=0, concat_axis=0, tiled=True)
    word_rows = returned.reshape(owners * capacity, width)[slot]
    kinds = token_type_embeddings.shape[0]
    selection_matrix = (type_ids[..., None] == jnp.arange(kinds)[None, None, :]).astype(jnp.float32)
    type_rows = jnp.einsum(
        "tcr,rb->tcb",
        selection_matrix,
        token_type_embeddings.astype(jnp.float32),
        precision=lax.Precision.HIGHEST,
    )
    embedded = (
        word_rows.reshape(seq_count, seq_len, width).astype(jnp.float32)
        + pos_table.astype(jnp.float32)[None]
        + type_rows
    )
    normed = layer_norm(embedded, emb_gain, emb_bias).reshape(tokens, width)
    normed_low = normed.astype(jnp.bfloat16)
    query = (matmul(normed_low, query_weight) + query_bias).astype(jnp.bfloat16)
    keys = matmul(normed_low, key_weight).astype(jnp.bfloat16)
    values = (matmul(normed_low, value_weight) + value_bias).astype(jnp.bfloat16)
    split_shape = (seq_count, seq_len, HEADS, HEAD)
    query_split = query.reshape(split_shape)
    keys_split = keys.reshape(split_shape)
    values_split = values.reshape(split_shape)
    mixed, logsum = lax.map(attend_forward, (query_split, keys_split, values_split, lengths))
    mixed_low = mixed.reshape(tokens, width)
    first = normed + matmul(mixed_low, out_weight) + out_bias
    hidden = layer_norm(first, attn_gain, attn_bias)
    hidden_reduced_precision = hidden.astype(jnp.bfloat16)
    upper = matmul(hidden_reduced_precision, up_weight) + up_bias
    active_low = jax.nn.gelu(upper, approximate=False).astype(jnp.bfloat16)
    second = hidden + matmul(active_low, down_weight) + down_bias
    encoded = layer_norm(second, final_gain, final_bias)
    grad_out = cotangent.reshape(tokens, width).astype(jnp.float32)
    _, final_pull = jax.vjp(layer_norm, second, final_gain, final_bias)
    grad_second, grad_final_gain, grad_final_bias = final_pull(grad_out)
    grad_down_bias = jnp.sum(grad_second, 0)
    second_matmul_gradient_reduced = grad_second.astype(jnp.bfloat16)
    grad_down = matmul_tn(active_low, second_matmul_gradient_reduced)
    grad_active = matmul_nt(second_matmul_gradient_reduced, down_weight)
    _, gelu_pull = jax.vjp(partial(jax.nn.gelu, approximate=False), upper)
    (grad_upper,) = gelu_pull(grad_active)
    grad_up_bias = jnp.sum(grad_upper, 0)
    grad_upper_low = grad_upper.astype(jnp.bfloat16)
    grad_up = matmul_tn(hidden_reduced_precision, grad_upper_low)
    grad_hidden = grad_second + matmul_nt(grad_upper_low, up_weight)
    _, attn_pull = jax.vjp(layer_norm, first, attn_gain, attn_bias)
    grad_first, grad_attn_gain, grad_attn_bias = attn_pull(grad_hidden)
    grad_out_bias = jnp.sum(grad_first, 0)
    grad_first_low = grad_first.astype(jnp.bfloat16)
    grad_out_weight = matmul_tn(mixed_low, grad_first_low)
    grad_mixed = matmul_nt(grad_first_low, out_weight).astype(jnp.bfloat16)
    grad_query, grad_keys, grad_values = lax.map(
        attend_backward,
        (query_split, keys_split, values_split, grad_mixed.reshape(split_shape), logsum, lengths),
    )
    grad_query = grad_query.reshape(tokens, width)
    grad_keys = grad_keys.reshape(tokens, width)
    grad_values = grad_values.reshape(tokens, width)
    grad_query_bias = jnp.sum(grad_query, 0)
    grad_value_bias = jnp.sum(grad_values, 0)
    grad_query_low = grad_query.astype(jnp.bfloat16)
    grad_keys_low = grad_keys.astype(jnp.bfloat16)
    grad_values_low = grad_values.astype(jnp.bfloat16)
    grad_query_weight = matmul_tn(normed_low, grad_query_low)
    grad_key_weight = matmul_tn(normed_low, grad_keys_low)
    grad_value_weight = matmul_tn(normed_low, grad_values_low)
    grad_normed = (
        grad_first
        + matmul_nt(grad_query_low, query_weight)
        + matmul_nt(grad_keys_low, key_weight)
        + matmul_nt(grad_values_low, value_weight)
    )
    _, emb_pull = jax.vjp(layer_norm, embedded, emb_gain, emb_bias)
    embedding_output_gradient, grad_emb_gain, grad_emb_bias = emb_pull(
        grad_normed.reshape(seq_count, seq_len, width)
    )
    grad_pos = jnp.sum(embedding_output_gradient, 0)
    token_type_gradient = jnp.einsum(
        "nox,noh->xh", selection_matrix, embedding_output_gradient, precision=lax.Precision.HIGHEST
    )
    bf = jnp.bfloat16
    per = width // owners
    grad_down_all = sum_over_all(grad_down.astype(bf))
    grad_up_all = sum_over_all(grad_up.astype(bf))
    small = jnp.stack(
        [
            grad_query_bias,
            grad_value_bias,
            grad_out_bias,
            grad_attn_gain,
            grad_attn_bias,
            grad_emb_gain,
            grad_emb_bias,
            grad_down_bias,
            grad_final_gain,
            grad_final_bias,
            token_type_gradient[0],
            token_type_gradient[1],
        ]
    )
    if owners == 8 and lax.axis_size("dp") == 4:
        ups = grad_up_bias.reshape(owners, 4, per).transpose(1, 0, 2).reshape(4, width)
        word_low, packed = tail(
            embedding_output_gradient.reshape(tokens, width).astype(bf),
            slot,
            asked,
            jnp.concatenate([small, ups], 0),
            normed_low,
            mixed_low,
            grad_first_low,
            grad_query_low,
            grad_keys_low,
            grad_values_low,
            rows_local,
            owners,
        )
        grad_word = word_low.astype(jnp.float32)
        packed = packed.astype(jnp.float32)
        grad_query_weight, grad_key_weight, grad_value_weight, grad_out_weight = [
            packed[:per, i * width : (i + 1) * width] for i in range(4)
        ]
        lines = seq_len // owners // 4
        grad_pos = (
            packed[per : per + lines].reshape(lines, 4, width).transpose(1, 0, 2).reshape(4 * lines, width)
        )
        small = packed[per + lines :, :per]
    else:
        places = slot[None, :] == jnp.arange(owners * capacity)[:, None]
        outgoing = matmul(
            places.astype(bf), embedding_output_gradient.reshape(tokens, width).astype(bf)
        ).astype(bf)
        hits = (jnp.arange(rows_local)[:, None] == asked.reshape(-1)[None, :]).astype(bf)
        pieces = []
        step = 256
        for start in range(0, width, step):
            incoming = lax.all_to_all(
                outgoing[:, start : start + step].reshape(owners, capacity, step),
                "vocab",
                split_axis=0,
                concat_axis=0,
                tiled=True,
            )
            dense = matmul(hits, incoming.reshape(owners * capacity, step)).astype(bf)
            pieces.append(sum_over_dp(dense))
        grad_word = jnp.concatenate(pieces, 1)
        small = small.reshape(12, owners, per).transpose(1, 0, 2).reshape(owners, 12 * per)
        small = jnp.concatenate([small, grad_up_bias.reshape(owners, 4 * per)], 1)
        wide = 4 * width
        lines = (seq_len // owners) * width // wide
        rest = per // 3 - lines
        small_lines = jnp.pad(small, ((0, 0), (0, rest * wide - 16 * per))).reshape(owners, rest, wide)
        mixed_grads = jnp.concatenate(
            [grad_query_weight, grad_key_weight, grad_value_weight, grad_out_weight], 1
        ).astype(bf)
        packed = jnp.concatenate(
            [
                mixed_grads.reshape(owners, per, wide),
                grad_pos.astype(bf).reshape(owners, lines, wide),
                small_lines.astype(bf),
            ],
            1,
        )
        packed = sum_over_all(packed.reshape(-1, wide))
        weights = packed[:per]
        grad_query_weight = weights[:, :width]
        grad_key_weight = weights[:, width : 2 * width]
        grad_value_weight = weights[:, 2 * width : 3 * width]
        grad_out_weight = weights[:, 3 * width :]
        grad_pos = packed[per : per + lines].reshape(seq_len // owners, width)
        small = packed[per + lines :].reshape(-1)[: 16 * per].reshape(16, per)
    (
        grad_query_bias,
        grad_value_bias,
        grad_out_bias,
        grad_attn_gain,
        grad_attn_bias,
        grad_emb_gain,
        grad_emb_bias,
        grad_down_bias,
        grad_final_gain,
        grad_final_bias,
    ) = [small[i] for i in range(10)]
    token_type_gradient = small[10:12]
    grad_up_bias = small[12:].reshape(-1)
    grad_up, grad_down = grad_up_all, grad_down_all
    return (
        encoded.reshape(seq_count, seq_len, width),
        grad_word,
        grad_pos,
        token_type_gradient,
        grad_emb_gain,
        grad_emb_bias,
        grad_query_weight,
        grad_query_bias,
        grad_key_weight,
        grad_value_weight,
        grad_value_bias,
        grad_out_weight,
        grad_out_bias,
        grad_attn_gain,
        grad_attn_bias,
        grad_up,
        grad_up_bias,
        grad_down,
        grad_down_bias,
        grad_final_gain,
        grad_final_bias,
    )


def solution(mesh):
    placed = (
        P(("dp", "vocab"), None),
        P(("dp", "vocab"), None),
        P(("dp", "vocab")),
        P("vocab", None),
        P(),
        P(),
        P(),
        P(),
        P(),
        P(),
        P(),
        P(),
        P(),
        P(),
        P(),
        P(),
        P(),
        P(),
        P(),
        P(),
        P(),
        P(),
        P(),
        P(("dp", "vocab"), None, None),
    )
    return jax.shard_map(
        local,
        mesh=mesh,
        in_specs=placed,
        out_specs=(
            P(("dp", "vocab"), None, None),
            P("vocab", None),
            P("vocab", None),
            P(None, "vocab"),
            P("vocab"),
            P("vocab"),
            P("vocab", None),
            P("vocab"),
            P("vocab", None),
            P("vocab", None),
            P("vocab"),
            P("vocab", None),
            P("vocab"),
            P("vocab"),
            P("vocab"),
            P("vocab", None),
            P("vocab"),
            P("vocab", None),
            P("vocab"),
            P("vocab"),
            P("vocab"),
        ),
        check_vma=False,
    )
```

```python
from functools import partial

import jax
import jax.numpy as jnp
from jax import lax
from jax.experimental import pallas as pl
from jax.experimental.pallas import tpu as pltpu
from jax.sharding import PartitionSpec as P

HEADS = 12
HEAD = 64
L = 512


EPSILON = 1e-12


def layer_norm(values, gain, bias):
    center = values - jnp.mean(values, -1, keepdims=True)
    spread = jnp.mean(center * center, -1, keepdims=True)
    return center * lax.rsqrt(spread + EPSILON) * gain + bias


def matmul(left, right):
    return jnp.dot(left, right, preferred_element_type=jnp.float32)


def matmul_tn(left, right):
    return lax.dot_general(
        left, right, (((0,), (0,)), ((), ())), preferred_element_type=jnp.float32
    )


def matmul_nt(left, right):
    return lax.dot_general(
        left, right, (((1,), (1,)), ((), ())), preferred_element_type=jnp.float32
    )


def swap(value, axis_name, bit):
    size = lax.axis_size(axis_name)
    return lax.ppermute(value, axis_name, [(i, i ^ bit) for i in range(size)])


def pick(value, index, axis):
    return lax.dynamic_index_in_dim(value, index, axis, keepdims=False)


def plus(left, right):
    return (left.astype(jnp.float32) + right.astype(jnp.float32)).astype(jnp.bfloat16)


def dp_bits():
    index = lax.axis_index("dp")
    return lax.rem(index, 2), index // 2


def reorder(own, across_x, across_y, across_both):
    xb, yb = dp_bits()
    flip_x, flip_y = xb == 1, yb == 1
    rows = [[own, across_y], [across_x, across_both]]
    rows = [
        [jnp.where(flip_x, rows[1 - i][j], rows[i][j]) for j in range(2)] for i in range(2)
    ]
    rows = [
        [jnp.where(flip_y, rows[i][1 - j], rows[i][j]) for j in range(2)] for i in range(2)
    ]
    return rows


def sum_over_all(grad):
    size = lax.axis_size("vocab")
    me = lax.axis_index("vocab")
    core = lax.rem(me, 2)
    place = me // 2
    places = size // 2
    total, n = grad.shape
    r = total // size
    xb, yb = dp_bits()
    grad = grad.reshape(places, 2, r, n)
    other = swap(pick(grad, 1 - core, 1), "vocab", 1)
    held = plus(pick(grad, core, 1), other).reshape(places, 2, 2, r // 4, n)
    first, last = held[: places // 2], held[places // 2 :]
    first_in = swap(pick(first, 1 - xb, 1), "dp", 1)
    last_in = swap(pick(last, 1 - yb, 2), "dp", 2)
    first = plus(pick(first, xb, 1), first_in)
    last = plus(pick(last, yb, 2), last_in)
    first_in = swap(pick(first, 1 - yb, 1), "dp", 2)
    last_in = swap(pick(last, 1 - xb, 1), "dp", 1)
    first = plus(pick(first, yb, 1), first_in)
    last = plus(pick(last, xb, 1), last_in)
    held = jnp.concatenate([first, last], 0)
    summed = pick(held, place, 0).astype(jnp.float32)
    for step in range(1, places):
        block = pick(held, lax.rem(place + step, places), 0)
        block = lax.ppermute(
            block, "vocab", [(i, (i + 2 * step) % size) for i in range(size)]
        )
        summed = summed + block.astype(jnp.float32)
    own = summed.astype(jnp.bfloat16)
    across_x = swap(own, "dp", 1)
    across_y = swap(own, "dp", 2)
    half = n // 2
    both = jnp.concatenate(
        [swap(across_x[:, :half], "dp", 2), swap(across_y[:, half:], "dp", 1)], 1
    )
    rows = reorder(own, across_x, across_y, both)
    return jnp.stack([rows[0][0], rows[0][1], rows[1][0], rows[1][1]]).reshape(r, n).astype(jnp.float32)


def sum_over_dp(grad):
    rows, n = grad.shape
    xb, yb = dp_bits()
    held = grad.reshape(2, 2, 2, rows // 8, n)
    first, last = held[0], held[1]
    first_in = swap(pick(first, 1 - xb, 0), "dp", 1)
    last_in = swap(pick(last, 1 - yb, 1), "dp", 2)
    first = plus(pick(first, xb, 0), first_in)
    last = plus(pick(last, yb, 1), last_in)
    first_in = swap(pick(first, 1 - yb, 0), "dp", 2)
    last_in = swap(pick(last, 1 - xb, 0), "dp", 1)
    first = plus(pick(first, yb, 0), first_in)
    last = plus(pick(last, xb, 0), last_in)
    first_x = swap(first, "dp", 1)
    last_y = swap(last, "dp", 2)
    first_y = swap(jnp.stack([first, first_x]), "dp", 2)
    last_x = swap(jnp.stack([last, last_y]), "dp", 1)
    a = reorder(first, first_x, first_y[0], first_y[1])
    b = reorder(last, last_x[0], last_y, last_x[1])
    parts = [p for group in (a, b) for line in group for p in line]
    return jnp.concatenate(parts, 0).astype(jnp.float32)


BF = jnp.bfloat16
F32 = jnp.float32
MIB = 1024 * 1024


def dot_nt(left, right):
    return lax.dot_general(left, right, (((1,), (1,)), ((), ())), preferred_element_type=F32)


def dot_nn(left, right):
    return jnp.dot(left, right, preferred_element_type=F32)


def stats(values):
    center = values - jnp.mean(values, -1, keepdims=True)
    inverse = lax.rsqrt(jnp.mean(center * center, -1, keepdims=True) + EPSILON)
    return center * inverse, inverse


def norm_back(grad, gain, unit, inverse):
    scaled = grad * gain
    return inverse * (
        scaled
        - jnp.mean(scaled, -1, keepdims=True)
        - unit * jnp.mean(scaled * unit, -1, keepdims=True)
    )


def column_sum(values):
    return jnp.sum(values, 0, keepdims=True)


TAIL_SCALE = 0.33
TAIL_TERMS = (
    -0.13534782292195252,
    0.4602463244004558,
    -0.3511662200543899,
    0.4085159085223644,
    0.04721176063633592,
    0.2012267561020528,
    0.1829554472050349,
    0.1863578383326851,
)


def normal_parts(u):
    t = 1.0 / (1.0 + (TAIL_SCALE * 0.5**0.5) * jnp.abs(u))
    poly = TAIL_TERMS[0]
    for term in TAIL_TERMS[1:]:
        poly = poly * t + term
    bell = jnp.exp(u * u * -0.5)
    below = (0.5 * t) * poly * bell
    return jnp.where(u >= 0, 1.0 - below, below), bell * 0.3989422804014327


def attend_kernel(
    lengths, normed, wq, wk, wv, wo, query_bias, value_bias, out_bias,
    low, q_out, k_out, v_out, mixed_out, first_out, probs_out, bias,
):
    tokens, width = normed.shape
    tile = 256
    low[...] = normed[...].astype(BF)

    def project(n, carry):
        at = pl.ds(pl.multiple_of(n * tile, tile), tile)
        x = low[...]
        query = (dot_nn(x, wq[:, at]) + query_bias[:, at]).astype(BF)
        q_out[:, at] = query * BF(HEAD**-0.5)
        k_out[:, at] = dot_nn(x, wk[:, at]).astype(BF)
        v_out[:, at] = (dot_nn(x, wv[:, at]) + value_bias[:, at]).astype(BF)
        return carry

    lax.fori_loop(0, width // tile, project, 0)
    seen = lax.broadcasted_iota(jnp.int32, bias.shape, 0) < lengths[pl.program_id(0)]
    bias[...] = jnp.where(seen, 0.0, -1000000000.0)

    def pair(j, carry):
        at = pl.ds(pl.multiple_of(j * 2 * HEAD, 2 * HEAD), 2 * HEAD)
        q, k, turned = q_out[:, at], k_out[:, at], v_out[:, at].T
        lane = lax.broadcasted_iota(jnp.int32, k.shape, 1)
        parts = []
        for side in range(2):
            mine = (lane >= HEAD) if side else (lane < HEAD)
            scores = dot_nt(jnp.where(mine, k, jnp.zeros_like(k)), q)
            scores = scores + jnp.concatenate([bias[...]] * (tokens // 128), 1)
            expd = jnp.exp(scores - jnp.max(scores, 0, keepdims=True))
            probs = (expd * (1.0 / jnp.sum(expd, 0, keepdims=True))).astype(BF)
            probs_out[0, 2 * j + side] = probs
            parts.append(dot_nn(turned[side * HEAD : (side + 1) * HEAD], probs))
        mixed_out[:, at] = jnp.concatenate(parts, 0).T.astype(BF)
        return carry

    lax.fori_loop(0, HEADS // 2, pair, 0)

    def close(n, carry):
        at = pl.ds(pl.multiple_of(n * tile, tile), tile)
        first_out[:, at] = normed[:, at] + dot_nn(mixed_out[...], wo[:, at]) + out_bias[:, at]
        return carry

    lax.fori_loop(0, width // tile, close, 0)


def fixed(shape):
    return pl.BlockSpec(shape, lambda i, *_: (0,) * len(shape), pipeline_mode=pl.Buffered(1))


def rows_of(rows, width):
    return pl.BlockSpec((rows, width), lambda i, *_: (i, 0))


def row(vector):
    return vector.reshape(1, -1)


def attend(lengths, normed, wq, wk, wv, wo, query_bias, value_bias, out_bias):
    tokens, width = normed.shape
    seqs = lengths.shape[0]
    size = tokens // seqs
    low = jax.ShapeDtypeStruct((tokens, width), BF)
    part = rows_of(size, width)
    return pl.pallas_call(
        attend_kernel,
        grid_spec=pltpu.PrefetchScalarGridSpec(
            num_scalar_prefetch=1,
            grid=(seqs,),
            in_specs=[part] + [fixed((width, width))] * 4 + [fixed((1, width))] * 3,
            out_specs=[part] * 6 + [pl.BlockSpec((1, HEADS, size, size), lambda i, *_: (i, 0, 0, 0))],
            scratch_shapes=[pltpu.VMEM((size, 128), F32)],
        ),
        out_shape=[low] * 5
        + [jax.ShapeDtypeStruct((tokens, width), F32), jax.ShapeDtypeStruct((seqs, HEADS, size, size), BF)],
        compiler_params=pltpu.CompilerParams(vmem_limit_bytes=60 * MIB),
        cost_estimate=pl.CostEstimate(flops=20 * 10**9, bytes_accessed=30 * 10**6, transcendentals=0),
        name="attend",
    )(lengths, normed, wq, wk, wv, wo, row(query_bias), row(value_bias), row(out_bias))


def feed_kernel(
    first, cotangent, up, down, up_bias, down_bias, attn_gain, attn_bias, final_gain, final_bias,
    encoded, active, second_low, hidden_low, upper_low, first_grad, sums, up_sum,
    slope,
):
    width = first.shape[1]
    units = up.shape[1]
    block = 768
    unit, inverse = stats(first[...])
    hidden = unit * attn_gain[...] + attn_bias[...]
    hidden_low[...] = hidden.astype(BF)
    total = hidden + down_bias[...]
    for n in range(units // block):
        at = pl.ds(n * block, block)
        upper = dot_nn(hidden_low[...], up[:, at]) + up_bias[:, at]
        below, density = normal_parts(upper)
        active[:, at] = (upper * below).astype(BF)
        slope[:, at] = below + upper * density
        total = total + dot_nn(active[:, at], down[at, :])
    unit_out, inverse_out = stats(total)
    encoded[...] = unit_out * final_gain[...] + final_bias[...]
    grad = cotangent[...].astype(F32)
    grad_second = norm_back(grad, final_gain[...], unit_out, inverse_out)
    second_low[...] = grad_second.astype(BF)

    @pl.when(pl.program_id(0) == 0)
    def _():
        sums[...] = jnp.zeros_like(sums)
        up_sum[...] = jnp.zeros_like(up_sum)

    sums[0:1, :] += column_sum(grad * unit_out)
    sums[1:2, :] += column_sum(grad)
    sums[2:3, :] += column_sum(grad_second)
    total = grad_second
    for n in range(units // block):
        at = pl.ds(n * block, block)
        grad_upper = dot_nt(second_low[...], down[at, :]) * slope[:, at]
        up_sum[:, at] += column_sum(grad_upper)
        upper_low[:, at] = grad_upper.astype(BF)
        total = total + dot_nt(upper_low[:, at], up[:, at])
    grad_first = norm_back(total, attn_gain[...], unit, inverse)
    sums[3:4, :] += column_sum(total * unit)
    sums[4:5, :] += column_sum(total)
    sums[5:6, :] += column_sum(grad_first)
    first_grad[...] = grad_first


def feed(first, cotangent, up, down, up_bias, down_bias, attn_gain, attn_bias, final_gain, final_bias):
    tokens, width = first.shape
    units = up.shape[1]
    tile = 256
    part, wide = rows_of(tile, width), rows_of(tile, units)
    vector = fixed((1, width))
    return pl.pallas_call(
        feed_kernel,
        grid=(tokens // tile,),
        in_specs=[part, part, fixed((width, units)), fixed((units, width)), fixed((1, units))] + [vector] * 5,
        out_specs=[part, wide, part, part, wide, part, fixed((8, width)), fixed((1, units))],
        out_shape=[
            jax.ShapeDtypeStruct((tokens, width), F32),
            jax.ShapeDtypeStruct((tokens, units), BF),
            jax.ShapeDtypeStruct((tokens, width), BF),
            jax.ShapeDtypeStruct((tokens, width), BF),
            jax.ShapeDtypeStruct((tokens, units), BF),
            jax.ShapeDtypeStruct((tokens, width), F32),
            jax.ShapeDtypeStruct((8, width), F32),
            jax.ShapeDtypeStruct((1, units), F32),
        ],
        scratch_shapes=[pltpu.VMEM((tile, units), F32)],
        compiler_params=pltpu.CompilerParams(vmem_limit_bytes=60 * MIB),
        cost_estimate=pl.CostEstimate(flops=40 * 10**9, bytes_accessed=40 * 10**6, transcendentals=0),
        name="feed",
    )(
        first, cotangent, up, down, row(up_bias), row(down_bias), row(attn_gain), row(attn_bias),
        row(final_gain), row(final_bias),
    )


def attend_back_kernel(
    grad_first, embedded, kinds, q_in, k_in, v_in, probs_in, wq, wk, wv, wo, emb_gain,
    first_low, dq, dk, dv, emb_low, sums,
    grad_mixed, total,
):
    tokens, width = grad_first.shape
    tile = 256

    @pl.when(pl.program_id(0) == 0)
    def _():
        sums[...] = jnp.zeros_like(sums)

    first_low[...] = grad_first[...].astype(BF)

    def open_(n, carry):
        at = pl.ds(pl.multiple_of(n * tile, tile), tile)
        grad_mixed[:, at] = dot_nt(first_low[...], wo[at, :]).astype(BF)
        return carry

    lax.fori_loop(0, width // tile, open_, 0)

    def pair(j, carry):
        at = pl.ds(pl.multiple_of(j * 2 * HEAD, 2 * HEAD), 2 * HEAD)
        q, k, v, grad = q_in[:, at], k_in[:, at], v_in[:, at], grad_mixed[:, at]
        turned = k.T
        lane = lax.broadcasted_iota(jnp.int32, k.shape, 1)
        parts = []
        grad_k = jnp.zeros(k.shape, F32)
        grad_v = jnp.zeros(k.shape, F32)
        for side in range(2):
            mine = (lane >= HEAD) if side else (lane < HEAD)
            none = jnp.zeros_like(k)
            probs = probs_in[0, 2 * j + side]
            grad_probs = dot_nt(jnp.where(mine, v, none), grad)
            grad_v = grad_v + dot_nn(probs, jnp.where(mine, grad, none))
            wide = probs.astype(F32)
            both = wide * grad_probs
            scores = (both - wide * jnp.sum(both, 0, keepdims=True)).astype(BF)
            grad_k = grad_k + dot_nn(scores, jnp.where(mine, q, none))
            parts.append(dot_nn(turned[side * HEAD : (side + 1) * HEAD], scores))
        grad_q = jnp.concatenate(parts, 0).T * HEAD**-0.5
        dq[:, at] = grad_q.astype(BF)
        dk[:, at] = grad_k.astype(BF)
        dv[:, at] = grad_v.astype(BF)
        sums[0:1, at] += column_sum(grad_q)
        sums[1:2, at] += column_sum(grad_v)
        return carry

    lax.fori_loop(0, HEADS // 2, pair, 0)

    def close(n, carry):
        at = pl.ds(pl.multiple_of(n * tile, tile), tile)
        total[:, at] = (
            grad_first[:, at]
            + dot_nt(dq[...], wq[at, :])
            + dot_nt(dk[...], wk[at, :])
            + dot_nt(dv[...], wv[at, :])
        )
        return carry

    lax.fori_loop(0, width // tile, close, 0)
    rows = 128

    def last(n, carry):
        at = pl.ds(pl.multiple_of(n * rows, rows), rows)
        unit, inverse = stats(embedded[at, :])
        grad = total[at, :]
        grad_emb = norm_back(grad, emb_gain[...], unit, inverse)
        emb_low[at, :] = grad_emb.astype(BF)
        sums[2:3, :] += column_sum(grad * unit)
        sums[3:4, :] += column_sum(grad)
        kind = kinds[at, :]
        for t in range(2):
            sums[4 + t : 5 + t, :] += column_sum(jnp.where(kind == t, grad_emb, 0.0))
        return carry

    lax.fori_loop(0, tokens // rows, last, 0)


def attend_back(grad_first, embedded, kinds, q, k, v, probs, wq, wk, wv, wo, emb_gain):
    tokens, width = grad_first.shape
    seqs, _, size, _ = probs.shape
    part = rows_of(size, width)
    low = jax.ShapeDtypeStruct((tokens, width), BF)
    return pl.pallas_call(
        attend_back_kernel,
        grid=(seqs,),
        in_specs=[part, part, rows_of(size, 1)]
        + [part] * 3
        + [pl.BlockSpec((1, HEADS, size, size), lambda i: (i, 0, 0, 0))]
        + [fixed((width, width))] * 4
        + [fixed((1, width))],
        out_specs=[part] * 5 + [fixed((8, width))],
        out_shape=[low] * 5 + [jax.ShapeDtypeStruct((8, width), F32)],
        scratch_shapes=[pltpu.VMEM((size, width), BF), pltpu.VMEM((size, width), F32)],
        compiler_params=pltpu.CompilerParams(vmem_limit_bytes=60 * MIB),
        cost_estimate=pl.CostEstimate(flops=30 * 10**9, bytes_accessed=40 * 10**6, transcendentals=0),
        name="attend_back",
    )(grad_first, embedded, kinds.reshape(tokens, 1), q, k, v, probs, wq, wk, wv, wo, row(emb_gain))


MESH = pl.DeviceIdType.MESH


def flipped(index, bits):
    out = 0
    for place in range(3):
        bit = lax.rem(lax.div(index, 1 << place), 2)
        out = out + (1 << place) * (1 - bit if (bits >> place) & 1 else bit)
    return out


ORDER = (6, 7, 4, 5, 2, 3, 1)


def tail_kernel(
    demb, slot, asked, small, normed, mixed, gfirst, dq, dk, dv,
    word, packed,
    og, inc, hits, dense, r1a, r1b, r2a, r2b,
    ops, turned, wbuf, wcore, w1a, w1b, w2a, w2b, wz, wown,
    load_sem, z_send, z_recv, d_send, d_recv, w_send, w_recv, own_sem,
):
    owners, cap = og.shape[1], og.shape[2]
    chunks, cols = og.shape[0], og.shape[3]
    tokens = demb.shape[0]
    part = dense.shape[4]
    me = lax.axis_index("vocab")
    spot = lax.axis_index("dp")
    core, place = lax.rem(me, 2), lax.div(me, 2)
    xb, yb = lax.rem(spot, 2), lax.div(spot, 2)
    across_x = {"dp": spot + 1 - 2 * xb}
    across_y = {"dp": spot + 2 - 4 * yb}

    loads = [
        pltpu.make_async_copy(ref, ops.at[i], load_sem.at[i])
        for i, ref in enumerate((normed, dq, dk, dv, mixed, gfirst))
    ]
    for load in loads:
        load.start()
    barrier = pltpu.get_barrier_semaphore()
    for k in ORDER:
        pl.semaphore_signal(barrier, inc=1, device_id={"vocab": flipped(me, k)}, device_id_type=MESH)
    for peer in (across_x, across_y):
        pl.semaphore_signal(barrier, inc=1, device_id=peer, device_id_type=MESH)
    pl.semaphore_wait(barrier, len(ORDER) + 2)

    def remote(src, dst, send, recv, peer):
        return pltpu.make_async_remote_copy(
            src_ref=src, dst_ref=dst, send_sem=send, recv_sem=recv, device_id=peer, device_id_type=MESH
        )

    def row_copy(c, k):
        peer = flipped(me, k)
        return remote(
            og.at[c, peer], inc.at[c, me], z_send.at[c, k], z_recv.at[c, k], {"vocab": peer}
        )

    def slots_of(peer):
        wanted = lax.broadcasted_iota(jnp.int32, (cap, tokens), 0) + peer * cap
        hot = jnp.where(wanted == slot[...], 1.0, 0.0).astype(BF)
        return jnp.dot(hot, demb[...], preferred_element_type=F32).astype(BF)

    for k in ORDER:
        peer = flipped(me, k)
        rows = slots_of(peer)
        for c in range(chunks):
            og[c, peer] = rows[:, c * cols : (c + 1) * cols]
        row_copy(0, k).start()
    rows = slots_of(me)
    for c in range(chunks):
        inc[c, me] = rows[:, c * cols : (c + 1) * cols]

    width = demb.shape[1]
    per = width // owners
    block = 256

    def turn(which):
        for i in range(tokens // block):
            for j in range(width // block):
                turned[pl.ds(j * block, block), pl.ds(i * block, block)] = ops[
                    which, pl.ds(i * block, block), pl.ds(j * block, block)
                ].T

    def weight(which, at):
        def one(n, carry):
            there = pl.multiple_of(n * block, block)
            out = jnp.dot(turned[...], ops[which, :, pl.ds(there, block)], preferred_element_type=F32).astype(BF)
            there = pl.multiple_of(at * width + n * block, block)
            for v in range(owners):
                wbuf[v // 2, v % 2, pl.ds(0, per), pl.ds(there, block)] = out[v * per : (v + 1) * per]
            return carry

        lax.fori_loop(0, width // block, one, 0)

    loads[0].wait()
    turn(0)
    for i in range(3):
        loads[1 + i].wait()
        weight(1 + i, i)
    loads[4].wait()
    turn(4)
    loads[5].wait()
    weight(5, 3)
    half = tokens // 2
    lines = half // owners // 4
    for v in range(owners):
        for j in range(4):
            at = v * (half // owners) + j * lines
            total = demb[pl.ds(at, lines), :].astype(F32) + demb[pl.ds(half + at, lines), :].astype(F32)
            wbuf[v // 2, v % 2, pl.ds(per, lines), pl.ds(j * width, width)] = total.astype(BF)
        wbuf[v // 2, v % 2, pl.ds(per + lines, 16), :] = jnp.zeros((16, 4 * width), BF)
        wbuf[v // 2, v % 2, pl.ds(per + lines, 16), pl.ds(0, 128)] = jnp.pad(
            small[:, v * per : (v + 1) * per], ((0, 0), (0, 128 - per))
        ).astype(BF)
    partner = {"vocab": flipped(me, 1)}
    core_copy = remote(wbuf.at[:, 1 - core], wcore, w_send.at[0], w_recv.at[0], partner)
    core_copy.start()

    tile = 240
    rows_local = 8 * part

    def match(t, carry):
        at = pl.multiple_of(t * tile, tile)
        row = lax.broadcasted_iota(jnp.int32, (tile, owners * cap), 0) + at
        hits[pl.ds(at, tile), :] = jnp.where(row == asked[...], 1.0, 0.0).astype(BF)
        return carry

    lax.fori_loop(0, rows_local // tile, match, 0)

    quarter = wown.shape[0]
    def w_view(z, x, y):
        return wbuf.at[z, core, pl.ds(pl.multiple_of((2 * x + y) * quarter, quarter), quarter), :]

    def w_half(z, x):
        return wbuf.at[z, core, pl.ds(pl.multiple_of(2 * x * quarter, quarter), 2 * quarter), :]

    def core_sum(i, carry):
        z = lax.div(i, 4)
        at = pl.multiple_of(lax.rem(i, 4) * quarter, quarter)
        mine = wbuf[z, core, pl.ds(at, quarter), :].astype(F32)
        wbuf[z, core, pl.ds(at, quarter), :] = (mine + wcore[z, pl.ds(at, quarter), :].astype(F32)).astype(BF)
        return carry

    def first_weights():
        copies = []
        for z in range(2):
            copies.append(remote(w_half(z, 1 - xb), w1a.at[z], w_send.at[1 + z], w_recv.at[1 + z], across_x))
            for x in range(2):
                at = 2 * z + x
                copies.append(
                    remote(w_view(2 + z, x, 1 - yb), w1b.at[z, x], w_send.at[3 + at], w_recv.at[3 + at], across_y)
                )
        return copies

    def add_to(z, x, y, value):
        view = w_view(z, x, y)
        view[...] = (view[...].astype(F32) + value.astype(F32)).astype(BF)

    def second_weights():
        copies = []
        for z in range(2):
            copies.append(remote(w_view(z, xb, 1 - yb), w2a.at[z], w_send.at[7 + z], w_recv.at[7 + z], across_y))
            copies.append(remote(w_view(2 + z, 1 - xb, yb), w2b.at[z], w_send.at[9 + z], w_recv.at[9 + z], across_x))
        return copies

    def place_copy(k):
        to = flipped(place, k)
        return remote(
            w_view(to, xb, yb), wz.at[k - 1], w_send.at[10 + k], w_recv.at[10 + k], {"vocab": 2 * to + core}
        )

    def third_weights():
        return [place_copy(k) for k in (3, 2, 1)]

    def own_weights():
        return pltpu.make_async_copy(wown, packed.at[xb, yb], own_sem.at[0])

    def fourth_weights():
        return [
            remote(wown, packed.at[xb, yb], w_send.at[14], w_recv.at[14], across_x),
            remote(wown, packed.at[xb, yb], w_send.at[15], w_recv.at[15], across_y),
        ]

    wide = 2 * width

    def fifth_weights():
        left, right = pl.ds(0, wide), pl.ds(wide, wide)
        return [
            remote(
                packed.at[1 - xb, yb, :, left], packed.at[1 - xb, yb, :, left], w_send.at[16], w_recv.at[16], across_y
            ),
            remote(
                packed.at[xb, 1 - yb, :, right], packed.at[xb, 1 - yb, :, right], w_send.at[17], w_recv.at[17], across_x
            ),
        ]

    def first_rows(c):
        return [
            remote(dense.at[c, 0, 1 - xb], r1a.at[c], d_send.at[c, 0], d_recv.at[c, 0], across_x),
            remote(dense.at[c, 1, :, 1 - yb], r1b.at[c], d_send.at[c, 1], d_recv.at[c, 1], across_y),
        ]

    def second_rows(c):
        return [
            remote(dense.at[c, 0, xb, 1 - yb], r2a.at[c], d_send.at[c, 2], d_recv.at[c, 2], across_y),
            remote(dense.at[c, 1, 1 - xb, yb], r2b.at[c], d_send.at[c, 3], d_recv.at[c, 3], across_x),
        ]

    def spread(c):
        return pl.ds(c * cols, cols)

    def own_rows(c):
        return [
            pltpu.make_async_copy(dense.at[c, h, xb, yb], word.at[h, xb, yb, :, spread(c)], own_sem.at[1 + 2 * c + h])
            for h in range(2)
        ]

    def third_rows(c):
        return [
            remote(dense.at[c, 0, xb, yb], word.at[0, xb, yb, :, spread(c)], d_send.at[c, 4], d_recv.at[c, 4], across_x),
            remote(dense.at[c, 1, xb, yb], word.at[1, xb, yb, :, spread(c)], d_send.at[c, 5], d_recv.at[c, 5], across_y),
        ]

    def fourth_rows(c):
        return [
            remote(
                word.at[0, :, yb, :, spread(c)], word.at[0, :, yb, :, spread(c)], d_send.at[c, 6], d_recv.at[c, 6], across_y
            ),
            remote(
                word.at[1, xb, :, :, spread(c)], word.at[1, xb, :, :, spread(c)], d_send.at[c, 7], d_recv.at[c, 7], across_x
            ),
        ]

    def start(copies):
        for copy in copies:
            copy.start()

    def arrived(copies):
        for copy in copies:
            copy.wait_recv()

    def gone(copies):
        for copy in copies:
            copy.wait_send()

    def arrive_slots(c):
        for k in ORDER:
            row_copy(c, k).wait_recv()

    def sum_slots(c):
        def one(t, carry):
            h, x, y = lax.div(t, 4), lax.rem(lax.div(t, 2), 2), lax.rem(t, 2)
            at = pl.multiple_of(t * part, part)
            total = jnp.zeros((part, cols), F32)
            for p in range(owners):
                total = total + jnp.dot(
                    hits[pl.ds(at, part), pl.ds(p * cap, cap)], inc[c, p], preferred_element_type=F32
                )
            dense[c, h, x, y] = total.astype(BF)
            return carry

        lax.fori_loop(0, 8, one, 0)

    def add_rows(c, h, x, y, value):
        dense[c, h, x, y] = (dense[c, h, x, y].astype(F32) + value.astype(F32)).astype(BF)

    def add_first(c):
        arrived(first_rows(c))
        for i in range(2):
            add_rows(c, 0, xb, i, r1a[c, i])
            add_rows(c, 1, i, yb, r1b[c, i])
        start(second_rows(c))

    def add_second(c):
        arrived(second_rows(c))
        add_rows(c, 0, xb, yb, r2a[c])
        add_rows(c, 1, xb, yb, r2b[c])
        start(third_rows(c))
        start(own_rows(c))

    def pass_on(c):
        for copy in own_rows(c):
            copy.wait()
        arrived(third_rows(c))
        start(fourth_rows(c))

    core_copy.wait_recv()
    core_copy.wait_send()
    lax.fori_loop(0, 16, core_sum, 0)
    start(first_weights())

    arrive_slots(0)
    for k in ORDER:
        row_copy(1, k).start()
    sum_slots(0)
    start(first_rows(0))

    arrived(first_weights())
    for z in range(2):
        for i in range(2):
            add_to(z, xb, i, w1a[z, pl.ds(i * quarter, quarter), :])
            add_to(2 + z, i, yb, w1b[z, i])
    start(second_weights())

    add_first(0)
    arrive_slots(1)
    for k in ORDER:
        row_copy(2, k).start()
    sum_slots(1)
    start(first_rows(1))
    add_second(0)

    arrived(second_weights())
    for z in range(2):
        add_to(z, xb, yb, w2a[z])
        add_to(2 + z, xb, yb, w2b[z])
    start(third_weights())

    pass_on(0)
    add_first(1)
    arrive_slots(2)
    sum_slots(2)
    start(first_rows(2))
    add_second(1)

    arrived(third_weights())
    mine = w_view(place, xb, yb)[...].astype(F32)
    for k in range(3):
        mine = mine + wz[k].astype(F32)
    wown[...] = mine.astype(BF)
    start(fourth_weights())
    own_weights().start()

    add_first(2)
    pass_on(1)
    own_weights().wait()
    arrived(fourth_weights())
    start(fifth_weights())
    add_second(2)
    pass_on(2)

    for c in range(chunks):
        arrived(fourth_rows(c))
    arrived(fifth_weights())
    for c in range(chunks):
        for k in ORDER:
            row_copy(c, k).wait_send()
        for step in (first_rows, second_rows, third_rows, fourth_rows):
            gone(step(c))
    for step in (first_weights, second_weights, third_weights, fourth_weights, fifth_weights):
        gone(step())


def tail(demb, slot, asked, small, normed, mixed, gfirst, dq, dk, dv, rows_local, owners):
    tokens, width = demb.shape
    cap = asked.size // owners
    chunks = 3
    cols = width // chunks
    part = rows_local // 8
    lines = 128
    wide = 4 * width
    vmem = pl.BlockSpec(memory_space=pltpu.VMEM)
    hbm = pl.BlockSpec(memory_space=pl.ANY)
    word, packed = pl.pallas_call(
        tail_kernel,
        out_shape=(
            jax.ShapeDtypeStruct((2, 2, 2, part, width), BF),
            jax.ShapeDtypeStruct((2, 2, lines // 4, wide), BF),
        ),
        in_specs=[vmem] * 4 + [hbm] * 6,
        out_specs=(hbm, hbm),
        scratch_shapes=[
            pltpu.VMEM((chunks, owners, cap, cols), BF),
            pltpu.VMEM((chunks, owners, cap, cols), BF),
            pltpu.VMEM((rows_local, owners * cap), BF),
            pltpu.VMEM((chunks, 2, 2, 2, part, cols), BF),
            pltpu.VMEM((chunks, 2, part, cols), BF),
            pltpu.VMEM((chunks, 2, part, cols), BF),
            pltpu.VMEM((chunks, part, cols), BF),
            pltpu.VMEM((chunks, part, cols), BF),
            pltpu.VMEM((6, tokens, width), BF),
            pltpu.VMEM((width, tokens), BF),
            pltpu.VMEM((4, 2, lines, wide), BF),
            pltpu.VMEM((4, lines, wide), BF),
            pltpu.VMEM((2, lines // 2, wide), BF),
            pltpu.VMEM((2, 2, lines // 4, wide), BF),
            pltpu.VMEM((2, lines // 4, wide), BF),
            pltpu.VMEM((2, lines // 4, wide), BF),
            pltpu.VMEM((3, lines // 4, wide), BF),
            pltpu.VMEM((lines // 4, wide), BF),
            pltpu.SemaphoreType.DMA((6,)),
            pltpu.SemaphoreType.DMA((chunks, owners)),
            pltpu.SemaphoreType.DMA((chunks, owners)),
            pltpu.SemaphoreType.DMA((chunks, 8)),
            pltpu.SemaphoreType.DMA((chunks, 8)),
            pltpu.SemaphoreType.DMA((18,)),
            pltpu.SemaphoreType.DMA((18,)),
            pltpu.SemaphoreType.DMA((7,)),
        ],
        compiler_params=pltpu.CompilerParams(
            collective_id=1, has_side_effects=True, vmem_limit_bytes=62 * 1024 * 1024
        ),
        name="tail",
    )(demb, slot.reshape(1, tokens), asked.reshape(1, owners * cap), small, normed, mixed, gfirst, dq, dk, dv)
    return word.reshape(rows_local, width), packed.reshape(lines, wide)


def local(
    token_ids,
    type_ids,
    lengths,
    word_table,
    pos_table,
    token_type_embeddings,
    emb_gain,
    emb_bias,
    query_weight,
    query_bias,
    key_weight,
    value_weight,
    value_bias,
    out_weight,
    out_bias,
    attn_gain,
    attn_bias,
    up_weight,
    up_bias,
    down_weight,
    down_bias,
    final_gain,
    final_bias,
    cotangent,
):
    seq_count, seq_len = token_ids.shape
    tokens = seq_count * seq_len
    width = word_table.shape[1]
    rows_local = word_table.shape[0]
    owners = lax.axis_size("vocab")
    capacity = max(2, 2 * tokens // owners)
    flat_ids = token_ids.reshape(tokens)
    owner = flat_ids // rows_local
    member = (owner[:, None] == jnp.arange(owners)[None, :]).astype(jnp.int32)
    earlier = jnp.cumsum(member, 0) - member
    rank = jnp.sum(earlier * member, 1)
    slot = owner * capacity + rank
    requests = (
        jnp.full((owners * capacity,), -1, jnp.int32).at[slot].set(flat_ids - owner * rows_local)
    )
    requests = requests.reshape(owners, capacity)
    asked = lax.all_to_all(requests, "vocab", split_axis=0, concat_axis=0, tiled=True)
    valid = asked >= 0
    found = word_table[jnp.maximum(asked, 0)]
    found = jnp.where(valid[..., None], found, jnp.zeros((), jnp.bfloat16))
    returned = lax.all_to_all(found, "vocab", split_axis=0, concat_axis=0, tiled=True)
    word_rows = returned.reshape(owners * capacity, width)[slot]
    kinds = token_type_embeddings.shape[0]
    selection_matrix = (type_ids[..., None] == jnp.arange(kinds)[None, None, :]).astype(jnp.float32)
    type_rows = jnp.einsum(
        "tcr,rb->tcb",
        selection_matrix,
        token_type_embeddings.astype(jnp.float32),
        precision=lax.Precision.HIGHEST,
    )
    embedded = (
        word_rows.reshape(seq_count, seq_len, width).astype(jnp.float32)
        + pos_table.astype(jnp.float32)[None]
        + type_rows
    )
    embedded = embedded.reshape(tokens, width)
    normed = layer_norm(embedded, emb_gain, emb_bias)
    normed_low, query, keys, values, mixed_low, first, probs = attend(
        lengths, normed, query_weight, key_weight, value_weight, out_weight, query_bias, value_bias, out_bias
    )
    encoded, active_low, grad_second_low, hidden_low, grad_upper_low, grad_first, sums, grad_up_bias = feed(
        first,
        cotangent.reshape(tokens, width),
        up_weight,
        down_weight,
        up_bias,
        down_bias,
        attn_gain,
        attn_bias,
        final_gain,
        final_bias,
    )
    grad_final_gain, grad_final_bias, grad_down_bias, grad_attn_gain, grad_attn_bias, grad_out_bias = [
        sums[i] for i in range(6)
    ]
    grad_up_bias = grad_up_bias[0]
    grad_down = matmul_tn(active_low, grad_second_low)
    grad_up = matmul_tn(hidden_low, grad_upper_low)
    grad_first_low, grad_query_low, grad_keys_low, grad_values_low, embedding_output_gradient, sums = attend_back(
        grad_first,
        embedded,
        type_ids,
        query,
        keys,
        values,
        probs,
        query_weight,
        key_weight,
        value_weight,
        out_weight,
        emb_gain,
    )
    grad_query_bias, grad_value_bias, grad_emb_gain, grad_emb_bias = [sums[i] for i in range(4)]
    token_type_gradient = sums[4:6]
    grad_pos = jnp.sum(embedding_output_gradient.astype(jnp.float32).reshape(seq_count, seq_len, width), 0)
    bf = jnp.bfloat16
    per = width // owners
    grad_down_all = sum_over_all(grad_down.astype(bf))
    grad_up_all = sum_over_all(grad_up.astype(bf))
    small = jnp.stack(
        [
            grad_query_bias,
            grad_value_bias,
            grad_out_bias,
            grad_attn_gain,
            grad_attn_bias,
            grad_emb_gain,
            grad_emb_bias,
            grad_down_bias,
            grad_final_gain,
            grad_final_bias,
            token_type_gradient[0],
            token_type_gradient[1],
        ]
    )
    if owners == 8 and lax.axis_size("dp") == 4:
        ups = grad_up_bias.reshape(owners, 4, per).transpose(1, 0, 2).reshape(4, width)
        word_low, packed = tail(
            embedding_output_gradient.reshape(tokens, width).astype(bf),
            slot,
            asked,
            jnp.concatenate([small, ups], 0),
            normed_low,
            mixed_low,
            grad_first_low,
            grad_query_low,
            grad_keys_low,
            grad_values_low,
            rows_local,
            owners,
        )
        grad_word = word_low.astype(jnp.float32)
        packed = packed.astype(jnp.float32)
        grad_query_weight, grad_key_weight, grad_value_weight, grad_out_weight = [
            packed[:per, i * width : (i + 1) * width] for i in range(4)
        ]
        lines = seq_len // owners // 4
        grad_pos = (
            packed[per : per + lines].reshape(lines, 4, width).transpose(1, 0, 2).reshape(4 * lines, width)
        )
        small = packed[per + lines :, :per]
    else:
        places = slot[None, :] == jnp.arange(owners * capacity)[:, None]
        outgoing = matmul(
            places.astype(bf), embedding_output_gradient.reshape(tokens, width).astype(bf)
        ).astype(bf)
        hits = (jnp.arange(rows_local)[:, None] == asked.reshape(-1)[None, :]).astype(bf)
        pieces = []
        step = 256
        for start in range(0, width, step):
            incoming = lax.all_to_all(
                outgoing[:, start : start + step].reshape(owners, capacity, step),
                "vocab",
                split_axis=0,
                concat_axis=0,
                tiled=True,
            )
            dense = matmul(hits, incoming.reshape(owners * capacity, step)).astype(bf)
            pieces.append(sum_over_dp(dense))
        grad_word = jnp.concatenate(pieces, 1)
        small = small.reshape(12, owners, per).transpose(1, 0, 2).reshape(owners, 12 * per)
        small = jnp.concatenate([small, grad_up_bias.reshape(owners, 4 * per)], 1)
        wide = 4 * width
        lines = (seq_len // owners) * width // wide
        rest = per // 3 - lines
        small_lines = jnp.pad(small, ((0, 0), (0, rest * wide - 16 * per))).reshape(owners, rest, wide)
        grad_query_weight, grad_key_weight, grad_value_weight = [
            matmul_tn(normed_low, g) for g in (grad_query_low, grad_keys_low, grad_values_low)
        ]
        grad_out_weight = matmul_tn(mixed_low, grad_first_low)
        mixed_grads = jnp.concatenate(
            [grad_query_weight, grad_key_weight, grad_value_weight, grad_out_weight], 1
        ).astype(bf)
        packed = jnp.concatenate(
            [
                mixed_grads.reshape(owners, per, wide),
                grad_pos.astype(bf).reshape(owners, lines, wide),
                small_lines.astype(bf),
            ],
            1,
        )
        packed = sum_over_all(packed.reshape(-1, wide))
        weights = packed[:per]
        grad_query_weight = weights[:, :width]
        grad_key_weight = weights[:, width : 2 * width]
        grad_value_weight = weights[:, 2 * width : 3 * width]
        grad_out_weight = weights[:, 3 * width :]
        grad_pos = packed[per : per + lines].reshape(seq_len // owners, width)
        small = packed[per + lines :].reshape(-1)[: 16 * per].reshape(16, per)
    (
        grad_query_bias,
        grad_value_bias,
        grad_out_bias,
        grad_attn_gain,
        grad_attn_bias,
        grad_emb_gain,
        grad_emb_bias,
        grad_down_bias,
        grad_final_gain,
        grad_final_bias,
    ) = [small[i] for i in range(10)]
    token_type_gradient = small[10:12]
    grad_up_bias = small[12:].reshape(-1)
    grad_up, grad_down = grad_up_all, grad_down_all
    return (
        encoded.reshape(seq_count, seq_len, width),
        grad_word,
        grad_pos,
        token_type_gradient,
        grad_emb_gain,
        grad_emb_bias,
        grad_query_weight,
        grad_query_bias,
        grad_key_weight,
        grad_value_weight,
        grad_value_bias,
        grad_out_weight,
        grad_out_bias,
        grad_attn_gain,
        grad_attn_bias,
        grad_up,
        grad_up_bias,
        grad_down,
        grad_down_bias,
        grad_final_gain,
        grad_final_bias,
    )


def solution(mesh):
    placed = (
        P(("dp", "vocab"), None),
        P(("dp", "vocab"), None),
        P(("dp", "vocab")),
        P("vocab", None),
        P(),
        P(),
        P(),
        P(),
        P(),
        P(),
        P(),
        P(),
        P(),
        P(),
        P(),
        P(),
        P(),
        P(),
        P(),
        P(),
        P(),
        P(),
        P(),
        P(("dp", "vocab"), None, None),
    )
    return jax.shard_map(
        local,
        mesh=mesh,
        in_specs=placed,
        out_specs=(
            P(("dp", "vocab"), None, None),
            P("vocab", None),
            P("vocab", None),
            P(None, "vocab"),
            P("vocab"),
            P("vocab"),
            P("vocab", None),
            P("vocab"),
            P("vocab", None),
            P("vocab", None),
            P("vocab"),
            P("vocab", None),
            P("vocab"),
            P("vocab"),
            P("vocab"),
            P("vocab", None),
            P("vocab"),
            P("vocab", None),
            P("vocab"),
            P("vocab"),
            P("vocab"),
        ),
        check_vma=False,
    )
```

```python
from functools import partial

import jax
import jax.numpy as jnp
from jax import lax
from jax.experimental import pallas as pl
from jax.experimental.pallas import tpu as pltpu
from jax.sharding import PartitionSpec as P

HEADS = 12
HEAD = 64
L = 512


EPSILON = 1e-12


def layer_norm(values, gain, bias):
    center = values - jnp.mean(values, -1, keepdims=True)
    spread = jnp.mean(center * center, -1, keepdims=True)
    return center * lax.rsqrt(spread + EPSILON) * gain + bias


def matmul(left, right):
    return jnp.dot(left, right, preferred_element_type=jnp.float32)


def matmul_tn(left, right):
    return lax.dot_general(
        left, right, (((0,), (0,)), ((), ())), preferred_element_type=jnp.float32
    )


def matmul_nt(left, right):
    return lax.dot_general(
        left, right, (((1,), (1,)), ((), ())), preferred_element_type=jnp.float32
    )


def swap(value, axis_name, bit):
    size = lax.axis_size(axis_name)
    return lax.ppermute(value, axis_name, [(i, i ^ bit) for i in range(size)])


def pick(value, index, axis):
    return lax.dynamic_index_in_dim(value, index, axis, keepdims=False)


def plus(left, right):
    return (left.astype(jnp.float32) + right.astype(jnp.float32)).astype(jnp.bfloat16)


def dp_bits():
    index = lax.axis_index("dp")
    return lax.rem(index, 2), index // 2


def reorder(own, across_x, across_y, across_both):
    xb, yb = dp_bits()
    flip_x, flip_y = xb == 1, yb == 1
    rows = [[own, across_y], [across_x, across_both]]
    rows = [
        [jnp.where(flip_x, rows[1 - i][j], rows[i][j]) for j in range(2)] for i in range(2)
    ]
    rows = [
        [jnp.where(flip_y, rows[i][1 - j], rows[i][j]) for j in range(2)] for i in range(2)
    ]
    return rows


def sum_over_all(grad):
    size = lax.axis_size("vocab")
    me = lax.axis_index("vocab")
    core = lax.rem(me, 2)
    place = me // 2
    places = size // 2
    total, n = grad.shape
    r = total // size
    xb, yb = dp_bits()
    grad = grad.reshape(places, 2, r, n)
    other = swap(pick(grad, 1 - core, 1), "vocab", 1)
    held = plus(pick(grad, core, 1), other).reshape(places, 2, 2, r // 4, n)
    first, last = held[: places // 2], held[places // 2 :]
    first_in = swap(pick(first, 1 - xb, 1), "dp", 1)
    last_in = swap(pick(last, 1 - yb, 2), "dp", 2)
    first = plus(pick(first, xb, 1), first_in)
    last = plus(pick(last, yb, 2), last_in)
    first_in = swap(pick(first, 1 - yb, 1), "dp", 2)
    last_in = swap(pick(last, 1 - xb, 1), "dp", 1)
    first = plus(pick(first, yb, 1), first_in)
    last = plus(pick(last, xb, 1), last_in)
    held = jnp.concatenate([first, last], 0)
    summed = pick(held, place, 0).astype(jnp.float32)
    for step in range(1, places):
        block = pick(held, lax.rem(place + step, places), 0)
        block = lax.ppermute(
            block, "vocab", [(i, (i + 2 * step) % size) for i in range(size)]
        )
        summed = summed + block.astype(jnp.float32)
    own = summed.astype(jnp.bfloat16)
    across_x = swap(own, "dp", 1)
    across_y = swap(own, "dp", 2)
    half = n // 2
    both = jnp.concatenate(
        [swap(across_x[:, :half], "dp", 2), swap(across_y[:, half:], "dp", 1)], 1
    )
    rows = reorder(own, across_x, across_y, both)
    return jnp.stack([rows[0][0], rows[0][1], rows[1][0], rows[1][1]]).reshape(r, n).astype(jnp.float32)


def sum_over_dp(grad):
    rows, n = grad.shape
    xb, yb = dp_bits()
    held = grad.reshape(2, 2, 2, rows // 8, n)
    first, last = held[0], held[1]
    first_in = swap(pick(first, 1 - xb, 0), "dp", 1)
    last_in = swap(pick(last, 1 - yb, 1), "dp", 2)
    first = plus(pick(first, xb, 0), first_in)
    last = plus(pick(last, yb, 1), last_in)
    first_in = swap(pick(first, 1 - yb, 0), "dp", 2)
    last_in = swap(pick(last, 1 - xb, 0), "dp", 1)
    first = plus(pick(first, yb, 0), first_in)
    last = plus(pick(last, xb, 0), last_in)
    first_x = swap(first, "dp", 1)
    last_y = swap(last, "dp", 2)
    first_y = swap(jnp.stack([first, first_x]), "dp", 2)
    last_x = swap(jnp.stack([last, last_y]), "dp", 1)
    a = reorder(first, first_x, first_y[0], first_y[1])
    b = reorder(last, last_x[0], last_y, last_x[1])
    parts = [p for group in (a, b) for line in group for p in line]
    return jnp.concatenate(parts, 0).astype(jnp.float32)


BF = jnp.bfloat16
F32 = jnp.float32
MIB = 1024 * 1024


def dot_nt(left, right):
    return lax.dot_general(left, right, (((1,), (1,)), ((), ())), preferred_element_type=F32)


def dot_nn(left, right):
    return jnp.dot(left, right, preferred_element_type=F32)


def stats(values):
    center = values - jnp.mean(values, -1, keepdims=True)
    inverse = lax.rsqrt(jnp.mean(center * center, -1, keepdims=True) + EPSILON)
    return center * inverse, inverse


def norm_back(grad, gain, unit, inverse):
    scaled = grad * gain
    return inverse * (
        scaled
        - jnp.mean(scaled, -1, keepdims=True)
        - unit * jnp.mean(scaled * unit, -1, keepdims=True)
    )


def column_sum(values):
    return jnp.sum(values, 0, keepdims=True)


TAIL_SCALE = 0.33
TAIL_TERMS = (
    -0.13534782292195252,
    0.4602463244004558,
    -0.3511662200543899,
    0.4085159085223644,
    0.04721176063633592,
    0.2012267561020528,
    0.1829554472050349,
    0.1863578383326851,
)


def normal_parts(u):
    t = 1.0 / (1.0 + (TAIL_SCALE * 0.5**0.5) * jnp.abs(u))
    poly = TAIL_TERMS[0]
    for term in TAIL_TERMS[1:]:
        poly = poly * t + term
    bell = jnp.exp(u * u * -0.5)
    below = (0.5 * t) * poly * bell
    return jnp.where(u >= 0, 1.0 - below, below), bell * 0.3989422804014327


def attend_kernel(
    lengths, normed, wq, wk, wv, wo, query_bias, value_bias, out_bias,
    low, q_out, k_out, v_out, mixed_out, first_out, probs_out, bias,
):
    tokens, width = normed.shape
    tile = 256
    low[...] = normed[...].astype(BF)

    def project(n, carry):
        at = pl.ds(pl.multiple_of(n * tile, tile), tile)
        x = low[...]
        query = (dot_nn(x, wq[:, at]) + query_bias[:, at]).astype(BF)
        q_out[:, at] = query * BF(HEAD**-0.5)
        k_out[:, at] = dot_nn(x, wk[:, at]).astype(BF)
        v_out[:, at] = (dot_nn(x, wv[:, at]) + value_bias[:, at]).astype(BF)
        return carry

    lax.fori_loop(0, width // tile, project, 0)
    seen = lax.broadcasted_iota(jnp.int32, bias.shape, 0) < lengths[pl.program_id(0)]
    bias[...] = jnp.where(seen, 0.0, -1000000000.0)

    def pair(j, carry):
        at = pl.ds(pl.multiple_of(j * 2 * HEAD, 2 * HEAD), 2 * HEAD)
        q, k, turned = q_out[:, at], k_out[:, at], v_out[:, at].T
        lane = lax.broadcasted_iota(jnp.int32, k.shape, 1)
        parts = []
        for side in range(2):
            mine = (lane >= HEAD) if side else (lane < HEAD)
            scores = dot_nt(jnp.where(mine, k, jnp.zeros_like(k)), q)
            scores = scores + jnp.concatenate([bias[...]] * (tokens // 128), 1)
            expd = jnp.exp(scores - jnp.max(scores, 0, keepdims=True))
            probs = (expd * (1.0 / jnp.sum(expd, 0, keepdims=True))).astype(BF)
            probs_out[0, 2 * j + side] = probs
            parts.append(dot_nn(turned[side * HEAD : (side + 1) * HEAD], probs))
        mixed_out[:, at] = jnp.concatenate(parts, 0).T.astype(BF)
        return carry

    lax.fori_loop(0, HEADS // 2, pair, 0)

    def close(n, carry):
        at = pl.ds(pl.multiple_of(n * tile, tile), tile)
        first_out[:, at] = normed[:, at] + dot_nn(mixed_out[...], wo[:, at]) + out_bias[:, at]
        return carry

    lax.fori_loop(0, width // tile, close, 0)


def fixed(shape):
    return pl.BlockSpec(shape, lambda i, *_: (0,) * len(shape), pipeline_mode=pl.Buffered(1))


def rows_of(rows, width):
    return pl.BlockSpec((rows, width), lambda i, *_: (i, 0))


def row(vector):
    return vector.reshape(1, -1)


def attend(lengths, normed, wq, wk, wv, wo, query_bias, value_bias, out_bias):
    tokens, width = normed.shape
    seqs = lengths.shape[0]
    size = tokens // seqs
    low = jax.ShapeDtypeStruct((tokens, width), BF)
    part = rows_of(size, width)
    return pl.pallas_call(
        attend_kernel,
        grid_spec=pltpu.PrefetchScalarGridSpec(
            num_scalar_prefetch=1,
            grid=(seqs,),
            in_specs=[part] + [fixed((width, width))] * 4 + [fixed((1, width))] * 3,
            out_specs=[part] * 6 + [pl.BlockSpec((1, HEADS, size, size), lambda i, *_: (i, 0, 0, 0))],
            scratch_shapes=[pltpu.VMEM((size, 128), F32)],
        ),
        out_shape=[low] * 5
        + [jax.ShapeDtypeStruct((tokens, width), F32), jax.ShapeDtypeStruct((seqs, HEADS, size, size), BF)],
        compiler_params=pltpu.CompilerParams(vmem_limit_bytes=60 * MIB),
        cost_estimate=pl.CostEstimate(flops=20 * 10**9, bytes_accessed=30 * 10**6, transcendentals=0),
        name="attend",
    )(lengths, normed, wq, wk, wv, wo, row(query_bias), row(value_bias), row(out_bias))


def feed_kernel(
    first, cotangent, up, down, up_bias, down_bias, attn_gain, attn_bias, final_gain, final_bias,
    encoded, active, second_low, hidden_low, upper_low, first_grad, sums, up_sum,
    slope,
):
    width = first.shape[1]
    units = up.shape[1]
    block = 768
    unit, inverse = stats(first[...])
    hidden = unit * attn_gain[...] + attn_bias[...]
    hidden_low[...] = hidden.astype(BF)
    total = hidden + down_bias[...]
    for n in range(units // block):
        at = pl.ds(n * block, block)
        upper = dot_nn(hidden_low[...], up[:, at]) + up_bias[:, at]
        below, density = normal_parts(upper)
        active[:, at] = (upper * below).astype(BF)
        slope[:, at] = below + upper * density
        total = total + dot_nn(active[:, at], down[at, :])
    unit_out, inverse_out = stats(total)
    encoded[...] = unit_out * final_gain[...] + final_bias[...]
    grad = cotangent[...].astype(F32)
    grad_second = norm_back(grad, final_gain[...], unit_out, inverse_out)
    second_low[...] = grad_second.astype(BF)

    @pl.when(pl.program_id(0) == 0)
    def _():
        sums[...] = jnp.zeros_like(sums)
        up_sum[...] = jnp.zeros_like(up_sum)

    sums[0:1, :] += column_sum(grad * unit_out)
    sums[1:2, :] += column_sum(grad)
    sums[2:3, :] += column_sum(grad_second)
    total = grad_second
    for n in range(units // block):
        at = pl.ds(n * block, block)
        grad_upper = dot_nt(second_low[...], down[at, :]) * slope[:, at]
        up_sum[:, at] += column_sum(grad_upper)
        upper_low[:, at] = grad_upper.astype(BF)
        total = total + dot_nt(upper_low[:, at], up[:, at])
    grad_first = norm_back(total, attn_gain[...], unit, inverse)
    sums[3:4, :] += column_sum(total * unit)
    sums[4:5, :] += column_sum(total)
    sums[5:6, :] += column_sum(grad_first)
    first_grad[...] = grad_first


def feed(first, cotangent, up, down, up_bias, down_bias, attn_gain, attn_bias, final_gain, final_bias):
    tokens, width = first.shape
    units = up.shape[1]
    tile = 256
    part, wide = rows_of(tile, width), rows_of(tile, units)
    vector = fixed((1, width))
    return pl.pallas_call(
        feed_kernel,
        grid=(tokens // tile,),
        in_specs=[part, part, fixed((width, units)), fixed((units, width)), fixed((1, units))] + [vector] * 5,
        out_specs=[part, wide, part, part, wide, part, fixed((8, width)), fixed((1, units))],
        out_shape=[
            jax.ShapeDtypeStruct((tokens, width), F32),
            jax.ShapeDtypeStruct((tokens, units), BF),
            jax.ShapeDtypeStruct((tokens, width), BF),
            jax.ShapeDtypeStruct((tokens, width), BF),
            jax.ShapeDtypeStruct((tokens, units), BF),
            jax.ShapeDtypeStruct((tokens, width), F32),
            jax.ShapeDtypeStruct((8, width), F32),
            jax.ShapeDtypeStruct((1, units), F32),
        ],
        scratch_shapes=[pltpu.VMEM((tile, units), F32)],
        compiler_params=pltpu.CompilerParams(vmem_limit_bytes=60 * MIB),
        cost_estimate=pl.CostEstimate(flops=40 * 10**9, bytes_accessed=40 * 10**6, transcendentals=0),
        name="feed",
    )(
        first, cotangent, up, down, row(up_bias), row(down_bias), row(attn_gain), row(attn_bias),
        row(final_gain), row(final_bias),
    )


def attend_back_kernel(
    grad_first, embedded, kinds, q_in, k_in, v_in, probs_in, wq, wk, wv, wo, emb_gain,
    first_low, dq, dk, dv, emb_low, sums,
    grad_mixed, total,
):
    tokens, width = grad_first.shape
    tile = 256

    @pl.when(pl.program_id(0) == 0)
    def _():
        sums[...] = jnp.zeros_like(sums)

    first_low[...] = grad_first[...].astype(BF)

    def open_(n, carry):
        at = pl.ds(pl.multiple_of(n * tile, tile), tile)
        grad_mixed[:, at] = dot_nt(first_low[...], wo[at, :]).astype(BF)
        return carry

    lax.fori_loop(0, width // tile, open_, 0)

    def pair(j, carry):
        at = pl.ds(pl.multiple_of(j * 2 * HEAD, 2 * HEAD), 2 * HEAD)
        q, k, v, grad = q_in[:, at], k_in[:, at], v_in[:, at], grad_mixed[:, at]
        turned = k.T
        lane = lax.broadcasted_iota(jnp.int32, k.shape, 1)
        parts = []
        grad_k = jnp.zeros(k.shape, F32)
        grad_v = jnp.zeros(k.shape, F32)
        for side in range(2):
            mine = (lane >= HEAD) if side else (lane < HEAD)
            none = jnp.zeros_like(k)
            probs = probs_in[0, 2 * j + side]
            grad_probs = dot_nt(jnp.where(mine, v, none), grad)
            grad_v = grad_v + dot_nn(probs, jnp.where(mine, grad, none))
            wide = probs.astype(F32)
            both = wide * grad_probs
            scores = (both - wide * jnp.sum(both, 0, keepdims=True)).astype(BF)
            grad_k = grad_k + dot_nn(scores, jnp.where(mine, q, none))
            parts.append(dot_nn(turned[side * HEAD : (side + 1) * HEAD], scores))
        grad_q = jnp.concatenate(parts, 0).T * HEAD**-0.5
        dq[:, at] = grad_q.astype(BF)
        dk[:, at] = grad_k.astype(BF)
        dv[:, at] = grad_v.astype(BF)
        sums[0:1, at] += column_sum(grad_q)
        sums[1:2, at] += column_sum(grad_v)
        return carry

    lax.fori_loop(0, HEADS // 2, pair, 0)

    def close(n, carry):
        at = pl.ds(pl.multiple_of(n * tile, tile), tile)
        total[:, at] = (
            grad_first[:, at]
            + dot_nt(dq[...], wq[at, :])
            + dot_nt(dk[...], wk[at, :])
            + dot_nt(dv[...], wv[at, :])
        )
        return carry

    lax.fori_loop(0, width // tile, close, 0)
    rows = 128

    def last(n, carry):
        at = pl.ds(pl.multiple_of(n * rows, rows), rows)
        unit, inverse = stats(embedded[at, :])
        grad = total[at, :]
        grad_emb = norm_back(grad, emb_gain[...], unit, inverse)
        emb_low[at, :] = grad_emb.astype(BF)
        sums[2:3, :] += column_sum(grad * unit)
        sums[3:4, :] += column_sum(grad)
        kind = kinds[at, :]
        for t in range(2):
            sums[4 + t : 5 + t, :] += column_sum(jnp.where(kind == t, grad_emb, 0.0))
        return carry

    lax.fori_loop(0, tokens // rows, last, 0)


def attend_back(grad_first, embedded, kinds, q, k, v, probs, wq, wk, wv, wo, emb_gain):
    tokens, width = grad_first.shape
    seqs, _, size, _ = probs.shape
    part = rows_of(size, width)
    low = jax.ShapeDtypeStruct((tokens, width), BF)
    return pl.pallas_call(
        attend_back_kernel,
        grid=(seqs,),
        in_specs=[part, part, rows_of(size, 1)]
        + [part] * 3
        + [pl.BlockSpec((1, HEADS, size, size), lambda i: (i, 0, 0, 0))]
        + [fixed((width, width))] * 4
        + [fixed((1, width))],
        out_specs=[part] * 5 + [fixed((8, width))],
        out_shape=[low] * 5 + [jax.ShapeDtypeStruct((8, width), F32)],
        scratch_shapes=[pltpu.VMEM((size, width), BF), pltpu.VMEM((size, width), F32)],
        compiler_params=pltpu.CompilerParams(vmem_limit_bytes=60 * MIB),
        cost_estimate=pl.CostEstimate(flops=30 * 10**9, bytes_accessed=40 * 10**6, transcendentals=0),
        name="attend_back",
    )(grad_first, embedded, kinds.reshape(tokens, 1), q, k, v, probs, wq, wk, wv, wo, row(emb_gain))


MESH = pl.DeviceIdType.MESH


def mid_kernel(
    active, upper_low, second_low, hidden_low, grad_first, embedded, q_in, k_in, v_in, probs_in, wq, wk, wv, wo,
    kinds, emb_gain,
    first_out, dq_out, dk_out, dv_out, raw_out, pos_out, feed_out, sums,
    stage, lhs, turned, grads, core_in, in_1a, in_1b, in_2a, in_2b, in_z, kept,
    first, low, grad_mixed, q, k, v, dq, dk, dv, weights, table, raw, pos, probs,
    load, stage_sem, probs_sem, out_sem, send, recv,
):
    tokens, width = lhs.shape
    size = probs.shape[2]
    seqs = tokens // size
    per = grads.shape[3]
    me = lax.axis_index("vocab")
    spot = lax.axis_index("dp")
    core, place = lax.rem(me, 2), lax.div(me, 2)
    xb, yb = lax.rem(spot, 2), lax.div(spot, 2)
    across_x = {"dp": spot + 1 - 2 * xb}
    across_y = {"dp": spot + 2 - 4 * yb}
    partner = {"vocab": me + 1 - 2 * core}
    block = 768
    blocks = active.shape[1] // block

    def stage_copy(n):
        source = active if n < blocks else upper_low
        at = pl.ds((n % blocks) * block, block)
        return pltpu.make_async_copy(source.at[:, at], stage.at[n % 2], stage_sem.at[n % 2])

    def probs_copy(n):
        return pltpu.make_async_copy(
            probs_in.at[lax.div(n, HEADS // 2), pl.ds(2 * lax.rem(n, HEADS // 2), 2)],
            probs.at[lax.rem(n, 2)],
            probs_sem.at[lax.rem(n, 2)],
        )

    second_copy = pltpu.make_async_copy(second_low, lhs, load.at[0])
    hidden_copy = pltpu.make_async_copy(hidden_low, lhs, load.at[1])
    second_copy.start()
    stage_copy(0).start()
    stage_copy(1).start()
    loads = [
        pltpu.make_async_copy(source, target, load.at[2 + i])
        for i, (source, target) in enumerate(
            (
                (grad_first, first),
                (wo, weights.at[3]),
                (q_in, q),
                (k_in, k),
                (v_in, v),
                (wq, weights.at[0]),
                (wk, weights.at[1]),
                (wv, weights.at[2]),
                (embedded, table),
            )
        )
    ]
    barrier = pltpu.get_barrier_semaphore()
    places = [{"vocab": 2 * flipped(place, k) + core} for k in (1, 2, 3)]
    for peer in [partner, across_x, across_y] + places:
        pl.semaphore_signal(barrier, inc=1, device_id=peer, device_id_type=MESH)
    pl.semaphore_wait(barrier, 6)

    def remote(src, dst, at, peer):
        return pltpu.make_async_remote_copy(
            src_ref=src, dst_ref=dst, send_sem=send.at[at], recv_sem=recv.at[at], device_id=peer, device_id_type=MESH
        )

    def core_copy(g):
        return remote(grads.at[g, :, 1 - core], core_in.at[g], 5 * g, partner)

    half = 2 * width

    def wide(b):
        return pl.ds(pl.multiple_of(b * half, half), half)

    def narrow(b, c):
        return pl.ds(pl.multiple_of(b * half + c * width, width), width)

    def first_copies(g):
        return [
            remote(grads.at[g, pl.ds(0, 2), core, :, wide(1 - xb)], in_1a.at[g], 5 * g + 1, across_x),
            remote(grads.at[g, pl.ds(2, 2), core, :, wide(1 - yb)], in_1b.at[g], 5 * g + 2, across_y),
        ]

    def second_copies(g):
        return [
            remote(grads.at[g, pl.ds(0, 2), core, :, narrow(xb, 1 - yb)], in_2a.at[g], 5 * g + 3, across_y),
            remote(grads.at[g, pl.ds(2, 2), core, :, narrow(yb, 1 - xb)], in_2b.at[g], 5 * g + 4, across_x),
        ]

    def add(view, value):
        view[...] = (view[...].astype(F32) + value.astype(F32)).astype(BF)

    def core_step(g):
        core_copy(g).wait_recv()
        rows = per // 2

        def one(i, carry):
            z = lax.div(i, 2)
            at = pl.ds(pl.multiple_of(lax.rem(i, 2) * rows, rows), rows)
            add(grads.at[g, z, core, at, :], core_in[g, z, at, :])
            return carry

        lax.fori_loop(0, 8, one, 0)
        for copy in first_copies(g):
            copy.start()

    def first_step(g):
        for copy in first_copies(g):
            copy.wait_recv()

        def one(z, carry):
            add(grads.at[g, z, core, :, wide(xb)], in_1a[g, z])
            add(grads.at[g, 2 + z, core, :, wide(yb)], in_1b[g, z])
            return carry

        lax.fori_loop(0, 2, one, 0)
        for copy in second_copies(g):
            copy.start()

    def owned(g, z):
        at = 2 * xb + yb + lax.div(z, 2) * (yb - xb)
        return grads.at[g, z, core, :, pl.ds(pl.multiple_of(at * width, width), width)]

    def place_copies(g):
        return [
            remote(owned(g, flipped(place, k)), in_z.at[g, k - 1], 10 + 3 * g + k - 1, places[k - 1]) for k in (3, 2, 1)
        ]

    def place_step(g):
        for copy in place_copies(g):
            copy.wait_recv()
        total = owned(g, place)[...].astype(F32)
        for k in range(3):
            total = total + in_z[g, k].astype(F32)
        kept[pl.ds(g * per, per), :] = total.astype(BF)

    def second_step(g):
        for copy in second_copies(g):
            copy.wait_recv()
        for z in range(2):
            add(grads.at[g, z, core, :, narrow(xb, yb)], in_2a[g, z])
            add(grads.at[g, 2 + z, core, :, narrow(yb, xb)], in_2b[g, z])
        for copy in place_copies(g):
            copy.start()

    corner = 256

    def turn():
        def one(i, carry):
            at = pl.ds(pl.multiple_of(i * corner, corner), corner)
            for j in range(width // corner):
                there = pl.ds(j * corner, corner)
                turned[there, at] = lhs[at, there].T
            return carry

        lax.fori_loop(0, tokens // corner, one, 0)

    second_copy.wait()
    turn()
    hidden_copy.start()
    share = block // 2
    for n in range(blocks):
        stage_copy(n).wait()
        for c in range(2):
            out = dot_nn(turned[...], stage[n % 2, :, c * share : (c + 1) * share]).astype(BF)
            for j in range(8):
                grads[0, n, c, :, j * share : (j + 1) * share] = out[j * per : (j + 1) * per]
        stage_copy(n + 2).start()
        if n == 0:
            for copy in loads[:5]:
                copy.start()
            probs_copy(0).start()
    core_copy(0).start()
    hidden_copy.wait()
    turn()
    for n in range(blocks, 2 * blocks):
        stage_copy(n).wait()
        for c in range(2):
            out = dot_nn(turned[...], stage[n % 2, :, c * share : (c + 1) * share]).astype(BF)
            at = (n - blocks) * block + c * share
            for j in range(8):
                grads[1, j // 2, j % 2, :, at : at + share] = out[j * per : (j + 1) * per]
        if n + 2 < 2 * blocks:
            stage_copy(n + 2).start()
        if n == blocks:
            for copy in loads[5:]:
                copy.start()
    core_copy(1).start()
    core_step(0)

    for copy in loads:
        copy.wait()
    sums[...] = jnp.zeros_like(sums)
    low[...] = first[...].astype(BF)
    first_copy = pltpu.make_async_copy(low, first_out, out_sem.at[4])
    first_copy.start()
    tile = 256

    def open_(n, carry):
        at = pl.ds(pl.multiple_of(n * tile, tile), tile)
        grad_mixed[:, at] = dot_nt(low[...], weights[3, at, :]).astype(BF)
        return carry

    lax.fori_loop(0, width // tile, open_, 0)

    def pair(n, carry):
        @pl.when(n + 1 < seqs * (HEADS // 2))
        def _():
            probs_copy(n + 1).start()

        probs_copy(n).wait()
        slot = lax.rem(n, 2)
        rows = pl.ds(pl.multiple_of(lax.div(n, HEADS // 2) * size, size), size)
        at = pl.ds(pl.multiple_of(lax.rem(n, HEADS // 2) * 2 * HEAD, 2 * HEAD), 2 * HEAD)
        q2, k2, v2, grad = q[rows, at], k[rows, at], v[rows, at], grad_mixed[rows, at]
        across = k2.T
        lane = lax.broadcasted_iota(jnp.int32, k2.shape, 1)
        parts = []
        grad_k = jnp.zeros(k2.shape, F32)
        grad_v = jnp.zeros(k2.shape, F32)
        for side in range(2):
            mine = (lane >= HEAD) if side else (lane < HEAD)
            none = jnp.zeros_like(k2)
            chances = probs[slot, side]
            grad_probs = dot_nt(jnp.where(mine, v2, none), grad)
            grad_v = grad_v + dot_nn(chances, jnp.where(mine, grad, none))
            full = chances.astype(F32)
            both = full * grad_probs
            scores = (both - full * jnp.sum(both, 0, keepdims=True)).astype(BF)
            grad_k = grad_k + dot_nn(scores, jnp.where(mine, q2, none))
            parts.append(dot_nn(across[side * HEAD : (side + 1) * HEAD], scores))
        grad_q = jnp.concatenate(parts, 0).T * HEAD**-0.5
        dq[rows, at] = grad_q.astype(BF)
        dk[rows, at] = grad_k.astype(BF)
        dv[rows, at] = grad_v.astype(BF)
        sums[0:1, at] += column_sum(grad_q)
        sums[1:2, at] += column_sum(grad_v)
        return carry

    lax.fori_loop(0, 2, pair, 0)
    core_step(1)
    lax.fori_loop(2, 5, pair, 0)
    first_step(0)
    lax.fori_loop(5, 8, pair, 0)
    second_step(0)
    first_step(1)
    lax.fori_loop(8, 11, pair, 0)
    second_step(1)
    lax.fori_loop(11, 12, pair, 0)
    out_copies = [
        pltpu.make_async_copy(source, target, out_sem.at[5 + i])
        for i, (source, target) in enumerate(((dq, dq_out), (dk, dk_out), (dv, dv_out)))
    ]
    for copy in out_copies:
        copy.start()

    def close(n, carry):
        at = pl.ds(pl.multiple_of(n * tile, tile), tile)
        first[:, at] = (
            first[:, at]
            + dot_nt(dq[...], weights[0, at, :])
            + dot_nt(dk[...], weights[1, at, :])
            + dot_nt(dv[...], weights[2, at, :])
        )
        return carry

    lax.fori_loop(0, width // tile, close, 0)
    few = 128
    lane = lax.broadcasted_iota(jnp.int32, (few, 128), 1)

    def back(at):
        unit, inverse = stats(table[at, :])
        grad = first[at, :]
        grad_emb = norm_back(grad, emb_gain[...], unit, inverse)
        sums[2:3, :] += column_sum(grad * unit)
        sums[3:4, :] += column_sum(grad)
        kind = kinds[at, :]
        for t in range(2):
            sums[4 + t : 5 + t, :] += column_sum(jnp.where(kind == t, grad_emb, 0.0))
        return grad_emb

    def last(n, carry):
        at = pl.ds(pl.multiple_of(n * few, few), few)
        left = back(at)
        right = back(pl.ds(pl.multiple_of(size + n * few, few), few))
        pos[at, :] = (left + right).astype(BF)
        for t in range(width // 128):
            one, two = left[:, t * 128 : (t + 1) * 128], right[:, t * 128 : (t + 1) * 128]
            q = 2 * (t % 2)
            raw[t // 2, q, at, :] = jnp.where(lane < 64, one, pltpu.roll(two, 64, 1)).astype(BF)
            raw[t // 2, q + 1, at, :] = jnp.where(lane < 64, pltpu.roll(one, 64, 1), two).astype(BF)
        return carry

    lax.fori_loop(0, size // few, last, 0)
    raw_copy = pltpu.make_async_copy(raw, raw_out, out_sem.at[0])
    raw_copy.start()
    pos_copy = pltpu.make_async_copy(pos, pos_out, out_sem.at[1])
    pos_copy.start()
    for g in range(2):
        place_step(g)
    feed_copy = pltpu.make_async_copy(kept, feed_out, out_sem.at[2])
    feed_copy.start()
    for copy in [first_copy, raw_copy, pos_copy, feed_copy] + out_copies:
        copy.wait()
    for g in range(2):
        for copy in [core_copy(g)] + first_copies(g) + second_copies(g) + place_copies(g):
            copy.wait_send()


def mid(
    active, upper_low, second_low, hidden_low, grad_first, embedded, q, k, v, probs, wq, wk, wv, wo, kinds, emb_gain
):
    tokens, width = grad_first.shape
    seqs, heads, size, _ = probs.shape
    units = active.shape[1]
    per = width // 8
    wide = 4 * width
    vmem = pl.BlockSpec(memory_space=pltpu.VMEM)
    hbm = pl.BlockSpec(memory_space=pl.ANY)
    low = jax.ShapeDtypeStruct((tokens, width), BF)
    small = pltpu.VMEM((tokens, width), BF)
    large = pltpu.VMEM((tokens, width), F32)
    return pl.pallas_call(
        mid_kernel,
        out_shape=[low] * 4
        + [
            jax.ShapeDtypeStruct((3, 4, size, 128), BF),
            jax.ShapeDtypeStruct((size, width), BF),
            jax.ShapeDtypeStruct((2 * per, width), BF),
            jax.ShapeDtypeStruct((8, width), F32),
        ],
        in_specs=[hbm] * 14 + [vmem] * 2,
        out_specs=[hbm] * 7 + [vmem],
        scratch_shapes=[
            pltpu.VMEM((2, tokens, 768), BF),
            small,
            pltpu.VMEM((width, tokens), BF),
            pltpu.VMEM((2, 4, 2, per, wide), BF),
            pltpu.VMEM((2, 4, per, wide), BF),
            pltpu.VMEM((2, 2, per, wide // 2), BF),
            pltpu.VMEM((2, 2, per, wide // 2), BF),
            pltpu.VMEM((2, 2, per, width), BF),
            pltpu.VMEM((2, 2, per, width), BF),
            pltpu.VMEM((2, 3, per, width), BF),
            pltpu.VMEM((2 * per, width), BF),
            large,
            small,
            small,
            small,
            small,
            small,
            small,
            small,
            small,
            pltpu.VMEM((4, width, width), BF),
            large,
            pltpu.VMEM((3, 4, size, 128), BF),
            pltpu.VMEM((size, width), BF),
            pltpu.VMEM((2, 2, size, size), BF),
            pltpu.SemaphoreType.DMA((11,)),
            pltpu.SemaphoreType.DMA((2,)),
            pltpu.SemaphoreType.DMA((2,)),
            pltpu.SemaphoreType.DMA((9,)),
            pltpu.SemaphoreType.DMA((16,)),
            pltpu.SemaphoreType.DMA((16,)),
        ],
        compiler_params=pltpu.CompilerParams(
            collective_id=2, has_side_effects=True, vmem_limit_bytes=62 * MIB
        ),
        name="mid",
    )(
        active, upper_low, second_low, hidden_low, grad_first, embedded, q, k, v, probs, wq, wk, wv, wo,
        kinds.reshape(tokens, 1), row(emb_gain),
    )


def flipped(index, bits):
    out = 0
    for place in range(3):
        bit = lax.rem(lax.div(index, 1 << place), 2)
        out = out + (1 << place) * (1 - bit if (bits >> place) & 1 else bit)
    return out


ORDER = (6, 7, 4, 5, 2, 3, 1)


def tail_kernel(
    slots, asked, asked_columns, pos, small, raw, normed, mixed, gfirst, dq, dk, dv, feed_own,
    word, packed, feed_out, small_out,
    tok, og, inc, rhs, dense, ops, turned, wbuf, wcore, w1a, w1b, w2a, w2b, wz, wown, small_by, small_in, small_dp,
    load_sem, t_send, t_recv, z_send, z_recv, d_send, d_recv, w_send, w_recv, s_send, s_recv, own_sem,
):
    chunks, owners, sources, pairs, lanes = og.shape
    half, width = pos.shape
    tokens = 2 * half
    tall = dense.shape[1]
    me = lax.axis_index("vocab")
    spot = lax.axis_index("dp")
    core, place = lax.rem(me, 2), lax.div(me, 2)
    xb, yb = lax.rem(spot, 2), lax.div(spot, 2)
    across_x = {"dp": spot + 1 - 2 * xb}
    across_y = {"dp": spot + 2 - 4 * yb}

    barrier = pltpu.get_barrier_semaphore()
    for k in ORDER:
        pl.semaphore_signal(barrier, inc=1, device_id={"vocab": flipped(me, k)}, device_id_type=MESH)
    for k in (1, 2, 3):
        pl.semaphore_signal(barrier, inc=1, device_id={"dp": flipped(spot, k)}, device_id_type=MESH)
    loads = [
        pltpu.make_async_copy(ref, ops.at[i], load_sem.at[i])
        for i, ref in enumerate((normed, dq, dk, dv, mixed, gfirst))
    ]
    for load in loads:
        load.start()
    for v in range(owners):
        per = width // owners
        small_by[v] = jnp.pad(small[:, v * per : (v + 1) * per], ((0, 0), (0, 128 - per)))
    pl.semaphore_wait(barrier, len(ORDER) + 3)

    def remote(src, dst, send, recv, peer):
        return pltpu.make_async_remote_copy(
            src_ref=src, dst_ref=dst, send_sem=send, recv_sem=recv, device_id=peer, device_id_type=MESH
        )

    def start(copies):
        for copy in copies:
            copy.start()

    def arrived(copies):
        for copy in copies:
            copy.wait_recv()

    def gone(copies):
        for copy in copies:
            copy.wait_send()

    def token_copies(c):
        copies = []
        for k in (3, 1, 2):
            peer = flipped(spot, k)
            copies.append(remote(raw.at[c, peer], tok.at[c, spot], t_send.at[c, k], t_recv.at[c, k], {"dp": peer}))
        return copies

    def token_own(c):
        return pltpu.make_async_copy(raw.at[c, spot], tok.at[c, spot], own_sem.at[c])

    for c in range(chunks):
        start(token_copies(c))
        token_own(c).start()

    def row_copy(c, k, peer):
        return remote(og.at[c, peer], inc.at[c, me], z_send.at[c, k], z_recv.at[c, k], {"vocab": peer})

    def row_copies(c):
        return [row_copy(c, k, flipped(me, k)) for k in ORDER]

    def fill(c, peer, target):
        def one(d, carry):
            lane = lax.broadcasted_iota(jnp.int32, (pairs, lanes), 1)
            wanted = lax.broadcasted_iota(jnp.int32, (2 * pairs, half), 0) + peer * (2 * pairs)
            tokens_in = tok[c, d]
            early = jnp.where(wanted == slots[d, :, :half], 1.0, 0.0).astype(BF)
            late = jnp.where(wanted == slots[d, :, half:], 1.0, 0.0).astype(BF)
            early = dot_nn(early, tokens_in)
            late = dot_nn(late, tokens_in)
            straight = jnp.where(lane < 64, early[:pairs], late[pairs:])
            crossed = jnp.where(lane < 64, early[pairs:], late[:pairs])
            target[d] = (straight + pltpu.roll(crossed, 64, 1)).astype(BF)
            return carry

        lax.fori_loop(0, sources, one, 0)

    def fill_all(c, send):
        for k in ORDER:
            peer = flipped(me, k)
            fill(c, peer, og.at[c, peer])
            if send:
                row_copy(c, k, peer).start()
        fill(c, me, inc.at[c, me])

    tile = 240
    depth = 1024

    def prepare(c):
        lane = lax.broadcasted_iota(jnp.int32, (pairs, lanes), 1)
        for v in range(owners):
            for d in range(sources):
                b = v * sources + d
                straight = inc[c, v, d].astype(F32)
                crossed = pltpu.roll(straight, 64, 1)
                for h in range(2):
                    column = asked_columns[:, h * owners * sources + b : h * owners * sources + b + 1]
                    value = jnp.where(lane < 64, crossed if h else straight, straight if h else crossed)
                    keep = (lane < 64) == (column < tall)
                    rhs[h, pl.ds(b * pairs, pairs), :] = jnp.where(keep, value, 0.0).astype(BF)

    def gather_rows(c, first, count):
        def one(t, carry):
            at = pl.multiple_of(t * tile, tile)
            total = jnp.zeros((tile, lanes), F32)
            for h in range(2):
                for b in range(owners * sources * pairs // depth):
                    ids = asked[h, :, b * depth : (b + 1) * depth]
                    ids = jnp.where(ids >= tall, ids - tall, ids) - at
                    hit = lax.broadcasted_iota(jnp.int32, (tile, depth), 0) == ids
                    total = total + dot_nn(
                        jnp.where(hit, 1.0, 0.0).astype(BF), rhs[h, pl.ds(b * depth, depth), :]
                    )
            dense[c, pl.ds(at, tile), :] = total.astype(BF)
            return carry

        lax.fori_loop(first, first + count, one, 0)

    part = tall // 2

    def lines_of(p):
        return pl.ds(p * part, part)

    def keep_copy(c, p):
        return pltpu.make_async_copy(
            dense.at[c, lines_of(p)], word.at[c, spot, lines_of(p)], own_sem.at[3 + 2 * c + p]
        )

    def near_copies(c, p):
        return [
            remote(
                dense.at[c, lines_of(p)], word.at[c, spot, lines_of(p)], d_send.at[c, 2 * p], d_recv.at[c, 2 * p], across_x
            ),
            remote(
                dense.at[c, lines_of(p)],
                word.at[c, spot, lines_of(p)],
                d_send.at[c, 2 * p + 1],
                d_recv.at[c, 2 * p + 1],
                across_y,
            ),
        ]

    def far_copy(c, p):
        source = flipped(spot, 1) if p == 0 else flipped(spot, 2)
        view = word.at[c, source, lines_of(p)]
        return remote(view, view, d_send.at[c, 4 + p], d_recv.at[c, 4 + p], across_y if p == 0 else across_x)

    per = width // owners
    block = 256
    quarter = wown.shape[0]

    def turn(which):
        def one(i, carry):
            at = pl.ds(pl.multiple_of(i * block, block), block)
            for j in range(width // block):
                there = pl.ds(j * block, block)
                turned[there, at] = ops[which, at, there].T
            return carry

        lax.fori_loop(0, tokens // block, one, 0)

    def weight(which, at):
        def one(n, carry):
            there = pl.ds(pl.multiple_of(n * block, block), block)
            out = dot_nn(turned[...], ops[which, :, there]).astype(BF)
            for v in range(owners):
                wbuf[v // 2, v % 2, pl.ds(at * per, per), there] = out[v * per : (v + 1) * per]
            return carry

        lax.fori_loop(0, width // block, one, 0)

    core_copy = remote(wbuf.at[:, 1 - core], wcore, w_send.at[0], w_recv.at[0], {"vocab": flipped(me, 1)})

    def wide(b):
        return pl.ds(pl.multiple_of(b * 2 * quarter, quarter), 2 * quarter)

    def narrow(b, c):
        return pl.ds(pl.multiple_of((2 * b + c) * quarter, quarter), quarter)

    def add(view, value):
        view[...] = (view[...].astype(F32) + value.astype(F32)).astype(BF)

    def core_step():
        core_copy.wait_recv()

        def one(i, carry):
            z = lax.div(i, 4)
            at = pl.ds(pl.multiple_of(lax.rem(i, 4) * quarter, quarter), quarter)
            add(wbuf.at[z, core, at, :], wcore[z, at, :])
            return carry

        lax.fori_loop(0, 16, one, 0)

    def first_weights():
        return [
            remote(wbuf.at[pl.ds(0, 2), core, wide(1 - xb), :], w1a, w_send.at[1], w_recv.at[1], across_x),
            remote(wbuf.at[pl.ds(2, 2), core, wide(1 - yb), :], w1b, w_send.at[2], w_recv.at[2], across_y),
        ]

    def second_weights():
        return [
            remote(wbuf.at[pl.ds(0, 2), core, narrow(xb, 1 - yb), :], w2a, w_send.at[3], w_recv.at[3], across_y),
            remote(wbuf.at[pl.ds(2, 2), core, narrow(yb, 1 - xb), :], w2b, w_send.at[4], w_recv.at[4], across_x),
        ]

    def first_step():
        arrived(first_weights())
        for z in range(2):
            add(wbuf.at[z, core, wide(xb), :], w1a[z])
            add(wbuf.at[2 + z, core, wide(yb), :], w1b[z])

    def second_step():
        arrived(second_weights())
        for z in range(2):
            add(wbuf.at[z, core, narrow(xb, yb), :], w2a[z])
            add(wbuf.at[2 + z, core, narrow(yb, xb), :], w2b[z])

    def owned(z):
        at = 2 * xb + yb + lax.div(z, 2) * (yb - xb)
        return wbuf.at[z, core, pl.ds(pl.multiple_of(at * quarter, quarter), quarter), :]

    def third_weights():
        copies = []
        for k in (3, 2, 1):
            to = flipped(place, k)
            copies.append(
                remote(owned(to), wz.at[k - 1], w_send.at[4 + k], w_recv.at[4 + k], {"vocab": 2 * to + core})
            )
        return copies

    def third_step():
        arrived(third_weights())
        total = owned(place)[...].astype(F32)
        for k in range(3):
            total = total + wz[k].astype(F32)
        wown[...] = total.astype(BF)

    def spread(own, target, at):
        wide_half = width // 2
        left, right = pl.ds(0, wide_half), pl.ds(wide_half, wide_half)
        kept = pltpu.make_async_copy(own, target.at[xb, yb], own_sem.at[9 + at])
        sems = [(w_send.at[8 + 4 * at + i], w_recv.at[8 + 4 * at + i]) for i in range(4)]
        near = [
            remote(own, target.at[xb, yb], *sems[0], across_x),
            remote(own, target.at[xb, yb], *sems[1], across_y),
        ]
        from_x, from_y = target.at[1 - xb, yb, :, left], target.at[xb, 1 - yb, :, right]
        far = [remote(from_x, from_x, *sems[2], across_y), remote(from_y, from_y, *sems[3], across_x)]
        return kept, near, far

    feed_kept, feed_near, feed_far = spread(feed_own, feed_out, 0)
    kept, fourth_weights, fifth_weights = spread(wown, packed, 1)

    def small_copies():
        copies = []
        for k in ORDER:
            peer = flipped(me, k)
            copies.append(remote(small_by.at[peer], small_in.at[k], s_send.at[k], s_recv.at[k], {"vocab": peer}))
        return copies

    def small_last():
        return [
            remote(small_in.at[0], small_dp.at[k - 1], s_send.at[7 + k], s_recv.at[7 + k], {"dp": flipped(spot, k)})
            for k in (1, 2, 3)
        ]

    start(small_copies())
    loads[0].wait()
    turn(0)
    loads[1].wait()
    weight(1, 0)
    token_own(0).wait()
    arrived(token_copies(0))
    fill_all(0, True)
    for i in (1, 2):
        loads[1 + i].wait()
        weight(1 + i, i)
    loads[4].wait()
    turn(4)
    loads[5].wait()
    weight(5, 3)
    share = half // owners
    for v in range(owners):
        wbuf[v // 2, v % 2, pl.ds(4 * per, share), :] = pos[pl.ds(v * share, share), :]
    core_copy.start()
    token_own(1).wait()
    arrived(token_copies(1))
    fill_all(1, False)
    core_step()
    start(first_weights())
    arrived(small_copies())
    total = small_by[me]
    for k in ORDER:
        total = total + small_in[k]
    small_in[0] = total
    start(small_last())
    token_own(2).wait()
    arrived(token_copies(2))
    fill_all(2, False)

    def close_chunk(c, between):
        arrived(row_copies(c))
        if c + 1 < chunks:
            start(row_copies(c + 1))
        else:
            start(third_weights())
        prepare(c)
        gather_rows(c, 0, 4)
        start(near_copies(c, 0))
        keep_copy(c, 0).start()
        between()
        gather_rows(c, 4, 4)
        start(near_copies(c, 1))
        keep_copy(c, 1).start()

    def pass_on(c):
        arrived(near_copies(c, 0))
        far_copy(c, 0).start()
        arrived(near_copies(c, 1))
        far_copy(c, 1).start()

    def nothing():
        return None

    first_step()
    start(second_weights())
    close_chunk(0, nothing)
    second_step()
    start(feed_near)
    feed_kept.start()
    pass_on(0)
    feed_kept.wait()
    arrived(feed_near)
    start(feed_far)
    close_chunk(1, nothing)
    arrived(small_last())
    total = small_in[0]
    for k in range(3):
        total = total + small_dp[k]
    small_out[...] = total
    pass_on(1)
    close_chunk(2, nothing)
    third_step()
    start(fourth_weights)
    kept.start()
    pass_on(2)
    kept.wait()
    arrived(fourth_weights)
    start(fifth_weights)

    for c in range(chunks):
        for p in range(2):
            keep_copy(c, p).wait()
            far_copy(c, p).wait_recv()
    arrived(feed_far)
    arrived(fifth_weights)
    core_copy.wait_send()
    gone(small_copies())
    gone(small_last())
    for c in range(chunks):
        gone(token_copies(c))
        gone(row_copies(c))
        for p in range(2):
            gone(near_copies(c, p))
            far_copy(c, p).wait_send()
    for copies in (first_weights(), second_weights(), third_weights(), fourth_weights, fifth_weights, feed_near, feed_far):
        gone(copies)


def tail(slots, asked, pos, small, raw, normed, mixed, gfirst, dq, dk, dv, feed_own, rows_local):
    half, width = pos.shape
    sources, owners, cap = asked.shape
    chunks = raw.shape[0]
    pairs = cap // 2
    tall = rows_local // 2
    lines = 4 * (width // owners) + half // owners
    vmem = pl.BlockSpec(memory_space=pltpu.VMEM)
    hbm = pl.BlockSpec(memory_space=pl.ANY)
    by_half = asked.reshape(sources, owners, 2, pairs).transpose(2, 1, 0, 3)
    columns = by_half.reshape(2 * owners * sources, pairs).T
    return pl.pallas_call(
        tail_kernel,
        out_shape=(
            jax.ShapeDtypeStruct((chunks, sources, tall, 128), BF),
            jax.ShapeDtypeStruct((2, 2, lines // 4, width), BF),
            jax.ShapeDtypeStruct((2, 2) + feed_own.shape, BF),
            jax.ShapeDtypeStruct((16, 128), F32),
        ),
        in_specs=[vmem] * 5 + [hbm] * 8,
        out_specs=(hbm, hbm, hbm, vmem),
        scratch_shapes=[
            pltpu.VMEM((chunks, sources, half, 128), BF),
            pltpu.VMEM((chunks, owners, sources, pairs, 128), BF),
            pltpu.VMEM((chunks, owners, sources, pairs, 128), BF),
            pltpu.VMEM((2, owners * sources * pairs, 128), BF),
            pltpu.VMEM((chunks, tall, 128), BF),
            pltpu.VMEM((6, 2 * half, width), BF),
            pltpu.VMEM((width, 2 * half), BF),
            pltpu.VMEM((4, 2, lines, width), BF),
            pltpu.VMEM((4, lines, width), BF),
            pltpu.VMEM((2, lines // 2, width), BF),
            pltpu.VMEM((2, lines // 2, width), BF),
            pltpu.VMEM((2, lines // 4, width), BF),
            pltpu.VMEM((2, lines // 4, width), BF),
            pltpu.VMEM((3, lines // 4, width), BF),
            pltpu.VMEM((lines // 4, width), BF),
            pltpu.VMEM((owners, 16, 128), F32),
            pltpu.VMEM((owners, 16, 128), F32),
            pltpu.VMEM((3, 16, 128), F32),
            pltpu.SemaphoreType.DMA((6,)),
            pltpu.SemaphoreType.DMA((chunks, 4)),
            pltpu.SemaphoreType.DMA((chunks, 4)),
            pltpu.SemaphoreType.DMA((chunks, owners)),
            pltpu.SemaphoreType.DMA((chunks, owners)),
            pltpu.SemaphoreType.DMA((chunks, 6)),
            pltpu.SemaphoreType.DMA((chunks, 6)),
            pltpu.SemaphoreType.DMA((16,)),
            pltpu.SemaphoreType.DMA((16,)),
            pltpu.SemaphoreType.DMA((11,)),
            pltpu.SemaphoreType.DMA((11,)),
            pltpu.SemaphoreType.DMA((11,)),
        ],
        compiler_params=pltpu.CompilerParams(collective_id=1, has_side_effects=True, vmem_limit_bytes=60 * MIB),
        name="tail",
    )(
        slots.reshape(sources, 1, 2 * half), by_half.reshape(2, 1, -1), columns, pos, small,
        raw, normed, mixed, gfirst, dq, dk, dv, feed_own,
    )


def finish_kernel(near, word_in, packed, feeds, word, query, keys, values, out, pos, up, down):
    lane = lax.broadcasted_iota(jnp.int32, word_in.shape[2:], 1)
    chunks, sources = word_in.shape[:2]
    for c in range(chunks):
        for q in range(0, sources, 2):
            one, two = word_in[c, q].astype(F32), word_in[c, q + 1].astype(F32)
            at = pl.ds((c * sources + q) * 64, 128)
            word[0, :, at] = jnp.where(lane < 64, one, pltpu.roll(two, 64, 1))
            word[1, :, at] = jnp.where(lane < 64, pltpu.roll(one, 64, 1), two)

    @pl.when(pl.program_id(0) == 0)
    def _():
        n = near[0]
        order = ((0, 0), (1 - n, n), (n, 1 - n), (1, 1))
        per, width = query.shape
        rows = jnp.concatenate([packed[a, b] for a, b in order], 0).astype(F32)
        for i, target in enumerate((query, keys, values, out)):
            target[...] = rows[i * per : (i + 1) * per]
        pos[...] = rows[4 * per :]
        lines = []
        for i, (a, b) in enumerate(order):
            up[:, pl.ds(i * width, width)] = feeds[a, b, per:, :].astype(F32)
            for j in range(2):
                lines.append(feeds[a, b, :per, j * 4 * per : (j + 1) * 4 * per])
        down[...] = jnp.concatenate(lines, 0).astype(F32).T


def finish(near, word, packed, feeds, rows_local, owners):
    chunks, sources, tall, _ = word.shape
    width = packed.shape[3]
    per = width // owners
    steps = 8
    part = tall // steps
    held = jax.ShapeDtypeStruct((per, width), F32)
    share = packed.shape[2] * 4 - 4 * per
    shapes = [held] * 4 + [
        jax.ShapeDtypeStruct((share, width), F32),
        jax.ShapeDtypeStruct((per, 4 * width), F32),
        jax.ShapeDtypeStruct((4 * per, width), F32),
    ]
    results = pl.pallas_call(
        finish_kernel,
        grid_spec=pltpu.PrefetchScalarGridSpec(
            num_scalar_prefetch=1,
            grid=(steps,),
            in_specs=[
                pl.BlockSpec((chunks, sources, part, 128), lambda i, *_: (0, 0, i, 0)),
                fixed(packed.shape),
                fixed(feeds.shape),
            ],
            out_specs=[pl.BlockSpec((2, part, width), lambda i, *_: (0, i, 0))] + [fixed(s.shape) for s in shapes],
        ),
        out_shape=[jax.ShapeDtypeStruct((2, tall, width), F32)] + shapes,
        compiler_params=pltpu.CompilerParams(vmem_limit_bytes=48 * MIB),
        name="finish",
    )(near.astype(jnp.int32).reshape(1), word, packed, feeds)
    return [results[0].reshape(rows_local, width)] + list(results[1:])


def local(
    token_ids,
    type_ids,
    lengths,
    word_table,
    pos_table,
    token_type_embeddings,
    emb_gain,
    emb_bias,
    query_weight,
    query_bias,
    key_weight,
    value_weight,
    value_bias,
    out_weight,
    out_bias,
    attn_gain,
    attn_bias,
    up_weight,
    up_bias,
    down_weight,
    down_bias,
    final_gain,
    final_bias,
    cotangent,
):
    seq_count, seq_len = token_ids.shape
    tokens = seq_count * seq_len
    width = word_table.shape[1]
    rows_local = word_table.shape[0]
    owners = lax.axis_size("vocab")
    capacity = max(2, 2 * tokens // owners)
    flat_ids = token_ids.reshape(tokens)
    owner = flat_ids // rows_local
    member = (owner[:, None] == jnp.arange(owners)[None, :]).astype(jnp.int32)
    earlier = jnp.cumsum(member, 0) - member
    rank = jnp.sum(earlier * member, 1)
    slot = owner * capacity + rank
    requests = (
        jnp.full((owners * capacity,), -1, jnp.int32).at[slot].set(flat_ids - owner * rows_local)
    )
    requests = requests.reshape(owners, capacity)
    asked = lax.all_to_all(requests, "vocab", split_axis=0, concat_axis=0, tiled=True)
    valid = asked >= 0
    found = word_table[jnp.maximum(asked, 0)]
    found = jnp.where(valid[..., None], found, jnp.zeros((), jnp.bfloat16))
    returned = lax.all_to_all(found, "vocab", split_axis=0, concat_axis=0, tiled=True)
    word_rows = returned.reshape(owners * capacity, width)[slot]
    kinds = token_type_embeddings.shape[0]
    selection_matrix = (type_ids[..., None] == jnp.arange(kinds)[None, None, :]).astype(jnp.float32)
    type_rows = jnp.einsum(
        "tcr,rb->tcb",
        selection_matrix,
        token_type_embeddings.astype(jnp.float32),
        precision=lax.Precision.HIGHEST,
    )
    embedded = (
        word_rows.reshape(seq_count, seq_len, width).astype(jnp.float32)
        + pos_table.astype(jnp.float32)[None]
        + type_rows
    )
    embedded = embedded.reshape(tokens, width)
    normed = layer_norm(embedded, emb_gain, emb_bias)
    normed_low, query, keys, values, mixed_low, first, probs = attend(
        lengths, normed, query_weight, key_weight, value_weight, out_weight, query_bias, value_bias, out_bias
    )
    encoded, active_low, grad_second_low, hidden_low, grad_upper_low, grad_first, sums, grad_up_bias = feed(
        first,
        cotangent.reshape(tokens, width),
        up_weight,
        down_weight,
        up_bias,
        down_bias,
        attn_gain,
        attn_bias,
        final_gain,
        final_bias,
    )
    grad_final_gain, grad_final_bias, grad_down_bias, grad_attn_gain, grad_attn_bias, grad_out_bias = [
        sums[i] for i in range(6)
    ]
    grad_up_bias = grad_up_bias[0]
    fast = owners == 8 and lax.axis_size("dp") == 4
    if fast:
        (
            grad_first_low,
            grad_query_low,
            grad_keys_low,
            grad_values_low,
            raw,
            grad_pos,
            feed_own,
            sums,
        ) = mid(
            active_low,
            grad_upper_low,
            grad_second_low,
            hidden_low,
            grad_first,
            embedded,
            query,
            keys,
            values,
            probs,
            query_weight,
            key_weight,
            value_weight,
            out_weight,
            type_ids,
            emb_gain,
        )
    else:
        grad_down = matmul_tn(active_low, grad_second_low)
        grad_up = matmul_tn(hidden_low, grad_upper_low)
        grad_first_low, grad_query_low, grad_keys_low, grad_values_low, embedding_output_gradient, sums = attend_back(
            grad_first,
            embedded,
            type_ids,
            query,
            keys,
            values,
            probs,
            query_weight,
            key_weight,
            value_weight,
            out_weight,
            emb_gain,
        )
        grad_pos = jnp.sum(embedding_output_gradient.astype(jnp.float32).reshape(seq_count, seq_len, width), 0)
    grad_query_bias, grad_value_bias, grad_emb_gain, grad_emb_bias = [sums[i] for i in range(4)]
    token_type_gradient = sums[4:6]
    bf = jnp.bfloat16
    per = width // owners
    small = jnp.stack(
        [
            grad_query_bias,
            grad_value_bias,
            grad_out_bias,
            grad_attn_gain,
            grad_attn_bias,
            grad_emb_gain,
            grad_emb_bias,
            grad_down_bias,
            grad_final_gain,
            grad_final_bias,
            token_type_gradient[0],
            token_type_gradient[1],
        ]
    )
    if fast:
        ups = grad_up_bias.reshape(owners, 4, per).transpose(1, 0, 2).reshape(4, width)
        lists = lax.all_gather(jnp.concatenate([slot, asked.reshape(-1)]), "dp")
        word_pairs, packed, feeds, small = tail(
            lists[:, :tokens],
            lists[:, tokens:].reshape(-1, owners, capacity),
            grad_pos,
            jnp.concatenate([small, ups], 0),
            raw,
            normed_low,
            mixed_low,
            grad_first_low,
            grad_query_low,
            grad_keys_low,
            grad_values_low,
            feed_own,
            rows_local,
        )
        near = lax.axis_index("vocab") < owners // 2
        (
            grad_word,
            grad_query_weight,
            grad_key_weight,
            grad_value_weight,
            grad_out_weight,
            grad_pos,
            grad_up,
            grad_down,
        ) = finish(near, word_pairs, packed, feeds, rows_local, owners)
        small = small[:, :per]
    else:
        grad_down = sum_over_all(grad_down.astype(bf))
        grad_up = sum_over_all(grad_up.astype(bf))
        places = slot[None, :] == jnp.arange(owners * capacity)[:, None]
        outgoing = matmul(
            places.astype(bf), embedding_output_gradient.reshape(tokens, width).astype(bf)
        ).astype(bf)
        hits = (jnp.arange(rows_local)[:, None] == asked.reshape(-1)[None, :]).astype(bf)
        pieces = []
        step = 256
        for start in range(0, width, step):
            incoming = lax.all_to_all(
                outgoing[:, start : start + step].reshape(owners, capacity, step),
                "vocab",
                split_axis=0,
                concat_axis=0,
                tiled=True,
            )
            dense = matmul(hits, incoming.reshape(owners * capacity, step)).astype(bf)
            pieces.append(sum_over_dp(dense))
        grad_word = jnp.concatenate(pieces, 1)
        small = small.reshape(12, owners, per).transpose(1, 0, 2).reshape(owners, 12 * per)
        small = jnp.concatenate([small, grad_up_bias.reshape(owners, 4 * per)], 1)
        wide = 4 * width
        lines = (seq_len // owners) * width // wide
        rest = per // 3 - lines
        small_lines = jnp.pad(small, ((0, 0), (0, rest * wide - 16 * per))).reshape(owners, rest, wide)
        grad_query_weight, grad_key_weight, grad_value_weight = [
            matmul_tn(normed_low, g) for g in (grad_query_low, grad_keys_low, grad_values_low)
        ]
        grad_out_weight = matmul_tn(mixed_low, grad_first_low)
        mixed_grads = jnp.concatenate(
            [grad_query_weight, grad_key_weight, grad_value_weight, grad_out_weight], 1
        ).astype(bf)
        packed = jnp.concatenate(
            [
                mixed_grads.reshape(owners, per, wide),
                grad_pos.astype(bf).reshape(owners, lines, wide),
                small_lines.astype(bf),
            ],
            1,
        )
        packed = sum_over_all(packed.reshape(-1, wide))
        weights = packed[:per]
        grad_query_weight = weights[:, :width]
        grad_key_weight = weights[:, width : 2 * width]
        grad_value_weight = weights[:, 2 * width : 3 * width]
        grad_out_weight = weights[:, 3 * width :]
        grad_pos = packed[per : per + lines].reshape(seq_len // owners, width)
        small = packed[per + lines :].reshape(-1)[: 16 * per].reshape(16, per)
    (
        grad_query_bias,
        grad_value_bias,
        grad_out_bias,
        grad_attn_gain,
        grad_attn_bias,
        grad_emb_gain,
        grad_emb_bias,
        grad_down_bias,
        grad_final_gain,
        grad_final_bias,
    ) = [small[i] for i in range(10)]
    token_type_gradient = small[10:12]
    grad_up_bias = small[12:].reshape(-1)
    return (
        encoded.reshape(seq_count, seq_len, width),
        grad_word,
        grad_pos,
        token_type_gradient,
        grad_emb_gain,
        grad_emb_bias,
        grad_query_weight,
        grad_query_bias,
        grad_key_weight,
        grad_value_weight,
        grad_value_bias,
        grad_out_weight,
        grad_out_bias,
        grad_attn_gain,
        grad_attn_bias,
        grad_up,
        grad_up_bias,
        grad_down,
        grad_down_bias,
        grad_final_gain,
        grad_final_bias,
    )


def solution(mesh):
    placed = (
        P(("dp", "vocab"), None),
        P(("dp", "vocab"), None),
        P(("dp", "vocab")),
        P("vocab", None),
        P(),
        P(),
        P(),
        P(),
        P(),
        P(),
        P(),
        P(),
        P(),
        P(),
        P(),
        P(),
        P(),
        P(),
        P(),
        P(),
        P(),
        P(),
        P(),
        P(("dp", "vocab"), None, None),
    )
    return jax.shard_map(
        local,
        mesh=mesh,
        in_specs=placed,
        out_specs=(
            P(("dp", "vocab"), None, None),
            P("vocab", None),
            P("vocab", None),
            P(None, "vocab"),
            P("vocab"),
            P("vocab"),
            P("vocab", None),
            P("vocab"),
            P("vocab", None),
            P("vocab", None),
            P("vocab"),
            P("vocab", None),
            P("vocab"),
            P("vocab"),
            P("vocab"),
            P("vocab", None),
            P("vocab"),
            P("vocab", None),
            P("vocab"),
            P("vocab"),
            P("vocab"),
        ),
        check_vma=False,
    )
```

```python
from functools import partial

import jax
import jax.numpy as jnp
from jax import lax
from jax.experimental import pallas as pl
from jax.experimental.pallas import tpu as pltpu
from jax.sharding import PartitionSpec as P

HEADS = 12
HEAD = 64
L = 512


EPSILON = 1e-12


def layer_norm(values, gain, bias):
    center = values - jnp.mean(values, -1, keepdims=True)
    spread = jnp.mean(center * center, -1, keepdims=True)
    return center * lax.rsqrt(spread + EPSILON) * gain + bias


def matmul(left, right):
    return jnp.dot(left, right, preferred_element_type=jnp.float32)


def matmul_tn(left, right):
    return lax.dot_general(
        left, right, (((0,), (0,)), ((), ())), preferred_element_type=jnp.float32
    )


def matmul_nt(left, right):
    return lax.dot_general(
        left, right, (((1,), (1,)), ((), ())), preferred_element_type=jnp.float32
    )


def swap(value, axis_name, bit):
    size = lax.axis_size(axis_name)
    return lax.ppermute(value, axis_name, [(i, i ^ bit) for i in range(size)])


def pick(value, index, axis):
    return lax.dynamic_index_in_dim(value, index, axis, keepdims=False)


def plus(left, right):
    return (left.astype(jnp.float32) + right.astype(jnp.float32)).astype(jnp.bfloat16)


def dp_bits():
    index = lax.axis_index("dp")
    return lax.rem(index, 2), index // 2


def reorder(own, across_x, across_y, across_both):
    xb, yb = dp_bits()
    flip_x, flip_y = xb == 1, yb == 1
    rows = [[own, across_y], [across_x, across_both]]
    rows = [
        [jnp.where(flip_x, rows[1 - i][j], rows[i][j]) for j in range(2)] for i in range(2)
    ]
    rows = [
        [jnp.where(flip_y, rows[i][1 - j], rows[i][j]) for j in range(2)] for i in range(2)
    ]
    return rows


def sum_over_all(grad):
    size = lax.axis_size("vocab")
    me = lax.axis_index("vocab")
    core = lax.rem(me, 2)
    place = me // 2
    places = size // 2
    total, n = grad.shape
    r = total // size
    xb, yb = dp_bits()
    grad = grad.reshape(places, 2, r, n)
    other = swap(pick(grad, 1 - core, 1), "vocab", 1)
    held = plus(pick(grad, core, 1), other).reshape(places, 2, 2, r // 4, n)
    first, last = held[: places // 2], held[places // 2 :]
    first_in = swap(pick(first, 1 - xb, 1), "dp", 1)
    last_in = swap(pick(last, 1 - yb, 2), "dp", 2)
    first = plus(pick(first, xb, 1), first_in)
    last = plus(pick(last, yb, 2), last_in)
    first_in = swap(pick(first, 1 - yb, 1), "dp", 2)
    last_in = swap(pick(last, 1 - xb, 1), "dp", 1)
    first = plus(pick(first, yb, 1), first_in)
    last = plus(pick(last, xb, 1), last_in)
    held = jnp.concatenate([first, last], 0)
    summed = pick(held, place, 0).astype(jnp.float32)
    for step in range(1, places):
        block = pick(held, lax.rem(place + step, places), 0)
        block = lax.ppermute(
            block, "vocab", [(i, (i + 2 * step) % size) for i in range(size)]
        )
        summed = summed + block.astype(jnp.float32)
    own = summed.astype(jnp.bfloat16)
    across_x = swap(own, "dp", 1)
    across_y = swap(own, "dp", 2)
    half = n // 2
    both = jnp.concatenate(
        [swap(across_x[:, :half], "dp", 2), swap(across_y[:, half:], "dp", 1)], 1
    )
    rows = reorder(own, across_x, across_y, both)
    return jnp.stack([rows[0][0], rows[0][1], rows[1][0], rows[1][1]]).reshape(r, n).astype(jnp.float32)


def sum_over_dp(grad):
    rows, n = grad.shape
    xb, yb = dp_bits()
    held = grad.reshape(2, 2, 2, rows // 8, n)
    first, last = held[0], held[1]
    first_in = swap(pick(first, 1 - xb, 0), "dp", 1)
    last_in = swap(pick(last, 1 - yb, 1), "dp", 2)
    first = plus(pick(first, xb, 0), first_in)
    last = plus(pick(last, yb, 1), last_in)
    first_in = swap(pick(first, 1 - yb, 0), "dp", 2)
    last_in = swap(pick(last, 1 - xb, 0), "dp", 1)
    first = plus(pick(first, yb, 0), first_in)
    last = plus(pick(last, xb, 0), last_in)
    first_x = swap(first, "dp", 1)
    last_y = swap(last, "dp", 2)
    first_y = swap(jnp.stack([first, first_x]), "dp", 2)
    last_x = swap(jnp.stack([last, last_y]), "dp", 1)
    a = reorder(first, first_x, first_y[0], first_y[1])
    b = reorder(last, last_x[0], last_y, last_x[1])
    parts = [p for group in (a, b) for line in group for p in line]
    return jnp.concatenate(parts, 0).astype(jnp.float32)


BF = jnp.bfloat16
F32 = jnp.float32
MIB = 1024 * 1024


def dot_nt(left, right):
    return lax.dot_general(left, right, (((1,), (1,)), ((), ())), preferred_element_type=F32)


def dot_nn(left, right):
    return jnp.dot(left, right, preferred_element_type=F32)


def stats(values):
    center = values - jnp.mean(values, -1, keepdims=True)
    inverse = lax.rsqrt(jnp.mean(center * center, -1, keepdims=True) + EPSILON)
    return center * inverse, inverse


def norm_back(grad, gain, unit, inverse):
    scaled = grad * gain
    return inverse * (
        scaled
        - jnp.mean(scaled, -1, keepdims=True)
        - unit * jnp.mean(scaled * unit, -1, keepdims=True)
    )


def column_sum(values):
    return jnp.sum(values, 0, keepdims=True)


TAIL_SCALE = 0.33
TAIL_TERMS = (
    -0.13534782292195252,
    0.4602463244004558,
    -0.3511662200543899,
    0.4085159085223644,
    0.04721176063633592,
    0.2012267561020528,
    0.1829554472050349,
    0.1863578383326851,
)


def normal_parts(u):
    t = 1.0 / (1.0 + (TAIL_SCALE * 0.5**0.5) * jnp.abs(u))
    poly = TAIL_TERMS[0]
    for term in TAIL_TERMS[1:]:
        poly = poly * t + term
    bell = jnp.exp(u * u * -0.5)
    below = (0.5 * t) * poly * bell
    return jnp.where(u >= 0, 1.0 - below, below), bell * 0.3989422804014327


def attend_kernel(
    lengths, normed, wq, wk, wv, wo, query_bias, value_bias, out_bias,
    low, q_out, k_out, v_out, mixed_out, first_out, probs_out, bias,
):
    tokens, width = normed.shape
    tile = 256
    low[...] = normed[...].astype(BF)

    def project(n, carry):
        at = pl.ds(pl.multiple_of(n * tile, tile), tile)
        x = low[...]
        query = (dot_nn(x, wq[:, at]) + query_bias[:, at]).astype(BF)
        q_out[:, at] = query * BF(HEAD**-0.5)
        k_out[:, at] = dot_nn(x, wk[:, at]).astype(BF)
        v_out[:, at] = (dot_nn(x, wv[:, at]) + value_bias[:, at]).astype(BF)
        return carry

    lax.fori_loop(0, width // tile, project, 0)
    seen = lax.broadcasted_iota(jnp.int32, bias.shape, 0) < lengths[pl.program_id(0)]
    bias[...] = jnp.where(seen, 0.0, -1000000000.0)

    def pair(j, carry):
        at = pl.ds(pl.multiple_of(j * 2 * HEAD, 2 * HEAD), 2 * HEAD)
        q, k, turned = q_out[:, at], k_out[:, at], v_out[:, at].T
        lane = lax.broadcasted_iota(jnp.int32, k.shape, 1)
        parts = []
        for side in range(2):
            mine = (lane >= HEAD) if side else (lane < HEAD)
            scores = dot_nt(jnp.where(mine, k, jnp.zeros_like(k)), q)
            scores = scores + jnp.concatenate([bias[...]] * (tokens // 128), 1)
            expd = jnp.exp(scores - jnp.max(scores, 0, keepdims=True))
            probs = (expd * (1.0 / jnp.sum(expd, 0, keepdims=True))).astype(BF)
            probs_out[0, 2 * j + side] = probs
            parts.append(dot_nn(turned[side * HEAD : (side + 1) * HEAD], probs))
        mixed_out[:, at] = jnp.concatenate(parts, 0).T.astype(BF)
        return carry

    lax.fori_loop(0, HEADS // 2, pair, 0)

    def close(n, carry):
        at = pl.ds(pl.multiple_of(n * tile, tile), tile)
        first_out[:, at] = normed[:, at] + dot_nn(mixed_out[...], wo[:, at]) + out_bias[:, at]
        return carry

    lax.fori_loop(0, width // tile, close, 0)


def fixed(shape):
    return pl.BlockSpec(shape, lambda i, *_: (0,) * len(shape), pipeline_mode=pl.Buffered(1))


def rows_of(rows, width):
    return pl.BlockSpec((rows, width), lambda i, *_: (i, 0))


def row(vector):
    return vector.reshape(1, -1)


def attend(lengths, normed, wq, wk, wv, wo, query_bias, value_bias, out_bias):
    tokens, width = normed.shape
    seqs = lengths.shape[0]
    size = tokens // seqs
    low = jax.ShapeDtypeStruct((tokens, width), BF)
    part = rows_of(size, width)
    return pl.pallas_call(
        attend_kernel,
        grid_spec=pltpu.PrefetchScalarGridSpec(
            num_scalar_prefetch=1,
            grid=(seqs,),
            in_specs=[part] + [fixed((width, width))] * 4 + [fixed((1, width))] * 3,
            out_specs=[part] * 6 + [pl.BlockSpec((1, HEADS, size, size), lambda i, *_: (i, 0, 0, 0))],
            scratch_shapes=[pltpu.VMEM((size, 128), F32)],
        ),
        out_shape=[low] * 5
        + [jax.ShapeDtypeStruct((tokens, width), F32), jax.ShapeDtypeStruct((seqs, HEADS, size, size), BF)],
        compiler_params=pltpu.CompilerParams(vmem_limit_bytes=60 * MIB),
        cost_estimate=pl.CostEstimate(flops=20 * 10**9, bytes_accessed=30 * 10**6, transcendentals=0),
        name="attend",
    )(lengths, normed, wq, wk, wv, wo, row(query_bias), row(value_bias), row(out_bias))


def feed_kernel(
    first, cotangent, up, down, up_bias, down_bias, attn_gain, attn_bias, final_gain, final_bias,
    encoded, active, second_low, hidden_low, upper_low, first_grad, sums, up_sum,
    slope,
):
    width = first.shape[1]
    units = up.shape[1]
    block = 768
    unit, inverse = stats(first[...])
    hidden = unit * attn_gain[...] + attn_bias[...]
    hidden_low[...] = hidden.astype(BF)
    total = hidden + down_bias[...]
    for n in range(units // block):
        at = pl.ds(n * block, block)
        upper = dot_nn(hidden_low[...], up[:, at]) + up_bias[:, at]
        below, density = normal_parts(upper)
        active[:, at] = (upper * below).astype(BF)
        slope[:, at] = below + upper * density
        total = total + dot_nn(active[:, at], down[at, :])
    unit_out, inverse_out = stats(total)
    encoded[...] = unit_out * final_gain[...] + final_bias[...]
    grad = cotangent[...].astype(F32)
    grad_second = norm_back(grad, final_gain[...], unit_out, inverse_out)
    second_low[...] = grad_second.astype(BF)

    @pl.when(pl.program_id(0) == 0)
    def _():
        sums[...] = jnp.zeros_like(sums)
        up_sum[...] = jnp.zeros_like(up_sum)

    sums[0:1, :] += column_sum(grad * unit_out)
    sums[1:2, :] += column_sum(grad)
    sums[2:3, :] += column_sum(grad_second)
    total = grad_second
    for n in range(units // block):
        at = pl.ds(n * block, block)
        grad_upper = dot_nt(second_low[...], down[at, :]) * slope[:, at]
        up_sum[:, at] += column_sum(grad_upper)
        upper_low[:, at] = grad_upper.astype(BF)
        total = total + dot_nt(upper_low[:, at], up[:, at])
    grad_first = norm_back(total, attn_gain[...], unit, inverse)
    sums[3:4, :] += column_sum(total * unit)
    sums[4:5, :] += column_sum(total)
    sums[5:6, :] += column_sum(grad_first)
    first_grad[...] = grad_first


def feed(first, cotangent, up, down, up_bias, down_bias, attn_gain, attn_bias, final_gain, final_bias):
    tokens, width = first.shape
    units = up.shape[1]
    tile = 256
    part, wide = rows_of(tile, width), rows_of(tile, units)
    vector = fixed((1, width))
    return pl.pallas_call(
        feed_kernel,
        grid=(tokens // tile,),
        in_specs=[part, part, fixed((width, units)), fixed((units, width)), fixed((1, units))] + [vector] * 5,
        out_specs=[part, wide, part, part, wide, part, fixed((8, width)), fixed((1, units))],
        out_shape=[
            jax.ShapeDtypeStruct((tokens, width), F32),
            jax.ShapeDtypeStruct((tokens, units), BF),
            jax.ShapeDtypeStruct((tokens, width), BF),
            jax.ShapeDtypeStruct((tokens, width), BF),
            jax.ShapeDtypeStruct((tokens, units), BF),
            jax.ShapeDtypeStruct((tokens, width), F32),
            jax.ShapeDtypeStruct((8, width), F32),
            jax.ShapeDtypeStruct((1, units), F32),
        ],
        scratch_shapes=[pltpu.VMEM((tile, units), F32)],
        compiler_params=pltpu.CompilerParams(vmem_limit_bytes=60 * MIB),
        cost_estimate=pl.CostEstimate(flops=40 * 10**9, bytes_accessed=40 * 10**6, transcendentals=0),
        name="feed",
    )(
        first, cotangent, up, down, row(up_bias), row(down_bias), row(attn_gain), row(attn_bias),
        row(final_gain), row(final_bias),
    )


def attend_back_kernel(
    grad_first, embedded, kinds, q_in, k_in, v_in, probs_in, wq, wk, wv, wo, emb_gain,
    first_low, dq, dk, dv, emb_low, sums,
    grad_mixed, total,
):
    tokens, width = grad_first.shape
    tile = 256

    @pl.when(pl.program_id(0) == 0)
    def _():
        sums[...] = jnp.zeros_like(sums)

    first_low[...] = grad_first[...].astype(BF)

    def open_(n, carry):
        at = pl.ds(pl.multiple_of(n * tile, tile), tile)
        grad_mixed[:, at] = dot_nt(first_low[...], wo[at, :]).astype(BF)
        return carry

    lax.fori_loop(0, width // tile, open_, 0)

    def pair(j, carry):
        at = pl.ds(pl.multiple_of(j * 2 * HEAD, 2 * HEAD), 2 * HEAD)
        q, k, v, grad = q_in[:, at], k_in[:, at], v_in[:, at], grad_mixed[:, at]
        turned = k.T
        lane = lax.broadcasted_iota(jnp.int32, k.shape, 1)
        parts = []
        grad_k = jnp.zeros(k.shape, F32)
        grad_v = jnp.zeros(k.shape, F32)
        for side in range(2):
            mine = (lane >= HEAD) if side else (lane < HEAD)
            none = jnp.zeros_like(k)
            probs = probs_in[0, 2 * j + side]
            grad_probs = dot_nt(jnp.where(mine, v, none), grad)
            grad_v = grad_v + dot_nn(probs, jnp.where(mine, grad, none))
            wide = probs.astype(F32)
            both = wide * grad_probs
            scores = (both - wide * jnp.sum(both, 0, keepdims=True)).astype(BF)
            grad_k = grad_k + dot_nn(scores, jnp.where(mine, q, none))
            parts.append(dot_nn(turned[side * HEAD : (side + 1) * HEAD], scores))
        grad_q = jnp.concatenate(parts, 0).T * HEAD**-0.5
        dq[:, at] = grad_q.astype(BF)
        dk[:, at] = grad_k.astype(BF)
        dv[:, at] = grad_v.astype(BF)
        sums[0:1, at] += column_sum(grad_q)
        sums[1:2, at] += column_sum(grad_v)
        return carry

    lax.fori_loop(0, HEADS // 2, pair, 0)

    def close(n, carry):
        at = pl.ds(pl.multiple_of(n * tile, tile), tile)
        total[:, at] = (
            grad_first[:, at]
            + dot_nt(dq[...], wq[at, :])
            + dot_nt(dk[...], wk[at, :])
            + dot_nt(dv[...], wv[at, :])
        )
        return carry

    lax.fori_loop(0, width // tile, close, 0)
    rows = 128

    def last(n, carry):
        at = pl.ds(pl.multiple_of(n * rows, rows), rows)
        unit, inverse = stats(embedded[at, :])
        grad = total[at, :]
        grad_emb = norm_back(grad, emb_gain[...], unit, inverse)
        emb_low[at, :] = grad_emb.astype(BF)
        sums[2:3, :] += column_sum(grad * unit)
        sums[3:4, :] += column_sum(grad)
        kind = kinds[at, :]
        for t in range(2):
            sums[4 + t : 5 + t, :] += column_sum(jnp.where(kind == t, grad_emb, 0.0))
        return carry

    lax.fori_loop(0, tokens // rows, last, 0)


def attend_back(grad_first, embedded, kinds, q, k, v, probs, wq, wk, wv, wo, emb_gain):
    tokens, width = grad_first.shape
    seqs, _, size, _ = probs.shape
    part = rows_of(size, width)
    low = jax.ShapeDtypeStruct((tokens, width), BF)
    return pl.pallas_call(
        attend_back_kernel,
        grid=(seqs,),
        in_specs=[part, part, rows_of(size, 1)]
        + [part] * 3
        + [pl.BlockSpec((1, HEADS, size, size), lambda i: (i, 0, 0, 0))]
        + [fixed((width, width))] * 4
        + [fixed((1, width))],
        out_specs=[part] * 5 + [fixed((8, width))],
        out_shape=[low] * 5 + [jax.ShapeDtypeStruct((8, width), F32)],
        scratch_shapes=[pltpu.VMEM((size, width), BF), pltpu.VMEM((size, width), F32)],
        compiler_params=pltpu.CompilerParams(vmem_limit_bytes=60 * MIB),
        cost_estimate=pl.CostEstimate(flops=30 * 10**9, bytes_accessed=40 * 10**6, transcendentals=0),
        name="attend_back",
    )(grad_first, embedded, kinds.reshape(tokens, 1), q, k, v, probs, wq, wk, wv, wo, row(emb_gain))


MESH = pl.DeviceIdType.MESH


def mid_kernel(
    active, upper_low, second_low, hidden_low, grad_first, embedded, q_in, k_in, v_in, probs_in, wq, wk, wv, wo,
    kinds, emb_gain,
    first_out, dq_out, dk_out, dv_out, raw_out, pos_out, feed_out, sums,
    stage, lhs, turned, grads, core_in, in_1a, in_1b, in_2a, in_2b, in_z, kept,
    first, low, grad_mixed, q, k, v, dq, dk, dv, weights, table, raw, pos, probs,
    load, stage_sem, probs_sem, out_sem, send, recv,
):
    tokens, width = lhs.shape
    size = probs.shape[2]
    seqs = tokens // size
    per = grads.shape[3]
    me = lax.axis_index("vocab")
    spot = lax.axis_index("dp")
    core, place = lax.rem(me, 2), lax.div(me, 2)
    xb, yb = lax.rem(spot, 2), lax.div(spot, 2)
    across_x = {"dp": spot + 1 - 2 * xb}
    across_y = {"dp": spot + 2 - 4 * yb}
    partner = {"vocab": me + 1 - 2 * core}
    block = 768
    blocks = active.shape[1] // block

    def stage_copy(n):
        source = active if n < blocks else upper_low
        at = pl.ds((n % blocks) * block, block)
        return pltpu.make_async_copy(source.at[:, at], stage.at[n % 2], stage_sem.at[n % 2])

    def probs_copy(n):
        return pltpu.make_async_copy(
            probs_in.at[lax.div(n, HEADS // 2), pl.ds(2 * lax.rem(n, HEADS // 2), 2)],
            probs.at[lax.rem(n, 2)],
            probs_sem.at[lax.rem(n, 2)],
        )

    second_copy = pltpu.make_async_copy(second_low, lhs, load.at[0])
    hidden_copy = pltpu.make_async_copy(hidden_low, lhs, load.at[1])
    second_copy.start()
    stage_copy(0).start()
    stage_copy(1).start()
    loads = [
        pltpu.make_async_copy(source, target, load.at[2 + i])
        for i, (source, target) in enumerate(
            (
                (grad_first, first),
                (wo, weights.at[3]),
                (q_in, q),
                (k_in, k),
                (v_in, v),
                (wq, weights.at[0]),
                (wk, weights.at[1]),
                (wv, weights.at[2]),
                (embedded, table),
            )
        )
    ]
    barrier = pltpu.get_barrier_semaphore()
    places = [{"vocab": 2 * flipped(place, k) + core} for k in (1, 2, 3)]
    for peer in [partner, across_x, across_y] + places:
        pl.semaphore_signal(barrier, inc=1, device_id=peer, device_id_type=MESH)
    pl.semaphore_wait(barrier, 6)

    def remote(src, dst, at, peer):
        return pltpu.make_async_remote_copy(
            src_ref=src, dst_ref=dst, send_sem=send.at[at], recv_sem=recv.at[at], device_id=peer, device_id_type=MESH
        )

    def core_copy(g):
        return remote(grads.at[g, :, 1 - core], core_in.at[g], 5 * g, partner)

    half = 2 * width

    def wide(b):
        return pl.ds(pl.multiple_of(b * half, half), half)

    def narrow(b, c):
        return pl.ds(pl.multiple_of(b * half + c * width, width), width)

    def first_copies(g):
        return [
            remote(grads.at[g, pl.ds(0, 2), core, :, wide(1 - xb)], in_1a.at[g], 5 * g + 1, across_x),
            remote(grads.at[g, pl.ds(2, 2), core, :, wide(1 - yb)], in_1b.at[g], 5 * g + 2, across_y),
        ]

    def second_copies(g):
        return [
            remote(grads.at[g, pl.ds(0, 2), core, :, narrow(xb, 1 - yb)], in_2a.at[g], 5 * g + 3, across_y),
            remote(grads.at[g, pl.ds(2, 2), core, :, narrow(yb, 1 - xb)], in_2b.at[g], 5 * g + 4, across_x),
        ]

    def add(view, value):
        view[...] = (view[...].astype(F32) + value.astype(F32)).astype(BF)

    def core_step(g):
        core_copy(g).wait_recv()
        rows = per // 2

        def one(i, carry):
            z = lax.div(i, 2)
            at = pl.ds(pl.multiple_of(lax.rem(i, 2) * rows, rows), rows)
            add(grads.at[g, z, core, at, :], core_in[g, z, at, :])
            return carry

        lax.fori_loop(0, 8, one, 0)
        for copy in first_copies(g):
            copy.start()

    def first_step(g):
        for copy in first_copies(g):
            copy.wait_recv()

        def one(z, carry):
            add(grads.at[g, z, core, :, wide(xb)], in_1a[g, z])
            add(grads.at[g, 2 + z, core, :, wide(yb)], in_1b[g, z])
            return carry

        lax.fori_loop(0, 2, one, 0)
        for copy in second_copies(g):
            copy.start()

    def owned(g, z):
        at = 2 * xb + yb + lax.div(z, 2) * (yb - xb)
        return grads.at[g, z, core, :, pl.ds(pl.multiple_of(at * width, width), width)]

    def place_copies(g):
        return [
            remote(owned(g, flipped(place, k)), in_z.at[g, k - 1], 10 + 3 * g + k - 1, places[k - 1]) for k in (3, 2, 1)
        ]

    def place_step(g):
        for copy in place_copies(g):
            copy.wait_recv()
        total = owned(g, place)[...].astype(F32)
        for k in range(3):
            total = total + in_z[g, k].astype(F32)
        kept[pl.ds(g * per, per), :] = total.astype(BF)

    def second_step(g):
        for copy in second_copies(g):
            copy.wait_recv()
        for z in range(2):
            add(grads.at[g, z, core, :, narrow(xb, yb)], in_2a[g, z])
            add(grads.at[g, 2 + z, core, :, narrow(yb, xb)], in_2b[g, z])
        for copy in place_copies(g):
            copy.start()

    corner = 256

    def turn():
        def one(i, carry):
            at = pl.ds(pl.multiple_of(i * corner, corner), corner)
            for j in range(width // corner):
                there = pl.ds(j * corner, corner)
                turned[there, at] = lhs[at, there].T
            return carry

        lax.fori_loop(0, tokens // corner, one, 0)

    second_copy.wait()
    turn()
    hidden_copy.start()
    share = block // 2
    for n in range(blocks):
        stage_copy(n).wait()
        for c in range(2):
            out = dot_nn(turned[...], stage[n % 2, :, c * share : (c + 1) * share]).astype(BF)
            for j in range(8):
                grads[0, n, c, :, j * share : (j + 1) * share] = out[j * per : (j + 1) * per]
        stage_copy(n + 2).start()
        if n == 0:
            for copy in loads[:5]:
                copy.start()
            probs_copy(0).start()
    core_copy(0).start()
    hidden_copy.wait()
    turn()
    for n in range(blocks, 2 * blocks):
        stage_copy(n).wait()
        for c in range(2):
            out = dot_nn(turned[...], stage[n % 2, :, c * share : (c + 1) * share]).astype(BF)
            at = (n - blocks) * block + c * share
            for j in range(8):
                grads[1, j // 2, j % 2, :, at : at + share] = out[j * per : (j + 1) * per]
        if n + 2 < 2 * blocks:
            stage_copy(n + 2).start()
        if n == blocks:
            for copy in loads[5:]:
                copy.start()
    core_copy(1).start()
    core_step(0)

    for copy in loads:
        copy.wait()
    sums[...] = jnp.zeros_like(sums)
    low[...] = first[...].astype(BF)
    first_copy = pltpu.make_async_copy(low, first_out, out_sem.at[4])
    first_copy.start()
    tile = 256

    def open_(n, carry):
        at = pl.ds(pl.multiple_of(n * tile, tile), tile)
        grad_mixed[:, at] = dot_nt(low[...], weights[3, at, :]).astype(BF)
        return carry

    lax.fori_loop(0, width // tile, open_, 0)

    def pair(n, carry):
        @pl.when(n + 1 < seqs * (HEADS // 2))
        def _():
            probs_copy(n + 1).start()

        probs_copy(n).wait()
        slot = lax.rem(n, 2)
        rows = pl.ds(pl.multiple_of(lax.div(n, HEADS // 2) * size, size), size)
        at = pl.ds(pl.multiple_of(lax.rem(n, HEADS // 2) * 2 * HEAD, 2 * HEAD), 2 * HEAD)
        q2, k2, v2, grad = q[rows, at], k[rows, at], v[rows, at], grad_mixed[rows, at]
        across = k2.T
        lane = lax.broadcasted_iota(jnp.int32, k2.shape, 1)
        parts = []
        grad_k = jnp.zeros(k2.shape, F32)
        grad_v = jnp.zeros(k2.shape, F32)
        for side in range(2):
            mine = (lane >= HEAD) if side else (lane < HEAD)
            none = jnp.zeros_like(k2)
            chances = probs[slot, side]
            grad_probs = dot_nt(jnp.where(mine, v2, none), grad)
            grad_v = grad_v + dot_nn(chances, jnp.where(mine, grad, none))
            full = chances.astype(F32)
            both = full * grad_probs
            scores = (both - full * jnp.sum(both, 0, keepdims=True)).astype(BF)
            grad_k = grad_k + dot_nn(scores, jnp.where(mine, q2, none))
            parts.append(dot_nn(across[side * HEAD : (side + 1) * HEAD], scores))
        grad_q = jnp.concatenate(parts, 0).T * HEAD**-0.5
        dq[rows, at] = grad_q.astype(BF)
        dk[rows, at] = grad_k.astype(BF)
        dv[rows, at] = grad_v.astype(BF)
        sums[0:1, at] += column_sum(grad_q)
        sums[1:2, at] += column_sum(grad_v)
        return carry

    lax.fori_loop(0, 2, pair, 0)
    core_step(1)
    lax.fori_loop(2, 5, pair, 0)
    first_step(0)
    lax.fori_loop(5, 8, pair, 0)
    second_step(0)
    first_step(1)
    lax.fori_loop(8, 11, pair, 0)
    second_step(1)
    lax.fori_loop(11, 12, pair, 0)
    out_copies = [
        pltpu.make_async_copy(source, target, out_sem.at[5 + i])
        for i, (source, target) in enumerate(((dq, dq_out), (dk, dk_out), (dv, dv_out)))
    ]
    for copy in out_copies:
        copy.start()

    def close(n, carry):
        at = pl.ds(pl.multiple_of(n * tile, tile), tile)
        first[:, at] = (
            first[:, at]
            + dot_nt(dq[...], weights[0, at, :])
            + dot_nt(dk[...], weights[1, at, :])
            + dot_nt(dv[...], weights[2, at, :])
        )
        return carry

    lax.fori_loop(0, width // tile, close, 0)
    few = 128
    lane = lax.broadcasted_iota(jnp.int32, (few, 128), 1)

    def back(at):
        unit, inverse = stats(table[at, :])
        grad = first[at, :]
        grad_emb = norm_back(grad, emb_gain[...], unit, inverse)
        sums[2:3, :] += column_sum(grad * unit)
        sums[3:4, :] += column_sum(grad)
        kind = kinds[at, :]
        for t in range(2):
            sums[4 + t : 5 + t, :] += column_sum(jnp.where(kind == t, grad_emb, 0.0))
        return grad_emb

    def last(n, carry):
        at = pl.ds(pl.multiple_of(n * few, few), few)
        left = back(at)
        right = back(pl.ds(pl.multiple_of(size + n * few, few), few))
        pos[at, :] = (left + right).astype(BF)
        for t in range(width // 128):
            one, two = left[:, t * 128 : (t + 1) * 128], right[:, t * 128 : (t + 1) * 128]
            q = 2 * (t % 2)
            raw[t // 2, q, at, :] = jnp.where(lane < 64, one, pltpu.roll(two, 64, 1)).astype(BF)
            raw[t // 2, q + 1, at, :] = jnp.where(lane < 64, pltpu.roll(one, 64, 1), two).astype(BF)
        return carry

    lax.fori_loop(0, size // few, last, 0)
    raw_copy = pltpu.make_async_copy(raw, raw_out, out_sem.at[0])
    raw_copy.start()
    pos_copy = pltpu.make_async_copy(pos, pos_out, out_sem.at[1])
    pos_copy.start()
    for g in range(2):
        place_step(g)
    feed_copy = pltpu.make_async_copy(kept, feed_out, out_sem.at[2])
    feed_copy.start()
    for copy in [first_copy, raw_copy, pos_copy, feed_copy] + out_copies:
        copy.wait()
    for g in range(2):
        for copy in [core_copy(g)] + first_copies(g) + second_copies(g) + place_copies(g):
            copy.wait_send()


def mid(
    active, upper_low, second_low, hidden_low, grad_first, embedded, q, k, v, probs, wq, wk, wv, wo, kinds, emb_gain
):
    tokens, width = grad_first.shape
    seqs, heads, size, _ = probs.shape
    units = active.shape[1]
    per = width // 8
    wide = 4 * width
    vmem = pl.BlockSpec(memory_space=pltpu.VMEM)
    hbm = pl.BlockSpec(memory_space=pl.ANY)
    low = jax.ShapeDtypeStruct((tokens, width), BF)
    small = pltpu.VMEM((tokens, width), BF)
    large = pltpu.VMEM((tokens, width), F32)
    return pl.pallas_call(
        mid_kernel,
        out_shape=[low] * 4
        + [
            jax.ShapeDtypeStruct((3, 4, size, 128), BF),
            jax.ShapeDtypeStruct((size, width), BF),
            jax.ShapeDtypeStruct((2 * per, width), BF),
            jax.ShapeDtypeStruct((8, width), F32),
        ],
        in_specs=[hbm] * 14 + [vmem] * 2,
        out_specs=[hbm] * 7 + [vmem],
        scratch_shapes=[
            pltpu.VMEM((2, tokens, 768), BF),
            small,
            pltpu.VMEM((width, tokens), BF),
            pltpu.VMEM((2, 4, 2, per, wide), BF),
            pltpu.VMEM((2, 4, per, wide), BF),
            pltpu.VMEM((2, 2, per, wide // 2), BF),
            pltpu.VMEM((2, 2, per, wide // 2), BF),
            pltpu.VMEM((2, 2, per, width), BF),
            pltpu.VMEM((2, 2, per, width), BF),
            pltpu.VMEM((2, 3, per, width), BF),
            pltpu.VMEM((2 * per, width), BF),
            large,
            small,
            small,
            small,
            small,
            small,
            small,
            small,
            small,
            pltpu.VMEM((4, width, width), BF),
            large,
            pltpu.VMEM((3, 4, size, 128), BF),
            pltpu.VMEM((size, width), BF),
            pltpu.VMEM((2, 2, size, size), BF),
            pltpu.SemaphoreType.DMA((11,)),
            pltpu.SemaphoreType.DMA((2,)),
            pltpu.SemaphoreType.DMA((2,)),
            pltpu.SemaphoreType.DMA((9,)),
            pltpu.SemaphoreType.DMA((16,)),
            pltpu.SemaphoreType.DMA((16,)),
        ],
        compiler_params=pltpu.CompilerParams(
            collective_id=2, has_side_effects=True, vmem_limit_bytes=62 * MIB
        ),
        name="mid",
    )(
        active, upper_low, second_low, hidden_low, grad_first, embedded, q, k, v, probs, wq, wk, wv, wo,
        kinds.reshape(tokens, 1), row(emb_gain),
    )


def flipped(index, bits):
    out = 0
    for place in range(3):
        bit = lax.rem(lax.div(index, 1 << place), 2)
        out = out + (1 << place) * (1 - bit if (bits >> place) & 1 else bit)
    return out


ORDER = (6, 7, 4, 5, 2, 3, 1)


def tail_kernel(
    slots, asked, asked_columns, pos, small, raw, normed, mixed, gfirst, dq, dk, dv, feed_own,
    word, packed, feed_out, small_out,
    tok, hot, og, inc, rhs, kinds, places, total, dense, ops, turned, wbuf, wcore, w1a, w1b, w2a, w2b, wz, wown, small_by, small_in, small_dp,
    load_sem, t_send, t_recv, z_send, z_recv, d_send, d_recv, w_send, w_recv, s_send, s_recv, own_sem,
):
    chunks, owners, sources, pairs, lanes = og.shape
    half, width = pos.shape
    tokens = 2 * half
    cap = 2 * pairs
    tall = dense.shape[1]
    me = lax.axis_index("vocab")
    spot = lax.axis_index("dp")
    core, place = lax.rem(me, 2), lax.div(me, 2)
    xb, yb = lax.rem(spot, 2), lax.div(spot, 2)
    across_x = {"dp": spot + 1 - 2 * xb}
    across_y = {"dp": spot + 2 - 4 * yb}

    barrier = pltpu.get_barrier_semaphore()
    for k in ORDER:
        pl.semaphore_signal(barrier, inc=1, device_id={"vocab": flipped(me, k)}, device_id_type=MESH)
    for k in (1, 2, 3):
        pl.semaphore_signal(barrier, inc=1, device_id={"dp": flipped(spot, k)}, device_id_type=MESH)
    loads = [
        pltpu.make_async_copy(ref, ops.at[i], load_sem.at[i])
        for i, ref in enumerate((normed, dq, dk, dv, mixed, gfirst))
    ]
    for load in loads:
        load.start()
    for v in range(owners):
        per = width // owners
        small_by[v] = jnp.pad(small[:, v * per : (v + 1) * per], ((0, 0), (0, 128 - per)))
    pl.semaphore_wait(barrier, len(ORDER) + 3)

    def remote(src, dst, send, recv, peer):
        return pltpu.make_async_remote_copy(
            src_ref=src, dst_ref=dst, send_sem=send, recv_sem=recv, device_id=peer, device_id_type=MESH
        )

    def start(copies):
        for copy in copies:
            copy.start()

    def arrived(copies):
        for copy in copies:
            copy.wait_recv()

    def gone(copies):
        for copy in copies:
            copy.wait_send()

    def token_copy(c, k):
        peer = flipped(spot, k)
        return remote(raw.at[c, peer], tok.at[c, spot], t_send.at[c, k], t_recv.at[c, k], {"dp": peer})

    def token_copies(c):
        return [token_copy(c, k) for k in (1, 2, 3)]

    def token_own(c):
        return pltpu.make_async_copy(raw.at[c, spot], tok.at[c, spot], own_sem.at[c])

    for c in range(chunks):
        start(token_copies(c))
        token_own(c).start()

    def row_copies(c, j):
        source = flipped(spot, j)
        copies = []
        for k in ORDER:
            peer = flipped(me, k)
            copies.append(
                remote(
                    og.at[c, peer, source],
                    inc.at[c, me, source],
                    z_send.at[c, j, k],
                    z_recv.at[c, j, k],
                    {"vocab": peer},
                )
            )
        return copies

    def make_hot(d):
        def one(v, carry):
            wanted = lax.broadcasted_iota(jnp.int32, (cap, half), 0) + v * cap
            for s in range(2):
                hit = wanted == slots[d, :, s * half : (s + 1) * half]
                hot[d, s, v] = jnp.where(hit, 1.0, 0.0).astype(BF)
            return carry

        lax.fori_loop(0, owners, one, 0)

    group = 2

    def fill(d, first, count):
        def one(n, carry):
            lane = lax.broadcasted_iota(jnp.int32, (pairs, lanes), 1)
            at = pl.ds(n * group, group)
            values = jnp.concatenate([tok[first + i, d] for i in range(count)], 1)
            early = dot_nn(hot[d, 0, at].reshape(group * cap, half), values)
            late = dot_nn(hot[d, 1, at].reshape(group * cap, half), values)
            for g in range(group):
                low, high = slice(g * cap, g * cap + pairs), slice(g * cap + pairs, (g + 1) * cap)
                for i in range(count):
                    there = slice(i * lanes, (i + 1) * lanes)
                    straight = jnp.where(lane < 64, early[low, there], late[high, there])
                    crossed = jnp.where(lane < 64, early[high, there], late[low, there])
                    og[first + i, n * group + g, d] = (straight + pltpu.roll(crossed, 64, 1)).astype(BF)
            return carry

        lax.fori_loop(0, owners // group, one, 0)

    def own_copy(c):
        return pltpu.make_async_copy(og.at[c, me], inc.at[c, me], own_sem.at[11 + c])

    def fill_first(j):
        d = flipped(spot, j)
        make_hot(d)
        if j == 0:
            token_own(0).wait()
        else:
            token_copy(0, j).wait_recv()
        fill(d, 0, 1)
        start(row_copies(0, j))

    depth = 1024

    def sort_rows():
        for v in range(owners):
            ids = asked_columns[v]
            kinds[v] = sum(jnp.where(ids >= n * tall, 1, 0) for n in (1, 2, 3))
        for h in range(2):
            ids = asked[h]
            places[h] = ids - tall * sum(jnp.where(ids >= n * tall, 1, 0) for n in (1, 2, 3))

    def prepare(c):
        def one(v, carry):
            lane = lax.broadcasted_iota(jnp.int32, (pairs, lanes), 1)
            side = jnp.where(lane < 64, 0, 1)
            for d in range(sources):
                at = pl.ds(pl.multiple_of((v * sources + d) * pairs, pairs), pairs)
                straight = inc[c, v, d].astype(F32)
                crossed = pltpu.roll(straight, 64, 1)
                for h in range(2):
                    kind = kinds[v, :, 2 * d + h : 2 * d + h + 1] - side
                    twice = jnp.where(lane < 64, crossed if h else straight, straight if h else crossed)
                    rhs[h, at, :lanes] = jnp.where(kind == 0, twice, 0.0).astype(BF)
                    rhs[h, at, lanes:] = jnp.where(kind == 2, twice, 0.0).astype(BF)
            return carry

        lax.fori_loop(0, owners, one, 0)

    def gather_rows(c, p):
        tile = tall // 2
        blocks = owners * sources * pairs // depth
        total[...] = jnp.zeros_like(total)

        def one(n, carry):
            h, b = lax.div(n, blocks), lax.rem(n, blocks)
            at = pl.ds(pl.multiple_of(b * depth, depth), depth)
            ids = places[h, :, at] - p * tile
            hit = lax.broadcasted_iota(jnp.int32, (tile, depth), 0) == ids
            total[...] += dot_nn(jnp.where(hit, 1.0, 0.0).astype(BF), rhs[h, at, :])
            return carry

        lax.fori_loop(0, 2 * blocks, one, 0)
        dense[c, pl.ds(p * tile, tile), :] = total[...].astype(BF)

    part = tall // 2

    def lines_of(p):
        return pl.ds(p * part, part)

    def keep_copy(c, p):
        return pltpu.make_async_copy(
            dense.at[c, lines_of(p)], word.at[c, spot, lines_of(p)], own_sem.at[3 + 2 * c + p]
        )

    def near_copies(c, p):
        return [
            remote(
                dense.at[c, lines_of(p)], word.at[c, spot, lines_of(p)], d_send.at[c, 2 * p], d_recv.at[c, 2 * p], across_x
            ),
            remote(
                dense.at[c, lines_of(p)],
                word.at[c, spot, lines_of(p)],
                d_send.at[c, 2 * p + 1],
                d_recv.at[c, 2 * p + 1],
                across_y,
            ),
        ]

    def far_copy(c, p):
        source = flipped(spot, 1) if p == 0 else flipped(spot, 2)
        view = word.at[c, source, lines_of(p)]
        return remote(view, view, d_send.at[c, 4 + p], d_recv.at[c, 4 + p], across_y if p == 0 else across_x)

    per = width // owners
    block = 256
    quarter = wown.shape[0]

    def turn(which):
        def one(i, carry):
            at = pl.ds(pl.multiple_of(i * block, block), block)
            for j in range(width // block):
                there = pl.ds(j * block, block)
                turned[there, at] = ops[which, at, there].T
            return carry

        lax.fori_loop(0, tokens // block, one, 0)

    def weight(which, at):
        def one(n, carry):
            there = pl.ds(pl.multiple_of(n * block, block), block)
            out = dot_nn(turned[...], ops[which, :, there]).astype(BF)
            for v in range(owners):
                wbuf[v // 2, v % 2, pl.ds(at * per, per), there] = out[v * per : (v + 1) * per]
            return carry

        lax.fori_loop(0, width // block, one, 0)

    core_copy = remote(wbuf.at[:, 1 - core], wcore, w_send.at[0], w_recv.at[0], {"vocab": flipped(me, 1)})

    def wide(b):
        return pl.ds(pl.multiple_of(b * 2 * quarter, quarter), 2 * quarter)

    def narrow(b, c):
        return pl.ds(pl.multiple_of((2 * b + c) * quarter, quarter), quarter)

    def add(view, value):
        view[...] = (view[...].astype(F32) + value.astype(F32)).astype(BF)

    def core_step():
        core_copy.wait_recv()

        def one(i, carry):
            z = lax.div(i, 4)
            at = pl.ds(pl.multiple_of(lax.rem(i, 4) * quarter, quarter), quarter)
            add(wbuf.at[z, core, at, :], wcore[z, at, :])
            return carry

        lax.fori_loop(0, 16, one, 0)

    def first_weights():
        return [
            remote(wbuf.at[pl.ds(0, 2), core, wide(1 - xb), :], w1a, w_send.at[1], w_recv.at[1], across_x),
            remote(wbuf.at[pl.ds(2, 2), core, wide(1 - yb), :], w1b, w_send.at[2], w_recv.at[2], across_y),
        ]

    def second_weights():
        return [
            remote(wbuf.at[pl.ds(0, 2), core, narrow(xb, 1 - yb), :], w2a, w_send.at[3], w_recv.at[3], across_y),
            remote(wbuf.at[pl.ds(2, 2), core, narrow(yb, 1 - xb), :], w2b, w_send.at[4], w_recv.at[4], across_x),
        ]

    def first_step():
        arrived(first_weights())
        for z in range(2):
            add(wbuf.at[z, core, wide(xb), :], w1a[z])
            add(wbuf.at[2 + z, core, wide(yb), :], w1b[z])

    def second_step():
        arrived(second_weights())
        for z in range(2):
            add(wbuf.at[z, core, narrow(xb, yb), :], w2a[z])
            add(wbuf.at[2 + z, core, narrow(yb, xb), :], w2b[z])

    def owned(z):
        at = 2 * xb + yb + lax.div(z, 2) * (yb - xb)
        return wbuf.at[z, core, pl.ds(pl.multiple_of(at * quarter, quarter), quarter), :]

    def third_weights():
        copies = []
        for k in (3, 2, 1):
            to = flipped(place, k)
            copies.append(
                remote(owned(to), wz.at[k - 1], w_send.at[4 + k], w_recv.at[4 + k], {"vocab": 2 * to + core})
            )
        return copies

    def third_step():
        arrived(third_weights())
        total = owned(place)[...].astype(F32)
        for k in range(3):
            total = total + wz[k].astype(F32)
        wown[...] = total.astype(BF)

    def spread(own, target, at):
        wide_half = width // 2
        left, right = pl.ds(0, wide_half), pl.ds(wide_half, wide_half)
        kept = pltpu.make_async_copy(own, target.at[xb, yb], own_sem.at[9 + at])
        sems = [(w_send.at[8 + 4 * at + i], w_recv.at[8 + 4 * at + i]) for i in range(4)]
        near = [
            remote(own, target.at[xb, yb], *sems[0], across_x),
            remote(own, target.at[xb, yb], *sems[1], across_y),
        ]
        from_x, from_y = target.at[1 - xb, yb, :, left], target.at[xb, 1 - yb, :, right]
        far = [remote(from_x, from_x, *sems[2], across_y), remote(from_y, from_y, *sems[3], across_x)]
        return kept, near, far

    feed_kept, feed_near, feed_far = spread(feed_own, feed_out, 0)
    kept, fourth_weights, fifth_weights = spread(wown, packed, 1)

    def small_copies():
        copies = []
        for k in ORDER:
            peer = flipped(me, k)
            copies.append(remote(small_by.at[peer], small_in.at[k], s_send.at[k], s_recv.at[k], {"vocab": peer}))
        return copies

    def small_last():
        return [
            remote(small_in.at[0], small_dp.at[k - 1], s_send.at[7 + k], s_recv.at[7 + k], {"dp": flipped(spot, k)})
            for k in (1, 2, 3)
        ]

    start(small_copies())
    fill_first(0)
    loads[0].wait()
    turn(0)
    loads[1].wait()
    weight(1, 0)
    fill_first(1)
    start(feed_near)
    feed_kept.start()
    loads[2].wait()
    weight(2, 1)
    fill_first(2)
    loads[3].wait()
    weight(3, 2)
    fill_first(3)
    own_copy(0).start()
    loads[4].wait()
    turn(4)
    loads[5].wait()
    weight(5, 3)
    share = half // owners
    for v in range(owners):
        wbuf[v // 2, v % 2, pl.ds(4 * per, share), :] = pos[pl.ds(v * share, share), :]
    core_copy.start()
    for c in (1, 2):
        token_own(c).wait()
        arrived(token_copies(c))

    def rest(d, carry):
        fill(d, 1, 2)
        return carry

    lax.fori_loop(0, 2, rest, 0)
    core_step()
    start(first_weights())
    lax.fori_loop(2, sources, rest, 0)
    for c in (1, 2):
        own_copy(c).start()
    sort_rows()
    feed_kept.wait()
    arrived(feed_near)
    start(feed_far)
    arrived(small_copies())
    short = small_by[me]
    for k in ORDER:
        short = short + small_in[k]
    small_in[0] = short
    start(small_last())

    def close_chunk(c):
        for j in range(sources):
            arrived(row_copies(c, j))
        own_copy(c).wait()
        if c + 1 < chunks:
            for j in range(sources):
                start(row_copies(c + 1, j))
        else:
            start(third_weights())
        prepare(c)
        for p in range(2):
            gather_rows(c, p)
            start(near_copies(c, p))
            keep_copy(c, p).start()

    def pass_on(c):
        arrived(near_copies(c, 0))
        far_copy(c, 0).start()
        arrived(near_copies(c, 1))
        far_copy(c, 1).start()

    close_chunk(0)
    first_step()
    start(second_weights())
    pass_on(0)
    close_chunk(1)
    second_step()
    arrived(small_last())
    short = small_in[0]
    for k in range(3):
        short = short + small_dp[k]
    small_out[...] = short
    pass_on(1)
    close_chunk(2)
    third_step()
    start(fourth_weights)
    kept.start()
    pass_on(2)
    kept.wait()
    arrived(fourth_weights)
    start(fifth_weights)

    for c in range(chunks):
        for p in range(2):
            keep_copy(c, p).wait()
            far_copy(c, p).wait_recv()
    arrived(feed_far)
    arrived(fifth_weights)
    core_copy.wait_send()
    gone(small_copies())
    gone(small_last())
    for c in range(chunks):
        gone(token_copies(c))
        for j in range(sources):
            gone(row_copies(c, j))
        for p in range(2):
            gone(near_copies(c, p))
            far_copy(c, p).wait_send()
    for copies in (first_weights(), second_weights(), third_weights(), fourth_weights, fifth_weights, feed_near, feed_far):
        gone(copies)


def tail(slots, asked, pos, small, raw, normed, mixed, gfirst, dq, dk, dv, feed_own, rows_local):
    half, width = pos.shape
    sources, owners, cap = asked.shape
    chunks = raw.shape[0]
    pairs = cap // 2
    tall = rows_local // 4
    lines = 4 * (width // owners) + half // owners
    vmem = pl.BlockSpec(memory_space=pltpu.VMEM)
    hbm = pl.BlockSpec(memory_space=pl.ANY)
    by_half = asked.reshape(sources, owners, 2, pairs).transpose(2, 1, 0, 3)
    columns = asked.reshape(sources, owners, 2, pairs).transpose(1, 3, 0, 2).reshape(owners, pairs, 2 * sources)
    return pl.pallas_call(
        tail_kernel,
        out_shape=(
            jax.ShapeDtypeStruct((chunks, sources, tall, 256), BF),
            jax.ShapeDtypeStruct((2, 2, lines // 4, width), BF),
            jax.ShapeDtypeStruct((2, 2) + feed_own.shape, BF),
            jax.ShapeDtypeStruct((16, 128), F32),
        ),
        in_specs=[vmem] * 5 + [hbm] * 8,
        out_specs=(hbm, hbm, hbm, vmem),
        scratch_shapes=[
            pltpu.VMEM((chunks, sources, half, 128), BF),
            pltpu.VMEM((sources, 2, owners, cap, half), BF),
            pltpu.VMEM((chunks, owners, sources, pairs, 128), BF),
            pltpu.VMEM((chunks, owners, sources, pairs, 128), BF),
            pltpu.VMEM((2, owners * sources * pairs, 256), BF),
            pltpu.VMEM((owners, pairs, 2 * sources), jnp.int32),
            pltpu.VMEM((2, 1, owners * sources * pairs), jnp.int32),
            pltpu.VMEM((tall // 2, 256), F32),
            pltpu.VMEM((chunks, tall, 256), BF),
            pltpu.VMEM((6, 2 * half, width), BF),
            pltpu.VMEM((width, 2 * half), BF),
            pltpu.VMEM((4, 2, lines, width), BF),
            pltpu.VMEM((4, lines, width), BF),
            pltpu.VMEM((2, lines // 2, width), BF),
            pltpu.VMEM((2, lines // 2, width), BF),
            pltpu.VMEM((2, lines // 4, width), BF),
            pltpu.VMEM((2, lines // 4, width), BF),
            pltpu.VMEM((3, lines // 4, width), BF),
            pltpu.VMEM((lines // 4, width), BF),
            pltpu.VMEM((owners, 16, 128), F32),
            pltpu.VMEM((owners, 16, 128), F32),
            pltpu.VMEM((3, 16, 128), F32),
            pltpu.SemaphoreType.DMA((6,)),
            pltpu.SemaphoreType.DMA((chunks, 4)),
            pltpu.SemaphoreType.DMA((chunks, 4)),
            pltpu.SemaphoreType.DMA((chunks, sources, owners)),
            pltpu.SemaphoreType.DMA((chunks, sources, owners)),
            pltpu.SemaphoreType.DMA((chunks, 6)),
            pltpu.SemaphoreType.DMA((chunks, 6)),
            pltpu.SemaphoreType.DMA((16,)),
            pltpu.SemaphoreType.DMA((16,)),
            pltpu.SemaphoreType.DMA((11,)),
            pltpu.SemaphoreType.DMA((11,)),
            pltpu.SemaphoreType.DMA((14,)),
        ],
        compiler_params=pltpu.CompilerParams(collective_id=1, has_side_effects=True, vmem_limit_bytes=60 * MIB),
        name="tail",
    )(
        slots.reshape(sources, 1, 2 * half), by_half.reshape(2, 1, -1), columns, pos, small,
        raw, normed, mixed, gfirst, dq, dk, dv, feed_own,
    )


def fetch_kernel(
    ids, kinds, pos, types, gain, bias, table_in,
    embedded_out, normed_out, slots_out, asked_out,
    table, request, asked_in, rows_out, rows_in, embedded, normed, column,
    load_sem, q_send, q_recv, s_send, s_recv, a_send, a_recv, z_send, z_recv, out_sem,
):
    owners, cap, width = rows_out.shape
    tokens = ids.shape[1]
    rows_local = table.shape[0]
    me = lax.axis_index("vocab")
    spot = lax.axis_index("dp")
    table_copy = pltpu.make_async_copy(table_in, table, load_sem.at[0])
    table_copy.start()
    barrier = pltpu.get_barrier_semaphore()
    for k in ORDER:
        pl.semaphore_signal(barrier, inc=1, device_id={"vocab": flipped(me, k)}, device_id_type=MESH)
    for k in (1, 2, 3):
        pl.semaphore_signal(barrier, inc=1, device_id={"dp": flipped(spot, k)}, device_id_type=MESH)

    def remote(src, dst, send, recv, peer):
        return pltpu.make_async_remote_copy(
            src_ref=src, dst_ref=dst, send_sem=send, recv_sem=recv, device_id=peer, device_id_type=MESH
        )

    owner = jnp.zeros(ids.shape, jnp.int32)
    for v in range(1, owners):
        owner = owner + jnp.where(ids[...] >= v * rows_local, 1, 0)
    member = jnp.where(lax.broadcasted_iota(jnp.int32, (owners, tokens), 0) == owner, 1.0, 0.0)
    block = 256
    rank = []
    for n in range(tokens // block):
        before = lax.broadcasted_iota(jnp.int32, (tokens, block), 0) < (
            lax.broadcasted_iota(jnp.int32, (tokens, block), 1) + n * block
        )
        earlier = dot_nn(member.astype(BF), jnp.where(before, 1.0, 0.0).astype(BF))
        rank.append(jnp.sum(earlier * member[:, n * block : (n + 1) * block], 0, keepdims=True))
    slot = owner * cap + jnp.concatenate(rank, 1).astype(jnp.int32)
    local = ids[...] - owner * rows_local
    line = lax.broadcasted_iota(jnp.int32, (8, tokens), 0)
    high = lax.shift_right_logical(local, 6)
    values = jnp.where(line == 0, high, jnp.where(line == 1, local - high * 64, jnp.where(line == 2, 1, 0)))
    values = values.astype(F32).astype(BF)
    for v in range(owners):
        wanted = lax.broadcasted_iota(jnp.int32, (cap, tokens), 0) + v * cap
        found = dot_nt(values, jnp.where(wanted == slot, 1.0, 0.0).astype(BF))
        number = found[0:1] * 64.0 + found[1:2]
        request[v] = jnp.where(found[2:3] > 0.5, number, -1.0).astype(jnp.int32)
    slots_out[spot] = slot
    pl.semaphore_wait(barrier, len(ORDER) + 3)
    asks = []
    for k in ORDER:
        peer = flipped(me, k)
        asks.append(remote(request.at[peer], asked_in.at[me], q_send.at[k], q_recv.at[k], {"vocab": peer}))
    for copy in asks:
        copy.start()
    asked_in[me] = request[me]
    lists = []
    for k in (1, 2, 3):
        peer = {"dp": flipped(spot, k)}
        lists.append(remote(slots_out.at[spot], slots_out.at[spot], s_send.at[k], s_recv.at[k], peer))
    for copy in lists:
        copy.start()
    column[...] = jnp.broadcast_to(slot.astype(F32), (8, tokens)).T[:, 0:1].astype(jnp.int32)
    half = tokens // 2
    for s in range(2):
        at = pl.ds(s * half, half)
        kind = jnp.where(kinds[at, :] == 0, types[0:1, :].astype(F32), types[1:2, :].astype(F32))
        embedded[at, :] = pos[...].astype(F32) + kind
    for copy in asks:
        copy.wait_recv()
    asked_out[spot] = asked_in[...]
    for k in (1, 2, 3):
        peer = {"dp": flipped(spot, k)}
        copy = remote(asked_in, asked_out.at[spot], a_send.at[k], a_recv.at[k], peer)
        lists.append(copy)
        copy.start()
    table_copy.wait()

    def find(source):
        asked = jnp.broadcast_to(asked_in[source].astype(F32), (8, cap)).T[:, 0:1]
        depth = rows_local // 3
        total = jnp.zeros((cap, width), F32)
        for n in range(3):
            at = lax.broadcasted_iota(jnp.int32, (cap, depth), 1) + n * depth
            hit = jnp.where(at == asked.astype(jnp.int32), 1.0, 0.0).astype(BF)
            total = total + dot_nn(hit, table[pl.ds(n * depth, depth), :])
        return total.astype(BF)

    def row_copy(k):
        peer = flipped(me, k)
        return remote(rows_out.at[peer], rows_in.at[me], z_send.at[k], z_recv.at[k], {"vocab": peer})

    for k in ORDER:
        peer = flipped(me, k)
        rows_out[peer] = find(peer)
        row_copy(k).start()
    rows_in[me] = find(me)

    def place(source):
        part = 256

        def one(n, carry):
            at = pl.ds(pl.multiple_of(n * part, part), part)
            hit = lax.broadcasted_iota(jnp.int32, (part, cap), 1) + source * cap
            hit = jnp.where(hit == column[at, :], 1.0, 0.0).astype(BF)
            embedded[at, :] += dot_nn(hit, rows_in[source])
            return carry

        lax.fori_loop(0, tokens // part, one, 0)

    place(me)
    for k in (1, 2, 3, 4, 5, 6, 7):
        row_copy(k).wait_recv()
        place(flipped(me, k))
    part = 128

    def out_copies(n):
        at = pl.ds(n * part, part)
        return [
            pltpu.make_async_copy(embedded.at[at, :], embedded_out.at[at, :], out_sem.at[n, 0]),
            pltpu.make_async_copy(normed.at[at, :], normed_out.at[at, :], out_sem.at[n, 1]),
        ]

    for n in range(tokens // part):
        at = pl.ds(n * part, part)
        unit, _ = stats(embedded[at, :])
        normed[at, :] = unit * gain[...] + bias[...]
        for copy in out_copies(n):
            copy.start()
    for n in range(tokens // part):
        for copy in out_copies(n):
            copy.wait()
    for copy in lists:
        copy.wait_recv()
        copy.wait_send()
    for copy in asks:
        copy.wait_send()
    for k in ORDER:
        row_copy(k).wait_send()


def fetch(ids, kinds, table, pos, types, gain, bias, owners):
    tokens = ids.size
    rows_local, width = table.shape
    cap = 2 * tokens // owners
    vmem = pl.BlockSpec(memory_space=pltpu.VMEM)
    hbm = pl.BlockSpec(memory_space=pl.ANY)
    full = jax.ShapeDtypeStruct((tokens, width), F32)
    dma = pltpu.SemaphoreType.DMA
    return pl.pallas_call(
        fetch_kernel,
        out_shape=(
            full,
            full,
            jax.ShapeDtypeStruct((4, 1, tokens), jnp.int32),
            jax.ShapeDtypeStruct((4, owners, 1, cap), jnp.int32),
        ),
        in_specs=[vmem] * 6 + [hbm],
        out_specs=(hbm, hbm, vmem, vmem),
        scratch_shapes=[
            pltpu.VMEM((rows_local, width), BF),
            pltpu.VMEM((owners, 1, cap), jnp.int32),
            pltpu.VMEM((owners, 1, cap), jnp.int32),
            pltpu.VMEM((owners, cap, width), BF),
            pltpu.VMEM((owners, cap, width), BF),
            pltpu.VMEM((tokens, width), F32),
            pltpu.VMEM((tokens, width), F32),
            pltpu.VMEM((tokens, 1), jnp.int32),
            dma((1,)),
            dma((owners,)),
            dma((owners,)),
            dma((4,)),
            dma((4,)),
            dma((4,)),
            dma((4,)),
            dma((owners,)),
            dma((owners,)),
            dma((tokens // 128, 2)),
        ],
        compiler_params=pltpu.CompilerParams(collective_id=3, has_side_effects=True, vmem_limit_bytes=48 * MIB),
        name="fetch",
    )(ids.reshape(1, tokens), kinds.reshape(tokens, 1), pos, types, row(gain), row(bias), table)


def finish_kernel(near, word_in, packed, feeds, word, query, keys, values, out, pos, up, down):
    chunks, sources, part, _ = word_in.shape
    lane = lax.broadcasted_iota(jnp.int32, (part, 128), 1)
    for c in range(chunks):
        for q in range(0, sources, 2):
            at = pl.ds((c * sources + q) * 64, 128)
            for j in range(2):
                there = pl.ds(j * 128, 128)
                one, two = word_in[c, q, :, there].astype(F32), word_in[c, q + 1, :, there].astype(F32)
                word[2 * j, :, at] = jnp.where(lane < 64, one, pltpu.roll(two, 64, 1))
                word[2 * j + 1, :, at] = jnp.where(lane < 64, pltpu.roll(one, 64, 1), two)

    @pl.when(pl.program_id(0) == 0)
    def _():
        n = near[0]
        order = ((0, 0), (1 - n, n), (n, 1 - n), (1, 1))
        per, width = query.shape
        rows = jnp.concatenate([packed[a, b] for a, b in order], 0).astype(F32)
        for i, target in enumerate((query, keys, values, out)):
            target[...] = rows[i * per : (i + 1) * per]
        pos[...] = rows[4 * per :]
        lines = []
        for i, (a, b) in enumerate(order):
            up[:, pl.ds(i * width, width)] = feeds[a, b, per:, :].astype(F32)
            for j in range(2):
                lines.append(feeds[a, b, :per, j * 4 * per : (j + 1) * 4 * per])
        down[...] = jnp.concatenate(lines, 0).astype(F32).T


def finish(near, word, packed, feeds, rows_local, owners):
    chunks, sources, tall, _ = word.shape
    width = packed.shape[3]
    per = width // owners
    steps = 6
    part = tall // steps
    held = jax.ShapeDtypeStruct((per, width), F32)
    share = packed.shape[2] * 4 - 4 * per
    shapes = [held] * 4 + [
        jax.ShapeDtypeStruct((share, width), F32),
        jax.ShapeDtypeStruct((per, 4 * width), F32),
        jax.ShapeDtypeStruct((4 * per, width), F32),
    ]
    results = pl.pallas_call(
        finish_kernel,
        grid_spec=pltpu.PrefetchScalarGridSpec(
            num_scalar_prefetch=1,
            grid=(steps,),
            in_specs=[
                pl.BlockSpec((chunks, sources, part, 256), lambda i, *_: (0, 0, i, 0)),
                fixed(packed.shape),
                fixed(feeds.shape),
            ],
            out_specs=[pl.BlockSpec((4, part, width), lambda i, *_: (0, i, 0))] + [fixed(s.shape) for s in shapes],
        ),
        out_shape=[jax.ShapeDtypeStruct((4, tall, width), F32)] + shapes,
        compiler_params=pltpu.CompilerParams(vmem_limit_bytes=48 * MIB),
        name="finish",
    )(near.astype(jnp.int32).reshape(1), word, packed, feeds)
    return [results[0].reshape(rows_local, width)] + list(results[1:])


def local(
    token_ids,
    type_ids,
    lengths,
    word_table,
    pos_table,
    token_type_embeddings,
    emb_gain,
    emb_bias,
    query_weight,
    query_bias,
    key_weight,
    value_weight,
    value_bias,
    out_weight,
    out_bias,
    attn_gain,
    attn_bias,
    up_weight,
    up_bias,
    down_weight,
    down_bias,
    final_gain,
    final_bias,
    cotangent,
):
    seq_count, seq_len = token_ids.shape
    tokens = seq_count * seq_len
    width = word_table.shape[1]
    rows_local = word_table.shape[0]
    owners = lax.axis_size("vocab")
    capacity = max(2, 2 * tokens // owners)
    fast = owners == 8 and lax.axis_size("dp") == 4
    if fast:
        embedded, normed, slots, askeds = fetch(
            token_ids, type_ids, word_table, pos_table, token_type_embeddings, emb_gain, emb_bias, owners
        )
    else:
        flat_ids = token_ids.reshape(tokens)
        owner = flat_ids // rows_local
        member = (owner[:, None] == jnp.arange(owners)[None, :]).astype(jnp.int32)
        earlier = jnp.cumsum(member, 0) - member
        rank = jnp.sum(earlier * member, 1)
        slot = owner * capacity + rank
        requests = (
            jnp.full((owners * capacity,), -1, jnp.int32).at[slot].set(flat_ids - owner * rows_local)
        )
        requests = requests.reshape(owners, capacity)
        asked = lax.all_to_all(requests, "vocab", split_axis=0, concat_axis=0, tiled=True)
        valid = asked >= 0
        found = word_table[jnp.maximum(asked, 0)]
        found = jnp.where(valid[..., None], found, jnp.zeros((), jnp.bfloat16))
        returned = lax.all_to_all(found, "vocab", split_axis=0, concat_axis=0, tiled=True)
        word_rows = returned.reshape(owners * capacity, width)[slot]
        kinds = token_type_embeddings.shape[0]
        selection_matrix = (type_ids[..., None] == jnp.arange(kinds)[None, None, :]).astype(jnp.float32)
        type_rows = jnp.einsum(
            "tcr,rb->tcb",
            selection_matrix,
            token_type_embeddings.astype(jnp.float32),
            precision=lax.Precision.HIGHEST,
        )
        embedded = (
            word_rows.reshape(seq_count, seq_len, width).astype(jnp.float32)
            + pos_table.astype(jnp.float32)[None]
            + type_rows
        )
        embedded = embedded.reshape(tokens, width)
        normed = layer_norm(embedded, emb_gain, emb_bias)
    normed_low, query, keys, values, mixed_low, first, probs = attend(
        lengths, normed, query_weight, key_weight, value_weight, out_weight, query_bias, value_bias, out_bias
    )
    encoded, active_low, grad_second_low, hidden_low, grad_upper_low, grad_first, sums, grad_up_bias = feed(
        first,
        cotangent.reshape(tokens, width),
        up_weight,
        down_weight,
        up_bias,
        down_bias,
        attn_gain,
        attn_bias,
        final_gain,
        final_bias,
    )
    grad_final_gain, grad_final_bias, grad_down_bias, grad_attn_gain, grad_attn_bias, grad_out_bias = [
        sums[i] for i in range(6)
    ]
    grad_up_bias = grad_up_bias[0]
    if fast:
        (
            grad_first_low,
            grad_query_low,
            grad_keys_low,
            grad_values_low,
            raw,
            grad_pos,
            feed_own,
            sums,
        ) = mid(
            active_low,
            grad_upper_low,
            grad_second_low,
            hidden_low,
            grad_first,
            embedded,
            query,
            keys,
            values,
            probs,
            query_weight,
            key_weight,
            value_weight,
            out_weight,
            type_ids,
            emb_gain,
        )
    else:
        grad_down = matmul_tn(active_low, grad_second_low)
        grad_up = matmul_tn(hidden_low, grad_upper_low)
        grad_first_low, grad_query_low, grad_keys_low, grad_values_low, embedding_output_gradient, sums = attend_back(
            grad_first,
            embedded,
            type_ids,
            query,
            keys,
            values,
            probs,
            query_weight,
            key_weight,
            value_weight,
            out_weight,
            emb_gain,
        )
        grad_pos = jnp.sum(embedding_output_gradient.astype(jnp.float32).reshape(seq_count, seq_len, width), 0)
    grad_query_bias, grad_value_bias, grad_emb_gain, grad_emb_bias = [sums[i] for i in range(4)]
    token_type_gradient = sums[4:6]
    bf = jnp.bfloat16
    per = width // owners
    small = jnp.stack(
        [
            grad_query_bias,
            grad_value_bias,
            grad_out_bias,
            grad_attn_gain,
            grad_attn_bias,
            grad_emb_gain,
            grad_emb_bias,
            grad_down_bias,
            grad_final_gain,
            grad_final_bias,
            token_type_gradient[0],
            token_type_gradient[1],
        ]
    )
    if fast:
        ups = grad_up_bias.reshape(owners, 4, per).transpose(1, 0, 2).reshape(4, width)
        word_pairs, packed, feeds, small = tail(
            slots,
            askeds.reshape(-1, owners, capacity),
            grad_pos,
            jnp.concatenate([small, ups], 0),
            raw,
            normed_low,
            mixed_low,
            grad_first_low,
            grad_query_low,
            grad_keys_low,
            grad_values_low,
            feed_own,
            rows_local,
        )
        near = lax.axis_index("vocab") < owners // 2
        (
            grad_word,
            grad_query_weight,
            grad_key_weight,
            grad_value_weight,
            grad_out_weight,
            grad_pos,
            grad_up,
            grad_down,
        ) = finish(near, word_pairs, packed, feeds, rows_local, owners)
        small = small[:, :per]
    else:
        grad_down = sum_over_all(grad_down.astype(bf))
        grad_up = sum_over_all(grad_up.astype(bf))
        places = slot[None, :] == jnp.arange(owners * capacity)[:, None]
        outgoing = matmul(
            places.astype(bf), embedding_output_gradient.reshape(tokens, width).astype(bf)
        ).astype(bf)
        hits = (jnp.arange(rows_local)[:, None] == asked.reshape(-1)[None, :]).astype(bf)
        pieces = []
        step = 256
        for start in range(0, width, step):
            incoming = lax.all_to_all(
                outgoing[:, start : start + step].reshape(owners, capacity, step),
                "vocab",
                split_axis=0,
                concat_axis=0,
                tiled=True,
            )
            dense = matmul(hits, incoming.reshape(owners * capacity, step)).astype(bf)
            pieces.append(sum_over_dp(dense))
        grad_word = jnp.concatenate(pieces, 1)
        small = small.reshape(12, owners, per).transpose(1, 0, 2).reshape(owners, 12 * per)
        small = jnp.concatenate([small, grad_up_bias.reshape(owners, 4 * per)], 1)
        wide = 4 * width
        lines = (seq_len // owners) * width // wide
        rest = per // 3 - lines
        small_lines = jnp.pad(small, ((0, 0), (0, rest * wide - 16 * per))).reshape(owners, rest, wide)
        grad_query_weight, grad_key_weight, grad_value_weight = [
            matmul_tn(normed_low, g) for g in (grad_query_low, grad_keys_low, grad_values_low)
        ]
        grad_out_weight = matmul_tn(mixed_low, grad_first_low)
        mixed_grads = jnp.concatenate(
            [grad_query_weight, grad_key_weight, grad_value_weight, grad_out_weight], 1
        ).astype(bf)
        packed = jnp.concatenate(
            [
                mixed_grads.reshape(owners, per, wide),
                grad_pos.astype(bf).reshape(owners, lines, wide),
                small_lines.astype(bf),
            ],
            1,
        )
        packed = sum_over_all(packed.reshape(-1, wide))
        weights = packed[:per]
        grad_query_weight = weights[:, :width]
        grad_key_weight = weights[:, width : 2 * width]
        grad_value_weight = weights[:, 2 * width : 3 * width]
        grad_out_weight = weights[:, 3 * width :]
        grad_pos = packed[per : per + lines].reshape(seq_len // owners, width)
        small = packed[per + lines :].reshape(-1)[: 16 * per].reshape(16, per)
    (
        grad_query_bias,
        grad_value_bias,
        grad_out_bias,
        grad_attn_gain,
        grad_attn_bias,
        grad_emb_gain,
        grad_emb_bias,
        grad_down_bias,
        grad_final_gain,
        grad_final_bias,
    ) = [small[i] for i in range(10)]
    token_type_gradient = small[10:12]
    grad_up_bias = small[12:].reshape(-1)
    return (
        encoded.reshape(seq_count, seq_len, width),
        grad_word,
        grad_pos,
        token_type_gradient,
        grad_emb_gain,
        grad_emb_bias,
        grad_query_weight,
        grad_query_bias,
        grad_key_weight,
        grad_value_weight,
        grad_value_bias,
        grad_out_weight,
        grad_out_bias,
        grad_attn_gain,
        grad_attn_bias,
        grad_up,
        grad_up_bias,
        grad_down,
        grad_down_bias,
        grad_final_gain,
        grad_final_bias,
    )


def solution(mesh):
    placed = (
        P(("dp", "vocab"), None),
        P(("dp", "vocab"), None),
        P(("dp", "vocab")),
        P("vocab", None),
        P(),
        P(),
        P(),
        P(),
        P(),
        P(),
        P(),
        P(),
        P(),
        P(),
        P(),
        P(),
        P(),
        P(),
        P(),
        P(),
        P(),
        P(),
        P(),
        P(("dp", "vocab"), None, None),
    )
    return jax.shard_map(
        local,
        mesh=mesh,
        in_specs=placed,
        out_specs=(
            P(("dp", "vocab"), None, None),
            P("vocab", None),
            P("vocab", None),
            P(None, "vocab"),
            P("vocab"),
            P("vocab"),
            P("vocab", None),
            P("vocab"),
            P("vocab", None),
            P("vocab", None),
            P("vocab"),
            P("vocab", None),
            P("vocab"),
            P("vocab"),
            P("vocab"),
            P("vocab", None),
            P("vocab"),
            P("vocab", None),
            P("vocab"),
            P("vocab"),
            P("vocab"),
        ),
        check_vma=False,
    )
```

```python
from functools import partial

import jax
import jax.numpy as jnp
from jax import lax
from jax.experimental import pallas as pl
from jax.experimental.pallas import tpu as pltpu
from jax.sharding import PartitionSpec as P

HEADS = 12
HEAD = 64
L = 512


EPSILON = 1e-12


def layer_norm(values, gain, bias):
    center = values - jnp.mean(values, -1, keepdims=True)
    spread = jnp.mean(center * center, -1, keepdims=True)
    return center * lax.rsqrt(spread + EPSILON) * gain + bias


def matmul(left, right):
    return jnp.dot(left, right, preferred_element_type=jnp.float32)


def matmul_tn(left, right):
    return lax.dot_general(
        left, right, (((0,), (0,)), ((), ())), preferred_element_type=jnp.float32
    )


def matmul_nt(left, right):
    return lax.dot_general(
        left, right, (((1,), (1,)), ((), ())), preferred_element_type=jnp.float32
    )


def swap(value, axis_name, bit):
    size = lax.axis_size(axis_name)
    return lax.ppermute(value, axis_name, [(i, i ^ bit) for i in range(size)])


def pick(value, index, axis):
    return lax.dynamic_index_in_dim(value, index, axis, keepdims=False)


def plus(left, right):
    return (left.astype(jnp.float32) + right.astype(jnp.float32)).astype(jnp.bfloat16)


def dp_bits():
    index = lax.axis_index("dp")
    return lax.rem(index, 2), index // 2


def reorder(own, across_x, across_y, across_both):
    xb, yb = dp_bits()
    flip_x, flip_y = xb == 1, yb == 1
    rows = [[own, across_y], [across_x, across_both]]
    rows = [
        [jnp.where(flip_x, rows[1 - i][j], rows[i][j]) for j in range(2)] for i in range(2)
    ]
    rows = [
        [jnp.where(flip_y, rows[i][1 - j], rows[i][j]) for j in range(2)] for i in range(2)
    ]
    return rows


def sum_over_all(grad):
    size = lax.axis_size("vocab")
    me = lax.axis_index("vocab")
    core = lax.rem(me, 2)
    place = me // 2
    places = size // 2
    total, n = grad.shape
    r = total // size
    xb, yb = dp_bits()
    grad = grad.reshape(places, 2, r, n)
    other = swap(pick(grad, 1 - core, 1), "vocab", 1)
    held = plus(pick(grad, core, 1), other).reshape(places, 2, 2, r // 4, n)
    first, last = held[: places // 2], held[places // 2 :]
    first_in = swap(pick(first, 1 - xb, 1), "dp", 1)
    last_in = swap(pick(last, 1 - yb, 2), "dp", 2)
    first = plus(pick(first, xb, 1), first_in)
    last = plus(pick(last, yb, 2), last_in)
    first_in = swap(pick(first, 1 - yb, 1), "dp", 2)
    last_in = swap(pick(last, 1 - xb, 1), "dp", 1)
    first = plus(pick(first, yb, 1), first_in)
    last = plus(pick(last, xb, 1), last_in)
    held = jnp.concatenate([first, last], 0)
    summed = pick(held, place, 0).astype(jnp.float32)
    for step in range(1, places):
        block = pick(held, lax.rem(place + step, places), 0)
        block = lax.ppermute(
            block, "vocab", [(i, (i + 2 * step) % size) for i in range(size)]
        )
        summed = summed + block.astype(jnp.float32)
    own = summed.astype(jnp.bfloat16)
    across_x = swap(own, "dp", 1)
    across_y = swap(own, "dp", 2)
    half = n // 2
    both = jnp.concatenate(
        [swap(across_x[:, :half], "dp", 2), swap(across_y[:, half:], "dp", 1)], 1
    )
    rows = reorder(own, across_x, across_y, both)
    return jnp.stack([rows[0][0], rows[0][1], rows[1][0], rows[1][1]]).reshape(r, n).astype(jnp.float32)


def sum_over_dp(grad):
    rows, n = grad.shape
    xb, yb = dp_bits()
    held = grad.reshape(2, 2, 2, rows // 8, n)
    first, last = held[0], held[1]
    first_in = swap(pick(first, 1 - xb, 0), "dp", 1)
    last_in = swap(pick(last, 1 - yb, 1), "dp", 2)
    first = plus(pick(first, xb, 0), first_in)
    last = plus(pick(last, yb, 1), last_in)
    first_in = swap(pick(first, 1 - yb, 0), "dp", 2)
    last_in = swap(pick(last, 1 - xb, 0), "dp", 1)
    first = plus(pick(first, yb, 0), first_in)
    last = plus(pick(last, xb, 0), last_in)
    first_x = swap(first, "dp", 1)
    last_y = swap(last, "dp", 2)
    first_y = swap(jnp.stack([first, first_x]), "dp", 2)
    last_x = swap(jnp.stack([last, last_y]), "dp", 1)
    a = reorder(first, first_x, first_y[0], first_y[1])
    b = reorder(last, last_x[0], last_y, last_x[1])
    parts = [p for group in (a, b) for line in group for p in line]
    return jnp.concatenate(parts, 0).astype(jnp.float32)


BF = jnp.bfloat16
F32 = jnp.float32
MIB = 1024 * 1024


def dot_nt(left, right):
    return lax.dot_general(left, right, (((1,), (1,)), ((), ())), preferred_element_type=F32)


def dot_nn(left, right):
    return jnp.dot(left, right, preferred_element_type=F32)


def stats(values):
    center = values - jnp.mean(values, -1, keepdims=True)
    inverse = lax.rsqrt(jnp.mean(center * center, -1, keepdims=True) + EPSILON)
    return center * inverse, inverse


def norm_back(grad, gain, unit, inverse):
    scaled = grad * gain
    return inverse * (
        scaled
        - jnp.mean(scaled, -1, keepdims=True)
        - unit * jnp.mean(scaled * unit, -1, keepdims=True)
    )


def column_sum(values):
    return jnp.sum(values, 0, keepdims=True)


TAIL_SCALE = 0.33
TAIL_TERMS = (
    -0.13534782292195252,
    0.4602463244004558,
    -0.3511662200543899,
    0.4085159085223644,
    0.04721176063633592,
    0.2012267561020528,
    0.1829554472050349,
    0.1863578383326851,
)


def normal_parts(u):
    t = 1.0 / (1.0 + (TAIL_SCALE * 0.5**0.5) * jnp.abs(u))
    poly = TAIL_TERMS[0]
    for term in TAIL_TERMS[1:]:
        poly = poly * t + term
    bell = jnp.exp(u * u * -0.5)
    below = (0.5 * t) * poly * bell
    return jnp.where(u >= 0, 1.0 - below, below), bell * 0.3989422804014327


def attend_kernel(
    lengths, normed, wq, wk, wv, wo, query_bias, value_bias, out_bias,
    low, q_out, k_out, v_out, mixed_out, first_out, probs_out, bias,
):
    tokens, width = normed.shape
    tile = 256
    low[...] = normed[...].astype(BF)

    def project(n, carry):
        at = pl.ds(pl.multiple_of(n * tile, tile), tile)
        x = low[...]
        query = (dot_nn(x, wq[:, at]) + query_bias[at][None]).astype(BF)
        q_out[:, at] = query * BF(HEAD**-0.5)
        k_out[:, at] = dot_nn(x, wk[:, at]).astype(BF)
        v_out[:, at] = (dot_nn(x, wv[:, at]) + value_bias[at][None]).astype(BF)
        return carry

    lax.fori_loop(0, width // tile, project, 0)
    seen = lax.broadcasted_iota(jnp.int32, bias.shape, 0) < lengths[pl.program_id(0)]
    bias[...] = jnp.where(seen, 0.0, -1000000000.0)

    def pair(j):
        at = pl.ds(pl.multiple_of(j * 2 * HEAD, 2 * HEAD), 2 * HEAD)
        q, k, turned = q_out[:, at], k_out[:, at], v_out[:, at].T
        lane = lax.broadcasted_iota(jnp.int32, k.shape, 1)
        parts = []
        for side in range(2):
            mine = (lane >= HEAD) if side else (lane < HEAD)
            scores = dot_nt(jnp.where(mine, k, jnp.zeros_like(k)), q)
            scores = scores + jnp.concatenate([bias[...]] * (tokens // 128), 1)
            expd = jnp.exp(scores - jnp.max(scores, 0, keepdims=True))
            probs = (expd * (1.0 / jnp.sum(expd, 0, keepdims=True))).astype(BF)
            probs_out[0, 2 * j + side] = probs
            parts.append(dot_nn(turned[side * HEAD : (side + 1) * HEAD], probs))
        mixed_out[:, at] = jnp.concatenate(parts, 0).T.astype(BF)

    def pairs(n, carry):
        for i in range(2):
            pair(2 * n + i)
        return carry

    lax.fori_loop(0, HEADS // 4, pairs, 0)

    def close(n, carry):
        at = pl.ds(pl.multiple_of(n * tile, tile), tile)
        first_out[:, at] = normed[:, at] + dot_nn(mixed_out[...], wo[:, at]) + out_bias[at][None]
        return carry

    lax.fori_loop(0, width // tile, close, 0)


def fixed(shape):
    return pl.BlockSpec(shape, lambda i, *_: (0,) * len(shape), pipeline_mode=pl.Buffered(1))


def rows_of(rows, width):
    return pl.BlockSpec((rows, width), lambda i, *_: (i, 0))


def row(vector):
    return vector.reshape(1, -1)


def attend(lengths, normed, wq, wk, wv, wo, query_bias, value_bias, out_bias):
    tokens, width = normed.shape
    seqs = lengths.shape[0]
    size = tokens // seqs
    low = jax.ShapeDtypeStruct((tokens, width), BF)
    part = rows_of(size, width)
    return pl.pallas_call(
        attend_kernel,
        grid_spec=pltpu.PrefetchScalarGridSpec(
            num_scalar_prefetch=1,
            grid=(seqs,),
            in_specs=[part] + [fixed((width, width))] * 4 + [fixed((width,))] * 3,
            out_specs=[part] * 6 + [pl.BlockSpec((1, HEADS, size, size), lambda i, *_: (i, 0, 0, 0))],
            scratch_shapes=[pltpu.VMEM((size, 128), F32)],
        ),
        out_shape=[low] * 5
        + [jax.ShapeDtypeStruct((tokens, width), F32), jax.ShapeDtypeStruct((seqs, HEADS, size, size), BF)],
        compiler_params=pltpu.CompilerParams(vmem_limit_bytes=60 * MIB),
        cost_estimate=pl.CostEstimate(flops=20 * 10**9, bytes_accessed=30 * 10**6, transcendentals=0),
        name="attend",
    )(lengths, normed, wq, wk, wv, wo, query_bias, value_bias, out_bias)


def feed_kernel(
    first, cotangent, up, down, up_bias, down_bias, attn_gain, attn_bias, final_gain, final_bias,
    encoded, active, second_low, hidden_low, upper_low, first_grad, sums, up_sum,
    slope,
):
    width = first.shape[1]
    units = up.shape[1]
    block = 768
    unit, inverse = stats(first[...])
    hidden = unit * attn_gain[...][None] + attn_bias[...][None]
    hidden_low[...] = hidden.astype(BF)
    total = hidden + down_bias[...][None]
    for n in range(units // block):
        at = pl.ds(n * block, block)
        upper = dot_nn(hidden_low[...], up[:, at]) + up_bias[at][None]
        below, density = normal_parts(upper)
        active[:, at] = (upper * below).astype(BF)
        slope[:, at] = below + upper * density
        total = total + dot_nn(active[:, at], down[at, :])
    unit_out, inverse_out = stats(total)
    encoded[...] = unit_out * final_gain[...][None] + final_bias[...][None]
    grad = cotangent[...].astype(F32)
    grad_second = norm_back(grad, final_gain[...][None], unit_out, inverse_out)
    second_low[...] = grad_second.astype(BF)

    @pl.when(pl.program_id(0) == 0)
    def _():
        sums[...] = jnp.zeros_like(sums)
        up_sum[...] = jnp.zeros_like(up_sum)

    sums[0:1, :] += column_sum(grad * unit_out)
    sums[1:2, :] += column_sum(grad)
    sums[2:3, :] += column_sum(grad_second)
    total = grad_second
    for n in range(units // block):
        at = pl.ds(n * block, block)
        grad_upper = dot_nt(second_low[...], down[at, :]) * slope[:, at]
        up_sum[:, at] += column_sum(grad_upper)
        upper_low[:, at] = grad_upper.astype(BF)
        total = total + dot_nt(upper_low[:, at], up[:, at])
    grad_first = norm_back(total, attn_gain[...][None], unit, inverse)
    sums[3:4, :] += column_sum(total * unit)
    sums[4:5, :] += column_sum(total)
    sums[5:6, :] += column_sum(grad_first)
    first_grad[...] = grad_first


def feed(first, cotangent, up, down, up_bias, down_bias, attn_gain, attn_bias, final_gain, final_bias):
    tokens, width = first.shape
    units = up.shape[1]
    tile = 512
    part, wide = rows_of(tile, width), rows_of(tile, units)
    vector = fixed((width,))
    return pl.pallas_call(
        feed_kernel,
        grid=(tokens // tile,),
        in_specs=[part, part, fixed((width, units)), fixed((units, width)), fixed((units,))] + [vector] * 5,
        out_specs=[part, wide, part, part, wide, part, fixed((8, width)), fixed((1, units))],
        out_shape=[
            jax.ShapeDtypeStruct((tokens, width), F32),
            jax.ShapeDtypeStruct((tokens, units), BF),
            jax.ShapeDtypeStruct((tokens, width), BF),
            jax.ShapeDtypeStruct((tokens, width), BF),
            jax.ShapeDtypeStruct((tokens, units), BF),
            jax.ShapeDtypeStruct((tokens, width), F32),
            jax.ShapeDtypeStruct((8, width), F32),
            jax.ShapeDtypeStruct((1, units), F32),
        ],
        scratch_shapes=[pltpu.VMEM((tile, units), F32)],
        compiler_params=pltpu.CompilerParams(vmem_limit_bytes=60 * MIB),
        cost_estimate=pl.CostEstimate(flops=40 * 10**9, bytes_accessed=40 * 10**6, transcendentals=0),
        name="feed",
    )(
        first, cotangent, up, down, up_bias, down_bias, attn_gain, attn_bias, final_gain, final_bias
    )


def attend_back_kernel(
    grad_first, embedded, kinds, q_in, k_in, v_in, probs_in, wq, wk, wv, wo, emb_gain,
    first_low, dq, dk, dv, emb_low, sums,
    grad_mixed, total,
):
    tokens, width = grad_first.shape
    tile = 256

    @pl.when(pl.program_id(0) == 0)
    def _():
        sums[...] = jnp.zeros_like(sums)

    first_low[...] = grad_first[...].astype(BF)

    def open_(n, carry):
        at = pl.ds(pl.multiple_of(n * tile, tile), tile)
        grad_mixed[:, at] = dot_nt(first_low[...], wo[at, :]).astype(BF)
        return carry

    lax.fori_loop(0, width // tile, open_, 0)

    def pair(j, carry):
        at = pl.ds(pl.multiple_of(j * 2 * HEAD, 2 * HEAD), 2 * HEAD)
        q, k, v, grad = q_in[:, at], k_in[:, at], v_in[:, at], grad_mixed[:, at]
        turned = k.T
        lane = lax.broadcasted_iota(jnp.int32, k.shape, 1)
        parts = []
        grad_k = jnp.zeros(k.shape, F32)
        grad_v = jnp.zeros(k.shape, F32)
        for side in range(2):
            mine = (lane >= HEAD) if side else (lane < HEAD)
            none = jnp.zeros_like(k)
            probs = probs_in[0, 2 * j + side]
            grad_probs = dot_nt(jnp.where(mine, v, none), grad)
            grad_v = grad_v + dot_nn(probs, jnp.where(mine, grad, none))
            wide = probs.astype(F32)
            both = wide * grad_probs
            scores = (both - wide * jnp.sum(both, 0, keepdims=True)).astype(BF)
            grad_k = grad_k + dot_nn(scores, jnp.where(mine, q, none))
            parts.append(dot_nn(turned[side * HEAD : (side + 1) * HEAD], scores))
        grad_q = jnp.concatenate(parts, 0).T * HEAD**-0.5
        dq[:, at] = grad_q.astype(BF)
        dk[:, at] = grad_k.astype(BF)
        dv[:, at] = grad_v.astype(BF)
        sums[0:1, at] += column_sum(grad_q)
        sums[1:2, at] += column_sum(grad_v)
        return carry

    lax.fori_loop(0, HEADS // 2, pair, 0)

    def close(n, carry):
        at = pl.ds(pl.multiple_of(n * tile, tile), tile)
        total[:, at] = (
            grad_first[:, at]
            + dot_nt(dq[...], wq[at, :])
            + dot_nt(dk[...], wk[at, :])
            + dot_nt(dv[...], wv[at, :])
        )
        return carry

    lax.fori_loop(0, width // tile, close, 0)
    rows = 128

    def last(n, carry):
        at = pl.ds(pl.multiple_of(n * rows, rows), rows)
        unit, inverse = stats(embedded[at, :])
        grad = total[at, :]
        grad_emb = norm_back(grad, emb_gain[...], unit, inverse)
        emb_low[at, :] = grad_emb.astype(BF)
        sums[2:3, :] += column_sum(grad * unit)
        sums[3:4, :] += column_sum(grad)
        kind = kinds[at, :]
        for t in range(2):
            sums[4 + t : 5 + t, :] += column_sum(jnp.where(kind == t, grad_emb, 0.0))
        return carry

    lax.fori_loop(0, tokens // rows, last, 0)


def attend_back(grad_first, embedded, kinds, q, k, v, probs, wq, wk, wv, wo, emb_gain):
    tokens, width = grad_first.shape
    seqs, _, size, _ = probs.shape
    part = rows_of(size, width)
    low = jax.ShapeDtypeStruct((tokens, width), BF)
    return pl.pallas_call(
        attend_back_kernel,
        grid=(seqs,),
        in_specs=[part, part, rows_of(size, 1)]
        + [part] * 3
        + [pl.BlockSpec((1, HEADS, size, size), lambda i: (i, 0, 0, 0))]
        + [fixed((width, width))] * 4
        + [fixed((1, width))],
        out_specs=[part] * 5 + [fixed((8, width))],
        out_shape=[low] * 5 + [jax.ShapeDtypeStruct((8, width), F32)],
        scratch_shapes=[pltpu.VMEM((size, width), BF), pltpu.VMEM((size, width), F32)],
        compiler_params=pltpu.CompilerParams(vmem_limit_bytes=60 * MIB),
        cost_estimate=pl.CostEstimate(flops=30 * 10**9, bytes_accessed=40 * 10**6, transcendentals=0),
        name="attend_back",
    )(grad_first, embedded, kinds.reshape(tokens, 1), q, k, v, probs, wq, wk, wv, wo, row(emb_gain))


MESH = pl.DeviceIdType.MESH


def column_of(lines, column):
    count, size = lines.shape
    for s in range(count):
        line = jnp.broadcast_to(lines[s : s + 1, :].astype(F32), (8, size))
        column[pl.ds(s * size, size), :] = line.T[:, 0:1].astype(jnp.int32)


def mid_kernel(
    active, upper_low, second_low, hidden_low, grad_first, embedded, q_in, k_in, v_in, probs_in, wq, wk, wv, wo,
    kinds_in, emb_gain_in,
    first_out, dq_out, dk_out, dv_out, raw_out, pos_out, feed_out, part_out, sums,
    stage, lhs, turned, grads, core_in, in_1a, in_1b, in_2a, in_2b, in_z, kept,
    first, low, grad_mixed, q, k, v, dq, dk, dv, weights, table, raw, pos, probs, kind_column, kinds, emb_gain,
    load, stage_sem, probs_sem, out_sem, send, recv,
):
    tokens, width = lhs.shape
    seqs, size = kinds.shape
    per = grads.shape[3]
    me = lax.axis_index("vocab")
    spot = lax.axis_index("dp")
    core, place = lax.rem(me, 2), lax.div(me, 2)
    xb, yb = lax.rem(spot, 2), lax.div(spot, 2)
    across_x = {"dp": spot + 1 - 2 * xb}
    across_y = {"dp": spot + 2 - 4 * yb}
    partner = {"vocab": me + 1 - 2 * core}
    block = 768
    blocks = active.shape[1] // block

    def stage_copy(source, n):
        at = pl.ds(pl.multiple_of(n * block, block), block)
        slot = lax.rem(n, 2)
        return pltpu.make_async_copy(source.at[:, at], stage.at[slot], stage_sem.at[slot])

    def probs_copy(n):
        group = HEADS // 4
        slot = lax.rem(n, 2)
        return pltpu.make_async_copy(
            probs_in.at[lax.div(n, group), pl.ds(4 * lax.rem(n, group), 4)], probs.at[slot], probs_sem.at[slot]
        )

    second_copy = pltpu.make_async_copy(second_low, lhs, load.at[0])
    hidden_copy = pltpu.make_async_copy(hidden_low, lhs, load.at[1])
    second_copy.start()
    stage_copy(active, 0).start()
    stage_copy(active, 1).start()
    loads = [
        pltpu.make_async_copy(source, target, load.at[2 + i])
        for i, (source, target) in enumerate(
            (
                (grad_first, first),
                (wo, weights.at[3]),
                (q_in, q),
                (k_in, k),
                (v_in, v),
                (wq, weights.at[0]),
                (wk, weights.at[1]),
                (wv, weights.at[2]),
                (embedded, table),
                (kinds_in, kinds),
                (emb_gain_in, emb_gain),
            )
        )
    ]
    barrier = pltpu.get_barrier_semaphore()
    places = [{"vocab": 2 * flipped(place, k) + core} for k in (1, 2, 3)]
    for peer in [partner, across_x, across_y] + places:
        pl.semaphore_signal(barrier, inc=1, device_id=peer, device_id_type=MESH)
    pl.semaphore_wait(barrier, 6)

    def remote(src, dst, at, peer):
        return pltpu.make_async_remote_copy(
            src_ref=src, dst_ref=dst, send_sem=send.at[at], recv_sem=recv.at[at], device_id=peer, device_id_type=MESH
        )

    def core_copy(g):
        return remote(grads.at[g, :, 1 - core], core_in.at[g], 5 * g, partner)

    half = 2 * width

    def wide(b):
        return pl.ds(pl.multiple_of(b * half, half), half)

    def narrow(b, c):
        return pl.ds(pl.multiple_of(b * half + c * width, width), width)

    def first_copies(g):
        return [
            remote(grads.at[g, pl.ds(0, 2), core, :, wide(1 - xb)], in_1a.at[g], 5 * g + 1, across_x),
            remote(grads.at[g, pl.ds(2, 2), core, :, wide(1 - yb)], in_1b.at[g], 5 * g + 2, across_y),
        ]

    def second_copies(g):
        return [
            remote(grads.at[g, pl.ds(0, 2), core, :, narrow(xb, 1 - yb)], in_2a.at[g], 5 * g + 3, across_y),
            remote(grads.at[g, pl.ds(2, 2), core, :, narrow(yb, 1 - xb)], in_2b.at[g], 5 * g + 4, across_x),
        ]

    def add(view, value):
        view[...] = (view[...].astype(F32) + value.astype(F32)).astype(BF)

    def core_step(g):
        core_copy(g).wait_recv()
        rows = per // 2

        def one(i, carry):
            z = lax.div(i, 2)
            at = pl.ds(pl.multiple_of(lax.rem(i, 2) * rows, rows), rows)
            add(grads.at[g, z, core, at, :], core_in[g, z, at, :])
            return carry

        lax.fori_loop(0, 8, one, 0)
        for copy in first_copies(g):
            copy.start()

    def first_step(g):
        for copy in first_copies(g):
            copy.wait_recv()

        def one(z, carry):
            add(grads.at[g, z, core, :, wide(xb)], in_1a[g, z])
            add(grads.at[g, 2 + z, core, :, wide(yb)], in_1b[g, z])
            return carry

        lax.fori_loop(0, 2, one, 0)
        for copy in second_copies(g):
            copy.start()

    def owned(g, z):
        at = 2 * xb + yb + lax.div(z, 2) * (yb - xb)
        return grads.at[g, z, core, :, pl.ds(pl.multiple_of(at * width, width), width)]

    def part_copies():
        return [
            pltpu.make_async_copy(
                grads.at[1, pl.ds(0, 2), core, :, narrow(xb, yb)], part_out.at[pl.ds(0, 2)], out_sem.at[0]
            ),
            pltpu.make_async_copy(
                grads.at[1, pl.ds(2, 2), core, :, narrow(yb, xb)], part_out.at[pl.ds(2, 2)], out_sem.at[1]
            ),
        ]

    def place_copies(g):
        return [
            remote(owned(g, flipped(place, k)), in_z.at[g, k - 1], 10 + 3 * g + k - 1, places[k - 1]) for k in (3, 2, 1)
        ]

    def place_step(g):
        for copy in place_copies(g):
            copy.wait_recv()
        total = owned(g, place)[...].astype(F32)
        for k in range(3):
            total = total + in_z[g, k].astype(F32)
        kept[...] = total.astype(BF)

    def second_step(g):
        for copy in second_copies(g):
            copy.wait_recv()
        for z in range(2):
            add(grads.at[g, z, core, :, narrow(xb, yb)], in_2a[g, z])
            add(grads.at[g, 2 + z, core, :, narrow(yb, xb)], in_2b[g, z])
        if g == 0:
            for copy in place_copies(g):
                copy.start()
        else:
            for copy in part_copies():
                copy.start()

    corner = 256

    def turn():
        def one(i, carry):
            at = pl.ds(pl.multiple_of(i * corner, corner), corner)
            for j in range(width // corner):
                there = pl.ds(j * corner, corner)
                turned[there, at] = lhs[at, there].T
            return carry

        lax.fori_loop(0, tokens // corner, one, 0)

    second_copy.wait()
    turn()
    hidden_copy.start()
    probs_copy(0).start()
    for copy in loads:
        copy.start()
    share = block // 2

    def down_block(n, carry):
        stage_copy(active, n).wait()
        slot = lax.rem(n, 2)
        for c in range(2):
            out = dot_nn(turned[...], stage[slot, :, c * share : (c + 1) * share]).astype(BF)
            for j in range(8):
                grads[0, n, c, :, j * share : (j + 1) * share] = out[j * per : (j + 1) * per]

        @pl.when(n < 2)
        def _():
            stage_copy(active, n + 2).start()

        @pl.when(n >= 2)
        def _():
            stage_copy(upper_low, n - 2).start()

        return carry

    lax.fori_loop(0, blocks, down_block, 0)
    core_copy(0).start()
    hidden_copy.wait()
    turn()

    def up_block(n, carry):
        stage_copy(upper_low, n).wait()
        slot = lax.rem(n, 2)
        for c in range(2):
            out = dot_nn(turned[...], stage[slot, :, c * share : (c + 1) * share]).astype(BF)
            at = pl.ds(pl.multiple_of(n * block + c * share, 128), share)
            for j in range(8):
                grads[1, j // 2, j % 2, :, at] = out[j * per : (j + 1) * per]

        @pl.when(n < 2)
        def _():
            stage_copy(upper_low, n + 2).start()

        return carry

    lax.fori_loop(0, blocks, up_block, 0)
    core_copy(1).start()
    core_step(0)

    for copy in loads:
        copy.wait()
    sums[...] = jnp.zeros_like(sums)
    low[...] = first[...].astype(BF)
    first_copy = pltpu.make_async_copy(low, first_out, out_sem.at[4])
    first_copy.start()
    tile = 256

    def open_(n, carry):
        at = pl.ds(pl.multiple_of(n * tile, tile), tile)
        grad_mixed[:, at] = dot_nt(low[...], weights[3, at, :]).astype(BF)
        return carry

    lax.fori_loop(0, width // tile, open_, 0)

    def pair(n, slot, i):
        rows = pl.ds(pl.multiple_of(lax.div(n, HEADS // 2) * size, size), size)
        at = pl.ds(pl.multiple_of(lax.rem(n, HEADS // 2) * 2 * HEAD, 2 * HEAD), 2 * HEAD)
        q2, k2, v2, grad = q[rows, at], k[rows, at], v[rows, at], grad_mixed[rows, at]
        across = k2.T
        lane = lax.broadcasted_iota(jnp.int32, k2.shape, 1)
        parts = []
        grad_k = jnp.zeros(k2.shape, F32)
        grad_v = jnp.zeros(k2.shape, F32)
        for side in range(2):
            mine = (lane >= HEAD) if side else (lane < HEAD)
            none = jnp.zeros_like(k2)
            chances = probs[slot, 2 * i + side]
            grad_probs = dot_nt(jnp.where(mine, v2, none), grad)
            grad_v = grad_v + dot_nn(chances, jnp.where(mine, grad, none))
            full = chances.astype(F32)
            both = full * grad_probs
            scores = (both - full * jnp.sum(both, 0, keepdims=True)).astype(BF)
            grad_k = grad_k + dot_nn(scores, jnp.where(mine, q2, none))
            parts.append(dot_nn(across[side * HEAD : (side + 1) * HEAD], scores))
        grad_q = jnp.concatenate(parts, 0).T * HEAD**-0.5
        dq[rows, at] = grad_q.astype(BF)
        dk[rows, at] = grad_k.astype(BF)
        dv[rows, at] = grad_v.astype(BF)
        sums[0:1, at] += column_sum(grad_q)
        sums[1:2, at] += column_sum(grad_v)

    groups = seqs * HEADS // 4

    def pairs(n, carry):
        @pl.when(n + 1 < groups)
        def _():
            probs_copy(n + 1).start()

        probs_copy(n).wait()
        slot = lax.rem(n, 2)
        for i in range(2):
            pair(2 * n + i, slot, i)

        @pl.when(n == 0)
        def _():
            core_step(1)

        @pl.when(n == 2)
        def _():
            first_step(0)

        @pl.when(n == 4)
        def _():
            second_step(0)
            first_step(1)

        return carry

    lax.fori_loop(0, groups, pairs, 0)
    out_copies = [
        pltpu.make_async_copy(source, target, out_sem.at[5 + i])
        for i, (source, target) in enumerate(((dq, dq_out), (dk, dk_out), (dv, dv_out)))
    ]
    for copy in out_copies:
        copy.start()

    def close(n, carry):
        at = pl.ds(pl.multiple_of(n * tile, tile), tile)
        first[:, at] = (
            first[:, at]
            + dot_nt(dq[...], weights[0, at, :])
            + dot_nt(dk[...], weights[1, at, :])
            + dot_nt(dv[...], weights[2, at, :])
        )
        return carry

    lax.fori_loop(0, width // tile, close, 0)
    second_step(1)
    column_of(kinds, kind_column)
    few = 128
    lane = lax.broadcasted_iota(jnp.int32, (few, 128), 1)

    def back(at):
        unit, inverse = stats(table[at, :])
        grad = first[at, :]
        grad_emb = norm_back(grad, emb_gain[...][None], unit, inverse)
        sums[2:3, :] += column_sum(grad * unit)
        sums[3:4, :] += column_sum(grad)
        kind = kind_column[at, :]
        for t in range(2):
            sums[4 + t : 5 + t, :] += column_sum(jnp.where(kind == t, grad_emb, 0.0))
        return grad_emb

    def last(n, carry):
        at = pl.ds(pl.multiple_of(n * few, few), few)
        left = back(at)
        right = back(pl.ds(pl.multiple_of(size + n * few, few), few))
        pos[at, :] = (left + right).astype(BF)
        for t in range(width // 128):
            one, two = left[:, t * 128 : (t + 1) * 128], right[:, t * 128 : (t + 1) * 128]
            q = 2 * (t % 2)
            raw[t // 2, q, at, :] = jnp.where(lane < 64, one, pltpu.roll(two, 64, 1)).astype(BF)
            raw[t // 2, q + 1, at, :] = jnp.where(lane < 64, pltpu.roll(one, 64, 1), two).astype(BF)
        return carry

    lax.fori_loop(0, size // few, last, 0)
    raw_copy = pltpu.make_async_copy(raw, raw_out, out_sem.at[3])
    raw_copy.start()
    pos_copy = pltpu.make_async_copy(pos, pos_out, out_sem.at[8])
    pos_copy.start()
    place_step(0)
    feed_copy = pltpu.make_async_copy(kept, feed_out, out_sem.at[2])
    feed_copy.start()
    for copy in [first_copy, raw_copy, pos_copy, feed_copy] + out_copies + part_copies():
        copy.wait()
    for g in range(2):
        for copy in [core_copy(g)] + first_copies(g) + second_copies(g):
            copy.wait_send()
    for copy in place_copies(0):
        copy.wait_send()


def mid(
    active, upper_low, second_low, hidden_low, grad_first, embedded, q, k, v, probs, wq, wk, wv, wo, kinds, emb_gain
):
    tokens, width = grad_first.shape
    seqs, heads, size, _ = probs.shape
    units = active.shape[1]
    per = width // 8
    wide = 4 * width
    vmem = pl.BlockSpec(memory_space=pltpu.VMEM)
    hbm = pl.BlockSpec(memory_space=pl.ANY)
    low = jax.ShapeDtypeStruct((tokens, width), BF)
    small = pltpu.VMEM((tokens, width), BF)
    large = pltpu.VMEM((tokens, width), F32)
    return pl.pallas_call(
        mid_kernel,
        out_shape=[low] * 4
        + [
            jax.ShapeDtypeStruct((3, 4, size, 128), BF),
            jax.ShapeDtypeStruct((size, width), BF),
            jax.ShapeDtypeStruct((per, width), BF),
            jax.ShapeDtypeStruct((4, per, width), BF),
            jax.ShapeDtypeStruct((8, width), F32),
        ],
        in_specs=[hbm] * 16,
        out_specs=[hbm] * 8 + [vmem],
        scratch_shapes=[
            pltpu.VMEM((2, tokens, 768), BF),
            small,
            pltpu.VMEM((width, tokens), BF),
            pltpu.VMEM((2, 4, 2, per, wide), BF),
            pltpu.VMEM((2, 4, per, wide), BF),
            pltpu.VMEM((2, 2, per, wide // 2), BF),
            pltpu.VMEM((2, 2, per, wide // 2), BF),
            pltpu.VMEM((2, 2, per, width), BF),
            pltpu.VMEM((2, 2, per, width), BF),
            pltpu.VMEM((1, 3, per, width), BF),
            pltpu.VMEM((per, width), BF),
            large,
            small,
            small,
            small,
            small,
            small,
            small,
            small,
            small,
            pltpu.VMEM((4, width, width), BF),
            large,
            pltpu.VMEM((3, 4, size, 128), BF),
            pltpu.VMEM((size, width), BF),
            pltpu.VMEM((2, 4, size, size), BF),
            pltpu.VMEM((tokens, 1), jnp.int32),
            pltpu.VMEM((seqs, size), jnp.int32),
            pltpu.VMEM((width,), F32),
            pltpu.SemaphoreType.DMA((13,)),
            pltpu.SemaphoreType.DMA((2,)),
            pltpu.SemaphoreType.DMA((2,)),
            pltpu.SemaphoreType.DMA((9,)),
            pltpu.SemaphoreType.DMA((16,)),
            pltpu.SemaphoreType.DMA((16,)),
        ],
        compiler_params=pltpu.CompilerParams(
            collective_id=2, has_side_effects=True, vmem_limit_bytes=62 * MIB
        ),
        name="mid",
    )(
        active, upper_low, second_low, hidden_low, grad_first, embedded, q, k, v, probs, wq, wk, wv, wo,
        kinds, emb_gain,
    )


def flipped(index, bits):
    out = 0
    for place in range(3):
        bit = lax.rem(lax.div(index, 1 << place), 2)
        out = out + (1 << place) * (1 - bit if (bits >> place) & 1 else bit)
    return out


ORDER = (6, 7, 4, 5, 2, 3, 1)


def tail_kernel(
    slots, asked, pos, feed_sums, up_sums, mid_sums, raw, normed, mixed, gfirst, dq, dk, dv, feed_own, up_part,
    word, packed, feed_out, up_out, small_out,
    tok, hot, og, inc, rhs, kinds, places, total, dense, ops, turned, wbuf, wcore, w1a, w1b, w2a, w2b, wz, wown, uz, uown, small_by, small_in, small_dp,
    load_sem, t_send, t_recv, z_send, z_recv, d_send, d_recv, w_send, w_recv, s_send, s_recv, own_sem,
):
    chunks, owners, sources, pairs, lanes = og.shape
    half, width = pos.shape
    tokens = 2 * half
    cap = 2 * pairs
    tall = dense.shape[1]
    me = lax.axis_index("vocab")
    spot = lax.axis_index("dp")
    core, place = lax.rem(me, 2), lax.div(me, 2)
    xb, yb = lax.rem(spot, 2), lax.div(spot, 2)
    across_x = {"dp": spot + 1 - 2 * xb}
    across_y = {"dp": spot + 2 - 4 * yb}

    barrier = pltpu.get_barrier_semaphore()
    for k in ORDER:
        pl.semaphore_signal(barrier, inc=1, device_id={"vocab": flipped(me, k)}, device_id_type=MESH)
    for k in (1, 2, 3):
        pl.semaphore_signal(barrier, inc=1, device_id={"dp": flipped(spot, k)}, device_id_type=MESH)
    loads = [
        pltpu.make_async_copy(ref, ops.at[i], load_sem.at[i])
        for i, ref in enumerate((normed, dq, dk, dv, mixed, gfirst))
    ]
    for load in loads:
        load.start()
    per = width // owners
    order = ((1, 0), (1, 1), (0, 5), (0, 3), (0, 4), (1, 2), (1, 3), (0, 2), (0, 0), (0, 1), (1, 4), (1, 5))
    for v in range(owners):
        small_by[v] = jnp.zeros(small_by.shape[1:], F32)
        for i, (which, line) in enumerate(order):
            source = (feed_sums, mid_sums)[which]
            small_by[v, i : i + 1, :per] = source[line : line + 1, v * per : (v + 1) * per]
        for i in range(4):
            at = (4 * v + i) * per
            small_by[v, 12 + i : 13 + i, :per] = up_sums[:, at : at + per]
    pl.semaphore_wait(barrier, len(ORDER) + 3)

    def remote(src, dst, send, recv, peer):
        return pltpu.make_async_remote_copy(
            src_ref=src, dst_ref=dst, send_sem=send, recv_sem=recv, device_id=peer, device_id_type=MESH
        )

    def start(copies):
        for copy in copies:
            copy.start()

    def arrived(copies):
        for copy in copies:
            copy.wait_recv()

    def gone(copies):
        for copy in copies:
            copy.wait_send()

    def token_copy(c, k):
        peer = flipped(spot, k)
        return remote(raw.at[c, peer], tok.at[c, spot], t_send.at[c, k], t_recv.at[c, k], {"dp": peer})

    def token_copies(c):
        return [token_copy(c, k) for k in (1, 2, 3)]

    def token_own(c):
        return pltpu.make_async_copy(raw.at[c, spot], tok.at[c, spot], own_sem.at[c])

    for c in range(chunks):
        start(token_copies(c))
        token_own(c).start()

    def up_copies():
        copies = []
        for k in (3, 2, 1):
            to = flipped(place, k)
            copies.append(
                remote(up_part.at[to], uz.at[k], s_send.at[10 + k], s_recv.at[10 + k], {"vocab": 2 * to + core})
            )
        return copies

    up_own = pltpu.make_async_copy(up_part.at[place], uz.at[0], own_sem.at[14])
    up_own.start()
    start(up_copies())

    def row_copies(c, j):
        source = flipped(spot, j)
        copies = []
        for k in ORDER:
            peer = flipped(me, k)
            copies.append(
                remote(
                    og.at[c, peer, source],
                    inc.at[c, me, source],
                    z_send.at[c, j, k],
                    z_recv.at[c, j, k],
                    {"vocab": peer},
                )
            )
        return copies

    def make_hot(d):
        def one(v, carry):
            wanted = lax.broadcasted_iota(jnp.int32, (cap, half), 0) + v * cap
            for s in range(2):
                hit = wanted == slots[d, :, s * half : (s + 1) * half]
                hot[d, s, v] = jnp.where(hit, 1.0, 0.0).astype(BF)
            return carry

        lax.fori_loop(0, owners, one, 0)

    def fill(d, first, count):
        lane = lax.broadcasted_iota(jnp.int32, (pairs, lanes), 1)
        values = jnp.concatenate([tok[first + i, d] for i in range(count)], 1)
        early = dot_nn(hot[d, 0].reshape(owners * cap, half), values)
        late = dot_nn(hot[d, 1].reshape(owners * cap, half), values)
        for v in range(owners):
            low, high = slice(v * cap, v * cap + pairs), slice(v * cap + pairs, (v + 1) * cap)
            for i in range(count):
                there = slice(i * lanes, (i + 1) * lanes)
                straight = jnp.where(lane < 64, early[low, there], late[high, there])
                crossed = jnp.where(lane < 64, early[high, there], late[low, there])
                og[first + i, v, d] = (straight + pltpu.roll(crossed, 64, 1)).astype(BF)

    def own_copy(c):
        return pltpu.make_async_copy(og.at[c, me], inc.at[c, me], own_sem.at[11 + c])

    def fill_first(j):
        d = flipped(spot, j)
        make_hot(d)
        if j == 0:
            token_own(0).wait()
        else:
            token_copy(0, j).wait_recv()
        fill(d, 0, 1)
        start(row_copies(0, j))

    depth = 1024

    def sort_rows():
        for v in range(owners):
            lines = []
            for d in range(sources):
                for h in range(2):
                    ids = asked[d, v, :, h * pairs : (h + 1) * pairs]
                    kind = sum(jnp.where(ids >= n * tall, 1, 0) for n in (1, 2, 3))
                    places[h, :, pl.ds((v * sources + d) * pairs, pairs)] = ids - tall * kind
                    lines.append(kind)
            kinds[v] = jnp.concatenate(lines, 0).astype(F32).T.astype(jnp.int32)

    def prepare(c):
        def one(v, carry):
            lane = lax.broadcasted_iota(jnp.int32, (pairs, lanes), 1)
            side = jnp.where(lane < 64, 0, 1)
            for d in range(sources):
                at = pl.ds(pl.multiple_of((v * sources + d) * pairs, pairs), pairs)
                straight = inc[c, v, d].astype(F32)
                crossed = pltpu.roll(straight, 64, 1)
                for h in range(2):
                    kind = kinds[v, :, 2 * d + h : 2 * d + h + 1] - side
                    twice = jnp.where(lane < 64, crossed if h else straight, straight if h else crossed)
                    rhs[h, at, :lanes] = jnp.where(kind == 0, twice, 0.0).astype(BF)
                    rhs[h, at, lanes:] = jnp.where(kind == 2, twice, 0.0).astype(BF)
            return carry

        lax.fori_loop(0, owners, one, 0)

    def gather_rows(c, p):
        tile = tall // 2
        blocks = owners * sources * pairs // depth
        total[...] = jnp.zeros_like(total)

        def one(n, carry):
            h, b = lax.div(n, blocks), lax.rem(n, blocks)
            at = pl.ds(pl.multiple_of(b * depth, depth), depth)
            ids = places[h, :, at] - p * tile
            hit = lax.broadcasted_iota(jnp.int32, (tile, depth), 0) == ids
            total[...] += dot_nn(jnp.where(hit, 1.0, 0.0).astype(BF), rhs[h, at, :])
            return carry

        lax.fori_loop(0, 2 * blocks, one, 0)
        dense[c, pl.ds(p * tile, tile), :] = total[...].astype(BF)

    part = tall // 2

    def lines_of(p):
        return pl.ds(p * part, part)

    def keep_copy(c, p):
        return pltpu.make_async_copy(
            dense.at[c, lines_of(p)], word.at[c, spot, lines_of(p)], own_sem.at[3 + 2 * c + p]
        )

    def near_copies(c, p):
        return [
            remote(
                dense.at[c, lines_of(p)], word.at[c, spot, lines_of(p)], d_send.at[c, 2 * p], d_recv.at[c, 2 * p], across_x
            ),
            remote(
                dense.at[c, lines_of(p)],
                word.at[c, spot, lines_of(p)],
                d_send.at[c, 2 * p + 1],
                d_recv.at[c, 2 * p + 1],
                across_y,
            ),
        ]

    def far_copy(c, p):
        source = flipped(spot, 1) if p == 0 else flipped(spot, 2)
        view = word.at[c, source, lines_of(p)]
        return remote(view, view, d_send.at[c, 4 + p], d_recv.at[c, 4 + p], across_y if p == 0 else across_x)

    corner = 256
    block = 384
    quarter = wown.shape[0]

    def turn(which):
        def one(i, carry):
            at = pl.ds(pl.multiple_of(i * corner, corner), corner)
            for j in range(width // corner):
                there = pl.ds(j * corner, corner)
                turned[there, at] = ops[which, at, there].T
            return carry

        lax.fori_loop(0, tokens // corner, one, 0)

    def weight(which, at):
        def one(n, carry):
            there = pl.ds(pl.multiple_of(n * block, block), block)
            out = dot_nn(turned[...], ops[which, :, there]).astype(BF)
            for v in range(owners):
                wbuf[v // 2, v % 2, pl.ds(at * per, per), there] = out[v * per : (v + 1) * per]
            return carry

        lax.fori_loop(0, width // block, one, 0)

    core_copy = remote(wbuf.at[:, 1 - core], wcore, w_send.at[0], w_recv.at[0], {"vocab": flipped(me, 1)})

    def wide(b):
        return pl.ds(pl.multiple_of(b * 2 * quarter, quarter), 2 * quarter)

    def narrow(b, c):
        return pl.ds(pl.multiple_of((2 * b + c) * quarter, quarter), quarter)

    def add(view, value):
        view[...] = (view[...].astype(F32) + value.astype(F32)).astype(BF)

    def core_step():
        core_copy.wait_recv()

        def one(i, carry):
            z = lax.div(i, 4)
            at = pl.ds(pl.multiple_of(lax.rem(i, 4) * quarter, quarter), quarter)
            add(wbuf.at[z, core, at, :], wcore[z, at, :])
            return carry

        lax.fori_loop(0, 16, one, 0)

    def first_weights():
        return [
            remote(wbuf.at[pl.ds(0, 2), core, wide(1 - xb), :], w1a, w_send.at[1], w_recv.at[1], across_x),
            remote(wbuf.at[pl.ds(2, 2), core, wide(1 - yb), :], w1b, w_send.at[2], w_recv.at[2], across_y),
        ]

    def second_weights():
        return [
            remote(wbuf.at[pl.ds(0, 2), core, narrow(xb, 1 - yb), :], w2a, w_send.at[3], w_recv.at[3], across_y),
            remote(wbuf.at[pl.ds(2, 2), core, narrow(yb, 1 - xb), :], w2b, w_send.at[4], w_recv.at[4], across_x),
        ]

    def first_step():
        arrived(first_weights())
        for z in range(2):
            add(wbuf.at[z, core, wide(xb), :], w1a[z])
            add(wbuf.at[2 + z, core, wide(yb), :], w1b[z])

    def second_step():
        arrived(second_weights())
        for z in range(2):
            add(wbuf.at[z, core, narrow(xb, yb), :], w2a[z])
            add(wbuf.at[2 + z, core, narrow(yb, xb), :], w2b[z])

    def owned(z):
        at = 2 * xb + yb + lax.div(z, 2) * (yb - xb)
        return wbuf.at[z, core, pl.ds(pl.multiple_of(at * quarter, quarter), quarter), :]

    def third_weights():
        copies = []
        for k in (3, 2, 1):
            to = flipped(place, k)
            copies.append(
                remote(owned(to), wz.at[k - 1], w_send.at[4 + k], w_recv.at[4 + k], {"vocab": 2 * to + core})
            )
        return copies

    def third_step():
        arrived(third_weights())
        total = owned(place)[...].astype(F32)
        for k in range(3):
            total = total + wz[k].astype(F32)
        wown[...] = total.astype(BF)

    def spread(own, target, at):
        wide_half = width // 2
        left, right = pl.ds(0, wide_half), pl.ds(wide_half, wide_half)
        kept = pltpu.make_async_copy(own, target.at[xb, yb], own_sem.at[(9, 10, 15)[at]])
        sems = [(w_send.at[8 + 4 * at + i], w_recv.at[8 + 4 * at + i]) for i in range(4)]
        near = [
            remote(own, target.at[xb, yb], *sems[0], across_x),
            remote(own, target.at[xb, yb], *sems[1], across_y),
        ]
        from_x, from_y = target.at[1 - xb, yb, :, left], target.at[xb, 1 - yb, :, right]
        far = [remote(from_x, from_x, *sems[2], across_y), remote(from_y, from_y, *sems[3], across_x)]
        return kept, near, far

    feed_kept, feed_near, feed_far = spread(feed_own, feed_out, 0)
    kept, fourth_weights, fifth_weights = spread(wown, packed, 1)
    up_kept, up_near, up_far = spread(uown, up_out, 2)

    def small_copies():
        copies = []
        for k in ORDER:
            peer = flipped(me, k)
            copies.append(remote(small_by.at[peer], small_in.at[k], s_send.at[k], s_recv.at[k], {"vocab": peer}))
        return copies

    def small_last():
        return [
            remote(small_in.at[0], small_dp.at[k - 1], s_send.at[7 + k], s_recv.at[7 + k], {"dp": flipped(spot, k)})
            for k in (1, 2, 3)
        ]

    start(small_copies())
    loads[0].wait()
    turn(0)
    for i in range(3):
        loads[1 + i].wait()
        weight(1 + i, i)
    loads[4].wait()
    turn(4)
    loads[5].wait()
    weight(5, 3)
    share = half // owners
    for v in range(owners):
        wbuf[v // 2, v % 2, pl.ds(4 * per, share), :] = pos[pl.ds(v * share, share), :]
    core_copy.start()
    for j in range(sources):
        fill_first(j)
    own_copy(0).start()
    start(feed_near)
    feed_kept.start()
    core_step()
    start(first_weights())
    for c in (1, 2):
        token_own(c).wait()
        arrived(token_copies(c))

    def rest(d, carry):
        fill(d, 1, 2)
        return carry

    lax.fori_loop(0, sources, rest, 0)
    for c in (1, 2):
        own_copy(c).start()
    sort_rows()
    feed_kept.wait()
    arrived(feed_near)
    start(feed_far)
    arrived(small_copies())
    short = small_by[me]
    for k in ORDER:
        short = short + small_in[k]
    small_in[0] = short
    start(small_last())

    def close_chunk(c):
        for j in range(sources):
            arrived(row_copies(c, j))
        own_copy(c).wait()
        if c + 1 < chunks:
            for j in range(sources):
                start(row_copies(c + 1, j))
        else:
            start(third_weights())
        prepare(c)
        for p in range(2):
            gather_rows(c, p)
            start(near_copies(c, p))
            keep_copy(c, p).start()

    def pass_on(c):
        arrived(near_copies(c, 0))
        far_copy(c, 0).start()
        arrived(near_copies(c, 1))
        far_copy(c, 1).start()

    close_chunk(0)
    first_step()
    start(second_weights())
    up_own.wait()
    arrived(up_copies())
    uown[...] = (uz[0].astype(F32) + uz[1].astype(F32) + uz[2].astype(F32) + uz[3].astype(F32)).astype(BF)
    start(up_near)
    up_kept.start()
    pass_on(0)
    up_kept.wait()
    arrived(up_near)
    start(up_far)
    close_chunk(1)
    second_step()
    arrived(small_last())
    short = small_in[0]
    for k in range(3):
        short = short + small_dp[k]
    small_out[...] = short
    pass_on(1)
    close_chunk(2)
    third_step()
    start(fourth_weights)
    kept.start()
    pass_on(2)
    kept.wait()
    arrived(fourth_weights)
    start(fifth_weights)

    for c in range(chunks):
        for p in range(2):
            keep_copy(c, p).wait()
            far_copy(c, p).wait_recv()
    arrived(feed_far)
    arrived(fifth_weights)
    arrived(up_far)
    gone(up_copies())
    gone(up_near)
    gone(up_far)
    core_copy.wait_send()
    gone(small_copies())
    gone(small_last())
    for c in range(chunks):
        gone(token_copies(c))
        for j in range(sources):
            gone(row_copies(c, j))
        for p in range(2):
            gone(near_copies(c, p))
            far_copy(c, p).wait_send()
    for copies in (first_weights(), second_weights(), third_weights(), fourth_weights, fifth_weights, feed_near, feed_far):
        gone(copies)


def tail(
    slots, asked, pos, feed_sums, up_sums, mid_sums, raw, normed, mixed, gfirst, dq, dk, dv, feed_own, up_part, rows_local
):
    half, width = pos.shape
    sources, owners, _, cap = asked.shape
    chunks = raw.shape[0]
    pairs = cap // 2
    tall = rows_local // 4
    lines = 4 * (width // owners) + half // owners
    vmem = pl.BlockSpec(memory_space=pltpu.VMEM)
    hbm = pl.BlockSpec(memory_space=pl.ANY)
    return pl.pallas_call(
        tail_kernel,
        out_shape=(
            jax.ShapeDtypeStruct((chunks, sources, tall, 256), BF),
            jax.ShapeDtypeStruct((2, 2, lines // 4, width), BF),
            jax.ShapeDtypeStruct((2, 2) + feed_own.shape, BF),
            jax.ShapeDtypeStruct((2, 2) + feed_own.shape, BF),
            jax.ShapeDtypeStruct((16, 128), F32),
        ),
        in_specs=[vmem] * 6 + [hbm] * 9,
        out_specs=(hbm, hbm, hbm, hbm, vmem),
        scratch_shapes=[
            pltpu.VMEM((chunks, sources, half, 128), BF),
            pltpu.VMEM((sources, 2, owners, cap, half), BF),
            pltpu.VMEM((chunks, owners, sources, pairs, 128), BF),
            pltpu.VMEM((chunks, owners, sources, pairs, 128), BF),
            pltpu.VMEM((2, owners * sources * pairs, 256), BF),
            pltpu.VMEM((owners, pairs, 2 * sources), jnp.int32),
            pltpu.VMEM((2, 1, owners * sources * pairs), jnp.int32),
            pltpu.VMEM((tall // 2, 256), F32),
            pltpu.VMEM((chunks, tall, 256), BF),
            pltpu.VMEM((6, 2 * half, width), BF),
            pltpu.VMEM((width, 2 * half), BF),
            pltpu.VMEM((4, 2, lines, width), BF),
            pltpu.VMEM((4, lines, width), BF),
            pltpu.VMEM((2, lines // 2, width), BF),
            pltpu.VMEM((2, lines // 2, width), BF),
            pltpu.VMEM((2, lines // 4, width), BF),
            pltpu.VMEM((2, lines // 4, width), BF),
            pltpu.VMEM((3, lines // 4, width), BF),
            pltpu.VMEM((lines // 4, width), BF),
            pltpu.VMEM(up_part.shape, BF),
            pltpu.VMEM(up_part.shape[1:], BF),
            pltpu.VMEM((owners, 16, 128), F32),
            pltpu.VMEM((owners, 16, 128), F32),
            pltpu.VMEM((3, 16, 128), F32),
            pltpu.SemaphoreType.DMA((6,)),
            pltpu.SemaphoreType.DMA((chunks, 4)),
            pltpu.SemaphoreType.DMA((chunks, 4)),
            pltpu.SemaphoreType.DMA((chunks, sources, owners)),
            pltpu.SemaphoreType.DMA((chunks, sources, owners)),
            pltpu.SemaphoreType.DMA((chunks, 6)),
            pltpu.SemaphoreType.DMA((chunks, 6)),
            pltpu.SemaphoreType.DMA((20,)),
            pltpu.SemaphoreType.DMA((20,)),
            pltpu.SemaphoreType.DMA((14,)),
            pltpu.SemaphoreType.DMA((14,)),
            pltpu.SemaphoreType.DMA((16,)),
        ],
        compiler_params=pltpu.CompilerParams(collective_id=1, has_side_effects=True, vmem_limit_bytes=60 * MIB),
        name="tail",
    )(
        slots, asked, pos, feed_sums, up_sums, mid_sums,
        raw, normed, mixed, gfirst, dq, dk, dv, feed_own, up_part,
    )


def fetch_kernel(
    token_ids_in, kinds_in, pos_in, types_in, gain_in, bias_in, table_in,
    embedded_out, normed_out, slots_out, asked_out,
    token_ids, kinds, pos, types, gain, bias, table, request, asked_in, rows_out, rows_in, embedded, normed, column, kind_column,
    load_sem, q_send, q_recv, s_send, s_recv, a_send, a_recv, z_send, z_recv, out_sem,
):
    owners, cap, width = rows_out.shape
    tokens = normed.shape[0]
    rows_local = table.shape[0]
    me = lax.axis_index("vocab")
    spot = lax.axis_index("dp")
    table_copy = pltpu.make_async_copy(table_in, table, load_sem.at[0])
    loads = [
        pltpu.make_async_copy(source, target, load_sem.at[1 + i])
        for i, (source, target) in enumerate(
            (
                (token_ids_in, token_ids),
                (kinds_in, kinds),
                (pos_in, pos),
                (types_in, types),
                (gain_in, gain),
                (bias_in, bias),
            )
        )
    ]
    for load in loads:
        load.start()
    table_copy.start()
    barrier = pltpu.get_barrier_semaphore()
    for k in ORDER:
        pl.semaphore_signal(barrier, inc=1, device_id={"vocab": flipped(me, k)}, device_id_type=MESH)
    for k in (1, 2, 3):
        pl.semaphore_signal(barrier, inc=1, device_id={"dp": flipped(spot, k)}, device_id_type=MESH)

    def remote(src, dst, send, recv, peer):
        return pltpu.make_async_remote_copy(
            src_ref=src, dst_ref=dst, send_sem=send, recv_sem=recv, device_id=peer, device_id_type=MESH
        )

    loads[0].wait()
    ids = jnp.concatenate([token_ids[s : s + 1, :] for s in range(token_ids.shape[0])], 1)
    owner = jnp.zeros(ids.shape, jnp.int32)
    for v in range(1, owners):
        owner = owner + jnp.where(ids >= v * rows_local, 1, 0)
    member = jnp.where(lax.broadcasted_iota(jnp.int32, (owners, tokens), 0) == owner, 1.0, 0.0)
    block = 256
    rank = []
    for n in range(tokens // block):
        before = lax.broadcasted_iota(jnp.int32, (tokens, block), 0) < (
            lax.broadcasted_iota(jnp.int32, (tokens, block), 1) + n * block
        )
        earlier = dot_nn(member.astype(BF), jnp.where(before, 1.0, 0.0).astype(BF))
        rank.append(jnp.sum(earlier * member[:, n * block : (n + 1) * block], 0, keepdims=True))
    slot = owner * cap + jnp.concatenate(rank, 1).astype(jnp.int32)
    local = ids - owner * rows_local
    line = lax.broadcasted_iota(jnp.int32, (8, tokens), 0)
    high = lax.shift_right_logical(local, 6)
    values = jnp.where(line == 0, high, jnp.where(line == 1, local - high * 64, jnp.where(line == 2, 1, 0)))
    values = values.astype(F32).astype(BF)
    slots_out[spot] = slot

    def ask(v, carry):
        wanted = lax.broadcasted_iota(jnp.int32, (cap, tokens), 0) + v * cap
        found = dot_nt(values, jnp.where(wanted == slots_out[spot], 1.0, 0.0).astype(BF))
        number = found[0:1] * 64.0 + found[1:2]
        request[v] = jnp.where(found[2:3] > 0.5, number, -1.0).astype(jnp.int32)
        return carry

    lax.fori_loop(0, owners, ask, 0)
    pl.semaphore_wait(barrier, len(ORDER) + 3)
    asks = []
    for k in ORDER:
        peer = flipped(me, k)
        asks.append(remote(request.at[peer], asked_in.at[me], q_send.at[k], q_recv.at[k], {"vocab": peer}))
    for copy in asks:
        copy.start()
    asked_in[me] = request[me]
    lists = []
    for k in (1, 2, 3):
        peer = {"dp": flipped(spot, k)}
        lists.append(remote(slots_out.at[spot], slots_out.at[spot], s_send.at[k], s_recv.at[k], peer))
    for copy in lists:
        copy.start()
    column[...] = jnp.broadcast_to(slot.astype(F32), (8, tokens)).T[:, 0:1].astype(jnp.int32)
    for load in loads[1:]:
        load.wait()
    column_of(kinds, kind_column)
    half = tokens // 2
    for s in range(2):
        at = pl.ds(s * half, half)
        kind = jnp.where(kind_column[at, :] == 0, types[0:1, :].astype(F32), types[1:2, :].astype(F32))
        embedded[at, :] = pos[...].astype(F32) + kind
    for copy in asks:
        copy.wait_recv()
    asked_out[spot] = asked_in[...]
    for k in (1, 2, 3):
        peer = {"dp": flipped(spot, k)}
        copy = remote(asked_in, asked_out.at[spot], a_send.at[k], a_recv.at[k], peer)
        lists.append(copy)
        copy.start()
    table_copy.wait()

    def find(source):
        asked = jnp.broadcast_to(asked_in[source].astype(F32), (8, cap)).T[:, 0:1]
        depth = rows_local // 3
        total = jnp.zeros((cap, width), F32)
        for n in range(3):
            at = lax.broadcasted_iota(jnp.int32, (cap, depth), 1) + n * depth
            hit = jnp.where(at == asked.astype(jnp.int32), 1.0, 0.0).astype(BF)
            total = total + dot_nn(hit, table[pl.ds(n * depth, depth), :])
        return total.astype(BF)

    def row_copy(peer):
        return remote(rows_out.at[peer], rows_in.at[me], z_send.at[peer], z_recv.at[me], {"vocab": peer})

    def row_arrival(peer):
        return remote(rows_out.at[peer], rows_in.at[peer], z_send.at[peer], z_recv.at[peer], {"vocab": peer})

    core, spot_z = lax.rem(me, 2), lax.div(me, 2)
    side = lax.div(spot_z, 2)

    def answer(i, carry):
        j = lax.div(i, 2)
        to_end = lax.div((1 - j) * (2 - j) * (3 - j), 6)
        to_middle = lax.div(j * (2 - j) * (3 - j), 2)
        to_next = lax.div(j * (j - 1) * (3 - j), 2)
        to_core = lax.div(j * (j - 1) * (j - 2), 6)
        chip = (
            to_end * 3 * (1 - side)
            + to_middle * (2 - side)
            + to_next * (spot_z + 1 - 2 * lax.rem(spot_z, 2))
            + to_core * spot_z
        )
        peer = 2 * chip + lax.rem(i, 2) * (1 - to_core) + (1 - core) * to_core
        rows_out[peer] = find(peer)
        row_copy(peer).start()
        return carry

    lax.fori_loop(0, owners - 1, answer, 0)
    rows_in[me] = find(me)

    def place(source):
        part = 256

        def one(n, carry):
            at = pl.ds(pl.multiple_of(n * part, part), part)
            hit = lax.broadcasted_iota(jnp.int32, (part, cap), 1) + source * cap
            hit = jnp.where(hit == column[at, :], 1.0, 0.0).astype(BF)
            embedded[at, :] += dot_nn(hit, rows_in[source])
            return carry

        lax.fori_loop(0, tokens // part, one, 0)

    place(me)
    for k in (1, 2, 3, 4, 5, 6, 7):
        peer = flipped(me, k)
        row_arrival(peer).wait_recv()
        place(peer)
    part = 128

    def out_copies(n):
        at = pl.ds(n * part, part)
        return [
            pltpu.make_async_copy(embedded.at[at, :], embedded_out.at[at, :], out_sem.at[n, 0]),
            pltpu.make_async_copy(normed.at[at, :], normed_out.at[at, :], out_sem.at[n, 1]),
        ]

    for n in range(tokens // part):
        at = pl.ds(n * part, part)
        unit, _ = stats(embedded[at, :])
        normed[at, :] = unit * gain[...][None] + bias[...][None]
        for copy in out_copies(n):
            copy.start()
    for n in range(tokens // part):
        for copy in out_copies(n):
            copy.wait()
    for copy in lists:
        copy.wait_recv()
        copy.wait_send()
    for copy in asks:
        copy.wait_send()
    for k in ORDER:
        row_copy(flipped(me, k)).wait_send()


def fetch(ids, kinds, table, pos, types, gain, bias, owners):
    tokens = ids.size
    rows_local, width = table.shape
    cap = 2 * tokens // owners
    vmem = pl.BlockSpec(memory_space=pltpu.VMEM)
    hbm = pl.BlockSpec(memory_space=pl.ANY)
    full = jax.ShapeDtypeStruct((tokens, width), F32)
    dma = pltpu.SemaphoreType.DMA
    return pl.pallas_call(
        fetch_kernel,
        out_shape=(
            full,
            full,
            jax.ShapeDtypeStruct((4, 1, tokens), jnp.int32),
            jax.ShapeDtypeStruct((4, owners, 1, cap), jnp.int32),
        ),
        in_specs=[hbm] * 7,
        out_specs=(hbm, hbm, vmem, vmem),
        scratch_shapes=[
            pltpu.VMEM(ids.shape, jnp.int32),
            pltpu.VMEM(ids.shape, jnp.int32),
            pltpu.VMEM(pos.shape, BF),
            pltpu.VMEM(types.shape, BF),
            pltpu.VMEM((width,), F32),
            pltpu.VMEM((width,), F32),
            pltpu.VMEM((rows_local, width), BF),
            pltpu.VMEM((owners, 1, cap), jnp.int32),
            pltpu.VMEM((owners, 1, cap), jnp.int32),
            pltpu.VMEM((owners, cap, width), BF),
            pltpu.VMEM((owners, cap, width), BF),
            pltpu.VMEM((tokens, width), F32),
            pltpu.VMEM((tokens, width), F32),
            pltpu.VMEM((tokens, 1), jnp.int32),
            pltpu.VMEM((tokens, 1), jnp.int32),
            dma((7,)),
            dma((owners,)),
            dma((owners,)),
            dma((4,)),
            dma((4,)),
            dma((4,)),
            dma((4,)),
            dma((owners,)),
            dma((owners,)),
            dma((tokens // 128, 2)),
        ],
        compiler_params=pltpu.CompilerParams(collective_id=3, has_side_effects=True, vmem_limit_bytes=62 * MIB),
        name="fetch",
    )(ids, kinds, pos, types, gain, bias, table)


def finish_kernel(
    near, word_in, packed, feeds, ups, small,
    word, query, keys, values, out, pos, up, down, kinds, up_bias, *vectors,
):
    chunks, sources, part, _ = word_in.shape
    lane = lax.broadcasted_iota(jnp.int32, (part, 128), 1)
    for c in range(chunks):
        for q in range(0, sources, 2):
            at = pl.ds((c * sources + q) * 64, 128)
            for j in range(2):
                there = pl.ds(j * 128, 128)
                one, two = word_in[c, q, :, there].astype(F32), word_in[c, q + 1, :, there].astype(F32)
                word[2 * j, :, at] = jnp.where(lane < 64, one, pltpu.roll(two, 64, 1))
                word[2 * j + 1, :, at] = jnp.where(lane < 64, pltpu.roll(one, 64, 1), two)

    @pl.when(pl.program_id(0) == 0)
    def _():
        n = near[0]
        order = ((0, 0), (1 - n, n), (n, 1 - n), (1, 1))
        per, width = query.shape
        rows = jnp.concatenate([packed[a, b] for a, b in order], 0).astype(F32)
        for i, target in enumerate((query, keys, values, out)):
            target[...] = rows[i * per : (i + 1) * per]
        pos[...] = rows[4 * per :]
        lines = []
        for i, (a, b) in enumerate(order):
            up[:, pl.ds(i * width, width)] = ups[a, b].astype(F32)
            for j in range(2):
                lines.append(feeds[a, b, :, j * 4 * per : (j + 1) * 4 * per])
        down[...] = jnp.concatenate(lines, 0).astype(F32).T
        for i, vector in enumerate(vectors):
            vector[...] = small[i, :per]
        kinds[...] = small[10:12, :per]
        up_bias[...] = jnp.concatenate([small[12 + i : 13 + i, :per] for i in range(4)], 1)[0]


def finish(near, word, packed, feeds, ups, small, rows_local, owners):
    chunks, sources, tall, _ = word.shape
    width = packed.shape[3]
    per = width // owners
    steps = 6
    part = tall // steps
    held = jax.ShapeDtypeStruct((per, width), F32)
    share = packed.shape[2] * 4 - 4 * per
    shapes = [held] * 4 + [
        jax.ShapeDtypeStruct((share, width), F32),
        jax.ShapeDtypeStruct((per, 4 * width), F32),
        jax.ShapeDtypeStruct((4 * per, width), F32),
        jax.ShapeDtypeStruct((2, per), F32),
        jax.ShapeDtypeStruct((4 * per,), F32),
    ] + [jax.ShapeDtypeStruct((per,), F32)] * 10
    results = pl.pallas_call(
        finish_kernel,
        grid_spec=pltpu.PrefetchScalarGridSpec(
            num_scalar_prefetch=1,
            grid=(steps,),
            in_specs=[
                pl.BlockSpec((chunks, sources, part, 256), lambda i, *_: (0, 0, i, 0)),
                fixed(packed.shape),
                fixed(feeds.shape),
                fixed(ups.shape),
                fixed(small.shape),
            ],
            out_specs=[pl.BlockSpec((4, part, width), lambda i, *_: (0, i, 0))] + [fixed(s.shape) for s in shapes],
        ),
        out_shape=[jax.ShapeDtypeStruct((4, tall, width), F32)] + shapes,
        compiler_params=pltpu.CompilerParams(vmem_limit_bytes=62 * MIB),
        name="finish",
    )(near.astype(jnp.int32).reshape(1), word, packed, feeds, ups, small)
    return [results[0].reshape(rows_local, width)] + list(results[1:])


def local(
    token_ids,
    type_ids,
    lengths,
    word_table,
    pos_table,
    token_type_embeddings,
    emb_gain,
    emb_bias,
    query_weight,
    query_bias,
    key_weight,
    value_weight,
    value_bias,
    out_weight,
    out_bias,
    attn_gain,
    attn_bias,
    up_weight,
    up_bias,
    down_weight,
    down_bias,
    final_gain,
    final_bias,
    cotangent,
):
    seq_count, seq_len = token_ids.shape
    tokens = seq_count * seq_len
    width = word_table.shape[1]
    rows_local = word_table.shape[0]
    owners = lax.axis_size("vocab")
    capacity = max(2, 2 * tokens // owners)
    fast = owners == 8 and lax.axis_size("dp") == 4
    if fast:
        embedded, normed, slots, askeds = fetch(
            token_ids, type_ids, word_table, pos_table, token_type_embeddings, emb_gain, emb_bias, owners
        )
    else:
        flat_ids = token_ids.reshape(tokens)
        owner = flat_ids // rows_local
        member = (owner[:, None] == jnp.arange(owners)[None, :]).astype(jnp.int32)
        earlier = jnp.cumsum(member, 0) - member
        rank = jnp.sum(earlier * member, 1)
        slot = owner * capacity + rank
        requests = (
            jnp.full((owners * capacity,), -1, jnp.int32).at[slot].set(flat_ids - owner * rows_local)
        )
        requests = requests.reshape(owners, capacity)
        asked = lax.all_to_all(requests, "vocab", split_axis=0, concat_axis=0, tiled=True)
        valid = asked >= 0
        found = word_table[jnp.maximum(asked, 0)]
        found = jnp.where(valid[..., None], found, jnp.zeros((), jnp.bfloat16))
        returned = lax.all_to_all(found, "vocab", split_axis=0, concat_axis=0, tiled=True)
        word_rows = returned.reshape(owners * capacity, width)[slot]
        kinds = token_type_embeddings.shape[0]
        selection_matrix = (type_ids[..., None] == jnp.arange(kinds)[None, None, :]).astype(jnp.float32)
        type_rows = jnp.einsum(
            "tcr,rb->tcb",
            selection_matrix,
            token_type_embeddings.astype(jnp.float32),
            precision=lax.Precision.HIGHEST,
        )
        embedded = (
            word_rows.reshape(seq_count, seq_len, width).astype(jnp.float32)
            + pos_table.astype(jnp.float32)[None]
            + type_rows
        )
        embedded = embedded.reshape(tokens, width)
        normed = layer_norm(embedded, emb_gain, emb_bias)
    normed_low, query, keys, values, mixed_low, first, probs = attend(
        lengths, normed, query_weight, key_weight, value_weight, out_weight, query_bias, value_bias, out_bias
    )
    encoded, active_low, grad_second_low, hidden_low, grad_upper_low, grad_first, feed_sums, up_sums = feed(
        first,
        cotangent.reshape(tokens, width),
        up_weight,
        down_weight,
        up_bias,
        down_bias,
        attn_gain,
        attn_bias,
        final_gain,
        final_bias,
    )
    grad_final_gain, grad_final_bias, grad_down_bias, grad_attn_gain, grad_attn_bias, grad_out_bias = [
        feed_sums[i] for i in range(6)
    ]
    grad_up_bias = up_sums[0]
    if fast:
        (
            grad_first_low,
            grad_query_low,
            grad_keys_low,
            grad_values_low,
            raw,
            grad_pos,
            feed_own,
            up_part,
            mid_sums,
        ) = mid(
            active_low,
            grad_upper_low,
            grad_second_low,
            hidden_low,
            grad_first,
            embedded,
            query,
            keys,
            values,
            probs,
            query_weight,
            key_weight,
            value_weight,
            out_weight,
            type_ids,
            emb_gain,
        )
    else:
        grad_down = matmul_tn(active_low, grad_second_low)
        grad_up = matmul_tn(hidden_low, grad_upper_low)
        grad_first_low, grad_query_low, grad_keys_low, grad_values_low, embedding_output_gradient, mid_sums = attend_back(
            grad_first,
            embedded,
            type_ids,
            query,
            keys,
            values,
            probs,
            query_weight,
            key_weight,
            value_weight,
            out_weight,
            emb_gain,
        )
        grad_pos = jnp.sum(embedding_output_gradient.astype(jnp.float32).reshape(seq_count, seq_len, width), 0)
    grad_query_bias, grad_value_bias, grad_emb_gain, grad_emb_bias = [mid_sums[i] for i in range(4)]
    token_type_gradient = mid_sums[4:6]
    bf = jnp.bfloat16
    per = width // owners
    small = jnp.stack(
        [
            grad_query_bias,
            grad_value_bias,
            grad_out_bias,
            grad_attn_gain,
            grad_attn_bias,
            grad_emb_gain,
            grad_emb_bias,
            grad_down_bias,
            grad_final_gain,
            grad_final_bias,
            token_type_gradient[0],
            token_type_gradient[1],
        ]
    )
    if fast:
        word_pairs, packed, feeds, ups, small = tail(
            slots,
            askeds,
            grad_pos,
            feed_sums,
            up_sums,
            mid_sums,
            raw,
            normed_low,
            mixed_low,
            grad_first_low,
            grad_query_low,
            grad_keys_low,
            grad_values_low,
            feed_own,
            up_part,
            rows_local,
        )
        near = lax.axis_index("vocab") < owners // 2
        (
            grad_word,
            grad_query_weight,
            grad_key_weight,
            grad_value_weight,
            grad_out_weight,
            grad_pos,
            grad_up,
            grad_down,
            token_type_gradient,
            grad_up_bias,
            *short,
        ) = finish(near, word_pairs, packed, feeds, ups, small, rows_local, owners)
    else:
        grad_down = sum_over_all(grad_down.astype(bf))
        grad_up = sum_over_all(grad_up.astype(bf))
        places = slot[None, :] == jnp.arange(owners * capacity)[:, None]
        outgoing = matmul(
            places.astype(bf), embedding_output_gradient.reshape(tokens, width).astype(bf)
        ).astype(bf)
        hits = (jnp.arange(rows_local)[:, None] == asked.reshape(-1)[None, :]).astype(bf)
        pieces = []
        step = 256
        for start in range(0, width, step):
            incoming = lax.all_to_all(
                outgoing[:, start : start + step].reshape(owners, capacity, step),
                "vocab",
                split_axis=0,
                concat_axis=0,
                tiled=True,
            )
            dense = matmul(hits, incoming.reshape(owners * capacity, step)).astype(bf)
            pieces.append(sum_over_dp(dense))
        grad_word = jnp.concatenate(pieces, 1)
        small = small.reshape(12, owners, per).transpose(1, 0, 2).reshape(owners, 12 * per)
        small = jnp.concatenate([small, grad_up_bias.reshape(owners, 4 * per)], 1)
        wide = 4 * width
        lines = (seq_len // owners) * width // wide
        rest = per // 3 - lines
        small_lines = jnp.pad(small, ((0, 0), (0, rest * wide - 16 * per))).reshape(owners, rest, wide)
        grad_query_weight, grad_key_weight, grad_value_weight = [
            matmul_tn(normed_low, g) for g in (grad_query_low, grad_keys_low, grad_values_low)
        ]
        grad_out_weight = matmul_tn(mixed_low, grad_first_low)
        mixed_grads = jnp.concatenate(
            [grad_query_weight, grad_key_weight, grad_value_weight, grad_out_weight], 1
        ).astype(bf)
        packed = jnp.concatenate(
            [
                mixed_grads.reshape(owners, per, wide),
                grad_pos.astype(bf).reshape(owners, lines, wide),
                small_lines.astype(bf),
            ],
            1,
        )
        packed = sum_over_all(packed.reshape(-1, wide))
        weights = packed[:per]
        grad_query_weight = weights[:, :width]
        grad_key_weight = weights[:, width : 2 * width]
        grad_value_weight = weights[:, 2 * width : 3 * width]
        grad_out_weight = weights[:, 3 * width :]
        grad_pos = packed[per : per + lines].reshape(seq_len // owners, width)
        small = packed[per + lines :].reshape(-1)[: 16 * per].reshape(16, per)
        short = [small[i] for i in range(10)]
        token_type_gradient = small[10:12]
        grad_up_bias = small[12:].reshape(-1)
    (
        grad_query_bias,
        grad_value_bias,
        grad_out_bias,
        grad_attn_gain,
        grad_attn_bias,
        grad_emb_gain,
        grad_emb_bias,
        grad_down_bias,
        grad_final_gain,
        grad_final_bias,
    ) = short
    return (
        encoded.reshape(seq_count, seq_len, width),
        grad_word,
        grad_pos,
        token_type_gradient,
        grad_emb_gain,
        grad_emb_bias,
        grad_query_weight,
        grad_query_bias,
        grad_key_weight,
        grad_value_weight,
        grad_value_bias,
        grad_out_weight,
        grad_out_bias,
        grad_attn_gain,
        grad_attn_bias,
        grad_up,
        grad_up_bias,
        grad_down,
        grad_down_bias,
        grad_final_gain,
        grad_final_bias,
    )


def solution(mesh):
    placed = (
        P(("dp", "vocab"), None),
        P(("dp", "vocab"), None),
        P(("dp", "vocab")),
        P("vocab", None),
        P(),
        P(),
        P(),
        P(),
        P(),
        P(),
        P(),
        P(),
        P(),
        P(),
        P(),
        P(),
        P(),
        P(),
        P(),
        P(),
        P(),
        P(),
        P(),
        P(("dp", "vocab"), None, None),
    )
    return jax.shard_map(
        local,
        mesh=mesh,
        in_specs=placed,
        out_specs=(
            P(("dp", "vocab"), None, None),
            P("vocab", None),
            P("vocab", None),
            P(None, "vocab"),
            P("vocab"),
            P("vocab"),
            P("vocab", None),
            P("vocab"),
            P("vocab", None),
            P("vocab", None),
            P("vocab"),
            P("vocab", None),
            P("vocab"),
            P("vocab"),
            P("vocab"),
            P("vocab", None),
            P("vocab"),
            P("vocab", None),
            P("vocab"),
            P("vocab"),
            P("vocab"),
        ),
        check_vma=False,
    )
```

```python
from functools import partial

import jax
import jax.numpy as jnp
from jax import lax
from jax.experimental import pallas as pl
from jax.experimental.pallas import tpu as pltpu
from jax.sharding import PartitionSpec as P

HEADS = 12
HEAD = 64
L = 512


EPSILON = 1e-12


def layer_norm(values, gain, bias):
    center = values - jnp.mean(values, -1, keepdims=True)
    spread = jnp.mean(center * center, -1, keepdims=True)
    return center * lax.rsqrt(spread + EPSILON) * gain + bias


def matmul(left, right):
    return jnp.dot(left, right, preferred_element_type=jnp.float32)


def matmul_tn(left, right):
    return lax.dot_general(
        left, right, (((0,), (0,)), ((), ())), preferred_element_type=jnp.float32
    )


def matmul_nt(left, right):
    return lax.dot_general(
        left, right, (((1,), (1,)), ((), ())), preferred_element_type=jnp.float32
    )


def swap(value, axis_name, bit):
    size = lax.axis_size(axis_name)
    return lax.ppermute(value, axis_name, [(i, i ^ bit) for i in range(size)])


def pick(value, index, axis):
    return lax.dynamic_index_in_dim(value, index, axis, keepdims=False)


def plus(left, right):
    return (left.astype(jnp.float32) + right.astype(jnp.float32)).astype(jnp.bfloat16)


def dp_bits():
    index = lax.axis_index("dp")
    return lax.rem(index, 2), index // 2


def reorder(own, across_x, across_y, across_both):
    xb, yb = dp_bits()
    flip_x, flip_y = xb == 1, yb == 1
    rows = [[own, across_y], [across_x, across_both]]
    rows = [
        [jnp.where(flip_x, rows[1 - i][j], rows[i][j]) for j in range(2)] for i in range(2)
    ]
    rows = [
        [jnp.where(flip_y, rows[i][1 - j], rows[i][j]) for j in range(2)] for i in range(2)
    ]
    return rows


def sum_over_all(grad):
    size = lax.axis_size("vocab")
    me = lax.axis_index("vocab")
    core = lax.rem(me, 2)
    place = me // 2
    places = size // 2
    total, n = grad.shape
    r = total // size
    xb, yb = dp_bits()
    grad = grad.reshape(places, 2, r, n)
    other = swap(pick(grad, 1 - core, 1), "vocab", 1)
    held = plus(pick(grad, core, 1), other).reshape(places, 2, 2, r // 4, n)
    first, last = held[: places // 2], held[places // 2 :]
    first_in = swap(pick(first, 1 - xb, 1), "dp", 1)
    last_in = swap(pick(last, 1 - yb, 2), "dp", 2)
    first = plus(pick(first, xb, 1), first_in)
    last = plus(pick(last, yb, 2), last_in)
    first_in = swap(pick(first, 1 - yb, 1), "dp", 2)
    last_in = swap(pick(last, 1 - xb, 1), "dp", 1)
    first = plus(pick(first, yb, 1), first_in)
    last = plus(pick(last, xb, 1), last_in)
    held = jnp.concatenate([first, last], 0)
    summed = pick(held, place, 0).astype(jnp.float32)
    for step in range(1, places):
        block = pick(held, lax.rem(place + step, places), 0)
        block = lax.ppermute(
            block, "vocab", [(i, (i + 2 * step) % size) for i in range(size)]
        )
        summed = summed + block.astype(jnp.float32)
    own = summed.astype(jnp.bfloat16)
    across_x = swap(own, "dp", 1)
    across_y = swap(own, "dp", 2)
    half = n // 2
    both = jnp.concatenate(
        [swap(across_x[:, :half], "dp", 2), swap(across_y[:, half:], "dp", 1)], 1
    )
    rows = reorder(own, across_x, across_y, both)
    return jnp.stack([rows[0][0], rows[0][1], rows[1][0], rows[1][1]]).reshape(r, n).astype(jnp.float32)


def sum_over_dp(grad):
    rows, n = grad.shape
    xb, yb = dp_bits()
    held = grad.reshape(2, 2, 2, rows // 8, n)
    first, last = held[0], held[1]
    first_in = swap(pick(first, 1 - xb, 0), "dp", 1)
    last_in = swap(pick(last, 1 - yb, 1), "dp", 2)
    first = plus(pick(first, xb, 0), first_in)
    last = plus(pick(last, yb, 1), last_in)
    first_in = swap(pick(first, 1 - yb, 0), "dp", 2)
    last_in = swap(pick(last, 1 - xb, 0), "dp", 1)
    first = plus(pick(first, yb, 0), first_in)
    last = plus(pick(last, xb, 0), last_in)
    first_x = swap(first, "dp", 1)
    last_y = swap(last, "dp", 2)
    first_y = swap(jnp.stack([first, first_x]), "dp", 2)
    last_x = swap(jnp.stack([last, last_y]), "dp", 1)
    a = reorder(first, first_x, first_y[0], first_y[1])
    b = reorder(last, last_x[0], last_y, last_x[1])
    parts = [p for group in (a, b) for line in group for p in line]
    return jnp.concatenate(parts, 0).astype(jnp.float32)


BF = jnp.bfloat16
F32 = jnp.float32
MIB = 1024 * 1024


def dot_nt(left, right):
    return lax.dot_general(left, right, (((1,), (1,)), ((), ())), preferred_element_type=F32)


def dot_nn(left, right):
    return jnp.dot(left, right, preferred_element_type=F32)


def stats(values):
    center = values - jnp.mean(values, -1, keepdims=True)
    inverse = lax.rsqrt(jnp.mean(center * center, -1, keepdims=True) + EPSILON)
    return center * inverse, inverse


def norm_back(grad, gain, unit, inverse):
    scaled = grad * gain
    return inverse * (
        scaled
        - jnp.mean(scaled, -1, keepdims=True)
        - unit * jnp.mean(scaled * unit, -1, keepdims=True)
    )


def column_sum(values):
    return jnp.sum(values, 0, keepdims=True)


TAIL_SCALE = 0.33
TAIL_TERMS = (
    -0.13534782292195252,
    0.4602463244004558,
    -0.3511662200543899,
    0.4085159085223644,
    0.04721176063633592,
    0.2012267561020528,
    0.1829554472050349,
    0.1863578383326851,
)


def normal_parts(u):
    t = 1.0 / (1.0 + (TAIL_SCALE * 0.5**0.5) * jnp.abs(u))
    poly = TAIL_TERMS[0]
    for term in TAIL_TERMS[1:]:
        poly = poly * t + term
    bell = jnp.exp(u * u * -0.5)
    below = (0.5 * t) * poly * bell
    return jnp.where(u >= 0, 1.0 - below, below), bell * 0.3989422804014327


def attend_kernel(
    lengths, normed_in, wq_in, wk_in, wv_in, wo_in, query_bias_in, value_bias_in, out_bias_in,
    low_out, q_out, k_out, v_out, mixed_out, first_out, probs_out,
    first, low, q, k, v, mixed, weights, query_bias, value_bias, out_bias, probs, bias,
    load, out_sem, probs_sem,
):
    tokens, width = first.shape
    size = probs.shape[2]
    seqs = tokens // size
    tile = 256
    loads = [
        pltpu.make_async_copy(source, target, load.at[i])
        for i, (source, target) in enumerate(
            (
                (normed_in, first),
                (wq_in, weights.at[0]),
                (query_bias_in, query_bias),
                (wk_in, weights.at[1]),
                (wv_in, weights.at[2]),
                (value_bias_in, value_bias),
                (wo_in, weights.at[3]),
                (out_bias_in, out_bias),
            )
        )
    ]
    for copy in loads:
        copy.start()
    for s in range(seqs):
        seen = lax.broadcasted_iota(jnp.int32, (size, 128), 0) < lengths[s]
        bias[s] = jnp.where(seen, 0.0, -1000000000.0)
    loads[0].wait()
    low[...] = first[...].astype(BF)
    outs = [
        pltpu.make_async_copy(source, target, out_sem.at[i])
        for i, (source, target) in enumerate(((low, low_out), (q, q_out), (k, k_out), (v, v_out), (mixed, mixed_out)))
    ]
    outs[0].start()

    def spot(n):
        return pl.ds(pl.multiple_of(n * tile, tile), tile)

    def queries(n, carry):
        at = spot(n)
        q[:, at] = (dot_nn(low[...], weights[0, :, at]) + query_bias[at][None]).astype(BF) * BF(HEAD**-0.5)
        return carry

    def keys(n, carry):
        k[:, spot(n)] = dot_nn(low[...], weights[1, :, spot(n)]).astype(BF)
        return carry

    def values(n, carry):
        at = spot(n)
        v[:, at] = (dot_nn(low[...], weights[2, :, at]) + value_bias[at][None]).astype(BF)
        return carry

    loads[1].wait()
    loads[2].wait()
    lax.fori_loop(0, width // tile, queries, 0)
    outs[1].start()
    loads[3].wait()
    lax.fori_loop(0, width // tile, keys, 0)
    outs[2].start()
    loads[4].wait()
    loads[5].wait()
    lax.fori_loop(0, width // tile, values, 0)
    outs[3].start()
    group = HEADS // 4

    def probs_copy(n):
        slot = lax.rem(n, 2)
        return pltpu.make_async_copy(
            probs.at[slot], probs_out.at[lax.div(n, group), pl.ds(4 * lax.rem(n, group), 4)], probs_sem.at[slot]
        )

    def heads(n, carry):
        @pl.when(n >= 2)
        def _():
            probs_copy(n - 2).wait()

        slot = lax.rem(n, 2)
        s = lax.div(n, group)
        rows = pl.ds(pl.multiple_of(s * size, size), size)
        held = []
        for i in range(2):
            j = 2 * lax.rem(n, group) + i
            at = pl.ds(pl.multiple_of(j * 2 * HEAD, 2 * HEAD), 2 * HEAD)
            q2, k2, turned = q[rows, at], k[rows, at], v[rows, at].T
            lane = lax.broadcasted_iota(jnp.int32, k2.shape, 1)
            for side in range(2):
                mine = (lane >= HEAD) if side else (lane < HEAD)
                held.append((at, turned[side * HEAD : (side + 1) * HEAD], jnp.where(mine, k2, jnp.zeros_like(k2)), q2))
        parts = []
        ahead = dot_nt(held[0][2], held[0][3])
        for i in range(4):
            at, turned, _, _ = held[i]
            scores = ahead + jnp.concatenate([bias[s]] * (size // 128), 1)
            if i < 3:
                ahead = dot_nt(held[i + 1][2], held[i + 1][3])
            expd = jnp.exp(scores - jnp.max(scores, 0, keepdims=True))
            chances = (expd * (1.0 / jnp.sum(expd, 0, keepdims=True))).astype(BF)
            probs[slot, i] = chances
            parts.append(dot_nn(turned, chances))
            if i % 2 == 1:
                mixed[rows, at] = jnp.concatenate(parts[-2:], 0).T.astype(BF)
        probs_copy(n).start()
        return carry

    lax.fori_loop(0, seqs * group, heads, 0)
    outs[4].start()
    loads[6].wait()
    loads[7].wait()

    def first_copy(n):
        return pltpu.make_async_copy(first.at[:, spot(n)], first_out.at[:, spot(n)], out_sem.at[5 + n])

    def close(n, carry):
        at = spot(n)
        first[:, at] += dot_nn(mixed[...], weights[3, :, at]) + out_bias[at][None]
        first_copy(n).start()
        return carry

    lax.fori_loop(0, width // tile, close, 0)
    for copy in outs + [first_copy(n) for n in range(width // tile)]:
        copy.wait()
    for n in (seqs * group - 2, seqs * group - 1):
        probs_copy(n).wait()


def fixed(shape):
    return pl.BlockSpec(shape, lambda i, *_: (0,) * len(shape), pipeline_mode=pl.Buffered(1))


def rows_of(rows, width):
    return pl.BlockSpec((rows, width), lambda i, *_: (i, 0))


def row(vector):
    return vector.reshape(1, -1)


def attend(lengths, normed, wq, wk, wv, wo, query_bias, value_bias, out_bias):
    tokens, width = normed.shape
    seqs = lengths.shape[0]
    size = tokens // seqs
    low = jax.ShapeDtypeStruct((tokens, width), BF)
    hbm = pl.BlockSpec(memory_space=pl.ANY)
    small = pltpu.VMEM((tokens, width), BF)
    vector = pltpu.VMEM((width,), F32)
    return pl.pallas_call(
        attend_kernel,
        in_specs=[pl.BlockSpec(memory_space=pltpu.SMEM)] + [hbm] * 8,
        out_specs=[hbm] * 7,
        out_shape=[low] * 5
        + [jax.ShapeDtypeStruct((tokens, width), F32), jax.ShapeDtypeStruct((seqs, HEADS, size, size), BF)],
        scratch_shapes=[
            pltpu.VMEM((tokens, width), F32),
            small,
            small,
            small,
            small,
            small,
            pltpu.VMEM((4, width, width), BF),
            vector,
            vector,
            vector,
            pltpu.VMEM((2, 4, size, size), BF),
            pltpu.VMEM((seqs, size, 128), F32),
            pltpu.SemaphoreType.DMA((8,)),
            pltpu.SemaphoreType.DMA((5 + width // 256,)),
            pltpu.SemaphoreType.DMA((2,)),
        ],
        compiler_params=pltpu.CompilerParams(vmem_limit_bytes=62 * MIB),
        cost_estimate=pl.CostEstimate(flops=20 * 10**9, bytes_accessed=30 * 10**6, transcendentals=0),
        name="attend",
    )(lengths, normed, wq, wk, wv, wo, query_bias, value_bias, out_bias)


def feed_kernel(
    first, cotangent, up, down, up_bias, down_bias, attn_gain, attn_bias, final_gain, final_bias,
    encoded, active, second_low, hidden_low, upper_low, first_grad, sums, up_sum,
    slope,
):
    width = first.shape[1]
    units = up.shape[1]
    block = 768
    unit, inverse = stats(first[...])
    hidden = unit * attn_gain[...][None] + attn_bias[...][None]
    hidden_low[...] = hidden.astype(BF)
    total = hidden + down_bias[...][None]
    for n in range(units // block):
        at = pl.ds(n * block, block)
        upper = dot_nn(hidden_low[...], up[:, at]) + up_bias[at][None]
        below, density = normal_parts(upper)
        active[:, at] = (upper * below).astype(BF)
        slope[:, at] = below + upper * density
        total = total + dot_nn(active[:, at], down[at, :])
    unit_out, inverse_out = stats(total)
    encoded[...] = unit_out * final_gain[...][None] + final_bias[...][None]
    grad = cotangent[...].astype(F32)
    grad_second = norm_back(grad, final_gain[...][None], unit_out, inverse_out)
    second_low[...] = grad_second.astype(BF)

    @pl.when(pl.program_id(0) == 0)
    def _():
        sums[...] = jnp.zeros_like(sums)
        up_sum[...] = jnp.zeros_like(up_sum)

    sums[0:1, :] += column_sum(grad * unit_out)
    sums[1:2, :] += column_sum(grad)
    sums[2:3, :] += column_sum(grad_second)
    total = grad_second
    for n in range(units // block):
        at = pl.ds(n * block, block)
        grad_upper = dot_nt(second_low[...], down[at, :]) * slope[:, at]
        up_sum[:, at] += column_sum(grad_upper)
        upper_low[:, at] = grad_upper.astype(BF)
        total = total + dot_nt(upper_low[:, at], up[:, at])
    grad_first = norm_back(total, attn_gain[...][None], unit, inverse)
    sums[3:4, :] += column_sum(total * unit)
    sums[4:5, :] += column_sum(total)
    sums[5:6, :] += column_sum(grad_first)
    first_grad[...] = grad_first


def feed(first, cotangent, up, down, up_bias, down_bias, attn_gain, attn_bias, final_gain, final_bias):
    tokens, width = first.shape
    units = up.shape[1]
    tile = 512
    part, wide = rows_of(tile, width), rows_of(tile, units)
    vector = fixed((width,))
    return pl.pallas_call(
        feed_kernel,
        grid=(tokens // tile,),
        in_specs=[part, part, fixed((width, units)), fixed((units, width)), fixed((units,))] + [vector] * 5,
        out_specs=[part, wide, part, part, wide, part, fixed((8, width)), fixed((1, units))],
        out_shape=[
            jax.ShapeDtypeStruct((tokens, width), F32),
            jax.ShapeDtypeStruct((tokens, units), BF),
            jax.ShapeDtypeStruct((tokens, width), BF),
            jax.ShapeDtypeStruct((tokens, width), BF),
            jax.ShapeDtypeStruct((tokens, units), BF),
            jax.ShapeDtypeStruct((tokens, width), F32),
            jax.ShapeDtypeStruct((8, width), F32),
            jax.ShapeDtypeStruct((1, units), F32),
        ],
        scratch_shapes=[pltpu.VMEM((tile, units), F32)],
        compiler_params=pltpu.CompilerParams(vmem_limit_bytes=60 * MIB),
        cost_estimate=pl.CostEstimate(flops=40 * 10**9, bytes_accessed=40 * 10**6, transcendentals=0),
        name="feed",
    )(
        first, cotangent, up, down, up_bias, down_bias, attn_gain, attn_bias, final_gain, final_bias
    )


def attend_back_kernel(
    grad_first, embedded, kinds, q_in, k_in, v_in, probs_in, wq, wk, wv, wo, emb_gain,
    first_low, dq, dk, dv, emb_low, sums,
    grad_mixed, total,
):
    tokens, width = grad_first.shape
    tile = 256

    @pl.when(pl.program_id(0) == 0)
    def _():
        sums[...] = jnp.zeros_like(sums)

    first_low[...] = grad_first[...].astype(BF)

    def open_(n, carry):
        at = pl.ds(pl.multiple_of(n * tile, tile), tile)
        grad_mixed[:, at] = dot_nt(first_low[...], wo[at, :]).astype(BF)
        return carry

    lax.fori_loop(0, width // tile, open_, 0)

    def pair(j, carry):
        at = pl.ds(pl.multiple_of(j * 2 * HEAD, 2 * HEAD), 2 * HEAD)
        q, k, v, grad = q_in[:, at], k_in[:, at], v_in[:, at], grad_mixed[:, at]
        turned = k.T
        lane = lax.broadcasted_iota(jnp.int32, k.shape, 1)
        parts = []
        grad_k = jnp.zeros(k.shape, F32)
        grad_v = jnp.zeros(k.shape, F32)
        for side in range(2):
            mine = (lane >= HEAD) if side else (lane < HEAD)
            none = jnp.zeros_like(k)
            probs = probs_in[0, 2 * j + side]
            grad_probs = dot_nt(jnp.where(mine, v, none), grad)
            grad_v = grad_v + dot_nn(probs, jnp.where(mine, grad, none))
            wide = probs.astype(F32)
            both = wide * grad_probs
            scores = (both - wide * jnp.sum(both, 0, keepdims=True)).astype(BF)
            grad_k = grad_k + dot_nn(scores, jnp.where(mine, q, none))
            parts.append(dot_nn(turned[side * HEAD : (side + 1) * HEAD], scores))
        grad_q = jnp.concatenate(parts, 0).T * HEAD**-0.5
        dq[:, at] = grad_q.astype(BF)
        dk[:, at] = grad_k.astype(BF)
        dv[:, at] = grad_v.astype(BF)
        sums[0:1, at] += column_sum(grad_q)
        sums[1:2, at] += column_sum(grad_v)
        return carry

    lax.fori_loop(0, HEADS // 2, pair, 0)

    def close(n, carry):
        at = pl.ds(pl.multiple_of(n * tile, tile), tile)
        total[:, at] = (
            grad_first[:, at]
            + dot_nt(dq[...], wq[at, :])
            + dot_nt(dk[...], wk[at, :])
            + dot_nt(dv[...], wv[at, :])
        )
        return carry

    lax.fori_loop(0, width // tile, close, 0)
    rows = 128

    def last(n, carry):
        at = pl.ds(pl.multiple_of(n * rows, rows), rows)
        unit, inverse = stats(embedded[at, :])
        grad = total[at, :]
        grad_emb = norm_back(grad, emb_gain[...], unit, inverse)
        emb_low[at, :] = grad_emb.astype(BF)
        sums[2:3, :] += column_sum(grad * unit)
        sums[3:4, :] += column_sum(grad)
        kind = kinds[at, :]
        for t in range(2):
            sums[4 + t : 5 + t, :] += column_sum(jnp.where(kind == t, grad_emb, 0.0))
        return carry

    lax.fori_loop(0, tokens // rows, last, 0)


def attend_back(grad_first, embedded, kinds, q, k, v, probs, wq, wk, wv, wo, emb_gain):
    tokens, width = grad_first.shape
    seqs, _, size, _ = probs.shape
    part = rows_of(size, width)
    low = jax.ShapeDtypeStruct((tokens, width), BF)
    return pl.pallas_call(
        attend_back_kernel,
        grid=(seqs,),
        in_specs=[part, part, rows_of(size, 1)]
        + [part] * 3
        + [pl.BlockSpec((1, HEADS, size, size), lambda i: (i, 0, 0, 0))]
        + [fixed((width, width))] * 4
        + [fixed((1, width))],
        out_specs=[part] * 5 + [fixed((8, width))],
        out_shape=[low] * 5 + [jax.ShapeDtypeStruct((8, width), F32)],
        scratch_shapes=[pltpu.VMEM((size, width), BF), pltpu.VMEM((size, width), F32)],
        compiler_params=pltpu.CompilerParams(vmem_limit_bytes=60 * MIB),
        cost_estimate=pl.CostEstimate(flops=30 * 10**9, bytes_accessed=40 * 10**6, transcendentals=0),
        name="attend_back",
    )(grad_first, embedded, kinds.reshape(tokens, 1), q, k, v, probs, wq, wk, wv, wo, row(emb_gain))


MESH = pl.DeviceIdType.MESH


def column_of(lines, column):
    count, size = lines.shape
    for s in range(count):
        line = jnp.broadcast_to(lines[s : s + 1, :].astype(F32), (8, size))
        column[pl.ds(s * size, size), :] = line.T[:, 0:1].astype(jnp.int32)


def mid_kernel(
    active, upper_low, second_low, hidden_low, grad_first, embedded, q_in, k_in, v_in, probs_in, wq, wk, wv, wo,
    kinds_in, emb_gain_in,
    first_out, dq_out, dk_out, dv_out, raw_out, pos_out, feed_out, part_out, sums,
    stage, lhs, turned, grads, core_in, in_1a, in_1b, in_2a, in_2b, in_z, kept,
    first, low, grad_mixed, q, k, v, dq, dk, dv, weights, table, raw, pos, probs, kind_column, kinds, emb_gain,
    load, stage_sem, probs_sem, out_sem, send, recv,
):
    tokens, width = lhs.shape
    seqs, size = kinds.shape
    per = grads.shape[3]
    me = lax.axis_index("vocab")
    spot = lax.axis_index("dp")
    core, place = lax.rem(me, 2), lax.div(me, 2)
    xb, yb = lax.rem(spot, 2), lax.div(spot, 2)
    across_x = {"dp": spot + 1 - 2 * xb}
    across_y = {"dp": spot + 2 - 4 * yb}
    partner = {"vocab": me + 1 - 2 * core}
    block = 768
    blocks = active.shape[1] // block

    def stage_copy(source, n):
        at = pl.ds(pl.multiple_of(n * block, block), block)
        slot = lax.rem(n, 2)
        return pltpu.make_async_copy(source.at[:, at], stage.at[slot], stage_sem.at[slot])

    def probs_copy(n):
        group = HEADS // 4
        slot = lax.rem(n, 2)
        return pltpu.make_async_copy(
            probs_in.at[lax.div(n, group), pl.ds(4 * lax.rem(n, group), 4)], probs.at[slot], probs_sem.at[slot]
        )

    second_copy = pltpu.make_async_copy(second_low, lhs, load.at[0])
    hidden_copy = pltpu.make_async_copy(hidden_low, lhs, load.at[1])
    second_copy.start()
    stage_copy(active, 0).start()
    stage_copy(active, 1).start()
    loads = [
        pltpu.make_async_copy(source, target, load.at[2 + i])
        for i, (source, target) in enumerate(
            (
                (grad_first, first),
                (wo, weights.at[3]),
                (q_in, q),
                (k_in, k),
                (v_in, v),
                (wq, weights.at[0]),
                (wk, weights.at[1]),
                (wv, weights.at[2]),
                (embedded, table),
                (kinds_in, kinds),
                (emb_gain_in, emb_gain),
            )
        )
    ]
    barrier = pltpu.get_barrier_semaphore()
    places = [{"vocab": 2 * flipped(place, k) + core} for k in (1, 2, 3)]
    for peer in [partner, across_x, across_y] + places:
        pl.semaphore_signal(barrier, inc=1, device_id=peer, device_id_type=MESH)
    pl.semaphore_wait(barrier, 6)

    def remote(src, dst, at, peer):
        return pltpu.make_async_remote_copy(
            src_ref=src, dst_ref=dst, send_sem=send.at[at], recv_sem=recv.at[at], device_id=peer, device_id_type=MESH
        )

    def columns(n):
        return pl.ds(pl.multiple_of(n * width, width), width)

    def core_copy(g, n):
        if g == 0:
            return remote(grads.at[0, n, 1 - core], core_in.at[0, n], 16 + n, partner)
        return remote(
            grads.at[1, :, 1 - core, :, columns(n)], core_in.at[1, :, :, columns(n)], 20 + n, partner
        )

    half = 2 * width

    def wide(b):
        return pl.ds(pl.multiple_of(b * half, half), half)

    def narrow(b, c):
        return pl.ds(pl.multiple_of(b * half + c * width, width), width)

    def first_copies(g):
        return [
            remote(grads.at[g, pl.ds(0, 2), core, :, wide(1 - xb)], in_1a.at[g], 5 * g + 1, across_x),
            remote(grads.at[g, pl.ds(2, 2), core, :, wide(1 - yb)], in_1b.at[g], 5 * g + 2, across_y),
        ]

    def second_copies(g):
        return [
            remote(grads.at[g, pl.ds(0, 2), core, :, narrow(xb, 1 - yb)], in_2a.at[g], 5 * g + 3, across_y),
            remote(grads.at[g, pl.ds(2, 2), core, :, narrow(yb, 1 - xb)], in_2b.at[g], 5 * g + 4, across_x),
        ]

    def add(view, value):
        view[...] = (view[...].astype(F32) + value.astype(F32)).astype(BF)

    def core_step(g):
        rows = per // 2

        def one(n, carry):
            core_copy(g, n).wait_recv()
            if g == 0:
                for i in range(2):
                    at = pl.ds(i * rows, rows)
                    add(grads.at[0, n, core, at, :], core_in[0, n, at, :])
            else:
                for z in range(4):
                    add(grads.at[1, z, core, :, columns(n)], core_in[1, z, :, columns(n)])
            return carry

        lax.fori_loop(0, 4, one, 0)
        for copy in first_copies(g):
            copy.start()

    def first_step(g):
        for copy in first_copies(g):
            copy.wait_recv()

        def one(z, carry):
            add(grads.at[g, z, core, :, wide(xb)], in_1a[g, z])
            add(grads.at[g, 2 + z, core, :, wide(yb)], in_1b[g, z])
            return carry

        lax.fori_loop(0, 2, one, 0)
        for copy in second_copies(g):
            copy.start()

    def owned(g, z):
        at = 2 * xb + yb + lax.div(z, 2) * (yb - xb)
        return grads.at[g, z, core, :, pl.ds(pl.multiple_of(at * width, width), width)]

    def place_copies(g):
        return [
            remote(owned(g, flipped(place, k)), in_z.at[g, k - 1], 10 + 3 * g + k - 1, places[k - 1]) for k in (3, 2, 1)
        ]

    def place_step(g):
        for copy in place_copies(g):
            copy.wait_recv()
        total = owned(g, place)[...].astype(F32)
        for k in range(3):
            total = total + in_z[g, k].astype(F32)
        kept[g] = total.astype(BF)

    def second_step(g):
        for copy in second_copies(g):
            copy.wait_recv()
        for z in range(2):
            add(grads.at[g, z, core, :, narrow(xb, yb)], in_2a[g, z])
            add(grads.at[g, 2 + z, core, :, narrow(yb, xb)], in_2b[g, z])
        for copy in place_copies(g):
            copy.start()

    corner = 256

    def turn():
        def one(i, carry):
            at = pl.ds(pl.multiple_of(i * corner, corner), corner)
            for j in range(width // corner):
                there = pl.ds(j * corner, corner)
                turned[there, at] = lhs[at, there].T
            return carry

        lax.fori_loop(0, tokens // corner, one, 0)

    second_copy.wait()
    turn()
    hidden_copy.start()
    probs_copy(0).start()
    for copy in loads:
        copy.start()
    share = block // 2

    def down_block(n, carry):
        stage_copy(active, n).wait()
        slot = lax.rem(n, 2)
        for c in range(2):
            out = dot_nn(turned[...], stage[slot, :, c * share : (c + 1) * share]).astype(BF)
            for j in range(8):
                grads[0, n, c, :, j * share : (j + 1) * share] = out[j * per : (j + 1) * per]
        core_copy(0, n).start()

        @pl.when(n < 2)
        def _():
            stage_copy(active, n + 2).start()

        @pl.when(n >= 2)
        def _():
            stage_copy(upper_low, n - 2).start()

        return carry

    lax.fori_loop(0, blocks, down_block, 0)
    core_step(0)
    hidden_copy.wait()
    turn()

    def up_block(n, carry):
        stage_copy(upper_low, n).wait()
        slot = lax.rem(n, 2)
        for c in range(2):
            out = dot_nn(turned[...], stage[slot, :, c * share : (c + 1) * share]).astype(BF)
            at = pl.ds(pl.multiple_of(n * block + c * share, 128), share)
            for j in range(8):
                grads[1, j // 2, j % 2, :, at] = out[j * per : (j + 1) * per]
        core_copy(1, n).start()

        @pl.when(n < 2)
        def _():
            stage_copy(upper_low, n + 2).start()

        return carry

    lax.fori_loop(0, blocks, up_block, 0)
    core_step(1)

    for copy in loads:
        copy.wait()
    sums[...] = jnp.zeros_like(sums)
    low[...] = first[...].astype(BF)
    first_copy = pltpu.make_async_copy(low, first_out, out_sem.at[4])
    first_copy.start()
    tile = 256

    def open_(n, carry):
        at = pl.ds(pl.multiple_of(n * tile, tile), tile)
        grad_mixed[:, at] = dot_nt(low[...], weights[3, at, :]).astype(BF)
        return carry

    lax.fori_loop(0, width // tile, open_, 0)

    def pair(n, slot, i):
        rows = pl.ds(pl.multiple_of(lax.div(n, HEADS // 2) * size, size), size)
        at = pl.ds(pl.multiple_of(lax.rem(n, HEADS // 2) * 2 * HEAD, 2 * HEAD), 2 * HEAD)
        q2, k2, v2, grad = q[rows, at], k[rows, at], v[rows, at], grad_mixed[rows, at]
        across = k2.T
        lane = lax.broadcasted_iota(jnp.int32, k2.shape, 1)
        parts = []
        grad_k = jnp.zeros(k2.shape, F32)
        grad_v = jnp.zeros(k2.shape, F32)
        for side in range(2):
            mine = (lane >= HEAD) if side else (lane < HEAD)
            none = jnp.zeros_like(k2)
            chances = probs[slot, 2 * i + side]
            grad_probs = dot_nt(jnp.where(mine, v2, none), grad)
            grad_v = grad_v + dot_nn(chances, jnp.where(mine, grad, none))
            full = chances.astype(F32)
            both = full * grad_probs
            scores = (both - full * jnp.sum(both, 0, keepdims=True)).astype(BF)
            grad_k = grad_k + dot_nn(scores, jnp.where(mine, q2, none))
            parts.append(dot_nn(across[side * HEAD : (side + 1) * HEAD], scores))
        grad_q = jnp.concatenate(parts, 0).T * HEAD**-0.5
        dq[rows, at] = grad_q.astype(BF)
        dk[rows, at] = grad_k.astype(BF)
        dv[rows, at] = grad_v.astype(BF)
        sums[0:1, at] += column_sum(grad_q)
        sums[1:2, at] += column_sum(grad_v)

    groups = seqs * HEADS // 4

    def pairs(n, carry):
        @pl.when(n + 1 < groups)
        def _():
            probs_copy(n + 1).start()

        probs_copy(n).wait()
        slot = lax.rem(n, 2)
        for i in range(2):
            pair(2 * n + i, slot, i)

        @pl.when(n == 0)
        def _():
            first_step(0)

        @pl.when(n == 3)
        def _():
            second_step(0)
            first_step(1)

        @pl.when(n == 5)
        def _():
            second_step(1)

        return carry

    lax.fori_loop(0, groups, pairs, 0)
    out_copies = [
        pltpu.make_async_copy(source, target, out_sem.at[5 + i])
        for i, (source, target) in enumerate(((dq, dq_out), (dk, dk_out), (dv, dv_out)))
    ]
    for copy in out_copies:
        copy.start()

    def close(n, carry):
        at = pl.ds(pl.multiple_of(n * tile, tile), tile)
        first[:, at] = (
            first[:, at]
            + dot_nt(dq[...], weights[0, at, :])
            + dot_nt(dk[...], weights[1, at, :])
            + dot_nt(dv[...], weights[2, at, :])
        )
        return carry

    lax.fori_loop(0, width // tile, close, 0)
    column_of(kinds, kind_column)
    few = 128
    lane = lax.broadcasted_iota(jnp.int32, (few, 128), 1)

    def back(at):
        unit, inverse = stats(table[at, :])
        grad = first[at, :]
        grad_emb = norm_back(grad, emb_gain[...][None], unit, inverse)
        sums[2:3, :] += column_sum(grad * unit)
        sums[3:4, :] += column_sum(grad)
        kind = kind_column[at, :]
        for t in range(2):
            sums[4 + t : 5 + t, :] += column_sum(jnp.where(kind == t, grad_emb, 0.0))
        return grad_emb

    def last(n, carry):
        at = pl.ds(pl.multiple_of(n * few, few), few)
        left = back(at)
        right = back(pl.ds(pl.multiple_of(size + n * few, few), few))
        pos[at, :] = (left + right).astype(BF)
        for t in range(width // 128):
            one, two = left[:, t * 128 : (t + 1) * 128], right[:, t * 128 : (t + 1) * 128]
            q = 2 * (t % 2)
            raw[t // 2, q, at, :] = jnp.where(lane < 64, one, pltpu.roll(two, 64, 1)).astype(BF)
            raw[t // 2, q + 1, at, :] = jnp.where(lane < 64, pltpu.roll(one, 64, 1), two).astype(BF)
        return carry

    lax.fori_loop(0, size // few, last, 0)
    raw_copy = pltpu.make_async_copy(raw, raw_out, out_sem.at[3])
    raw_copy.start()
    pos_copy = pltpu.make_async_copy(pos, pos_out, out_sem.at[8])
    pos_copy.start()
    place_step(0)
    place_step(1)
    feed_copy = pltpu.make_async_copy(kept.at[0], feed_out, out_sem.at[2])
    feed_copy.start()
    part_copy = pltpu.make_async_copy(kept.at[1], part_out, out_sem.at[0])
    part_copy.start()
    for copy in [first_copy, raw_copy, pos_copy, feed_copy, part_copy] + out_copies:
        copy.wait()
    for g in range(2):
        for copy in [core_copy(g, n) for n in range(4)] + first_copies(g) + second_copies(g) + place_copies(g):
            copy.wait_send()


def mid(
    active, upper_low, second_low, hidden_low, grad_first, embedded, q, k, v, probs, wq, wk, wv, wo, kinds, emb_gain
):
    tokens, width = grad_first.shape
    seqs, heads, size, _ = probs.shape
    units = active.shape[1]
    per = width // 8
    wide = 4 * width
    vmem = pl.BlockSpec(memory_space=pltpu.VMEM)
    hbm = pl.BlockSpec(memory_space=pl.ANY)
    low = jax.ShapeDtypeStruct((tokens, width), BF)
    small = pltpu.VMEM((tokens, width), BF)
    large = pltpu.VMEM((tokens, width), F32)
    return pl.pallas_call(
        mid_kernel,
        out_shape=[low] * 4
        + [
            jax.ShapeDtypeStruct((3, 4, size, 128), BF),
            jax.ShapeDtypeStruct((size, width), BF),
            jax.ShapeDtypeStruct((per, width), BF),
            jax.ShapeDtypeStruct((per, width), BF),
            jax.ShapeDtypeStruct((8, width), F32),
        ],
        in_specs=[hbm] * 16,
        out_specs=[hbm] * 8 + [vmem],
        scratch_shapes=[
            pltpu.VMEM((2, tokens, 768), BF),
            small,
            pltpu.VMEM((width, tokens), BF),
            pltpu.VMEM((2, 4, 2, per, wide), BF),
            pltpu.VMEM((2, 4, per, wide), BF),
            pltpu.VMEM((2, 2, per, wide // 2), BF),
            pltpu.VMEM((2, 2, per, wide // 2), BF),
            pltpu.VMEM((2, 2, per, width), BF),
            pltpu.VMEM((2, 2, per, width), BF),
            pltpu.VMEM((2, 3, per, width), BF),
            pltpu.VMEM((2, per, width), BF),
            large,
            small,
            small,
            small,
            small,
            small,
            small,
            small,
            small,
            pltpu.VMEM((4, width, width), BF),
            large,
            pltpu.VMEM((3, 4, size, 128), BF),
            pltpu.VMEM((size, width), BF),
            pltpu.VMEM((2, 4, size, size), BF),
            pltpu.VMEM((tokens, 1), jnp.int32),
            pltpu.VMEM((seqs, size), jnp.int32),
            pltpu.VMEM((width,), F32),
            pltpu.SemaphoreType.DMA((13,)),
            pltpu.SemaphoreType.DMA((2,)),
            pltpu.SemaphoreType.DMA((2,)),
            pltpu.SemaphoreType.DMA((9,)),
            pltpu.SemaphoreType.DMA((24,)),
            pltpu.SemaphoreType.DMA((24,)),
        ],
        compiler_params=pltpu.CompilerParams(
            collective_id=2, has_side_effects=True, vmem_limit_bytes=62 * MIB
        ),
        name="mid",
    )(
        active, upper_low, second_low, hidden_low, grad_first, embedded, q, k, v, probs, wq, wk, wv, wo,
        kinds, emb_gain,
    )


def flipped(index, bits):
    out = 0
    for place in range(3):
        bit = lax.rem(lax.div(index, 1 << place), 2)
        out = out + (1 << place) * (1 - bit if (bits >> place) & 1 else bit)
    return out


ORDER = (6, 7, 4, 5, 2, 3, 1)


def tail_kernel(
    slots, asked, pos, feed_sums, up_sums, mid_sums, raw, normed, mixed, gfirst, dq, dk, dv, feed_own, up_part,
    word, packed, feed_out, up_out, small_out,
    tok, hot, og, inc, rhs, kinds, places, total, dense, ops, turned, wbuf, wcore, w1a, w1b, w2a, w2b, wz, wown, small_by, small_in, small_dp,
    load_sem, t_send, t_recv, z_send, z_recv, d_send, d_recv, w_send, w_recv, s_send, s_recv, own_sem,
):
    chunks, owners, sources, pairs, lanes = og.shape
    half, width = pos.shape
    tokens = 2 * half
    cap = 2 * pairs
    tall = dense.shape[1]
    me = lax.axis_index("vocab")
    spot = lax.axis_index("dp")
    core, place = lax.rem(me, 2), lax.div(me, 2)
    xb, yb = lax.rem(spot, 2), lax.div(spot, 2)
    across_x = {"dp": spot + 1 - 2 * xb}
    across_y = {"dp": spot + 2 - 4 * yb}

    barrier = pltpu.get_barrier_semaphore()
    for k in ORDER:
        pl.semaphore_signal(barrier, inc=1, device_id={"vocab": flipped(me, k)}, device_id_type=MESH)
    for k in (1, 2, 3):
        pl.semaphore_signal(barrier, inc=1, device_id={"dp": flipped(spot, k)}, device_id_type=MESH)
    loads = [
        pltpu.make_async_copy(ref, ops.at[i], load_sem.at[i])
        for i, ref in enumerate((normed, dq, dk, dv, mixed, gfirst))
    ]
    for load in loads:
        load.start()
    per = width // owners
    order = ((1, 0), (1, 1), (0, 5), (0, 3), (0, 4), (1, 2), (1, 3), (0, 2), (0, 0), (0, 1), (1, 4), (1, 5))
    for v in range(owners):
        small_by[v] = jnp.zeros(small_by.shape[1:], F32)
        for i, (which, line) in enumerate(order):
            source = (feed_sums, mid_sums)[which]
            small_by[v, i : i + 1, :per] = source[line : line + 1, v * per : (v + 1) * per]
        for i in range(4):
            at = (4 * v + i) * per
            small_by[v, 12 + i : 13 + i, :per] = up_sums[:, at : at + per]
    pl.semaphore_wait(barrier, len(ORDER) + 3)

    def remote(src, dst, send, recv, peer):
        return pltpu.make_async_remote_copy(
            src_ref=src, dst_ref=dst, send_sem=send, recv_sem=recv, device_id=peer, device_id_type=MESH
        )

    def start(copies):
        for copy in copies:
            copy.start()

    def arrived(copies):
        for copy in copies:
            copy.wait_recv()

    def gone(copies):
        for copy in copies:
            copy.wait_send()

    def token_copy(c, k):
        peer = flipped(spot, k)
        return remote(raw.at[c, peer], tok.at[c, spot], t_send.at[c, k], t_recv.at[c, k], {"dp": peer})

    def token_copies(c):
        return [token_copy(c, k) for k in (1, 2, 3)]

    def token_own(c):
        return pltpu.make_async_copy(raw.at[c, spot], tok.at[c, spot], own_sem.at[c])

    for c in range(chunks):
        start(token_copies(c))
        token_own(c).start()

    def row_copies(c, j):
        source = flipped(spot, j)
        copies = []
        for k in ORDER:
            peer = flipped(me, k)
            copies.append(
                remote(
                    og.at[c, peer, source],
                    inc.at[c, me, source],
                    z_send.at[c, j, k],
                    z_recv.at[c, j, k],
                    {"vocab": peer},
                )
            )
        return copies

    def make_hot(d):
        def one(v, carry):
            wanted = lax.broadcasted_iota(jnp.int32, (cap, half), 0) + v * cap
            for s in range(2):
                hit = wanted == slots[d, :, s * half : (s + 1) * half]
                hot[d, s, v] = jnp.where(hit, 1.0, 0.0).astype(BF)
            return carry

        lax.fori_loop(0, owners, one, 0)

    def fill(d, first, count):
        lane = lax.broadcasted_iota(jnp.int32, (pairs, lanes), 1)
        values = jnp.concatenate([tok[first + i, d] for i in range(count)], 1)
        early = dot_nn(hot[d, 0].reshape(owners * cap, half), values)
        late = dot_nn(hot[d, 1].reshape(owners * cap, half), values)
        for v in range(owners):
            low, high = slice(v * cap, v * cap + pairs), slice(v * cap + pairs, (v + 1) * cap)
            for i in range(count):
                there = slice(i * lanes, (i + 1) * lanes)
                straight = jnp.where(lane < 64, early[low, there], late[high, there])
                crossed = jnp.where(lane < 64, early[high, there], late[low, there])
                og[first + i, v, d] = (straight + pltpu.roll(crossed, 64, 1)).astype(BF)

    def own_copy(c):
        return pltpu.make_async_copy(og.at[c, me], inc.at[c, me], own_sem.at[11 + c])

    def fill_first(j):
        d = flipped(spot, j)
        make_hot(d)
        if j == 0:
            token_own(0).wait()
        else:
            token_copy(0, j).wait_recv()
        fill(d, 0, 1)
        start(row_copies(0, j))

    depth = 1024

    def sort_rows():
        for v in range(owners):
            lines = []
            for d in range(sources):
                for h in range(2):
                    ids = asked[d, v, :, h * pairs : (h + 1) * pairs]
                    kind = sum(jnp.where(ids >= n * tall, 1, 0) for n in (1, 2, 3))
                    places[h, :, pl.ds((v * sources + d) * pairs, pairs)] = ids - tall * kind
                    lines.append(kind)
            kinds[v] = jnp.concatenate(lines, 0).astype(F32).T.astype(jnp.int32)

    def prepare(c):
        def one(v, carry):
            lane = lax.broadcasted_iota(jnp.int32, (pairs, lanes), 1)
            side = jnp.where(lane < 64, 0, 1)
            for d in range(sources):
                at = pl.ds(pl.multiple_of((v * sources + d) * pairs, pairs), pairs)
                straight = inc[c, v, d].astype(F32)
                crossed = pltpu.roll(straight, 64, 1)
                for h in range(2):
                    kind = kinds[v, :, 2 * d + h : 2 * d + h + 1] - side
                    twice = jnp.where(lane < 64, crossed if h else straight, straight if h else crossed)
                    rhs[h, at, :lanes] = jnp.where(kind == 0, twice, 0.0).astype(BF)
                    rhs[h, at, lanes:] = jnp.where(kind == 2, twice, 0.0).astype(BF)
            return carry

        lax.fori_loop(0, owners, one, 0)

    def gather_rows(c, p):
        tile = tall // 2
        blocks = owners * sources * pairs // depth
        total[...] = jnp.zeros_like(total)

        def one(n, carry):
            h, b = lax.div(n, blocks), lax.rem(n, blocks)
            at = pl.ds(pl.multiple_of(b * depth, depth), depth)
            ids = places[h, :, at] - p * tile
            hit = lax.broadcasted_iota(jnp.int32, (tile, depth), 0) == ids
            total[...] += dot_nn(jnp.where(hit, 1.0, 0.0).astype(BF), rhs[h, at, :])
            return carry

        lax.fori_loop(0, 2 * blocks, one, 0, unroll=2)
        dense[c, pl.ds(p * tile, tile), :] = total[...].astype(BF)

    part = tall // 2

    def lines_of(p):
        return pl.ds(p * part, part)

    def keep_copy(c, p):
        return pltpu.make_async_copy(
            dense.at[c, lines_of(p)], word.at[c, spot, lines_of(p)], own_sem.at[3 + 2 * c + p]
        )

    def near_copies(c, p):
        return [
            remote(
                dense.at[c, lines_of(p)], word.at[c, spot, lines_of(p)], d_send.at[c, 2 * p], d_recv.at[c, 2 * p], across_x
            ),
            remote(
                dense.at[c, lines_of(p)],
                word.at[c, spot, lines_of(p)],
                d_send.at[c, 2 * p + 1],
                d_recv.at[c, 2 * p + 1],
                across_y,
            ),
        ]

    def far_copy(c, p):
        source = flipped(spot, 1) if p == 0 else flipped(spot, 2)
        view = word.at[c, source, lines_of(p)]
        return remote(view, view, d_send.at[c, 4 + p], d_recv.at[c, 4 + p], across_y if p == 0 else across_x)

    corner = 256
    block = 384
    quarter = wown.shape[0]

    def turn(which):
        def one(i, carry):
            at = pl.ds(pl.multiple_of(i * corner, corner), corner)
            for j in range(width // corner):
                there = pl.ds(j * corner, corner)
                turned[there, at] = ops[which, at, there].T
            return carry

        lax.fori_loop(0, tokens // corner, one, 0)

    def weight(which, at):
        def one(n, carry):
            there = pl.ds(pl.multiple_of(n * block, block), block)
            out = dot_nn(turned[...], ops[which, :, there]).astype(BF)
            for v in range(owners):
                wbuf[v // 2, v % 2, pl.ds(at * per, per), there] = out[v * per : (v + 1) * per]
            return carry

        lax.fori_loop(0, width // block, one, 0)

    core_copy = remote(wbuf.at[:, 1 - core], wcore, w_send.at[0], w_recv.at[0], {"vocab": flipped(me, 1)})

    def wide(b):
        return pl.ds(pl.multiple_of(b * 2 * quarter, quarter), 2 * quarter)

    def narrow(b, c):
        return pl.ds(pl.multiple_of((2 * b + c) * quarter, quarter), quarter)

    def add(view, value):
        view[...] = (view[...].astype(F32) + value.astype(F32)).astype(BF)

    def core_step():
        core_copy.wait_recv()

        def one(i, carry):
            z = lax.div(i, 4)
            at = pl.ds(pl.multiple_of(lax.rem(i, 4) * quarter, quarter), quarter)
            add(wbuf.at[z, core, at, :], wcore[z, at, :])
            return carry

        lax.fori_loop(0, 16, one, 0)

    def first_weights():
        return [
            remote(wbuf.at[pl.ds(0, 2), core, wide(1 - xb), :], w1a, w_send.at[1], w_recv.at[1], across_x),
            remote(wbuf.at[pl.ds(2, 2), core, wide(1 - yb), :], w1b, w_send.at[2], w_recv.at[2], across_y),
        ]

    def second_weights():
        return [
            remote(wbuf.at[pl.ds(0, 2), core, narrow(xb, 1 - yb), :], w2a, w_send.at[3], w_recv.at[3], across_y),
            remote(wbuf.at[pl.ds(2, 2), core, narrow(yb, 1 - xb), :], w2b, w_send.at[4], w_recv.at[4], across_x),
        ]

    def first_step():
        arrived(first_weights())
        for z in range(2):
            add(wbuf.at[z, core, wide(xb), :], w1a[z])
            add(wbuf.at[2 + z, core, wide(yb), :], w1b[z])

    def second_step():
        arrived(second_weights())
        for z in range(2):
            add(wbuf.at[z, core, narrow(xb, yb), :], w2a[z])
            add(wbuf.at[2 + z, core, narrow(yb, xb), :], w2b[z])

    def owned(z):
        at = 2 * xb + yb + lax.div(z, 2) * (yb - xb)
        return wbuf.at[z, core, pl.ds(pl.multiple_of(at * quarter, quarter), quarter), :]

    def third_weights():
        copies = []
        for k in (3, 2, 1):
            to = flipped(place, k)
            copies.append(
                remote(owned(to), wz.at[k - 1], w_send.at[4 + k], w_recv.at[4 + k], {"vocab": 2 * to + core})
            )
        return copies

    def third_step():
        arrived(third_weights())
        total = owned(place)[...].astype(F32)
        for k in range(3):
            total = total + wz[k].astype(F32)
        wown[...] = total.astype(BF)

    def spread(own, target, at):
        wide_half = width // 2
        left, right = pl.ds(0, wide_half), pl.ds(wide_half, wide_half)
        kept = pltpu.make_async_copy(own, target.at[xb, yb], own_sem.at[(9, 10, 15)[at]])
        sems = [(w_send.at[8 + 4 * at + i], w_recv.at[8 + 4 * at + i]) for i in range(4)]
        near = [
            remote(own, target.at[xb, yb], *sems[0], across_x),
            remote(own, target.at[xb, yb], *sems[1], across_y),
        ]
        from_x, from_y = target.at[1 - xb, yb, :, left], target.at[xb, 1 - yb, :, right]
        far = [remote(from_x, from_x, *sems[2], across_y), remote(from_y, from_y, *sems[3], across_x)]
        return kept, near, far

    feed_kept, feed_near, feed_far = spread(feed_own, feed_out, 0)
    kept, fourth_weights, fifth_weights = spread(wown, packed, 1)
    up_kept, up_near, up_far = spread(up_part, up_out, 2)

    def small_copies():
        copies = []
        for k in ORDER:
            peer = flipped(me, k)
            copies.append(remote(small_by.at[peer], small_in.at[k], s_send.at[k], s_recv.at[k], {"vocab": peer}))
        return copies

    def small_last():
        return [
            remote(small_in.at[0], small_dp.at[k - 1], s_send.at[7 + k], s_recv.at[7 + k], {"dp": flipped(spot, k)})
            for k in (1, 2, 3)
        ]

    start(small_copies())
    fill_first(0)
    for near, kept_copy in ((feed_near, feed_kept), (up_near, up_kept)):
        start(near)
        kept_copy.start()
    loads[0].wait()
    turn(0)
    for i in range(3):
        loads[1 + i].wait()
        weight(1 + i, i)
    loads[4].wait()
    turn(4)
    loads[5].wait()
    weight(5, 3)
    share = half // owners
    for v in range(owners):
        wbuf[v // 2, v % 2, pl.ds(4 * per, share), :] = pos[pl.ds(v * share, share), :]
    core_copy.start()
    for j in (1, 2, 3):
        fill_first(j)
    own_copy(0).start()
    for near, far, kept_copy in ((feed_near, feed_far, feed_kept), (up_near, up_far, up_kept)):
        kept_copy.wait()
        arrived(near)
        start(far)
    core_step()
    start(first_weights())
    for c in (1, 2):
        token_own(c).wait()
        arrived(token_copies(c))

    def rest(d, carry):
        fill(d, 1, 2)
        return carry

    lax.fori_loop(0, sources, rest, 0)
    for c in (1, 2):
        own_copy(c).start()
    sort_rows()
    arrived(small_copies())
    short = small_by[me]
    for k in ORDER:
        short = short + small_in[k]
    small_in[0] = short
    start(small_last())

    def close_chunk(c):
        for j in range(sources):
            arrived(row_copies(c, j))
        own_copy(c).wait()
        if c + 1 < chunks:
            for j in range(sources):
                start(row_copies(c + 1, j))
        else:
            start(third_weights())
        prepare(c)
        for p in range(2):
            gather_rows(c, p)
            start(near_copies(c, p))
            keep_copy(c, p).start()

    def pass_on(c):
        arrived(near_copies(c, 0))
        far_copy(c, 0).start()
        arrived(near_copies(c, 1))
        far_copy(c, 1).start()

    close_chunk(0)
    first_step()
    start(second_weights())
    pass_on(0)
    close_chunk(1)
    second_step()
    arrived(small_last())
    short = small_in[0]
    for k in range(3):
        short = short + small_dp[k]
    small_out[...] = short
    pass_on(1)
    close_chunk(2)
    third_step()
    start(fourth_weights)
    kept.start()
    pass_on(2)
    kept.wait()
    arrived(fourth_weights)
    start(fifth_weights)

    for c in range(chunks):
        for p in range(2):
            keep_copy(c, p).wait()
            far_copy(c, p).wait_recv()
    arrived(feed_far)
    arrived(fifth_weights)
    arrived(up_far)
    gone(up_near)
    gone(up_far)
    core_copy.wait_send()
    gone(small_copies())
    gone(small_last())
    for c in range(chunks):
        gone(token_copies(c))
        for j in range(sources):
            gone(row_copies(c, j))
        for p in range(2):
            gone(near_copies(c, p))
            far_copy(c, p).wait_send()
    for copies in (first_weights(), second_weights(), third_weights(), fourth_weights, fifth_weights, feed_near, feed_far):
        gone(copies)


def tail(
    slots, asked, pos, feed_sums, up_sums, mid_sums, raw, normed, mixed, gfirst, dq, dk, dv, feed_own, up_part, rows_local
):
    half, width = pos.shape
    sources, owners, _, cap = asked.shape
    chunks = raw.shape[0]
    pairs = cap // 2
    tall = rows_local // 4
    lines = 4 * (width // owners) + half // owners
    vmem = pl.BlockSpec(memory_space=pltpu.VMEM)
    hbm = pl.BlockSpec(memory_space=pl.ANY)
    return pl.pallas_call(
        tail_kernel,
        out_shape=(
            jax.ShapeDtypeStruct((chunks, sources, tall, 256), BF),
            jax.ShapeDtypeStruct((2, 2, lines // 4, width), BF),
            jax.ShapeDtypeStruct((2, 2) + feed_own.shape, BF),
            jax.ShapeDtypeStruct((2, 2) + feed_own.shape, BF),
            jax.ShapeDtypeStruct((16, 128), F32),
        ),
        in_specs=[vmem] * 6 + [hbm] * 9,
        out_specs=(hbm, hbm, hbm, hbm, vmem),
        scratch_shapes=[
            pltpu.VMEM((chunks, sources, half, 128), BF),
            pltpu.VMEM((sources, 2, owners, cap, half), BF),
            pltpu.VMEM((chunks, owners, sources, pairs, 128), BF),
            pltpu.VMEM((chunks, owners, sources, pairs, 128), BF),
            pltpu.VMEM((2, owners * sources * pairs, 256), BF),
            pltpu.VMEM((owners, pairs, 2 * sources), jnp.int32),
            pltpu.VMEM((2, 1, owners * sources * pairs), jnp.int32),
            pltpu.VMEM((tall // 2, 256), F32),
            pltpu.VMEM((chunks, tall, 256), BF),
            pltpu.VMEM((6, 2 * half, width), BF),
            pltpu.VMEM((width, 2 * half), BF),
            pltpu.VMEM((4, 2, lines, width), BF),
            pltpu.VMEM((4, lines, width), BF),
            pltpu.VMEM((2, lines // 2, width), BF),
            pltpu.VMEM((2, lines // 2, width), BF),
            pltpu.VMEM((2, lines // 4, width), BF),
            pltpu.VMEM((2, lines // 4, width), BF),
            pltpu.VMEM((3, lines // 4, width), BF),
            pltpu.VMEM((lines // 4, width), BF),
            pltpu.VMEM((owners, 16, 128), F32),
            pltpu.VMEM((owners, 16, 128), F32),
            pltpu.VMEM((3, 16, 128), F32),
            pltpu.SemaphoreType.DMA((6,)),
            pltpu.SemaphoreType.DMA((chunks, 4)),
            pltpu.SemaphoreType.DMA((chunks, 4)),
            pltpu.SemaphoreType.DMA((chunks, sources, owners)),
            pltpu.SemaphoreType.DMA((chunks, sources, owners)),
            pltpu.SemaphoreType.DMA((chunks, 6)),
            pltpu.SemaphoreType.DMA((chunks, 6)),
            pltpu.SemaphoreType.DMA((20,)),
            pltpu.SemaphoreType.DMA((20,)),
            pltpu.SemaphoreType.DMA((14,)),
            pltpu.SemaphoreType.DMA((14,)),
            pltpu.SemaphoreType.DMA((16,)),
        ],
        compiler_params=pltpu.CompilerParams(collective_id=1, has_side_effects=True, vmem_limit_bytes=60 * MIB),
        name="tail",
    )(
        slots, asked, pos, feed_sums, up_sums, mid_sums,
        raw, normed, mixed, gfirst, dq, dk, dv, feed_own, up_part,
    )


def fetch_kernel(
    token_ids_in, kinds_in, pos_in, types_in, gain_in, bias_in, table_in,
    embedded_out, normed_out, slots_out, asked_out,
    token_ids, kinds, pos, types, gain, bias, table, request, asked_in, rows_out, rows_in, embedded, normed, column, kind_column,
    load_sem, q_send, q_recv, s_send, s_recv, a_send, a_recv, z_send, z_recv, out_sem,
):
    owners, cap, width = rows_out.shape
    tokens = normed.shape[0]
    rows_local = table.shape[0]
    me = lax.axis_index("vocab")
    spot = lax.axis_index("dp")
    table_copy = pltpu.make_async_copy(table_in, table, load_sem.at[0])
    loads = [
        pltpu.make_async_copy(source, target, load_sem.at[1 + i])
        for i, (source, target) in enumerate(
            (
                (token_ids_in, token_ids),
                (kinds_in, kinds),
                (pos_in, pos),
                (types_in, types),
                (gain_in, gain),
                (bias_in, bias),
            )
        )
    ]
    for load in loads:
        load.start()
    table_copy.start()
    barrier = pltpu.get_barrier_semaphore()
    for k in ORDER:
        pl.semaphore_signal(barrier, inc=1, device_id={"vocab": flipped(me, k)}, device_id_type=MESH)
    for k in (1, 2, 3):
        pl.semaphore_signal(barrier, inc=1, device_id={"dp": flipped(spot, k)}, device_id_type=MESH)

    def remote(src, dst, send, recv, peer):
        return pltpu.make_async_remote_copy(
            src_ref=src, dst_ref=dst, send_sem=send, recv_sem=recv, device_id=peer, device_id_type=MESH
        )

    loads[0].wait()
    ids = jnp.concatenate([token_ids[s : s + 1, :] for s in range(token_ids.shape[0])], 1)
    owner = jnp.zeros(ids.shape, jnp.int32)
    for v in range(1, owners):
        owner = owner + jnp.where(ids >= v * rows_local, 1, 0)
    member = jnp.where(lax.broadcasted_iota(jnp.int32, (owners, tokens), 0) == owner, 1.0, 0.0)
    block = 256
    rank = []
    for n in range(tokens // block):
        before = lax.broadcasted_iota(jnp.int32, (tokens, block), 0) < (
            lax.broadcasted_iota(jnp.int32, (tokens, block), 1) + n * block
        )
        earlier = dot_nn(member.astype(BF), jnp.where(before, 1.0, 0.0).astype(BF))
        rank.append(jnp.sum(earlier * member[:, n * block : (n + 1) * block], 0, keepdims=True))
    slot = owner * cap + jnp.concatenate(rank, 1).astype(jnp.int32)
    local = ids - owner * rows_local
    line = lax.broadcasted_iota(jnp.int32, (8, tokens), 0)
    high = lax.shift_right_logical(local, 6)
    values = jnp.where(line == 0, high, jnp.where(line == 1, local - high * 64, jnp.where(line == 2, 1, 0)))
    values = values.astype(F32).astype(BF)
    slots_out[spot] = slot

    def ask(v, carry):
        wanted = lax.broadcasted_iota(jnp.int32, (cap, tokens), 0) + v * cap
        found = dot_nt(values, jnp.where(wanted == slots_out[spot], 1.0, 0.0).astype(BF))
        number = found[0:1] * 64.0 + found[1:2]
        request[v] = jnp.where(found[2:3] > 0.5, number, -1.0).astype(jnp.int32)
        return carry

    lax.fori_loop(0, owners, ask, 0)
    pl.semaphore_wait(barrier, len(ORDER) + 3)
    asks = []
    for k in ORDER:
        peer = flipped(me, k)
        asks.append(remote(request.at[peer], asked_in.at[me], q_send.at[k], q_recv.at[k], {"vocab": peer}))
    for copy in asks:
        copy.start()
    asked_in[me] = request[me]
    lists = []
    for k in (1, 2, 3):
        peer = {"dp": flipped(spot, k)}
        lists.append(remote(slots_out.at[spot], slots_out.at[spot], s_send.at[k], s_recv.at[k], peer))
    for copy in lists:
        copy.start()
    column[...] = jnp.broadcast_to(slot.astype(F32), (8, tokens)).T[:, 0:1].astype(jnp.int32)
    for load in loads[1:]:
        load.wait()
    column_of(kinds, kind_column)
    half = tokens // 2
    for s in range(2):
        at = pl.ds(s * half, half)
        kind = jnp.where(kind_column[at, :] == 0, types[0:1, :].astype(F32), types[1:2, :].astype(F32))
        embedded[at, :] = pos[...].astype(F32) + kind
    for copy in asks:
        copy.wait_recv()
    asked_out[spot] = asked_in[...]
    for k in (1, 2, 3):
        peer = {"dp": flipped(spot, k)}
        copy = remote(asked_in, asked_out.at[spot], a_send.at[k], a_recv.at[k], peer)
        lists.append(copy)
        copy.start()
    table_copy.wait()

    def find(source):
        asked = jnp.broadcast_to(asked_in[source].astype(F32), (8, cap)).T[:, 0:1]
        depth = rows_local // 3
        total = jnp.zeros((cap, width), F32)
        for n in range(3):
            at = lax.broadcasted_iota(jnp.int32, (cap, depth), 1) + n * depth
            hit = jnp.where(at == asked.astype(jnp.int32), 1.0, 0.0).astype(BF)
            total = total + dot_nn(hit, table[pl.ds(n * depth, depth), :])
        return total.astype(BF)

    def row_copy(peer):
        return remote(rows_out.at[peer], rows_in.at[me], z_send.at[peer], z_recv.at[me], {"vocab": peer})

    def row_arrival(peer):
        return remote(rows_out.at[peer], rows_in.at[peer], z_send.at[peer], z_recv.at[peer], {"vocab": peer})

    core, spot_z = lax.rem(me, 2), lax.div(me, 2)
    side = lax.div(spot_z, 2)

    def answer(i, carry):
        j = lax.div(i, 2)
        to_end = lax.div((1 - j) * (2 - j) * (3 - j), 6)
        to_middle = lax.div(j * (2 - j) * (3 - j), 2)
        to_next = lax.div(j * (j - 1) * (3 - j), 2)
        to_core = lax.div(j * (j - 1) * (j - 2), 6)
        chip = (
            to_end * 3 * (1 - side)
            + to_middle * (2 - side)
            + to_next * (spot_z + 1 - 2 * lax.rem(spot_z, 2))
            + to_core * spot_z
        )
        peer = 2 * chip + lax.rem(i, 2) * (1 - to_core) + (1 - core) * to_core
        rows_out[peer] = find(peer)
        row_copy(peer).start()
        return carry

    lax.fori_loop(0, owners - 1, answer, 0)
    rows_in[me] = find(me)

    def place(source):
        part = 256

        def one(n, carry):
            at = pl.ds(pl.multiple_of(n * part, part), part)
            hit = lax.broadcasted_iota(jnp.int32, (part, cap), 1) + source * cap
            hit = jnp.where(hit == column[at, :], 1.0, 0.0).astype(BF)
            embedded[at, :] += dot_nn(hit, rows_in[source])
            return carry

        lax.fori_loop(0, tokens // part, one, 0)

    place(me)
    for k in (1, 2, 3, 4, 5, 6, 7):
        peer = flipped(me, k)
        row_arrival(peer).wait_recv()
        place(peer)
    part = 128

    def out_copies(n):
        at = pl.ds(n * part, part)
        return [
            pltpu.make_async_copy(embedded.at[at, :], embedded_out.at[at, :], out_sem.at[n, 0]),
            pltpu.make_async_copy(normed.at[at, :], normed_out.at[at, :], out_sem.at[n, 1]),
        ]

    for n in range(tokens // part):
        at = pl.ds(n * part, part)
        unit, _ = stats(embedded[at, :])
        normed[at, :] = unit * gain[...][None] + bias[...][None]
        for copy in out_copies(n):
            copy.start()
    for n in range(tokens // part):
        for copy in out_copies(n):
            copy.wait()
    for copy in lists:
        copy.wait_recv()
        copy.wait_send()
    for copy in asks:
        copy.wait_send()
    for k in ORDER:
        row_copy(flipped(me, k)).wait_send()


def fetch(ids, kinds, table, pos, types, gain, bias, owners):
    tokens = ids.size
    rows_local, width = table.shape
    cap = 2 * tokens // owners
    vmem = pl.BlockSpec(memory_space=pltpu.VMEM)
    hbm = pl.BlockSpec(memory_space=pl.ANY)
    full = jax.ShapeDtypeStruct((tokens, width), F32)
    dma = pltpu.SemaphoreType.DMA
    return pl.pallas_call(
        fetch_kernel,
        out_shape=(
            full,
            full,
            jax.ShapeDtypeStruct((4, 1, tokens), jnp.int32),
            jax.ShapeDtypeStruct((4, owners, 1, cap), jnp.int32),
        ),
        in_specs=[hbm] * 7,
        out_specs=(hbm, hbm, vmem, vmem),
        scratch_shapes=[
            pltpu.VMEM(ids.shape, jnp.int32),
            pltpu.VMEM(ids.shape, jnp.int32),
            pltpu.VMEM(pos.shape, BF),
            pltpu.VMEM(types.shape, BF),
            pltpu.VMEM((width,), F32),
            pltpu.VMEM((width,), F32),
            pltpu.VMEM((rows_local, width), BF),
            pltpu.VMEM((owners, 1, cap), jnp.int32),
            pltpu.VMEM((owners, 1, cap), jnp.int32),
            pltpu.VMEM((owners, cap, width), BF),
            pltpu.VMEM((owners, cap, width), BF),
            pltpu.VMEM((tokens, width), F32),
            pltpu.VMEM((tokens, width), F32),
            pltpu.VMEM((tokens, 1), jnp.int32),
            pltpu.VMEM((tokens, 1), jnp.int32),
            dma((7,)),
            dma((owners,)),
            dma((owners,)),
            dma((4,)),
            dma((4,)),
            dma((4,)),
            dma((4,)),
            dma((owners,)),
            dma((owners,)),
            dma((tokens // 128, 2)),
        ],
        compiler_params=pltpu.CompilerParams(collective_id=3, has_side_effects=True, vmem_limit_bytes=62 * MIB),
        name="fetch",
    )(ids, kinds, pos, types, gain, bias, table)


def finish_kernel(
    near, word_in, packed, feeds, ups, small,
    word, query_out, keys_out, values_out, out_out, pos_out, up_out, down_out, kinds, up_bias, *rest,
):
    vectors, (query, keys, values, out, pos, up, down, sem) = rest[:10], rest[10:]
    copies = [
        pltpu.make_async_copy(source, target, sem.at[i])
        for i, (source, target) in enumerate(
            (
                (query, query_out),
                (keys, keys_out),
                (values, values_out),
                (out, out_out),
                (pos, pos_out),
                (up, up_out),
                (down, down_out),
            )
        )
    ]
    chunks, sources, part, _ = word_in.shape
    lane = lax.broadcasted_iota(jnp.int32, (part, 128), 1)
    for c in range(chunks):
        for q in range(0, sources, 2):
            at = pl.ds((c * sources + q) * 64, 128)
            for j in range(2):
                there = pl.ds(j * 128, 128)
                one, two = word_in[c, q, :, there].astype(F32), word_in[c, q + 1, :, there].astype(F32)
                word[2 * j, :, at] = jnp.where(lane < 64, one, pltpu.roll(two, 64, 1))
                word[2 * j + 1, :, at] = jnp.where(lane < 64, pltpu.roll(one, 64, 1), two)

    @pl.when(pl.program_id(0) == 0)
    def _():
        n = near[0]
        order = ((0, 0), (1 - n, n), (n, 1 - n), (1, 1))
        per, width = query.shape
        rows = jnp.concatenate([packed[a, b] for a, b in order], 0).astype(F32)
        for i, target in enumerate((query, keys, values, out)):
            target[...] = rows[i * per : (i + 1) * per]
        pos[...] = rows[4 * per :]
        lines = []
        for i, (a, b) in enumerate(order):
            up[:, pl.ds(i * width, width)] = ups[a, b].astype(F32)
            for j in range(2):
                lines.append(feeds[a, b, :, j * 4 * per : (j + 1) * 4 * per])
        down[...] = jnp.concatenate(lines, 0).astype(F32).T
        for copy in copies:
            copy.start()
        for i, vector in enumerate(vectors):
            vector[...] = small[i, :per]
        kinds[...] = small[10:12, :per]
        up_bias[...] = jnp.concatenate([small[12 + i : 13 + i, :per] for i in range(4)], 1)[0]

    @pl.when(pl.program_id(0) == pl.num_programs(0) - 1)
    def _():
        for copy in copies:
            copy.wait()


def finish(near, word, packed, feeds, ups, small, rows_local, owners):
    chunks, sources, tall, _ = word.shape
    width = packed.shape[3]
    per = width // owners
    steps = 3
    part = tall // steps
    held = jax.ShapeDtypeStruct((per, width), F32)
    share = packed.shape[2] * 4 - 4 * per
    shapes = [held] * 4 + [
        jax.ShapeDtypeStruct((share, width), F32),
        jax.ShapeDtypeStruct((per, 4 * width), F32),
        jax.ShapeDtypeStruct((4 * per, width), F32),
        jax.ShapeDtypeStruct((2, per), F32),
        jax.ShapeDtypeStruct((4 * per,), F32),
    ] + [jax.ShapeDtypeStruct((per,), F32)] * 10
    results = pl.pallas_call(
        finish_kernel,
        grid_spec=pltpu.PrefetchScalarGridSpec(
            num_scalar_prefetch=1,
            grid=(steps,),
            in_specs=[
                pl.BlockSpec((chunks, sources, part, 256), lambda i, *_: (0, 0, i, 0)),
                fixed(packed.shape),
                fixed(feeds.shape),
                fixed(ups.shape),
                fixed(small.shape),
            ],
            out_specs=[pl.BlockSpec((4, part, width), lambda i, *_: (0, i, 0))]
            + [pl.BlockSpec(memory_space=pl.ANY)] * 7
            + [fixed(s.shape) for s in shapes[7:]],
            scratch_shapes=[pltpu.VMEM(s.shape, F32) for s in shapes[:7]] + [pltpu.SemaphoreType.DMA((7,))],
        ),
        out_shape=[jax.ShapeDtypeStruct((4, tall, width), F32)] + shapes,
        compiler_params=pltpu.CompilerParams(vmem_limit_bytes=62 * MIB),
        name="finish",
    )(near.astype(jnp.int32).reshape(1), word, packed, feeds, ups, small)
    return [results[0].reshape(rows_local, width)] + list(results[1:])


def local(
    token_ids,
    type_ids,
    lengths,
    word_table,
    pos_table,
    token_type_embeddings,
    emb_gain,
    emb_bias,
    query_weight,
    query_bias,
    key_weight,
    value_weight,
    value_bias,
    out_weight,
    out_bias,
    attn_gain,
    attn_bias,
    up_weight,
    up_bias,
    down_weight,
    down_bias,
    final_gain,
    final_bias,
    cotangent,
):
    seq_count, seq_len = token_ids.shape
    tokens = seq_count * seq_len
    width = word_table.shape[1]
    rows_local = word_table.shape[0]
    owners = lax.axis_size("vocab")
    capacity = max(2, 2 * tokens // owners)
    fast = owners == 8 and lax.axis_size("dp") == 4
    if fast:
        embedded, normed, slots, askeds = fetch(
            token_ids, type_ids, word_table, pos_table, token_type_embeddings, emb_gain, emb_bias, owners
        )
    else:
        flat_ids = token_ids.reshape(tokens)
        owner = flat_ids // rows_local
        member = (owner[:, None] == jnp.arange(owners)[None, :]).astype(jnp.int32)
        earlier = jnp.cumsum(member, 0) - member
        rank = jnp.sum(earlier * member, 1)
        slot = owner * capacity + rank
        requests = (
            jnp.full((owners * capacity,), -1, jnp.int32).at[slot].set(flat_ids - owner * rows_local)
        )
        requests = requests.reshape(owners, capacity)
        asked = lax.all_to_all(requests, "vocab", split_axis=0, concat_axis=0, tiled=True)
        valid = asked >= 0
        found = word_table[jnp.maximum(asked, 0)]
        found = jnp.where(valid[..., None], found, jnp.zeros((), jnp.bfloat16))
        returned = lax.all_to_all(found, "vocab", split_axis=0, concat_axis=0, tiled=True)
        word_rows = returned.reshape(owners * capacity, width)[slot]
        kinds = token_type_embeddings.shape[0]
        selection_matrix = (type_ids[..., None] == jnp.arange(kinds)[None, None, :]).astype(jnp.float32)
        type_rows = jnp.einsum(
            "tcr,rb->tcb",
            selection_matrix,
            token_type_embeddings.astype(jnp.float32),
            precision=lax.Precision.HIGHEST,
        )
        embedded = (
            word_rows.reshape(seq_count, seq_len, width).astype(jnp.float32)
            + pos_table.astype(jnp.float32)[None]
            + type_rows
        )
        embedded = embedded.reshape(tokens, width)
        normed = layer_norm(embedded, emb_gain, emb_bias)
    normed_low, query, keys, values, mixed_low, first, probs = attend(
        lengths, normed, query_weight, key_weight, value_weight, out_weight, query_bias, value_bias, out_bias
    )
    encoded, active_low, grad_second_low, hidden_low, grad_upper_low, grad_first, feed_sums, up_sums = feed(
        first,
        cotangent.reshape(tokens, width),
        up_weight,
        down_weight,
        up_bias,
        down_bias,
        attn_gain,
        attn_bias,
        final_gain,
        final_bias,
    )
    grad_final_gain, grad_final_bias, grad_down_bias, grad_attn_gain, grad_attn_bias, grad_out_bias = [
        feed_sums[i] for i in range(6)
    ]
    grad_up_bias = up_sums[0]
    if fast:
        (
            grad_first_low,
            grad_query_low,
            grad_keys_low,
            grad_values_low,
            raw,
            grad_pos,
            feed_own,
            up_part,
            mid_sums,
        ) = mid(
            active_low,
            grad_upper_low,
            grad_second_low,
            hidden_low,
            grad_first,
            embedded,
            query,
            keys,
            values,
            probs,
            query_weight,
            key_weight,
            value_weight,
            out_weight,
            type_ids,
            emb_gain,
        )
    else:
        grad_down = matmul_tn(active_low, grad_second_low)
        grad_up = matmul_tn(hidden_low, grad_upper_low)
        grad_first_low, grad_query_low, grad_keys_low, grad_values_low, embedding_output_gradient, mid_sums = attend_back(
            grad_first,
            embedded,
            type_ids,
            query,
            keys,
            values,
            probs,
            query_weight,
            key_weight,
            value_weight,
            out_weight,
            emb_gain,
        )
        grad_pos = jnp.sum(embedding_output_gradient.astype(jnp.float32).reshape(seq_count, seq_len, width), 0)
    grad_query_bias, grad_value_bias, grad_emb_gain, grad_emb_bias = [mid_sums[i] for i in range(4)]
    token_type_gradient = mid_sums[4:6]
    bf = jnp.bfloat16
    per = width // owners
    small = jnp.stack(
        [
            grad_query_bias,
            grad_value_bias,
            grad_out_bias,
            grad_attn_gain,
            grad_attn_bias,
            grad_emb_gain,
            grad_emb_bias,
            grad_down_bias,
            grad_final_gain,
            grad_final_bias,
            token_type_gradient[0],
            token_type_gradient[1],
        ]
    )
    if fast:
        word_pairs, packed, feeds, ups, small = tail(
            slots,
            askeds,
            grad_pos,
            feed_sums,
            up_sums,
            mid_sums,
            raw,
            normed_low,
            mixed_low,
            grad_first_low,
            grad_query_low,
            grad_keys_low,
            grad_values_low,
            feed_own,
            up_part,
            rows_local,
        )
        near = lax.axis_index("vocab") < owners // 2
        (
            grad_word,
            grad_query_weight,
            grad_key_weight,
            grad_value_weight,
            grad_out_weight,
            grad_pos,
            grad_up,
            grad_down,
            token_type_gradient,
            grad_up_bias,
            *short,
        ) = finish(near, word_pairs, packed, feeds, ups, small, rows_local, owners)
    else:
        grad_down = sum_over_all(grad_down.astype(bf))
        grad_up = sum_over_all(grad_up.astype(bf))
        places = slot[None, :] == jnp.arange(owners * capacity)[:, None]
        outgoing = matmul(
            places.astype(bf), embedding_output_gradient.reshape(tokens, width).astype(bf)
        ).astype(bf)
        hits = (jnp.arange(rows_local)[:, None] == asked.reshape(-1)[None, :]).astype(bf)
        pieces = []
        step = 256
        for start in range(0, width, step):
            incoming = lax.all_to_all(
                outgoing[:, start : start + step].reshape(owners, capacity, step),
                "vocab",
                split_axis=0,
                concat_axis=0,
                tiled=True,
            )
            dense = matmul(hits, incoming.reshape(owners * capacity, step)).astype(bf)
            pieces.append(sum_over_dp(dense))
        grad_word = jnp.concatenate(pieces, 1)
        small = small.reshape(12, owners, per).transpose(1, 0, 2).reshape(owners, 12 * per)
        small = jnp.concatenate([small, grad_up_bias.reshape(owners, 4 * per)], 1)
        wide = 4 * width
        lines = (seq_len // owners) * width // wide
        rest = per // 3 - lines
        small_lines = jnp.pad(small, ((0, 0), (0, rest * wide - 16 * per))).reshape(owners, rest, wide)
        grad_query_weight, grad_key_weight, grad_value_weight = [
            matmul_tn(normed_low, g) for g in (grad_query_low, grad_keys_low, grad_values_low)
        ]
        grad_out_weight = matmul_tn(mixed_low, grad_first_low)
        mixed_grads = jnp.concatenate(
            [grad_query_weight, grad_key_weight, grad_value_weight, grad_out_weight], 1
        ).astype(bf)
        packed = jnp.concatenate(
            [
                mixed_grads.reshape(owners, per, wide),
                grad_pos.astype(bf).reshape(owners, lines, wide),
                small_lines.astype(bf),
            ],
            1,
        )
        packed = sum_over_all(packed.reshape(-1, wide))
        weights = packed[:per]
        grad_query_weight = weights[:, :width]
        grad_key_weight = weights[:, width : 2 * width]
        grad_value_weight = weights[:, 2 * width : 3 * width]
        grad_out_weight = weights[:, 3 * width :]
        grad_pos = packed[per : per + lines].reshape(seq_len // owners, width)
        small = packed[per + lines :].reshape(-1)[: 16 * per].reshape(16, per)
        short = [small[i] for i in range(10)]
        token_type_gradient = small[10:12]
        grad_up_bias = small[12:].reshape(-1)
    (
        grad_query_bias,
        grad_value_bias,
        grad_out_bias,
        grad_attn_gain,
        grad_attn_bias,
        grad_emb_gain,
        grad_emb_bias,
        grad_down_bias,
        grad_final_gain,
        grad_final_bias,
    ) = short
    return (
        encoded.reshape(seq_count, seq_len, width),
        grad_word,
        grad_pos,
        token_type_gradient,
        grad_emb_gain,
        grad_emb_bias,
        grad_query_weight,
        grad_query_bias,
        grad_key_weight,
        grad_value_weight,
        grad_value_bias,
        grad_out_weight,
        grad_out_bias,
        grad_attn_gain,
        grad_attn_bias,
        grad_up,
        grad_up_bias,
        grad_down,
        grad_down_bias,
        grad_final_gain,
        grad_final_bias,
    )


def solution(mesh):
    placed = (
        P(("dp", "vocab"), None),
        P(("dp", "vocab"), None),
        P(("dp", "vocab")),
        P("vocab", None),
        P(),
        P(),
        P(),
        P(),
        P(),
        P(),
        P(),
        P(),
        P(),
        P(),
        P(),
        P(),
        P(),
        P(),
        P(),
        P(),
        P(),
        P(),
        P(),
        P(("dp", "vocab"), None, None),
    )
    return jax.shard_map(
        local,
        mesh=mesh,
        in_specs=placed,
        out_specs=(
            P(("dp", "vocab"), None, None),
            P("vocab", None),
            P("vocab", None),
            P(None, "vocab"),
            P("vocab"),
            P("vocab"),
            P("vocab", None),
            P("vocab"),
            P("vocab", None),
            P("vocab", None),
            P("vocab"),
            P("vocab", None),
            P("vocab"),
            P("vocab"),
            P("vocab"),
            P("vocab", None),
            P("vocab"),
            P("vocab", None),
            P("vocab"),
            P("vocab"),
            P("vocab"),
        ),
        check_vma=False,
    )
```

```python
from functools import partial

import jax
import jax.numpy as jnp
from jax import lax
from jax.experimental import pallas as pl
from jax.experimental.pallas import tpu as pltpu
from jax.sharding import PartitionSpec as P

HEADS = 12
HEAD = 64
L = 512


EPSILON = 1e-12


def layer_norm(values, gain, bias):
    center = values - jnp.mean(values, -1, keepdims=True)
    spread = jnp.mean(center * center, -1, keepdims=True)
    return center * lax.rsqrt(spread + EPSILON) * gain + bias


def matmul(left, right):
    return jnp.dot(left, right, preferred_element_type=jnp.float32)


def matmul_tn(left, right):
    return lax.dot_general(
        left, right, (((0,), (0,)), ((), ())), preferred_element_type=jnp.float32
    )


def matmul_nt(left, right):
    return lax.dot_general(
        left, right, (((1,), (1,)), ((), ())), preferred_element_type=jnp.float32
    )


def swap(value, axis_name, bit):
    size = lax.axis_size(axis_name)
    return lax.ppermute(value, axis_name, [(i, i ^ bit) for i in range(size)])


def pick(value, index, axis):
    return lax.dynamic_index_in_dim(value, index, axis, keepdims=False)


def plus(left, right):
    return (left.astype(jnp.float32) + right.astype(jnp.float32)).astype(jnp.bfloat16)


def dp_bits():
    index = lax.axis_index("dp")
    return lax.rem(index, 2), index // 2


def reorder(own, across_x, across_y, across_both):
    xb, yb = dp_bits()
    flip_x, flip_y = xb == 1, yb == 1
    rows = [[own, across_y], [across_x, across_both]]
    rows = [
        [jnp.where(flip_x, rows[1 - i][j], rows[i][j]) for j in range(2)] for i in range(2)
    ]
    rows = [
        [jnp.where(flip_y, rows[i][1 - j], rows[i][j]) for j in range(2)] for i in range(2)
    ]
    return rows


def sum_over_all(grad):
    size = lax.axis_size("vocab")
    me = lax.axis_index("vocab")
    core = lax.rem(me, 2)
    place = me // 2
    places = size // 2
    total, n = grad.shape
    r = total // size
    xb, yb = dp_bits()
    grad = grad.reshape(places, 2, r, n)
    other = swap(pick(grad, 1 - core, 1), "vocab", 1)
    held = plus(pick(grad, core, 1), other).reshape(places, 2, 2, r // 4, n)
    first, last = held[: places // 2], held[places // 2 :]
    first_in = swap(pick(first, 1 - xb, 1), "dp", 1)
    last_in = swap(pick(last, 1 - yb, 2), "dp", 2)
    first = plus(pick(first, xb, 1), first_in)
    last = plus(pick(last, yb, 2), last_in)
    first_in = swap(pick(first, 1 - yb, 1), "dp", 2)
    last_in = swap(pick(last, 1 - xb, 1), "dp", 1)
    first = plus(pick(first, yb, 1), first_in)
    last = plus(pick(last, xb, 1), last_in)
    held = jnp.concatenate([first, last], 0)
    summed = pick(held, place, 0).astype(jnp.float32)
    for step in range(1, places):
        block = pick(held, lax.rem(place + step, places), 0)
        block = lax.ppermute(
            block, "vocab", [(i, (i + 2 * step) % size) for i in range(size)]
        )
        summed = summed + block.astype(jnp.float32)
    own = summed.astype(jnp.bfloat16)
    across_x = swap(own, "dp", 1)
    across_y = swap(own, "dp", 2)
    half = n // 2
    both = jnp.concatenate(
        [swap(across_x[:, :half], "dp", 2), swap(across_y[:, half:], "dp", 1)], 1
    )
    rows = reorder(own, across_x, across_y, both)
    return jnp.stack([rows[0][0], rows[0][1], rows[1][0], rows[1][1]]).reshape(r, n).astype(jnp.float32)


def sum_over_dp(grad):
    rows, n = grad.shape
    xb, yb = dp_bits()
    held = grad.reshape(2, 2, 2, rows // 8, n)
    first, last = held[0], held[1]
    first_in = swap(pick(first, 1 - xb, 0), "dp", 1)
    last_in = swap(pick(last, 1 - yb, 1), "dp", 2)
    first = plus(pick(first, xb, 0), first_in)
    last = plus(pick(last, yb, 1), last_in)
    first_in = swap(pick(first, 1 - yb, 0), "dp", 2)
    last_in = swap(pick(last, 1 - xb, 0), "dp", 1)
    first = plus(pick(first, yb, 0), first_in)
    last = plus(pick(last, xb, 0), last_in)
    first_x = swap(first, "dp", 1)
    last_y = swap(last, "dp", 2)
    first_y = swap(jnp.stack([first, first_x]), "dp", 2)
    last_x = swap(jnp.stack([last, last_y]), "dp", 1)
    a = reorder(first, first_x, first_y[0], first_y[1])
    b = reorder(last, last_x[0], last_y, last_x[1])
    parts = [p for group in (a, b) for line in group for p in line]
    return jnp.concatenate(parts, 0).astype(jnp.float32)


BF = jnp.bfloat16
F32 = jnp.float32
MIB = 1024 * 1024


def dot_nt(left, right):
    return lax.dot_general(left, right, (((1,), (1,)), ((), ())), preferred_element_type=F32)


def dot_nn(left, right):
    return jnp.dot(left, right, preferred_element_type=F32)


def stats(values):
    center = values - jnp.mean(values, -1, keepdims=True)
    inverse = lax.rsqrt(jnp.mean(center * center, -1, keepdims=True) + EPSILON)
    return center * inverse, inverse


def norm_back(grad, gain, unit, inverse):
    scaled = grad * gain
    return inverse * (
        scaled
        - jnp.mean(scaled, -1, keepdims=True)
        - unit * jnp.mean(scaled * unit, -1, keepdims=True)
    )


def column_sum(values):
    return jnp.sum(values, 0, keepdims=True)


TAIL_SCALE = 0.33
TAIL_TERMS = (
    -0.13534782292195252,
    0.4602463244004558,
    -0.3511662200543899,
    0.4085159085223644,
    0.04721176063633592,
    0.2012267561020528,
    0.1829554472050349,
    0.1863578383326851,
)


def normal_parts(u):
    t = 1.0 / (1.0 + (TAIL_SCALE * 0.5**0.5) * jnp.abs(u))
    poly = TAIL_TERMS[0]
    for term in TAIL_TERMS[1:]:
        poly = poly * t + term
    bell = jnp.exp(u * u * -0.5)
    below = (0.5 * t) * poly * bell
    return jnp.where(u >= 0, 1.0 - below, below), bell * 0.3989422804014327


def attend_kernel(
    lengths, normed_in, wq_in, wk_in, wv_in, wo_in, query_bias_in, value_bias_in, out_bias_in,
    low_out, q_out, k_out, v_out, mixed_out, first_out, probs_out,
    first, low, q, k, v, mixed, weights, query_bias, value_bias, out_bias, probs, bias,
    load, out_sem, probs_sem,
):
    tokens, width = first.shape
    size = probs.shape[2]
    seqs = tokens // size
    tile = 256
    loads = [
        pltpu.make_async_copy(source, target, load.at[i])
        for i, (source, target) in enumerate(
            (
                (normed_in, first),
                (wq_in, weights.at[0]),
                (query_bias_in, query_bias),
                (wk_in, weights.at[1]),
                (wv_in, weights.at[2]),
                (value_bias_in, value_bias),
                (wo_in, weights.at[3]),
                (out_bias_in, out_bias),
            )
        )
    ]
    for copy in loads:
        copy.start()
    for s in range(seqs):
        seen = lax.broadcasted_iota(jnp.int32, (size, 128), 0) < lengths[s]
        bias[s] = jnp.where(seen, 0.0, -1000000000.0)
    loads[0].wait()
    low[...] = first[...].astype(BF)
    outs = [
        pltpu.make_async_copy(source, target, out_sem.at[i])
        for i, (source, target) in enumerate(((low, low_out), (q, q_out), (k, k_out), (v, v_out), (mixed, mixed_out)))
    ]
    outs[0].start()

    def spot(n):
        return pl.ds(pl.multiple_of(n * tile, tile), tile)

    def queries(n, carry):
        at = spot(n)
        q[:, at] = (dot_nn(low[...], weights[0, :, at]) + query_bias[at][None]).astype(BF) * BF(HEAD**-0.5)
        return carry

    def keys(n, carry):
        k[:, spot(n)] = dot_nn(low[...], weights[1, :, spot(n)]).astype(BF)
        return carry

    def values(n, carry):
        at = spot(n)
        v[:, at] = (dot_nn(low[...], weights[2, :, at]) + value_bias[at][None]).astype(BF)
        return carry

    loads[1].wait()
    loads[2].wait()
    lax.fori_loop(0, width // tile, queries, 0)
    outs[1].start()
    loads[3].wait()
    lax.fori_loop(0, width // tile, keys, 0)
    outs[2].start()
    loads[4].wait()
    loads[5].wait()
    lax.fori_loop(0, width // tile, values, 0)
    outs[3].start()
    group = HEADS // 4

    def probs_copy(n):
        slot = lax.rem(n, 2)
        return pltpu.make_async_copy(
            probs.at[slot], probs_out.at[lax.div(n, group), pl.ds(4 * lax.rem(n, group), 4)], probs_sem.at[slot]
        )

    def heads(n, carry):
        @pl.when(n >= 2)
        def _():
            probs_copy(n - 2).wait()

        slot = lax.rem(n, 2)
        s = lax.div(n, group)
        rows = pl.ds(pl.multiple_of(s * size, size), size)
        held = []
        for i in range(2):
            j = 2 * lax.rem(n, group) + i
            at = pl.ds(pl.multiple_of(j * 2 * HEAD, 2 * HEAD), 2 * HEAD)
            q2, k2, turned = q[rows, at], k[rows, at], v[rows, at].T
            lane = lax.broadcasted_iota(jnp.int32, k2.shape, 1)
            for side in range(2):
                mine = (lane >= HEAD) if side else (lane < HEAD)
                held.append((at, turned[side * HEAD : (side + 1) * HEAD], jnp.where(mine, k2, jnp.zeros_like(k2)), q2))
        parts = []
        ahead = dot_nt(held[0][2], held[0][3])
        for i in range(4):
            at, turned, _, _ = held[i]
            scores = ahead + jnp.concatenate([bias[s]] * (size // 128), 1)
            if i < 3:
                ahead = dot_nt(held[i + 1][2], held[i + 1][3])
            expd = jnp.exp(scores - jnp.max(scores, 0, keepdims=True))
            chances = (expd * (1.0 / jnp.sum(expd, 0, keepdims=True))).astype(BF)
            probs[slot, i] = chances
            parts.append(dot_nn(turned, chances))
            if i % 2 == 1:
                mixed[rows, at] = jnp.concatenate(parts[-2:], 0).T.astype(BF)
        probs_copy(n).start()
        return carry

    lax.fori_loop(0, seqs * group, heads, 0)
    outs[4].start()
    loads[6].wait()
    loads[7].wait()

    def first_copy(n):
        return pltpu.make_async_copy(first.at[:, spot(n)], first_out.at[:, spot(n)], out_sem.at[5 + n])

    def close(n, carry):
        at = spot(n)
        first[:, at] += dot_nn(mixed[...], weights[3, :, at]) + out_bias[at][None]
        first_copy(n).start()
        return carry

    lax.fori_loop(0, width // tile, close, 0)
    for copy in outs + [first_copy(n) for n in range(width // tile)]:
        copy.wait()
    for n in (seqs * group - 2, seqs * group - 1):
        probs_copy(n).wait()


def fixed(shape):
    return pl.BlockSpec(shape, lambda i, *_: (0,) * len(shape), pipeline_mode=pl.Buffered(1))


def rows_of(rows, width):
    return pl.BlockSpec((rows, width), lambda i, *_: (i, 0))


def row(vector):
    return vector.reshape(1, -1)


def attend(lengths, normed, wq, wk, wv, wo, query_bias, value_bias, out_bias):
    tokens, width = normed.shape
    seqs = lengths.shape[0]
    size = tokens // seqs
    low = jax.ShapeDtypeStruct((tokens, width), BF)
    hbm = pl.BlockSpec(memory_space=pl.ANY)
    small = pltpu.VMEM((tokens, width), BF)
    vector = pltpu.VMEM((width,), F32)
    return pl.pallas_call(
        attend_kernel,
        in_specs=[pl.BlockSpec(memory_space=pltpu.SMEM)] + [hbm] * 8,
        out_specs=[hbm] * 7,
        out_shape=[low] * 5
        + [jax.ShapeDtypeStruct((tokens, width), F32), jax.ShapeDtypeStruct((seqs, HEADS, size, size), BF)],
        scratch_shapes=[
            pltpu.VMEM((tokens, width), F32),
            small,
            small,
            small,
            small,
            small,
            pltpu.VMEM((4, width, width), BF),
            vector,
            vector,
            vector,
            pltpu.VMEM((2, 4, size, size), BF),
            pltpu.VMEM((seqs, size, 128), F32),
            pltpu.SemaphoreType.DMA((8,)),
            pltpu.SemaphoreType.DMA((5 + width // 256,)),
            pltpu.SemaphoreType.DMA((2,)),
        ],
        compiler_params=pltpu.CompilerParams(vmem_limit_bytes=62 * MIB),
        cost_estimate=pl.CostEstimate(flops=20 * 10**9, bytes_accessed=30 * 10**6, transcendentals=0),
        name="attend",
    )(lengths, normed, wq, wk, wv, wo, query_bias, value_bias, out_bias)


def feed_kernel(
    first, cotangent, up, down, up_bias, down_bias, attn_gain, attn_bias, final_gain, final_bias,
    encoded, active, second_low, hidden_low, upper_low, first_grad, sums, up_sum,
    slope,
):
    width = first.shape[1]
    units = up.shape[1]
    block = 768
    unit, inverse = stats(first[...])
    hidden = unit * attn_gain[...][None] + attn_bias[...][None]
    hidden_low[...] = hidden.astype(BF)
    total = hidden + down_bias[...][None]
    for n in range(units // block):
        at = pl.ds(n * block, block)
        upper = dot_nn(hidden_low[...], up[:, at]) + up_bias[at][None]
        below, density = normal_parts(upper)
        active[:, at] = (upper * below).astype(BF)
        slope[:, at] = below + upper * density
        total = total + dot_nn(active[:, at], down[at, :])
    unit_out, inverse_out = stats(total)
    encoded[...] = unit_out * final_gain[...][None] + final_bias[...][None]
    grad = cotangent[...].astype(F32)
    grad_second = norm_back(grad, final_gain[...][None], unit_out, inverse_out)
    second_low[...] = grad_second.astype(BF)

    @pl.when(pl.program_id(0) == 0)
    def _():
        sums[...] = jnp.zeros_like(sums)
        up_sum[...] = jnp.zeros_like(up_sum)

    sums[0:1, :] += column_sum(grad * unit_out)
    sums[1:2, :] += column_sum(grad)
    sums[2:3, :] += column_sum(grad_second)
    total = grad_second
    for n in range(units // block):
        at = pl.ds(n * block, block)
        grad_upper = dot_nt(second_low[...], down[at, :]) * slope[:, at]
        up_sum[:, at] += column_sum(grad_upper)
        upper_low[:, at] = grad_upper.astype(BF)
        total = total + dot_nt(upper_low[:, at], up[:, at])
    grad_first = norm_back(total, attn_gain[...][None], unit, inverse)
    sums[3:4, :] += column_sum(total * unit)
    sums[4:5, :] += column_sum(total)
    sums[5:6, :] += column_sum(grad_first)
    first_grad[...] = grad_first


def feed(first, cotangent, up, down, up_bias, down_bias, attn_gain, attn_bias, final_gain, final_bias):
    tokens, width = first.shape
    units = up.shape[1]
    tile = 512
    part, wide = rows_of(tile, width), rows_of(tile, units)
    vector = fixed((width,))
    return pl.pallas_call(
        feed_kernel,
        grid=(tokens // tile,),
        in_specs=[part, part, fixed((width, units)), fixed((units, width)), fixed((units,))] + [vector] * 5,
        out_specs=[part, wide, part, part, wide, part, fixed((8, width)), fixed((1, units))],
        out_shape=[
            jax.ShapeDtypeStruct((tokens, width), F32),
            jax.ShapeDtypeStruct((tokens, units), BF),
            jax.ShapeDtypeStruct((tokens, width), BF),
            jax.ShapeDtypeStruct((tokens, width), BF),
            jax.ShapeDtypeStruct((tokens, units), BF),
            jax.ShapeDtypeStruct((tokens, width), F32),
            jax.ShapeDtypeStruct((8, width), F32),
            jax.ShapeDtypeStruct((1, units), F32),
        ],
        scratch_shapes=[pltpu.VMEM((tile, units), F32)],
        compiler_params=pltpu.CompilerParams(vmem_limit_bytes=60 * MIB),
        cost_estimate=pl.CostEstimate(flops=40 * 10**9, bytes_accessed=40 * 10**6, transcendentals=0),
        name="feed",
    )(
        first, cotangent, up, down, up_bias, down_bias, attn_gain, attn_bias, final_gain, final_bias
    )


def attend_back_kernel(
    grad_first, embedded, kinds, q_in, k_in, v_in, probs_in, wq, wk, wv, wo, emb_gain,
    first_low, dq, dk, dv, emb_low, sums,
    grad_mixed, total,
):
    tokens, width = grad_first.shape
    tile = 256

    @pl.when(pl.program_id(0) == 0)
    def _():
        sums[...] = jnp.zeros_like(sums)

    first_low[...] = grad_first[...].astype(BF)

    def open_(n, carry):
        at = pl.ds(pl.multiple_of(n * tile, tile), tile)
        grad_mixed[:, at] = dot_nt(first_low[...], wo[at, :]).astype(BF)
        return carry

    lax.fori_loop(0, width // tile, open_, 0)

    def pair(j, carry):
        at = pl.ds(pl.multiple_of(j * 2 * HEAD, 2 * HEAD), 2 * HEAD)
        q, k, v, grad = q_in[:, at], k_in[:, at], v_in[:, at], grad_mixed[:, at]
        turned = k.T
        lane = lax.broadcasted_iota(jnp.int32, k.shape, 1)
        parts = []
        grad_k = jnp.zeros(k.shape, F32)
        grad_v = jnp.zeros(k.shape, F32)
        for side in range(2):
            mine = (lane >= HEAD) if side else (lane < HEAD)
            none = jnp.zeros_like(k)
            probs = probs_in[0, 2 * j + side]
            grad_probs = dot_nt(jnp.where(mine, v, none), grad)
            grad_v = grad_v + dot_nn(probs, jnp.where(mine, grad, none))
            wide = probs.astype(F32)
            both = wide * grad_probs
            scores = (both - wide * jnp.sum(both, 0, keepdims=True)).astype(BF)
            grad_k = grad_k + dot_nn(scores, jnp.where(mine, q, none))
            parts.append(dot_nn(turned[side * HEAD : (side + 1) * HEAD], scores))
        grad_q = jnp.concatenate(parts, 0).T * HEAD**-0.5
        dq[:, at] = grad_q.astype(BF)
        dk[:, at] = grad_k.astype(BF)
        dv[:, at] = grad_v.astype(BF)
        sums[0:1, at] += column_sum(grad_q)
        sums[1:2, at] += column_sum(grad_v)
        return carry

    lax.fori_loop(0, HEADS // 2, pair, 0)

    def close(n, carry):
        at = pl.ds(pl.multiple_of(n * tile, tile), tile)
        total[:, at] = (
            grad_first[:, at]
            + dot_nt(dq[...], wq[at, :])
            + dot_nt(dk[...], wk[at, :])
            + dot_nt(dv[...], wv[at, :])
        )
        return carry

    lax.fori_loop(0, width // tile, close, 0)
    rows = 128

    def last(n, carry):
        at = pl.ds(pl.multiple_of(n * rows, rows), rows)
        unit, inverse = stats(embedded[at, :])
        grad = total[at, :]
        grad_emb = norm_back(grad, emb_gain[...], unit, inverse)
        emb_low[at, :] = grad_emb.astype(BF)
        sums[2:3, :] += column_sum(grad * unit)
        sums[3:4, :] += column_sum(grad)
        kind = kinds[at, :]
        for t in range(2):
            sums[4 + t : 5 + t, :] += column_sum(jnp.where(kind == t, grad_emb, 0.0))
        return carry

    lax.fori_loop(0, tokens // rows, last, 0)


def attend_back(grad_first, embedded, kinds, q, k, v, probs, wq, wk, wv, wo, emb_gain):
    tokens, width = grad_first.shape
    seqs, _, size, _ = probs.shape
    part = rows_of(size, width)
    low = jax.ShapeDtypeStruct((tokens, width), BF)
    return pl.pallas_call(
        attend_back_kernel,
        grid=(seqs,),
        in_specs=[part, part, rows_of(size, 1)]
        + [part] * 3
        + [pl.BlockSpec((1, HEADS, size, size), lambda i: (i, 0, 0, 0))]
        + [fixed((width, width))] * 4
        + [fixed((1, width))],
        out_specs=[part] * 5 + [fixed((8, width))],
        out_shape=[low] * 5 + [jax.ShapeDtypeStruct((8, width), F32)],
        scratch_shapes=[pltpu.VMEM((size, width), BF), pltpu.VMEM((size, width), F32)],
        compiler_params=pltpu.CompilerParams(vmem_limit_bytes=60 * MIB),
        cost_estimate=pl.CostEstimate(flops=30 * 10**9, bytes_accessed=40 * 10**6, transcendentals=0),
        name="attend_back",
    )(grad_first, embedded, kinds.reshape(tokens, 1), q, k, v, probs, wq, wk, wv, wo, row(emb_gain))


MESH = pl.DeviceIdType.MESH


def column_of(lines, column):
    count, size = lines.shape
    for s in range(count):
        line = jnp.broadcast_to(lines[s : s + 1, :].astype(F32), (8, size))
        column[pl.ds(s * size, size), :] = line.T[:, 0:1].astype(jnp.int32)


def mid_kernel(
    active, upper_low, second_low, hidden_low, grad_first, embedded, q_in, k_in, v_in, probs_in, wq, wk, wv, wo,
    kinds_in, emb_gain_in,
    first_out, dq_out, dk_out, dv_out, raw_out, pos_out, feed_out, part_out, sums,
    stage, lhs, turned, grads, core_in, in_1a, in_1b, in_2a, in_2b, in_z, kept,
    first, low, grad_mixed, q, k, v, dq, dk, dv, weights, table, raw, pos, probs, kind_column, kinds, emb_gain,
    load, stage_sem, probs_sem, out_sem, send, recv,
):
    tokens, width = lhs.shape
    seqs, size = kinds.shape
    per = grads.shape[3]
    me = lax.axis_index("vocab")
    spot = lax.axis_index("dp")
    core, place = lax.rem(me, 2), lax.div(me, 2)
    xb, yb = lax.rem(spot, 2), lax.div(spot, 2)
    across_x = {"dp": spot + 1 - 2 * xb}
    across_y = {"dp": spot + 2 - 4 * yb}
    partner = {"vocab": me + 1 - 2 * core}
    block = 768
    blocks = active.shape[1] // block

    def stage_copy(source, n):
        at = pl.ds(pl.multiple_of(n * block, block), block)
        slot = lax.rem(n, 2)
        return pltpu.make_async_copy(source.at[:, at], stage.at[slot], stage_sem.at[slot])

    def probs_copy(n):
        group = HEADS // 4
        slot = lax.rem(n, 2)
        return pltpu.make_async_copy(
            probs_in.at[lax.div(n, group), pl.ds(4 * lax.rem(n, group), 4)], probs.at[slot], probs_sem.at[slot]
        )

    second_copy = pltpu.make_async_copy(second_low, lhs, load.at[0])
    hidden_copy = pltpu.make_async_copy(hidden_low, lhs, load.at[1])
    second_copy.start()
    stage_copy(active, 0).start()
    stage_copy(active, 1).start()
    loads = [
        pltpu.make_async_copy(source, target, load.at[2 + i])
        for i, (source, target) in enumerate(
            (
                (grad_first, first),
                (wo, weights.at[3]),
                (q_in, q),
                (k_in, k),
                (v_in, v),
                (wq, weights.at[0]),
                (wk, weights.at[1]),
                (wv, weights.at[2]),
                (embedded, table),
                (kinds_in, kinds),
                (emb_gain_in, emb_gain),
            )
        )
    ]
    barrier = pltpu.get_barrier_semaphore()
    places = [{"vocab": 2 * flipped(place, k) + core} for k in (1, 2, 3)]
    for peer in [partner, across_x, across_y] + places:
        pl.semaphore_signal(barrier, inc=1, device_id=peer, device_id_type=MESH)
    pl.semaphore_wait(barrier, 6)

    def remote(src, dst, at, peer):
        return pltpu.make_async_remote_copy(
            src_ref=src, dst_ref=dst, send_sem=send.at[at], recv_sem=recv.at[at], device_id=peer, device_id_type=MESH
        )

    def columns(n):
        return pl.ds(pl.multiple_of(n * width, width), width)

    def core_copy(g, n):
        if g == 0:
            return remote(grads.at[0, n, 1 - core], core_in.at[0, n], 16 + n, partner)
        return remote(
            grads.at[1, :, 1 - core, :, columns(n)], core_in.at[1, :, :, columns(n)], 20 + n, partner
        )

    half = 2 * width

    def wide(b):
        return pl.ds(pl.multiple_of(b * half, half), half)

    def narrow(b, c):
        return pl.ds(pl.multiple_of(b * half + c * width, width), width)

    def first_copies(g):
        return [
            remote(grads.at[g, pl.ds(0, 2), core, :, wide(1 - xb)], in_1a.at[g], 5 * g + 1, across_x),
            remote(grads.at[g, pl.ds(2, 2), core, :, wide(1 - yb)], in_1b.at[g], 5 * g + 2, across_y),
        ]

    def second_copies(g):
        return [
            remote(grads.at[g, pl.ds(0, 2), core, :, narrow(xb, 1 - yb)], in_2a.at[g], 5 * g + 3, across_y),
            remote(grads.at[g, pl.ds(2, 2), core, :, narrow(yb, 1 - xb)], in_2b.at[g], 5 * g + 4, across_x),
        ]

    def add(view, value):
        view[...] = (view[...].astype(F32) + value.astype(F32)).astype(BF)

    def core_step(g):
        rows = per // 2

        def one(n, carry):
            core_copy(g, n).wait_recv()
            if g == 0:
                for i in range(2):
                    at = pl.ds(i * rows, rows)
                    add(grads.at[0, n, core, at, :], core_in[0, n, at, :])
            else:
                for z in range(4):
                    add(grads.at[1, z, core, :, columns(n)], core_in[1, z, :, columns(n)])
            return carry

        lax.fori_loop(0, 4, one, 0)
        for copy in first_copies(g):
            copy.start()

    def first_step(g):
        for copy in first_copies(g):
            copy.wait_recv()

        def one(z, carry):
            add(grads.at[g, z, core, :, wide(xb)], in_1a[g, z])
            add(grads.at[g, 2 + z, core, :, wide(yb)], in_1b[g, z])
            return carry

        lax.fori_loop(0, 2, one, 0)
        for copy in second_copies(g):
            copy.start()

    def owned(g, z):
        at = 2 * xb + yb + lax.div(z, 2) * (yb - xb)
        return grads.at[g, z, core, :, pl.ds(pl.multiple_of(at * width, width), width)]

    def place_copies(g):
        return [
            remote(owned(g, flipped(place, k)), in_z.at[g, k - 1], 10 + 3 * g + k - 1, places[k - 1]) for k in (3, 2, 1)
        ]

    def place_step(g):
        for copy in place_copies(g):
            copy.wait_recv()
        total = owned(g, place)[...].astype(F32)
        for k in range(3):
            total = total + in_z[g, k].astype(F32)
        kept[g] = total.astype(BF)

    def second_step(g):
        for copy in second_copies(g):
            copy.wait_recv()
        for z in range(2):
            add(grads.at[g, z, core, :, narrow(xb, yb)], in_2a[g, z])
            add(grads.at[g, 2 + z, core, :, narrow(yb, xb)], in_2b[g, z])
        for copy in place_copies(g):
            copy.start()

    corner = 256

    def turn():
        def one(i, carry):
            at = pl.ds(pl.multiple_of(i * corner, corner), corner)
            for j in range(width // corner):
                there = pl.ds(j * corner, corner)
                turned[there, at] = lhs[at, there].T
            return carry

        lax.fori_loop(0, tokens // corner, one, 0)

    second_copy.wait()
    turn()
    hidden_copy.start()
    probs_copy(0).start()
    for copy in loads:
        copy.start()
    share = block // 2

    def down_block(n, carry):
        stage_copy(active, n).wait()
        slot = lax.rem(n, 2)
        for c in range(2):
            out = dot_nn(turned[...], stage[slot, :, c * share : (c + 1) * share]).astype(BF)
            for j in range(8):
                grads[0, n, c, :, j * share : (j + 1) * share] = out[j * per : (j + 1) * per]
        core_copy(0, n).start()

        @pl.when(n < 2)
        def _():
            stage_copy(active, n + 2).start()

        @pl.when(n >= 2)
        def _():
            stage_copy(upper_low, n - 2).start()

        return carry

    lax.fori_loop(0, blocks, down_block, 0)
    core_step(0)
    hidden_copy.wait()
    turn()

    def up_block(n, carry):
        stage_copy(upper_low, n).wait()
        slot = lax.rem(n, 2)
        for c in range(2):
            out = dot_nn(turned[...], stage[slot, :, c * share : (c + 1) * share]).astype(BF)
            at = pl.ds(pl.multiple_of(n * block + c * share, 128), share)
            for j in range(8):
                grads[1, j // 2, j % 2, :, at] = out[j * per : (j + 1) * per]
        core_copy(1, n).start()

        @pl.when(n < 2)
        def _():
            stage_copy(upper_low, n + 2).start()

        return carry

    lax.fori_loop(0, blocks, up_block, 0)
    core_step(1)

    for copy in loads:
        copy.wait()
    sums[...] = jnp.zeros_like(sums)
    low[...] = first[...].astype(BF)
    first_copy = pltpu.make_async_copy(low, first_out, out_sem.at[4])
    first_copy.start()
    tile = 256

    def open_(n, carry):
        at = pl.ds(pl.multiple_of(n * tile, tile), tile)
        grad_mixed[:, at] = dot_nt(low[...], weights[3, at, :]).astype(BF)
        return carry

    lax.fori_loop(0, width // tile, open_, 0)

    def pair(n, slot, i):
        rows = pl.ds(pl.multiple_of(lax.div(n, HEADS // 2) * size, size), size)
        at = pl.ds(pl.multiple_of(lax.rem(n, HEADS // 2) * 2 * HEAD, 2 * HEAD), 2 * HEAD)
        q2, k2, v2, grad = q[rows, at], k[rows, at], v[rows, at], grad_mixed[rows, at]
        across = k2.T
        lane = lax.broadcasted_iota(jnp.int32, k2.shape, 1)
        parts = []
        grad_k = jnp.zeros(k2.shape, F32)
        grad_v = jnp.zeros(k2.shape, F32)
        for side in range(2):
            mine = (lane >= HEAD) if side else (lane < HEAD)
            none = jnp.zeros_like(k2)
            chances = probs[slot, 2 * i + side]
            grad_probs = dot_nt(jnp.where(mine, v2, none), grad)
            grad_v = grad_v + dot_nn(chances, jnp.where(mine, grad, none))
            full = chances.astype(F32)
            both = full * grad_probs
            scores = (both - full * jnp.sum(both, 0, keepdims=True)).astype(BF)
            grad_k = grad_k + dot_nn(scores, jnp.where(mine, q2, none))
            parts.append(dot_nn(across[side * HEAD : (side + 1) * HEAD], scores))
        grad_q = jnp.concatenate(parts, 0).T * HEAD**-0.5
        dq[rows, at] = grad_q.astype(BF)
        dk[rows, at] = grad_k.astype(BF)
        dv[rows, at] = grad_v.astype(BF)
        sums[0:1, at] += column_sum(grad_q)
        sums[1:2, at] += column_sum(grad_v)

    groups = seqs * HEADS // 4

    def pairs(n, carry):
        @pl.when(n + 1 < groups)
        def _():
            probs_copy(n + 1).start()

        probs_copy(n).wait()
        slot = lax.rem(n, 2)
        for i in range(2):
            pair(2 * n + i, slot, i)

        @pl.when(n == 2)
        def _():
            second_step(0)

        @pl.when(n == 3)
        def _():
            first_step(1)

        @pl.when(n == 5)
        def _():
            second_step(1)

        return carry

    first_step(0)
    lax.fori_loop(0, groups, pairs, 0)
    out_copies = [
        pltpu.make_async_copy(source, target, out_sem.at[5 + i])
        for i, (source, target) in enumerate(((dq, dq_out), (dk, dk_out), (dv, dv_out)))
    ]
    for copy in out_copies:
        copy.start()

    def close(n, carry):
        at = pl.ds(pl.multiple_of(n * tile, tile), tile)
        first[:, at] = (
            first[:, at]
            + dot_nt(dq[...], weights[0, at, :])
            + dot_nt(dk[...], weights[1, at, :])
            + dot_nt(dv[...], weights[2, at, :])
        )
        return carry

    lax.fori_loop(0, width // tile, close, 0)
    column_of(kinds, kind_column)
    few = 128
    lane = lax.broadcasted_iota(jnp.int32, (few, 128), 1)

    def back(at):
        unit, inverse = stats(table[at, :])
        grad = first[at, :]
        grad_emb = norm_back(grad, emb_gain[...][None], unit, inverse)
        sums[2:3, :] += column_sum(grad * unit)
        sums[3:4, :] += column_sum(grad)
        kind = kind_column[at, :]
        for t in range(2):
            sums[4 + t : 5 + t, :] += column_sum(jnp.where(kind == t, grad_emb, 0.0))
        return grad_emb

    def last(n, carry):
        at = pl.ds(pl.multiple_of(n * few, few), few)
        left = back(at)
        right = back(pl.ds(pl.multiple_of(size + n * few, few), few))
        pos[at, :] = (left + right).astype(BF)
        for t in range(width // 128):
            one, two = left[:, t * 128 : (t + 1) * 128], right[:, t * 128 : (t + 1) * 128]
            q = 2 * (t % 2)
            raw[t // 2, q, at, :] = jnp.where(lane < 64, one, pltpu.roll(two, 64, 1)).astype(BF)
            raw[t // 2, q + 1, at, :] = jnp.where(lane < 64, pltpu.roll(one, 64, 1), two).astype(BF)
        return carry

    lax.fori_loop(0, size // few, last, 0)
    raw_copy = pltpu.make_async_copy(raw, raw_out, out_sem.at[3])
    raw_copy.start()
    pos_copy = pltpu.make_async_copy(pos, pos_out, out_sem.at[8])
    pos_copy.start()
    place_step(0)
    place_step(1)
    feed_copy = pltpu.make_async_copy(kept.at[0], feed_out, out_sem.at[2])
    feed_copy.start()
    part_copy = pltpu.make_async_copy(kept.at[1], part_out, out_sem.at[0])
    part_copy.start()
    for copy in [first_copy, raw_copy, pos_copy, feed_copy, part_copy] + out_copies:
        copy.wait()
    for g in range(2):
        for copy in [core_copy(g, n) for n in range(4)] + first_copies(g) + second_copies(g) + place_copies(g):
            copy.wait_send()


def mid(
    active, upper_low, second_low, hidden_low, grad_first, embedded, q, k, v, probs, wq, wk, wv, wo, kinds, emb_gain
):
    tokens, width = grad_first.shape
    seqs, heads, size, _ = probs.shape
    units = active.shape[1]
    per = width // 8
    wide = 4 * width
    vmem = pl.BlockSpec(memory_space=pltpu.VMEM)
    hbm = pl.BlockSpec(memory_space=pl.ANY)
    low = jax.ShapeDtypeStruct((tokens, width), BF)
    small = pltpu.VMEM((tokens, width), BF)
    large = pltpu.VMEM((tokens, width), F32)
    return pl.pallas_call(
        mid_kernel,
        out_shape=[low] * 4
        + [
            jax.ShapeDtypeStruct((3, 4, size, 128), BF),
            jax.ShapeDtypeStruct((size, width), BF),
            jax.ShapeDtypeStruct((per, width), BF),
            jax.ShapeDtypeStruct((per, width), BF),
            jax.ShapeDtypeStruct((8, width), F32),
        ],
        in_specs=[hbm] * 16,
        out_specs=[hbm] * 8 + [vmem],
        scratch_shapes=[
            pltpu.VMEM((2, tokens, 768), BF),
            small,
            pltpu.VMEM((width, tokens), BF),
            pltpu.VMEM((2, 4, 2, per, wide), BF),
            pltpu.VMEM((2, 4, per, wide), BF),
            pltpu.VMEM((2, 2, per, wide // 2), BF),
            pltpu.VMEM((2, 2, per, wide // 2), BF),
            pltpu.VMEM((2, 2, per, width), BF),
            pltpu.VMEM((2, 2, per, width), BF),
            pltpu.VMEM((2, 3, per, width), BF),
            pltpu.VMEM((2, per, width), BF),
            large,
            small,
            small,
            small,
            small,
            small,
            small,
            small,
            small,
            pltpu.VMEM((4, width, width), BF),
            large,
            pltpu.VMEM((3, 4, size, 128), BF),
            pltpu.VMEM((size, width), BF),
            pltpu.VMEM((2, 4, size, size), BF),
            pltpu.VMEM((tokens, 1), jnp.int32),
            pltpu.VMEM((seqs, size), jnp.int32),
            pltpu.VMEM((width,), F32),
            pltpu.SemaphoreType.DMA((13,)),
            pltpu.SemaphoreType.DMA((2,)),
            pltpu.SemaphoreType.DMA((2,)),
            pltpu.SemaphoreType.DMA((9,)),
            pltpu.SemaphoreType.DMA((24,)),
            pltpu.SemaphoreType.DMA((24,)),
        ],
        compiler_params=pltpu.CompilerParams(
            collective_id=2, has_side_effects=True, vmem_limit_bytes=62 * MIB
        ),
        name="mid",
    )(
        active, upper_low, second_low, hidden_low, grad_first, embedded, q, k, v, probs, wq, wk, wv, wo,
        kinds, emb_gain,
    )


def flipped(index, bits):
    out = 0
    for place in range(3):
        bit = lax.rem(lax.div(index, 1 << place), 2)
        out = out + (1 << place) * (1 - bit if (bits >> place) & 1 else bit)
    return out


def exchanged(index, bits):
    out = 0
    for place in range(2):
        one = lax.rem(lax.div(index, 1 << place), 2)
        two = lax.rem(lax.div(bits, 1 << place), 2)
        out = out + (1 << place) * (one + two - 2 * one * two)
    return out


ORDER = (6, 7, 4, 5, 2, 3, 1)


def tail_kernel(
    slots, asked, pos, feed_sums, up_sums, mid_sums, raw, normed, mixed, gfirst, dq, dk, dv, feed_own, up_part,
    word, packed, feed_out, up_out, small_out,
    tok, hot, og, inc, rhs, kinds, places, total, dense, ops, turned, wbuf, wcore, w1a, w1b, w2a, w2b, wz, wown, small_by, small_in, small_dp,
    load_sem, t_send, t_recv, z_send, z_recv, d_send, d_recv, w_send, w_recv, s_send, s_recv, own_sem,
):
    chunks, owners, sources, pairs, lanes = og.shape
    half, width = pos.shape
    tokens = 2 * half
    cap = 2 * pairs
    tall = dense.shape[1]
    me = lax.axis_index("vocab")
    spot = lax.axis_index("dp")
    core, place = lax.rem(me, 2), lax.div(me, 2)
    xb, yb = lax.rem(spot, 2), lax.div(spot, 2)
    across_x = {"dp": spot + 1 - 2 * xb}
    across_y = {"dp": spot + 2 - 4 * yb}

    barrier = pltpu.get_barrier_semaphore()
    for k in ORDER:
        pl.semaphore_signal(barrier, inc=1, device_id={"vocab": flipped(me, k)}, device_id_type=MESH)
    for k in (1, 2, 3):
        pl.semaphore_signal(barrier, inc=1, device_id={"dp": flipped(spot, k)}, device_id_type=MESH)
    loads = [
        pltpu.make_async_copy(ref, ops.at[i], load_sem.at[i])
        for i, ref in enumerate((normed, dq, dk, dv, mixed, gfirst))
    ]
    for load in loads:
        load.start()
    per = width // owners
    order = ((1, 0), (1, 1), (0, 5), (0, 3), (0, 4), (1, 2), (1, 3), (0, 2), (0, 0), (0, 1), (1, 4), (1, 5))
    for v in range(owners):
        small_by[v] = jnp.zeros(small_by.shape[1:], F32)
        for i, (which, line) in enumerate(order):
            source = (feed_sums, mid_sums)[which]
            small_by[v, i : i + 1, :per] = source[line : line + 1, v * per : (v + 1) * per]
        for i in range(4):
            at = (4 * v + i) * per
            small_by[v, 12 + i : 13 + i, :per] = up_sums[:, at : at + per]
    pl.semaphore_wait(barrier, len(ORDER) + 3)

    def remote(src, dst, send, recv, peer):
        return pltpu.make_async_remote_copy(
            src_ref=src, dst_ref=dst, send_sem=send, recv_sem=recv, device_id=peer, device_id_type=MESH
        )

    def start(copies):
        for copy in copies:
            copy.start()

    def arrived(copies):
        for copy in copies:
            copy.wait_recv()

    def gone(copies):
        for copy in copies:
            copy.wait_send()

    def token_copy(c, k):
        peer = flipped(spot, k) if isinstance(k, int) else exchanged(spot, k)
        return remote(raw.at[c, peer], tok.at[c, spot], t_send.at[c, k], t_recv.at[c, k], {"dp": peer})

    def token_copies(c):
        return [token_copy(c, k) for k in (1, 2, 3)]

    def token_own(c):
        return pltpu.make_async_copy(raw.at[c, spot], tok.at[c, spot], own_sem.at[c])

    for c in range(chunks):
        start(token_copies(c))
        token_own(c).start()

    def row_copies(c, j):
        source = flipped(spot, j) if isinstance(j, int) else exchanged(spot, j)
        copies = []
        for k in ORDER:
            peer = flipped(me, k)
            copies.append(
                remote(
                    og.at[c, peer, source],
                    inc.at[c, me, source],
                    z_send.at[c, j, k],
                    z_recv.at[c, j, k],
                    {"vocab": peer},
                )
            )
        return copies

    def make_hot(d):
        def one(v, carry):
            wanted = lax.broadcasted_iota(jnp.int32, (cap, half), 0) + v * cap
            for s in range(2):
                hit = wanted == slots[d, :, s * half : (s + 1) * half]
                hot[d, s, v] = jnp.where(hit, 1.0, 0.0).astype(BF)
            return carry

        lax.fori_loop(0, owners, one, 0)

    def fill(d, first, count):
        lane = lax.broadcasted_iota(jnp.int32, (pairs, lanes), 1)
        values = jnp.concatenate([tok[first + i, d] for i in range(count)], 1)
        early = dot_nn(hot[d, 0].reshape(owners * cap, half), values)
        late = dot_nn(hot[d, 1].reshape(owners * cap, half), values)
        for v in range(owners):
            low, high = slice(v * cap, v * cap + pairs), slice(v * cap + pairs, (v + 1) * cap)
            for i in range(count):
                there = slice(i * lanes, (i + 1) * lanes)
                straight = jnp.where(lane < 64, early[low, there], late[high, there])
                crossed = jnp.where(lane < 64, early[high, there], late[low, there])
                og[first + i, v, d] = (straight + pltpu.roll(crossed, 64, 1)).astype(BF)

    def own_copy(c):
        return pltpu.make_async_copy(og.at[c, me], inc.at[c, me], own_sem.at[11 + c])

    def fill_first(j):
        d = flipped(spot, j) if isinstance(j, int) else exchanged(spot, j)
        make_hot(d)
        if isinstance(j, int) and j == 0:
            token_own(0).wait()
        else:
            token_copy(0, j).wait_recv()
        fill(d, 0, 1)
        start(row_copies(0, j))

    depth = 1024

    def sort_rows():
        for v in range(owners):
            lines = []
            for d in range(sources):
                for h in range(2):
                    ids = asked[d, v, :, h * pairs : (h + 1) * pairs]
                    kind = sum(jnp.where(ids >= n * tall, 1, 0) for n in (1, 2, 3))
                    places[h, :, pl.ds((v * sources + d) * pairs, pairs)] = ids - tall * kind
                    lines.append(kind)
            kinds[v] = jnp.concatenate(lines, 0).astype(F32).T.astype(jnp.int32)

    def prepare(c):
        def one(v, carry):
            lane = lax.broadcasted_iota(jnp.int32, (pairs, lanes), 1)
            side = jnp.where(lane < 64, 0, 1)
            for d in range(sources):
                at = pl.ds(pl.multiple_of((v * sources + d) * pairs, pairs), pairs)
                straight = inc[c, v, d].astype(F32)
                crossed = pltpu.roll(straight, 64, 1)
                for h in range(2):
                    kind = kinds[v, :, 2 * d + h : 2 * d + h + 1] - side
                    twice = jnp.where(lane < 64, crossed if h else straight, straight if h else crossed)
                    rhs[h, at, :lanes] = jnp.where(kind == 0, twice, 0.0).astype(BF)
                    rhs[h, at, lanes:] = jnp.where(kind == 2, twice, 0.0).astype(BF)
            return carry

        lax.fori_loop(0, owners, one, 0)

    def gather_rows(c, p):
        tile = tall // 2
        blocks = owners * sources * pairs // depth
        total[...] = jnp.zeros_like(total)

        def one(n, carry):
            h, b = lax.div(n, blocks), lax.rem(n, blocks)
            at = pl.ds(pl.multiple_of(b * depth, depth), depth)
            ids = places[h, :, at] - p * tile
            hit = lax.broadcasted_iota(jnp.int32, (tile, depth), 0) == ids
            total[...] += dot_nn(jnp.where(hit, 1.0, 0.0).astype(BF), rhs[h, at, :])
            return carry

        lax.fori_loop(0, 2 * blocks, one, 0, unroll=2)
        dense[c, pl.ds(pl.multiple_of(p * tile, tile), tile), :] = total[...].astype(BF)

    part = tall // 2

    def lines_of(p):
        return pl.ds(pl.multiple_of(p * part, part), part)

    def keep_copy(c, p):
        return pltpu.make_async_copy(
            dense.at[c, lines_of(p)], word.at[c, spot, lines_of(p)], own_sem.at[3 + 2 * c + p]
        )

    def near_copies(c, p):
        return [
            remote(
                dense.at[c, lines_of(p)], word.at[c, spot, lines_of(p)], d_send.at[c, 2 * p], d_recv.at[c, 2 * p], across_x
            ),
            remote(
                dense.at[c, lines_of(p)],
                word.at[c, spot, lines_of(p)],
                d_send.at[c, 2 * p + 1],
                d_recv.at[c, 2 * p + 1],
                across_y,
            ),
        ]

    def far_copy(c, p):
        source = flipped(spot, 1) if p == 0 else flipped(spot, 2)
        view = word.at[c, source, lines_of(p)]
        return remote(view, view, d_send.at[c, 4 + p], d_recv.at[c, 4 + p], across_y if p == 0 else across_x)

    corner = 256
    block = 384
    quarter = wown.shape[0]

    def turn(which):
        def one(i, carry):
            at = pl.ds(pl.multiple_of(i * corner, corner), corner)
            for j in range(width // corner):
                there = pl.ds(j * corner, corner)
                turned[there, at] = ops[which, at, there].T
            return carry

        lax.fori_loop(0, tokens // corner, one, 0)

    def weight(which, at):
        def one(n, carry):
            there = pl.ds(pl.multiple_of(n * block, block), block)
            out = dot_nn(turned[...], ops[which, :, there]).astype(BF)
            for v in range(owners):
                wbuf[v // 2, v % 2, pl.ds(at * per, per), there] = out[v * per : (v + 1) * per]
            return carry

        lax.fori_loop(0, width // block, one, 0)

    core_copy = remote(wbuf.at[:, 1 - core], wcore, w_send.at[0], w_recv.at[0], {"vocab": flipped(me, 1)})

    def wide(b):
        return pl.ds(pl.multiple_of(b * 2 * quarter, quarter), 2 * quarter)

    def narrow(b, c):
        return pl.ds(pl.multiple_of((2 * b + c) * quarter, quarter), quarter)

    def add(view, value):
        view[...] = (view[...].astype(F32) + value.astype(F32)).astype(BF)

    def core_step():
        core_copy.wait_recv()

        def one(i, carry):
            z = lax.div(i, 4)
            at = pl.ds(pl.multiple_of(lax.rem(i, 4) * quarter, quarter), quarter)
            add(wbuf.at[z, core, at, :], wcore[z, at, :])
            return carry

        lax.fori_loop(0, 16, one, 0)

    def first_weights():
        return [
            remote(wbuf.at[pl.ds(0, 2), core, wide(1 - xb), :], w1a, w_send.at[1], w_recv.at[1], across_x),
            remote(wbuf.at[pl.ds(2, 2), core, wide(1 - yb), :], w1b, w_send.at[2], w_recv.at[2], across_y),
        ]

    def second_weights():
        return [
            remote(wbuf.at[pl.ds(0, 2), core, narrow(xb, 1 - yb), :], w2a, w_send.at[3], w_recv.at[3], across_y),
            remote(wbuf.at[pl.ds(2, 2), core, narrow(yb, 1 - xb), :], w2b, w_send.at[4], w_recv.at[4], across_x),
        ]

    def first_step():
        arrived(first_weights())
        for z in range(2):
            add(wbuf.at[z, core, wide(xb), :], w1a[z])
            add(wbuf.at[2 + z, core, wide(yb), :], w1b[z])

    def second_step():
        arrived(second_weights())
        for z in range(2):
            add(wbuf.at[z, core, narrow(xb, yb), :], w2a[z])
            add(wbuf.at[2 + z, core, narrow(yb, xb), :], w2b[z])

    def owned(z):
        at = 2 * xb + yb + lax.div(z, 2) * (yb - xb)
        return wbuf.at[z, core, pl.ds(pl.multiple_of(at * quarter, quarter), quarter), :]

    def third_weights():
        copies = []
        for k in (3, 2, 1):
            to = flipped(place, k)
            copies.append(
                remote(owned(to), wz.at[k - 1], w_send.at[4 + k], w_recv.at[4 + k], {"vocab": 2 * to + core})
            )
        return copies

    def third_step():
        arrived(third_weights())
        total = owned(place)[...].astype(F32)
        for k in range(3):
            total = total + wz[k].astype(F32)
        wown[...] = total.astype(BF)

    def spread(own, target, at):
        wide_half = width // 2
        left, right = pl.ds(0, wide_half), pl.ds(wide_half, wide_half)
        kept = pltpu.make_async_copy(own, target.at[xb, yb], own_sem.at[(9, 10, 15)[at]])
        sems = [(w_send.at[8 + 4 * at + i], w_recv.at[8 + 4 * at + i]) for i in range(4)]
        near = [
            remote(own, target.at[xb, yb], *sems[0], across_x),
            remote(own, target.at[xb, yb], *sems[1], across_y),
        ]
        from_x, from_y = target.at[1 - xb, yb, :, left], target.at[xb, 1 - yb, :, right]
        far = [remote(from_x, from_x, *sems[2], across_y), remote(from_y, from_y, *sems[3], across_x)]
        return kept, near, far

    feed_kept, feed_near, feed_far = spread(feed_own, feed_out, 0)
    kept, fourth_weights, fifth_weights = spread(wown, packed, 1)
    up_kept, up_near, up_far = spread(up_part, up_out, 2)

    def small_copies():
        copies = []
        for k in ORDER:
            peer = flipped(me, k)
            copies.append(remote(small_by.at[peer], small_in.at[k], s_send.at[k], s_recv.at[k], {"vocab": peer}))
        return copies

    def small_last():
        return [
            remote(small_in.at[0], small_dp.at[k - 1], s_send.at[7 + k], s_recv.at[7 + k], {"dp": flipped(spot, k)})
            for k in (1, 2, 3)
        ]

    start(small_copies())
    fill_first(0)
    for near, kept_copy in ((feed_near, feed_kept), (up_near, up_kept)):
        start(near)
        kept_copy.start()
    loads[0].wait()
    turn(0)
    for i in range(3):
        loads[1 + i].wait()
        weight(1 + i, i)
        if i == 0:
            fill_first(1)
    loads[4].wait()
    turn(4)
    loads[5].wait()
    weight(5, 3)
    share = half // owners
    for v in range(owners):
        wbuf[v // 2, v % 2, pl.ds(4 * per, share), :] = pos[pl.ds(v * share, share), :]
    core_copy.start()

    def fill_next(j, carry):
        fill_first(j)
        return carry

    lax.fori_loop(2, sources, fill_next, 0)
    own_copy(0).start()
    for near, far, kept_copy in ((feed_near, feed_far, feed_kept), (up_near, up_far, up_kept)):
        kept_copy.wait()
        arrived(near)
        start(far)
    core_step()
    start(first_weights())
    for c in (1, 2):
        token_own(c).wait()
        arrived(token_copies(c))

    def rest(d, carry):
        fill(d, 1, 2)
        return carry

    lax.fori_loop(0, sources, rest, 0)
    for c in (1, 2):
        own_copy(c).start()
    sort_rows()
    arrived(small_copies())
    short = small_by[me]
    for k in ORDER:
        short = short + small_in[k]
    small_in[0] = short
    start(small_last())

    def close_chunk(c):
        for j in range(sources):
            arrived(row_copies(c, j))
        own_copy(c).wait()
        if c + 1 < chunks:
            for j in range(sources):
                start(row_copies(c + 1, j))
        else:
            start(third_weights())
        prepare(c)
        def half_rows(p, carry):
            gather_rows(c, p)
            start(near_copies(c, p))
            keep_copy(c, p).start()
            return carry

        lax.fori_loop(0, 2, half_rows, 0)

    def pass_on(c):
        arrived(near_copies(c, 0))
        far_copy(c, 0).start()
        arrived(near_copies(c, 1))
        far_copy(c, 1).start()

    close_chunk(0)
    first_step()
    start(second_weights())
    pass_on(0)
    close_chunk(1)
    second_step()
    arrived(small_last())
    short = small_in[0]
    for k in range(3):
        short = short + small_dp[k]
    small_out[...] = short
    pass_on(1)
    close_chunk(2)
    third_step()
    start(fourth_weights)
    kept.start()
    pass_on(2)
    kept.wait()
    arrived(fourth_weights)
    start(fifth_weights)

    for c in range(chunks):
        for p in range(2):
            keep_copy(c, p).wait()
            far_copy(c, p).wait_recv()
    arrived(feed_far)
    arrived(fifth_weights)
    arrived(up_far)
    gone(up_near)
    gone(up_far)
    core_copy.wait_send()
    gone(small_copies())
    gone(small_last())
    for c in range(chunks):
        gone(token_copies(c))
        for j in range(sources):
            gone(row_copies(c, j))
        for p in range(2):
            gone(near_copies(c, p))
            far_copy(c, p).wait_send()
    for copies in (first_weights(), second_weights(), third_weights(), fourth_weights, fifth_weights, feed_near, feed_far):
        gone(copies)


def tail(
    slots, asked, pos, feed_sums, up_sums, mid_sums, raw, normed, mixed, gfirst, dq, dk, dv, feed_own, up_part, rows_local
):
    half, width = pos.shape
    sources, owners, _, cap = asked.shape
    chunks = raw.shape[0]
    pairs = cap // 2
    tall = rows_local // 4
    lines = 4 * (width // owners) + half // owners
    vmem = pl.BlockSpec(memory_space=pltpu.VMEM)
    hbm = pl.BlockSpec(memory_space=pl.ANY)
    return pl.pallas_call(
        tail_kernel,
        out_shape=(
            jax.ShapeDtypeStruct((chunks, sources, tall, 256), BF),
            jax.ShapeDtypeStruct((2, 2, lines // 4, width), BF),
            jax.ShapeDtypeStruct((2, 2) + feed_own.shape, BF),
            jax.ShapeDtypeStruct((2, 2) + feed_own.shape, BF),
            jax.ShapeDtypeStruct((16, 128), F32),
        ),
        in_specs=[vmem] * 6 + [hbm] * 9,
        out_specs=(hbm, hbm, hbm, hbm, vmem),
        scratch_shapes=[
            pltpu.VMEM((chunks, sources, half, 128), BF),
            pltpu.VMEM((sources, 2, owners, cap, half), BF),
            pltpu.VMEM((chunks, owners, sources, pairs, 128), BF),
            pltpu.VMEM((chunks, owners, sources, pairs, 128), BF),
            pltpu.VMEM((2, owners * sources * pairs, 256), BF),
            pltpu.VMEM((owners, pairs, 2 * sources), jnp.int32),
            pltpu.VMEM((2, 1, owners * sources * pairs), jnp.int32),
            pltpu.VMEM((tall // 2, 256), F32),
            pltpu.VMEM((chunks, tall, 256), BF),
            pltpu.VMEM((6, 2 * half, width), BF),
            pltpu.VMEM((width, 2 * half), BF),
            pltpu.VMEM((4, 2, lines, width), BF),
            pltpu.VMEM((4, lines, width), BF),
            pltpu.VMEM((2, lines // 2, width), BF),
            pltpu.VMEM((2, lines // 2, width), BF),
            pltpu.VMEM((2, lines // 4, width), BF),
            pltpu.VMEM((2, lines // 4, width), BF),
            pltpu.VMEM((3, lines // 4, width), BF),
            pltpu.VMEM((lines // 4, width), BF),
            pltpu.VMEM((owners, 16, 128), F32),
            pltpu.VMEM((owners, 16, 128), F32),
            pltpu.VMEM((3, 16, 128), F32),
            pltpu.SemaphoreType.DMA((6,)),
            pltpu.SemaphoreType.DMA((chunks, 4)),
            pltpu.SemaphoreType.DMA((chunks, 4)),
            pltpu.SemaphoreType.DMA((chunks, sources, owners)),
            pltpu.SemaphoreType.DMA((chunks, sources, owners)),
            pltpu.SemaphoreType.DMA((chunks, 6)),
            pltpu.SemaphoreType.DMA((chunks, 6)),
            pltpu.SemaphoreType.DMA((20,)),
            pltpu.SemaphoreType.DMA((20,)),
            pltpu.SemaphoreType.DMA((14,)),
            pltpu.SemaphoreType.DMA((14,)),
            pltpu.SemaphoreType.DMA((16,)),
        ],
        compiler_params=pltpu.CompilerParams(collective_id=1, has_side_effects=True, vmem_limit_bytes=60 * MIB),
        name="tail",
    )(
        slots, asked, pos, feed_sums, up_sums, mid_sums,
        raw, normed, mixed, gfirst, dq, dk, dv, feed_own, up_part,
    )


def fetch_kernel(
    token_ids_in, kinds_in, pos_in, types_in, gain_in, bias_in, table_in,
    embedded_out, normed_out, slots_out, asked_out,
    token_ids, kinds, pos, types, gain, bias, table, request, asked_in, rows_out, rows_in, embedded, normed, column, kind_column,
    load_sem, q_send, q_recv, s_send, s_recv, a_send, a_recv, z_send, z_recv, out_sem,
):
    owners, cap, width = rows_out.shape
    tokens = normed.shape[0]
    rows_local = table.shape[0]
    me = lax.axis_index("vocab")
    spot = lax.axis_index("dp")
    table_copy = pltpu.make_async_copy(table_in, table, load_sem.at[0])
    loads = [
        pltpu.make_async_copy(source, target, load_sem.at[1 + i])
        for i, (source, target) in enumerate(
            (
                (token_ids_in, token_ids),
                (kinds_in, kinds),
                (pos_in, pos),
                (types_in, types),
                (gain_in, gain),
                (bias_in, bias),
            )
        )
    ]
    for load in loads:
        load.start()
    table_copy.start()
    barrier = pltpu.get_barrier_semaphore()
    for k in ORDER:
        pl.semaphore_signal(barrier, inc=1, device_id={"vocab": flipped(me, k)}, device_id_type=MESH)
    for k in (1, 2, 3):
        pl.semaphore_signal(barrier, inc=1, device_id={"dp": flipped(spot, k)}, device_id_type=MESH)

    def remote(src, dst, send, recv, peer):
        return pltpu.make_async_remote_copy(
            src_ref=src, dst_ref=dst, send_sem=send, recv_sem=recv, device_id=peer, device_id_type=MESH
        )

    loads[0].wait()
    ids = jnp.concatenate([token_ids[s : s + 1, :] for s in range(token_ids.shape[0])], 1)
    owner = jnp.zeros(ids.shape, jnp.int32)
    for v in range(1, owners):
        owner = owner + jnp.where(ids >= v * rows_local, 1, 0)
    member = jnp.where(lax.broadcasted_iota(jnp.int32, (owners, tokens), 0) == owner, 1.0, 0.0)
    block = 256
    rank = []
    for n in range(tokens // block):
        before = lax.broadcasted_iota(jnp.int32, (tokens, block), 0) < (
            lax.broadcasted_iota(jnp.int32, (tokens, block), 1) + n * block
        )
        earlier = dot_nn(member.astype(BF), jnp.where(before, 1.0, 0.0).astype(BF))
        rank.append(jnp.sum(earlier * member[:, n * block : (n + 1) * block], 0, keepdims=True))
    slot = owner * cap + jnp.concatenate(rank, 1).astype(jnp.int32)
    local = ids - owner * rows_local
    line = lax.broadcasted_iota(jnp.int32, (8, tokens), 0)
    high = lax.shift_right_logical(local, 6)
    values = jnp.where(line == 0, high, jnp.where(line == 1, local - high * 64, jnp.where(line == 2, 1, 0)))
    values = values.astype(F32).astype(BF)
    slots_out[spot] = slot

    def ask(v, carry):
        wanted = lax.broadcasted_iota(jnp.int32, (cap, tokens), 0) + v * cap
        found = dot_nt(values, jnp.where(wanted == slots_out[spot], 1.0, 0.0).astype(BF))
        number = found[0:1] * 64.0 + found[1:2]
        request[v] = jnp.where(found[2:3] > 0.5, number, -1.0).astype(jnp.int32)
        return carry

    lax.fori_loop(0, owners, ask, 0)
    pl.semaphore_wait(barrier, len(ORDER) + 3)
    asks = []
    for k in ORDER:
        peer = flipped(me, k)
        asks.append(remote(request.at[peer], asked_in.at[me], q_send.at[k], q_recv.at[k], {"vocab": peer}))
    for copy in asks:
        copy.start()
    asked_in[me] = request[me]
    lists = []
    for k in (1, 2, 3):
        peer = {"dp": flipped(spot, k)}
        lists.append(remote(slots_out.at[spot], slots_out.at[spot], s_send.at[k], s_recv.at[k], peer))
    for copy in lists:
        copy.start()
    column[...] = jnp.broadcast_to(slot.astype(F32), (8, tokens)).T[:, 0:1].astype(jnp.int32)
    for load in loads[1:]:
        load.wait()
    column_of(kinds, kind_column)
    half = tokens // 2
    for s in range(2):
        at = pl.ds(s * half, half)
        kind = jnp.where(kind_column[at, :] == 0, types[0:1, :].astype(F32), types[1:2, :].astype(F32))
        embedded[at, :] = pos[...].astype(F32) + kind
    for copy in asks:
        copy.wait_recv()
    asked_out[spot] = asked_in[...]
    for k in (1, 2, 3):
        peer = {"dp": flipped(spot, k)}
        copy = remote(asked_in, asked_out.at[spot], a_send.at[k], a_recv.at[k], peer)
        lists.append(copy)
        copy.start()
    table_copy.wait()

    def find(source):
        asked = jnp.broadcast_to(asked_in[source].astype(F32), (8, cap)).T[:, 0:1]
        depth = rows_local // 3
        total = jnp.zeros((cap, width), F32)
        for n in range(3):
            at = lax.broadcasted_iota(jnp.int32, (cap, depth), 1) + n * depth
            hit = jnp.where(at == asked.astype(jnp.int32), 1.0, 0.0).astype(BF)
            total = total + dot_nn(hit, table[pl.ds(n * depth, depth), :])
        return total.astype(BF)

    def row_copy(peer):
        return remote(rows_out.at[peer], rows_in.at[me], z_send.at[peer], z_recv.at[me], {"vocab": peer})

    def row_arrival(peer):
        return remote(rows_out.at[peer], rows_in.at[peer], z_send.at[peer], z_recv.at[peer], {"vocab": peer})

    core, spot_z = lax.rem(me, 2), lax.div(me, 2)
    side = lax.div(spot_z, 2)

    def answer(i, carry):
        j = lax.div(i, 2)
        to_end = lax.div((1 - j) * (2 - j) * (3 - j), 6)
        to_middle = lax.div(j * (2 - j) * (3 - j), 2)
        to_next = lax.div(j * (j - 1) * (3 - j), 2)
        to_core = lax.div(j * (j - 1) * (j - 2), 6)
        chip = (
            to_end * 3 * (1 - side)
            + to_middle * (2 - side)
            + to_next * (spot_z + 1 - 2 * lax.rem(spot_z, 2))
            + to_core * spot_z
        )
        peer = 2 * chip + lax.rem(i, 2) * (1 - to_core) + (1 - core) * to_core
        rows_out[peer] = find(peer)
        row_copy(peer).start()
        return carry

    lax.fori_loop(0, owners - 1, answer, 0)
    rows_in[me] = find(me)

    def place(source):
        part = 256

        def one(n, carry):
            at = pl.ds(pl.multiple_of(n * part, part), part)
            hit = lax.broadcasted_iota(jnp.int32, (part, cap), 1) + source * cap
            hit = jnp.where(hit == column[at, :], 1.0, 0.0).astype(BF)
            embedded[at, :] += dot_nn(hit, rows_in[source])
            return carry

        lax.fori_loop(0, tokens // part, one, 0)

    place(me)
    for k in (1, 2, 3, 4, 5, 6, 7):
        peer = flipped(me, k)
        row_arrival(peer).wait_recv()
        place(peer)
    part = 128

    def out_copies(n):
        at = pl.ds(n * part, part)
        return [
            pltpu.make_async_copy(embedded.at[at, :], embedded_out.at[at, :], out_sem.at[n, 0]),
            pltpu.make_async_copy(normed.at[at, :], normed_out.at[at, :], out_sem.at[n, 1]),
        ]

    for n in range(tokens // part):
        at = pl.ds(n * part, part)
        unit, _ = stats(embedded[at, :])
        normed[at, :] = unit * gain[...][None] + bias[...][None]
        for copy in out_copies(n):
            copy.start()
    for n in range(tokens // part):
        for copy in out_copies(n):
            copy.wait()
    for copy in lists:
        copy.wait_recv()
        copy.wait_send()
    for copy in asks:
        copy.wait_send()
    for k in ORDER:
        row_copy(flipped(me, k)).wait_send()


def fetch(ids, kinds, table, pos, types, gain, bias, owners):
    tokens = ids.size
    rows_local, width = table.shape
    cap = 2 * tokens // owners
    vmem = pl.BlockSpec(memory_space=pltpu.VMEM)
    hbm = pl.BlockSpec(memory_space=pl.ANY)
    full = jax.ShapeDtypeStruct((tokens, width), F32)
    dma = pltpu.SemaphoreType.DMA
    return pl.pallas_call(
        fetch_kernel,
        out_shape=(
            full,
            full,
            jax.ShapeDtypeStruct((4, 1, tokens), jnp.int32),
            jax.ShapeDtypeStruct((4, owners, 1, cap), jnp.int32),
        ),
        in_specs=[hbm] * 7,
        out_specs=(hbm, hbm, vmem, vmem),
        scratch_shapes=[
            pltpu.VMEM(ids.shape, jnp.int32),
            pltpu.VMEM(ids.shape, jnp.int32),
            pltpu.VMEM(pos.shape, BF),
            pltpu.VMEM(types.shape, BF),
            pltpu.VMEM((width,), F32),
            pltpu.VMEM((width,), F32),
            pltpu.VMEM((rows_local, width), BF),
            pltpu.VMEM((owners, 1, cap), jnp.int32),
            pltpu.VMEM((owners, 1, cap), jnp.int32),
            pltpu.VMEM((owners, cap, width), BF),
            pltpu.VMEM((owners, cap, width), BF),
            pltpu.VMEM((tokens, width), F32),
            pltpu.VMEM((tokens, width), F32),
            pltpu.VMEM((tokens, 1), jnp.int32),
            pltpu.VMEM((tokens, 1), jnp.int32),
            dma((7,)),
            dma((owners,)),
            dma((owners,)),
            dma((4,)),
            dma((4,)),
            dma((4,)),
            dma((4,)),
            dma((owners,)),
            dma((owners,)),
            dma((tokens // 128, 2)),
        ],
        compiler_params=pltpu.CompilerParams(collective_id=3, has_side_effects=True, vmem_limit_bytes=62 * MIB),
        name="fetch",
    )(ids, kinds, pos, types, gain, bias, table)


def finish_kernel(
    near, word_in, packed, feeds, ups, small,
    word, query_out, keys_out, values_out, out_out, pos_out, up_out, down_out, kinds, up_bias, *rest,
):
    vectors, (query, keys, values, out, pos, up, down, sem) = rest[:10], rest[10:]
    copies = [
        pltpu.make_async_copy(source, target, sem.at[i])
        for i, (source, target) in enumerate(
            (
                (query, query_out),
                (keys, keys_out),
                (values, values_out),
                (out, out_out),
                (pos, pos_out),
                (up, up_out),
                (down, down_out),
            )
        )
    ]
    chunks, sources, part, _ = word_in.shape
    lane = lax.broadcasted_iota(jnp.int32, (part, 128), 1)
    for c in range(chunks):
        for q in range(0, sources, 2):
            at = pl.ds((c * sources + q) * 64, 128)
            for j in range(2):
                there = pl.ds(j * 128, 128)
                one, two = word_in[c, q, :, there].astype(F32), word_in[c, q + 1, :, there].astype(F32)
                word[2 * j, :, at] = jnp.where(lane < 64, one, pltpu.roll(two, 64, 1))
                word[2 * j + 1, :, at] = jnp.where(lane < 64, pltpu.roll(one, 64, 1), two)

    @pl.when(pl.program_id(0) == 0)
    def _():
        n = near[0]
        order = ((0, 0), (1 - n, n), (n, 1 - n), (1, 1))
        per, width = query.shape
        rows = jnp.concatenate([packed[a, b] for a, b in order], 0).astype(F32)
        for i, target in enumerate((query, keys, values, out)):
            target[...] = rows[i * per : (i + 1) * per]
        pos[...] = rows[4 * per :]
        lines = []
        for i, (a, b) in enumerate(order):
            up[:, pl.ds(i * width, width)] = ups[a, b].astype(F32)
            for j in range(2):
                lines.append(feeds[a, b, :, j * 4 * per : (j + 1) * 4 * per])
        down[...] = jnp.concatenate(lines, 0).astype(F32).T
        for copy in copies:
            copy.start()
        for i, vector in enumerate(vectors):
            vector[...] = small[i, :per]
        kinds[...] = small[10:12, :per]
        up_bias[...] = jnp.concatenate([small[12 + i : 13 + i, :per] for i in range(4)], 1)[0]

    @pl.when(pl.program_id(0) == pl.num_programs(0) - 1)
    def _():
        for copy in copies:
            copy.wait()


def finish(near, word, packed, feeds, ups, small, rows_local, owners):
    chunks, sources, tall, _ = word.shape
    width = packed.shape[3]
    per = width // owners
    steps = 3
    part = tall // steps
    held = jax.ShapeDtypeStruct((per, width), F32)
    share = packed.shape[2] * 4 - 4 * per
    shapes = [held] * 4 + [
        jax.ShapeDtypeStruct((share, width), F32),
        jax.ShapeDtypeStruct((per, 4 * width), F32),
        jax.ShapeDtypeStruct((4 * per, width), F32),
        jax.ShapeDtypeStruct((2, per), F32),
        jax.ShapeDtypeStruct((4 * per,), F32),
    ] + [jax.ShapeDtypeStruct((per,), F32)] * 10
    results = pl.pallas_call(
        finish_kernel,
        grid_spec=pltpu.PrefetchScalarGridSpec(
            num_scalar_prefetch=1,
            grid=(steps,),
            in_specs=[
                pl.BlockSpec((chunks, sources, part, 256), lambda i, *_: (0, 0, i, 0)),
                fixed(packed.shape),
                fixed(feeds.shape),
                fixed(ups.shape),
                fixed(small.shape),
            ],
            out_specs=[pl.BlockSpec((4, part, width), lambda i, *_: (0, i, 0))]
            + [pl.BlockSpec(memory_space=pl.ANY)] * 7
            + [fixed(s.shape) for s in shapes[7:]],
            scratch_shapes=[pltpu.VMEM(s.shape, F32) for s in shapes[:7]] + [pltpu.SemaphoreType.DMA((7,))],
        ),
        out_shape=[jax.ShapeDtypeStruct((4, tall, width), F32)] + shapes,
        compiler_params=pltpu.CompilerParams(vmem_limit_bytes=62 * MIB),
        name="finish",
    )(near.astype(jnp.int32).reshape(1), word, packed, feeds, ups, small)
    return [results[0].reshape(rows_local, width)] + list(results[1:])


def local(
    token_ids,
    type_ids,
    lengths,
    word_table,
    pos_table,
    token_type_embeddings,
    emb_gain,
    emb_bias,
    query_weight,
    query_bias,
    key_weight,
    value_weight,
    value_bias,
    out_weight,
    out_bias,
    attn_gain,
    attn_bias,
    up_weight,
    up_bias,
    down_weight,
    down_bias,
    final_gain,
    final_bias,
    cotangent,
):
    seq_count, seq_len = token_ids.shape
    tokens = seq_count * seq_len
    width = word_table.shape[1]
    rows_local = word_table.shape[0]
    owners = lax.axis_size("vocab")
    capacity = max(2, 2 * tokens // owners)
    fast = owners == 8 and lax.axis_size("dp") == 4
    if fast:
        embedded, normed, slots, askeds = fetch(
            token_ids, type_ids, word_table, pos_table, token_type_embeddings, emb_gain, emb_bias, owners
        )
    else:
        flat_ids = token_ids.reshape(tokens)
        owner = flat_ids // rows_local
        member = (owner[:, None] == jnp.arange(owners)[None, :]).astype(jnp.int32)
        earlier = jnp.cumsum(member, 0) - member
        rank = jnp.sum(earlier * member, 1)
        slot = owner * capacity + rank
        requests = (
            jnp.full((owners * capacity,), -1, jnp.int32).at[slot].set(flat_ids - owner * rows_local)
        )
        requests = requests.reshape(owners, capacity)
        asked = lax.all_to_all(requests, "vocab", split_axis=0, concat_axis=0, tiled=True)
        valid = asked >= 0
        found = word_table[jnp.maximum(asked, 0)]
        found = jnp.where(valid[..., None], found, jnp.zeros((), jnp.bfloat16))
        returned = lax.all_to_all(found, "vocab", split_axis=0, concat_axis=0, tiled=True)
        word_rows = returned.reshape(owners * capacity, width)[slot]
        kinds = token_type_embeddings.shape[0]
        selection_matrix = (type_ids[..., None] == jnp.arange(kinds)[None, None, :]).astype(jnp.float32)
        type_rows = jnp.einsum(
            "tcr,rb->tcb",
            selection_matrix,
            token_type_embeddings.astype(jnp.float32),
            precision=lax.Precision.HIGHEST,
        )
        embedded = (
            word_rows.reshape(seq_count, seq_len, width).astype(jnp.float32)
            + pos_table.astype(jnp.float32)[None]
            + type_rows
        )
        embedded = embedded.reshape(tokens, width)
        normed = layer_norm(embedded, emb_gain, emb_bias)
    normed_low, query, keys, values, mixed_low, first, probs = attend(
        lengths, normed, query_weight, key_weight, value_weight, out_weight, query_bias, value_bias, out_bias
    )
    encoded, active_low, grad_second_low, hidden_low, grad_upper_low, grad_first, feed_sums, up_sums = feed(
        first,
        cotangent.reshape(tokens, width),
        up_weight,
        down_weight,
        up_bias,
        down_bias,
        attn_gain,
        attn_bias,
        final_gain,
        final_bias,
    )
    grad_final_gain, grad_final_bias, grad_down_bias, grad_attn_gain, grad_attn_bias, grad_out_bias = [
        feed_sums[i] for i in range(6)
    ]
    grad_up_bias = up_sums[0]
    if fast:
        (
            grad_first_low,
            grad_query_low,
            grad_keys_low,
            grad_values_low,
            raw,
            grad_pos,
            feed_own,
            up_part,
            mid_sums,
        ) = mid(
            active_low,
            grad_upper_low,
            grad_second_low,
            hidden_low,
            grad_first,
            embedded,
            query,
            keys,
            values,
            probs,
            query_weight,
            key_weight,
            value_weight,
            out_weight,
            type_ids,
            emb_gain,
        )
    else:
        grad_down = matmul_tn(active_low, grad_second_low)
        grad_up = matmul_tn(hidden_low, grad_upper_low)
        grad_first_low, grad_query_low, grad_keys_low, grad_values_low, embedding_output_gradient, mid_sums = attend_back(
            grad_first,
            embedded,
            type_ids,
            query,
            keys,
            values,
            probs,
            query_weight,
            key_weight,
            value_weight,
            out_weight,
            emb_gain,
        )
        grad_pos = jnp.sum(embedding_output_gradient.astype(jnp.float32).reshape(seq_count, seq_len, width), 0)
    grad_query_bias, grad_value_bias, grad_emb_gain, grad_emb_bias = [mid_sums[i] for i in range(4)]
    token_type_gradient = mid_sums[4:6]
    bf = jnp.bfloat16
    per = width // owners
    small = jnp.stack(
        [
            grad_query_bias,
            grad_value_bias,
            grad_out_bias,
            grad_attn_gain,
            grad_attn_bias,
            grad_emb_gain,
            grad_emb_bias,
            grad_down_bias,
            grad_final_gain,
            grad_final_bias,
            token_type_gradient[0],
            token_type_gradient[1],
        ]
    )
    if fast:
        word_pairs, packed, feeds, ups, small = tail(
            slots,
            askeds,
            grad_pos,
            feed_sums,
            up_sums,
            mid_sums,
            raw,
            normed_low,
            mixed_low,
            grad_first_low,
            grad_query_low,
            grad_keys_low,
            grad_values_low,
            feed_own,
            up_part,
            rows_local,
        )
        near = lax.axis_index("vocab") < owners // 2
        (
            grad_word,
            grad_query_weight,
            grad_key_weight,
            grad_value_weight,
            grad_out_weight,
            grad_pos,
            grad_up,
            grad_down,
            token_type_gradient,
            grad_up_bias,
            *short,
        ) = finish(near, word_pairs, packed, feeds, ups, small, rows_local, owners)
    else:
        grad_down = sum_over_all(grad_down.astype(bf))
        grad_up = sum_over_all(grad_up.astype(bf))
        places = slot[None, :] == jnp.arange(owners * capacity)[:, None]
        outgoing = matmul(
            places.astype(bf), embedding_output_gradient.reshape(tokens, width).astype(bf)
        ).astype(bf)
        hits = (jnp.arange(rows_local)[:, None] == asked.reshape(-1)[None, :]).astype(bf)
        pieces = []
        step = 256
        for start in range(0, width, step):
            incoming = lax.all_to_all(
                outgoing[:, start : start + step].reshape(owners, capacity, step),
                "vocab",
                split_axis=0,
                concat_axis=0,
                tiled=True,
            )
            dense = matmul(hits, incoming.reshape(owners * capacity, step)).astype(bf)
            pieces.append(sum_over_dp(dense))
        grad_word = jnp.concatenate(pieces, 1)
        small = small.reshape(12, owners, per).transpose(1, 0, 2).reshape(owners, 12 * per)
        small = jnp.concatenate([small, grad_up_bias.reshape(owners, 4 * per)], 1)
        wide = 4 * width
        lines = (seq_len // owners) * width // wide
        rest = per // 3 - lines
        small_lines = jnp.pad(small, ((0, 0), (0, rest * wide - 16 * per))).reshape(owners, rest, wide)
        grad_query_weight, grad_key_weight, grad_value_weight = [
            matmul_tn(normed_low, g) for g in (grad_query_low, grad_keys_low, grad_values_low)
        ]
        grad_out_weight = matmul_tn(mixed_low, grad_first_low)
        mixed_grads = jnp.concatenate(
            [grad_query_weight, grad_key_weight, grad_value_weight, grad_out_weight], 1
        ).astype(bf)
        packed = jnp.concatenate(
            [
                mixed_grads.reshape(owners, per, wide),
                grad_pos.astype(bf).reshape(owners, lines, wide),
                small_lines.astype(bf),
            ],
            1,
        )
        packed = sum_over_all(packed.reshape(-1, wide))
        weights = packed[:per]
        grad_query_weight = weights[:, :width]
        grad_key_weight = weights[:, width : 2 * width]
        grad_value_weight = weights[:, 2 * width : 3 * width]
        grad_out_weight = weights[:, 3 * width :]
        grad_pos = packed[per : per + lines].reshape(seq_len // owners, width)
        small = packed[per + lines :].reshape(-1)[: 16 * per].reshape(16, per)
        short = [small[i] for i in range(10)]
        token_type_gradient = small[10:12]
        grad_up_bias = small[12:].reshape(-1)
    (
        grad_query_bias,
        grad_value_bias,
        grad_out_bias,
        grad_attn_gain,
        grad_attn_bias,
        grad_emb_gain,
        grad_emb_bias,
        grad_down_bias,
        grad_final_gain,
        grad_final_bias,
    ) = short
    return (
        encoded.reshape(seq_count, seq_len, width),
        grad_word,
        grad_pos,
        token_type_gradient,
        grad_emb_gain,
        grad_emb_bias,
        grad_query_weight,
        grad_query_bias,
        grad_key_weight,
        grad_value_weight,
        grad_value_bias,
        grad_out_weight,
        grad_out_bias,
        grad_attn_gain,
        grad_attn_bias,
        grad_up,
        grad_up_bias,
        grad_down,
        grad_down_bias,
        grad_final_gain,
        grad_final_bias,
    )


def solution(mesh):
    placed = (
        P(("dp", "vocab"), None),
        P(("dp", "vocab"), None),
        P(("dp", "vocab")),
        P("vocab", None),
        P(),
        P(),
        P(),
        P(),
        P(),
        P(),
        P(),
        P(),
        P(),
        P(),
        P(),
        P(),
        P(),
        P(),
        P(),
        P(),
        P(),
        P(),
        P(),
        P(("dp", "vocab"), None, None),
    )
    return jax.shard_map(
        local,
        mesh=mesh,
        in_specs=placed,
        out_specs=(
            P(("dp", "vocab"), None, None),
            P("vocab", None),
            P("vocab", None),
            P(None, "vocab"),
            P("vocab"),
            P("vocab"),
            P("vocab", None),
            P("vocab"),
            P("vocab", None),
            P("vocab", None),
            P("vocab"),
            P("vocab", None),
            P("vocab"),
            P("vocab"),
            P("vocab"),
            P("vocab", None),
            P("vocab"),
            P("vocab", None),
            P("vocab"),
            P("vocab"),
            P("vocab"),
        ),
        check_vma=False,
    )
```

```python
from functools import partial

import jax
import jax.numpy as jnp
from jax import lax
from jax.experimental import pallas as pl
from jax.experimental.pallas import tpu as pltpu
from jax.sharding import PartitionSpec as P

HEADS = 12
HEAD = 64
L = 512


EPSILON = 1e-12


def layer_norm(values, gain, bias):
    center = values - jnp.mean(values, -1, keepdims=True)
    spread = jnp.mean(center * center, -1, keepdims=True)
    return center * lax.rsqrt(spread + EPSILON) * gain + bias


def matmul(left, right):
    return jnp.dot(left, right, preferred_element_type=jnp.float32)


def matmul_tn(left, right):
    return lax.dot_general(
        left, right, (((0,), (0,)), ((), ())), preferred_element_type=jnp.float32
    )


def matmul_nt(left, right):
    return lax.dot_general(
        left, right, (((1,), (1,)), ((), ())), preferred_element_type=jnp.float32
    )


def swap(value, axis_name, bit):
    size = lax.axis_size(axis_name)
    return lax.ppermute(value, axis_name, [(i, i ^ bit) for i in range(size)])


def pick(value, index, axis):
    return lax.dynamic_index_in_dim(value, index, axis, keepdims=False)


def plus(left, right):
    return (left.astype(jnp.float32) + right.astype(jnp.float32)).astype(jnp.bfloat16)


def dp_bits():
    index = lax.axis_index("dp")
    return lax.rem(index, 2), index // 2


def reorder(own, across_x, across_y, across_both):
    xb, yb = dp_bits()
    flip_x, flip_y = xb == 1, yb == 1
    rows = [[own, across_y], [across_x, across_both]]
    rows = [
        [jnp.where(flip_x, rows[1 - i][j], rows[i][j]) for j in range(2)] for i in range(2)
    ]
    rows = [
        [jnp.where(flip_y, rows[i][1 - j], rows[i][j]) for j in range(2)] for i in range(2)
    ]
    return rows


def sum_over_all(grad):
    size = lax.axis_size("vocab")
    me = lax.axis_index("vocab")
    core = lax.rem(me, 2)
    place = me // 2
    places = size // 2
    total, n = grad.shape
    r = total // size
    xb, yb = dp_bits()
    grad = grad.reshape(places, 2, r, n)
    other = swap(pick(grad, 1 - core, 1), "vocab", 1)
    held = plus(pick(grad, core, 1), other).reshape(places, 2, 2, r // 4, n)
    first, last = held[: places // 2], held[places // 2 :]
    first_in = swap(pick(first, 1 - xb, 1), "dp", 1)
    last_in = swap(pick(last, 1 - yb, 2), "dp", 2)
    first = plus(pick(first, xb, 1), first_in)
    last = plus(pick(last, yb, 2), last_in)
    first_in = swap(pick(first, 1 - yb, 1), "dp", 2)
    last_in = swap(pick(last, 1 - xb, 1), "dp", 1)
    first = plus(pick(first, yb, 1), first_in)
    last = plus(pick(last, xb, 1), last_in)
    held = jnp.concatenate([first, last], 0)
    summed = pick(held, place, 0).astype(jnp.float32)
    for step in range(1, places):
        block = pick(held, lax.rem(place + step, places), 0)
        block = lax.ppermute(
            block, "vocab", [(i, (i + 2 * step) % size) for i in range(size)]
        )
        summed = summed + block.astype(jnp.float32)
    own = summed.astype(jnp.bfloat16)
    across_x = swap(own, "dp", 1)
    across_y = swap(own, "dp", 2)
    half = n // 2
    both = jnp.concatenate(
        [swap(across_x[:, :half], "dp", 2), swap(across_y[:, half:], "dp", 1)], 1
    )
    rows = reorder(own, across_x, across_y, both)
    return jnp.stack([rows[0][0], rows[0][1], rows[1][0], rows[1][1]]).reshape(r, n).astype(jnp.float32)


def sum_over_dp(grad):
    rows, n = grad.shape
    xb, yb = dp_bits()
    held = grad.reshape(2, 2, 2, rows // 8, n)
    first, last = held[0], held[1]
    first_in = swap(pick(first, 1 - xb, 0), "dp", 1)
    last_in = swap(pick(last, 1 - yb, 1), "dp", 2)
    first = plus(pick(first, xb, 0), first_in)
    last = plus(pick(last, yb, 1), last_in)
    first_in = swap(pick(first, 1 - yb, 0), "dp", 2)
    last_in = swap(pick(last, 1 - xb, 0), "dp", 1)
    first = plus(pick(first, yb, 0), first_in)
    last = plus(pick(last, xb, 0), last_in)
    first_x = swap(first, "dp", 1)
    last_y = swap(last, "dp", 2)
    first_y = swap(jnp.stack([first, first_x]), "dp", 2)
    last_x = swap(jnp.stack([last, last_y]), "dp", 1)
    a = reorder(first, first_x, first_y[0], first_y[1])
    b = reorder(last, last_x[0], last_y, last_x[1])
    parts = [p for group in (a, b) for line in group for p in line]
    return jnp.concatenate(parts, 0).astype(jnp.float32)


BF = jnp.bfloat16
F32 = jnp.float32
MIB = 1024 * 1024


def dot_nt(left, right):
    return lax.dot_general(left, right, (((1,), (1,)), ((), ())), preferred_element_type=F32)


def dot_nn(left, right):
    return jnp.dot(left, right, preferred_element_type=F32)


def stats(values):
    center = values - jnp.mean(values, -1, keepdims=True)
    inverse = lax.rsqrt(jnp.mean(center * center, -1, keepdims=True) + EPSILON)
    return center * inverse, inverse


def norm_back(grad, gain, unit, inverse):
    scaled = grad * gain
    return inverse * (
        scaled
        - jnp.mean(scaled, -1, keepdims=True)
        - unit * jnp.mean(scaled * unit, -1, keepdims=True)
    )


def column_sum(values):
    return jnp.sum(values, 0, keepdims=True)


TAIL_SCALE = 0.33
TAIL_TERMS = (
    -0.13534782292195252,
    0.4602463244004558,
    -0.3511662200543899,
    0.4085159085223644,
    0.04721176063633592,
    0.2012267561020528,
    0.1829554472050349,
    0.1863578383326851,
)


def normal_parts(u):
    t = 1.0 / (1.0 + (TAIL_SCALE * 0.5**0.5) * jnp.abs(u))
    poly = TAIL_TERMS[0]
    for term in TAIL_TERMS[1:]:
        poly = poly * t + term
    bell = jnp.exp(u * u * -0.5)
    below = (0.5 * t) * poly * bell
    return jnp.where(u >= 0, 1.0 - below, below), bell * 0.3989422804014327


def attend_kernel(
    lengths, normed_in, wq_in, wk_in, wv_in, wo_in, query_bias_in, value_bias_in, out_bias_in,
    low_out, q_out, k_out, v_out, mixed_out, first_out, probs_out,
    first, low, q, k, v, mixed, weights, query_bias, value_bias, out_bias, probs, bias,
    load, out_sem, probs_sem,
):
    tokens, width = first.shape
    size = probs.shape[2]
    seqs = tokens // size
    tile = 256
    loads = [
        pltpu.make_async_copy(source, target, load.at[i])
        for i, (source, target) in enumerate(
            (
                (normed_in, first),
                (wq_in, weights.at[0]),
                (query_bias_in, query_bias),
                (wk_in, weights.at[1]),
                (wv_in, weights.at[2]),
                (value_bias_in, value_bias),
                (wo_in, weights.at[3]),
                (out_bias_in, out_bias),
            )
        )
    ]
    for copy in loads:
        copy.start()
    for s in range(seqs):
        seen = lax.broadcasted_iota(jnp.int32, (size, 128), 0) < lengths[s]
        bias[s] = jnp.where(seen, 0.0, -1000000000.0)
    loads[0].wait()
    low[...] = first[...].astype(BF)
    outs = [
        pltpu.make_async_copy(source, target, out_sem.at[i])
        for i, (source, target) in enumerate(((low, low_out), (q, q_out), (k, k_out), (v, v_out), (mixed, mixed_out)))
    ]
    outs[0].start()

    def spot(n):
        return pl.ds(pl.multiple_of(n * tile, tile), tile)

    def queries(n, carry):
        at = spot(n)
        q[:, at] = (dot_nn(low[...], weights[0, :, at]) + query_bias[at][None]).astype(BF) * BF(HEAD**-0.5)
        return carry

    def keys(n, carry):
        k[:, spot(n)] = dot_nn(low[...], weights[1, :, spot(n)]).astype(BF)
        return carry

    def values(n, carry):
        at = spot(n)
        v[:, at] = (dot_nn(low[...], weights[2, :, at]) + value_bias[at][None]).astype(BF)
        return carry

    loads[1].wait()
    loads[2].wait()
    lax.fori_loop(0, width // tile, queries, 0)
    outs[1].start()
    loads[3].wait()
    lax.fori_loop(0, width // tile, keys, 0)
    outs[2].start()
    loads[4].wait()
    loads[5].wait()
    lax.fori_loop(0, width // tile, values, 0)
    outs[3].start()
    group = HEADS // 4

    def probs_copy(n):
        slot = lax.rem(n, 2)
        return pltpu.make_async_copy(
            probs.at[slot], probs_out.at[lax.div(n, group), pl.ds(4 * lax.rem(n, group), 4)], probs_sem.at[slot]
        )

    def heads(n, carry):
        @pl.when(n >= 2)
        def _():
            probs_copy(n - 2).wait()

        slot = lax.rem(n, 2)
        s = lax.div(n, group)
        rows = pl.ds(pl.multiple_of(s * size, size), size)
        held = []
        for i in range(2):
            j = 2 * lax.rem(n, group) + i
            at = pl.ds(pl.multiple_of(j * 2 * HEAD, 2 * HEAD), 2 * HEAD)
            q2, k2, turned = q[rows, at], k[rows, at], v[rows, at].T
            lane = lax.broadcasted_iota(jnp.int32, k2.shape, 1)
            for side in range(2):
                mine = (lane >= HEAD) if side else (lane < HEAD)
                held.append((at, turned[side * HEAD : (side + 1) * HEAD], jnp.where(mine, k2, jnp.zeros_like(k2)), q2))
        parts = []
        ahead = dot_nt(held[0][2], held[0][3])
        for i in range(4):
            at, turned, _, _ = held[i]
            scores = ahead + jnp.concatenate([bias[s]] * (size // 128), 1)
            if i < 3:
                ahead = dot_nt(held[i + 1][2], held[i + 1][3])
            expd = jnp.exp(scores - jnp.max(scores, 0, keepdims=True))
            chances = (expd * (1.0 / jnp.sum(expd, 0, keepdims=True))).astype(BF)
            probs[slot, i] = chances
            parts.append(dot_nn(turned, chances))
            if i % 2 == 1:
                mixed[rows, at] = jnp.concatenate(parts[-2:], 0).T.astype(BF)
        probs_copy(n).start()
        return carry

    lax.fori_loop(0, seqs * group, heads, 0)
    outs[4].start()
    loads[6].wait()
    loads[7].wait()

    def first_copy(n):
        return pltpu.make_async_copy(first.at[:, spot(n)], first_out.at[:, spot(n)], out_sem.at[5 + n])

    def close(n, carry):
        at = spot(n)
        first[:, at] += dot_nn(mixed[...], weights[3, :, at]) + out_bias[at][None]
        first_copy(n).start()
        return carry

    lax.fori_loop(0, width // tile, close, 0)
    for copy in outs + [first_copy(n) for n in range(width // tile)]:
        copy.wait()
    for n in (seqs * group - 2, seqs * group - 1):
        probs_copy(n).wait()


def fixed(shape):
    return pl.BlockSpec(shape, lambda i, *_: (0,) * len(shape), pipeline_mode=pl.Buffered(1))


def rows_of(rows, width):
    return pl.BlockSpec((rows, width), lambda i, *_: (i, 0))


def row(vector):
    return vector.reshape(1, -1)


def attend(lengths, normed, wq, wk, wv, wo, query_bias, value_bias, out_bias):
    tokens, width = normed.shape
    seqs = lengths.shape[0]
    size = tokens // seqs
    low = jax.ShapeDtypeStruct((tokens, width), BF)
    hbm = pl.BlockSpec(memory_space=pl.ANY)
    small = pltpu.VMEM((tokens, width), BF)
    vector = pltpu.VMEM((width,), F32)
    return pl.pallas_call(
        attend_kernel,
        in_specs=[pl.BlockSpec(memory_space=pltpu.SMEM)] + [hbm] * 8,
        out_specs=[hbm] * 7,
        out_shape=[low] * 5
        + [jax.ShapeDtypeStruct((tokens, width), F32), jax.ShapeDtypeStruct((seqs, HEADS, size, size), BF)],
        scratch_shapes=[
            pltpu.VMEM((tokens, width), F32),
            small,
            small,
            small,
            small,
            small,
            pltpu.VMEM((4, width, width), BF),
            vector,
            vector,
            vector,
            pltpu.VMEM((2, 4, size, size), BF),
            pltpu.VMEM((seqs, size, 128), F32),
            pltpu.SemaphoreType.DMA((8,)),
            pltpu.SemaphoreType.DMA((5 + width // 256,)),
            pltpu.SemaphoreType.DMA((2,)),
        ],
        compiler_params=pltpu.CompilerParams(vmem_limit_bytes=62 * MIB),
        cost_estimate=pl.CostEstimate(flops=20 * 10**9, bytes_accessed=30 * 10**6, transcendentals=0),
        name="attend",
    )(lengths, normed, wq, wk, wv, wo, query_bias, value_bias, out_bias)


def feed_kernel(
    first, cotangent, up, down, up_bias, down_bias, attn_gain, attn_bias, final_gain, final_bias,
    encoded, active, second_low, hidden_low, upper_low, first_grad, sums, up_sum,
    slope,
):
    width = first.shape[1]
    units = up.shape[1]
    block = 768
    unit, inverse = stats(first[...])
    hidden = unit * attn_gain[...][None] + attn_bias[...][None]
    hidden_low[...] = hidden.astype(BF)
    total = hidden + down_bias[...][None]
    for n in range(units // block):
        at = pl.ds(n * block, block)
        upper = dot_nn(hidden_low[...], up[:, at]) + up_bias[at][None]
        below, density = normal_parts(upper)
        active[:, at] = (upper * below).astype(BF)
        slope[:, at] = below + upper * density
        total = total + dot_nn(active[:, at], down[at, :])
    unit_out, inverse_out = stats(total)
    encoded[...] = unit_out * final_gain[...][None] + final_bias[...][None]
    grad = cotangent[...].astype(F32)
    grad_second = norm_back(grad, final_gain[...][None], unit_out, inverse_out)
    second_low[...] = grad_second.astype(BF)

    @pl.when(pl.program_id(0) == 0)
    def _():
        sums[...] = jnp.zeros_like(sums)
        up_sum[...] = jnp.zeros_like(up_sum)

    sums[0:1, :] += column_sum(grad * unit_out)
    sums[1:2, :] += column_sum(grad)
    sums[2:3, :] += column_sum(grad_second)
    total = grad_second
    for n in range(units // block):
        at = pl.ds(n * block, block)
        grad_upper = dot_nt(second_low[...], down[at, :]) * slope[:, at]
        up_sum[:, at] += column_sum(grad_upper)
        upper_low[:, at] = grad_upper.astype(BF)
        total = total + dot_nt(upper_low[:, at], up[:, at])
    grad_first = norm_back(total, attn_gain[...][None], unit, inverse)
    sums[3:4, :] += column_sum(total * unit)
    sums[4:5, :] += column_sum(total)
    sums[5:6, :] += column_sum(grad_first)
    first_grad[...] = grad_first


def feed(first, cotangent, up, down, up_bias, down_bias, attn_gain, attn_bias, final_gain, final_bias):
    tokens, width = first.shape
    units = up.shape[1]
    tile = 512
    part, wide = rows_of(tile, width), rows_of(tile, units)
    vector = fixed((width,))
    return pl.pallas_call(
        feed_kernel,
        grid=(tokens // tile,),
        in_specs=[part, part, fixed((width, units)), fixed((units, width)), fixed((units,))] + [vector] * 5,
        out_specs=[part, wide, part, part, wide, part, fixed((8, width)), fixed((1, units))],
        out_shape=[
            jax.ShapeDtypeStruct((tokens, width), F32),
            jax.ShapeDtypeStruct((tokens, units), BF),
            jax.ShapeDtypeStruct((tokens, width), BF),
            jax.ShapeDtypeStruct((tokens, width), BF),
            jax.ShapeDtypeStruct((tokens, units), BF),
            jax.ShapeDtypeStruct((tokens, width), F32),
            jax.ShapeDtypeStruct((8, width), F32),
            jax.ShapeDtypeStruct((1, units), F32),
        ],
        scratch_shapes=[pltpu.VMEM((tile, units), F32)],
        compiler_params=pltpu.CompilerParams(vmem_limit_bytes=60 * MIB),
        cost_estimate=pl.CostEstimate(flops=40 * 10**9, bytes_accessed=40 * 10**6, transcendentals=0),
        name="feed",
    )(
        first, cotangent, up, down, up_bias, down_bias, attn_gain, attn_bias, final_gain, final_bias
    )


def attend_back_kernel(
    grad_first, embedded, kinds, q_in, k_in, v_in, probs_in, wq, wk, wv, wo, emb_gain,
    first_low, dq, dk, dv, emb_low, sums,
    grad_mixed, total,
):
    tokens, width = grad_first.shape
    tile = 256

    @pl.when(pl.program_id(0) == 0)
    def _():
        sums[...] = jnp.zeros_like(sums)

    first_low[...] = grad_first[...].astype(BF)

    def open_(n, carry):
        at = pl.ds(pl.multiple_of(n * tile, tile), tile)
        grad_mixed[:, at] = dot_nt(first_low[...], wo[at, :]).astype(BF)
        return carry

    lax.fori_loop(0, width // tile, open_, 0)

    def pair(j, carry):
        at = pl.ds(pl.multiple_of(j * 2 * HEAD, 2 * HEAD), 2 * HEAD)
        q, k, v, grad = q_in[:, at], k_in[:, at], v_in[:, at], grad_mixed[:, at]
        turned = k.T
        lane = lax.broadcasted_iota(jnp.int32, k.shape, 1)
        parts = []
        grad_k = jnp.zeros(k.shape, F32)
        grad_v = jnp.zeros(k.shape, F32)
        for side in range(2):
            mine = (lane >= HEAD) if side else (lane < HEAD)
            none = jnp.zeros_like(k)
            probs = probs_in[0, 2 * j + side]
            grad_probs = dot_nt(jnp.where(mine, v, none), grad)
            grad_v = grad_v + dot_nn(probs, jnp.where(mine, grad, none))
            wide = probs.astype(F32)
            both = wide * grad_probs
            scores = (both - wide * jnp.sum(both, 0, keepdims=True)).astype(BF)
            grad_k = grad_k + dot_nn(scores, jnp.where(mine, q, none))
            parts.append(dot_nn(turned[side * HEAD : (side + 1) * HEAD], scores))
        grad_q = jnp.concatenate(parts, 0).T * HEAD**-0.5
        dq[:, at] = grad_q.astype(BF)
        dk[:, at] = grad_k.astype(BF)
        dv[:, at] = grad_v.astype(BF)
        sums[0:1, at] += column_sum(grad_q)
        sums[1:2, at] += column_sum(grad_v)
        return carry

    lax.fori_loop(0, HEADS // 2, pair, 0)

    def close(n, carry):
        at = pl.ds(pl.multiple_of(n * tile, tile), tile)
        total[:, at] = (
            grad_first[:, at]
            + dot_nt(dq[...], wq[at, :])
            + dot_nt(dk[...], wk[at, :])
            + dot_nt(dv[...], wv[at, :])
        )
        return carry

    lax.fori_loop(0, width // tile, close, 0)
    rows = 128

    def last(n, carry):
        at = pl.ds(pl.multiple_of(n * rows, rows), rows)
        unit, inverse = stats(embedded[at, :])
        grad = total[at, :]
        grad_emb = norm_back(grad, emb_gain[...], unit, inverse)
        emb_low[at, :] = grad_emb.astype(BF)
        sums[2:3, :] += column_sum(grad * unit)
        sums[3:4, :] += column_sum(grad)
        kind = kinds[at, :]
        for t in range(2):
            sums[4 + t : 5 + t, :] += column_sum(jnp.where(kind == t, grad_emb, 0.0))
        return carry

    lax.fori_loop(0, tokens // rows, last, 0)


def attend_back(grad_first, embedded, kinds, q, k, v, probs, wq, wk, wv, wo, emb_gain):
    tokens, width = grad_first.shape
    seqs, _, size, _ = probs.shape
    part = rows_of(size, width)
    low = jax.ShapeDtypeStruct((tokens, width), BF)
    return pl.pallas_call(
        attend_back_kernel,
        grid=(seqs,),
        in_specs=[part, part, rows_of(size, 1)]
        + [part] * 3
        + [pl.BlockSpec((1, HEADS, size, size), lambda i: (i, 0, 0, 0))]
        + [fixed((width, width))] * 4
        + [fixed((1, width))],
        out_specs=[part] * 5 + [fixed((8, width))],
        out_shape=[low] * 5 + [jax.ShapeDtypeStruct((8, width), F32)],
        scratch_shapes=[pltpu.VMEM((size, width), BF), pltpu.VMEM((size, width), F32)],
        compiler_params=pltpu.CompilerParams(vmem_limit_bytes=60 * MIB),
        cost_estimate=pl.CostEstimate(flops=30 * 10**9, bytes_accessed=40 * 10**6, transcendentals=0),
        name="attend_back",
    )(grad_first, embedded, kinds.reshape(tokens, 1), q, k, v, probs, wq, wk, wv, wo, row(emb_gain))


MESH = pl.DeviceIdType.MESH


def column_of(lines, column):
    count, size = lines.shape
    for s in range(count):
        line = jnp.broadcast_to(lines[s : s + 1, :].astype(F32), (8, size))
        column[pl.ds(s * size, size), :] = line.T[:, 0:1].astype(jnp.int32)


def mid_kernel(
    active, upper_low, second_low, hidden_low, grad_first, embedded, q_in, k_in, v_in, probs_in, wq, wk, wv, wo,
    kinds_in, emb_gain_in,
    first_out, dq_out, dk_out, dv_out, raw_out, pos_out, feed_out, part_out, sums,
    stage, lhs, turned, grads, core_in, in_1a, in_1b, in_2a, in_2b, in_z, kept,
    first, low, grad_mixed, q, k, v, dq, dk, dv, weights, table, raw, pos, probs, kind_column, kinds, emb_gain,
    load, stage_sem, probs_sem, out_sem, send, recv,
):
    tokens, width = lhs.shape
    seqs, size = kinds.shape
    per = grads.shape[3]
    me = lax.axis_index("vocab")
    spot = lax.axis_index("dp")
    core, place = lax.rem(me, 2), lax.div(me, 2)
    xb, yb = lax.rem(spot, 2), lax.div(spot, 2)
    across_x = {"dp": spot + 1 - 2 * xb}
    across_y = {"dp": spot + 2 - 4 * yb}
    partner = {"vocab": me + 1 - 2 * core}
    block = 768
    blocks = active.shape[1] // block

    def stage_copy(source, n):
        at = pl.ds(pl.multiple_of(n * block, block), block)
        slot = lax.rem(n, 2)
        return pltpu.make_async_copy(source.at[:, at], stage.at[slot], stage_sem.at[slot])

    def probs_copy(n):
        group = HEADS // 4
        slot = lax.rem(n, 2)
        return pltpu.make_async_copy(
            probs_in.at[lax.div(n, group), pl.ds(4 * lax.rem(n, group), 4)], probs.at[slot], probs_sem.at[slot]
        )

    second_copy = pltpu.make_async_copy(second_low, lhs, load.at[0])
    hidden_copy = pltpu.make_async_copy(hidden_low, lhs, load.at[1])
    second_copy.start()
    stage_copy(active, 0).start()
    stage_copy(active, 1).start()
    loads = [
        pltpu.make_async_copy(source, target, load.at[2 + i])
        for i, (source, target) in enumerate(
            (
                (grad_first, first),
                (wo, weights.at[3]),
                (q_in, q),
                (k_in, k),
                (v_in, v),
                (wq, weights.at[0]),
                (wk, weights.at[1]),
                (wv, weights.at[2]),
                (embedded, table),
                (kinds_in, kinds),
                (emb_gain_in, emb_gain),
            )
        )
    ]
    barrier = pltpu.get_barrier_semaphore()
    places = [{"vocab": 2 * flipped(place, k) + core} for k in (1, 2, 3)]
    for peer in [partner, across_x, across_y] + places:
        pl.semaphore_signal(barrier, inc=1, device_id=peer, device_id_type=MESH)
    pl.semaphore_wait(barrier, 6)

    def remote(src, dst, at, peer):
        return pltpu.make_async_remote_copy(
            src_ref=src, dst_ref=dst, send_sem=send.at[at], recv_sem=recv.at[at], device_id=peer, device_id_type=MESH
        )

    def columns(n):
        return pl.ds(pl.multiple_of(n * width, width), width)

    def core_copy(g, n):
        if g == 0:
            return remote(grads.at[0, n, 1 - core], core_in.at[0, n], 16 + n, partner)
        return remote(
            grads.at[1, :, 1 - core, :, columns(n)], core_in.at[1, :, :, columns(n)], 20 + n, partner
        )

    half = 2 * width

    def wide(b):
        return pl.ds(pl.multiple_of(b * half, half), half)

    def narrow(b, c):
        return pl.ds(pl.multiple_of(b * half + c * width, width), width)

    def first_copies(g):
        return [
            remote(grads.at[g, pl.ds(0, 2), core, :, wide(1 - xb)], in_1a.at[g], 5 * g + 1, across_x),
            remote(grads.at[g, pl.ds(2, 2), core, :, wide(1 - yb)], in_1b.at[g], 5 * g + 2, across_y),
        ]

    def second_copies(g):
        return [
            remote(grads.at[g, pl.ds(0, 2), core, :, narrow(xb, 1 - yb)], in_2a.at[g], 5 * g + 3, across_y),
            remote(grads.at[g, pl.ds(2, 2), core, :, narrow(yb, 1 - xb)], in_2b.at[g], 5 * g + 4, across_x),
        ]

    def add(view, value):
        view[...] = (view[...].astype(F32) + value.astype(F32)).astype(BF)

    def core_step(g):
        rows = per // 2

        def one(n, carry):
            core_copy(g, n).wait_recv()
            if g == 0:
                for i in range(2):
                    at = pl.ds(i * rows, rows)
                    add(grads.at[0, n, core, at, :], core_in[0, n, at, :])
            else:
                for z in range(4):
                    add(grads.at[1, z, core, :, columns(n)], core_in[1, z, :, columns(n)])
            return carry

        lax.fori_loop(0, 4, one, 0)
        for copy in first_copies(g):
            copy.start()

    def first_step(g):
        for copy in first_copies(g):
            copy.wait_recv()

        def one(z, carry):
            add(grads.at[g, z, core, :, wide(xb)], in_1a[g, z])
            add(grads.at[g, 2 + z, core, :, wide(yb)], in_1b[g, z])
            return carry

        lax.fori_loop(0, 2, one, 0)
        for copy in second_copies(g):
            copy.start()

    def owned(g, z):
        at = 2 * xb + yb + lax.div(z, 2) * (yb - xb)
        return grads.at[g, z, core, :, pl.ds(pl.multiple_of(at * width, width), width)]

    def place_copies(g):
        return [
            remote(owned(g, flipped(place, k)), in_z.at[g, k - 1], 10 + 3 * g + k - 1, places[k - 1]) for k in (3, 2, 1)
        ]

    def place_step(g):
        for copy in place_copies(g):
            copy.wait_recv()
        total = owned(g, place)[...].astype(F32)
        for k in range(3):
            total = total + in_z[g, k].astype(F32)
        kept[g] = total.astype(BF)

    def second_step(g):
        for copy in second_copies(g):
            copy.wait_recv()
        for z in range(2):
            add(grads.at[g, z, core, :, narrow(xb, yb)], in_2a[g, z])
            add(grads.at[g, 2 + z, core, :, narrow(yb, xb)], in_2b[g, z])
        for copy in place_copies(g):
            copy.start()

    corner = 256

    def turn():
        def one(i, carry):
            at = pl.ds(pl.multiple_of(i * corner, corner), corner)
            for j in range(width // corner):
                there = pl.ds(j * corner, corner)
                turned[there, at] = lhs[at, there].T
            return carry

        lax.fori_loop(0, tokens // corner, one, 0)

    second_copy.wait()
    turn()
    hidden_copy.start()
    probs_copy(0).start()
    for copy in loads:
        copy.start()
    share = block // 2

    def down_block(n, carry):
        stage_copy(active, n).wait()
        slot = lax.rem(n, 2)
        for c in range(2):
            out = dot_nn(turned[...], stage[slot, :, c * share : (c + 1) * share]).astype(BF)
            for j in range(8):
                grads[0, n, c, :, j * share : (j + 1) * share] = out[j * per : (j + 1) * per]
        core_copy(0, n).start()

        @pl.when(n < 2)
        def _():
            stage_copy(active, n + 2).start()

        @pl.when(n >= 2)
        def _():
            stage_copy(upper_low, n - 2).start()

        return carry

    lax.fori_loop(0, blocks, down_block, 0)
    core_step(0)
    hidden_copy.wait()
    turn()

    def up_block(n, carry):
        stage_copy(upper_low, n).wait()
        slot = lax.rem(n, 2)
        for c in range(2):
            out = dot_nn(turned[...], stage[slot, :, c * share : (c + 1) * share]).astype(BF)
            at = pl.ds(pl.multiple_of(n * block + c * share, 128), share)
            for j in range(8):
                grads[1, j // 2, j % 2, :, at] = out[j * per : (j + 1) * per]
        core_copy(1, n).start()

        @pl.when(n < 2)
        def _():
            stage_copy(upper_low, n + 2).start()

        return carry

    lax.fori_loop(0, blocks, up_block, 0)
    core_step(1)

    for copy in loads:
        copy.wait()
    sums[...] = jnp.zeros_like(sums)
    low[...] = first[...].astype(BF)
    first_copy = pltpu.make_async_copy(low, first_out, out_sem.at[4])
    first_copy.start()
    tile = 256

    def open_(n, carry):
        at = pl.ds(pl.multiple_of(n * tile, tile), tile)
        grad_mixed[:, at] = dot_nt(low[...], weights[3, at, :]).astype(BF)
        return carry

    lax.fori_loop(0, width // tile, open_, 0)

    def pair(n, slot, i):
        rows = pl.ds(pl.multiple_of(lax.div(n, HEADS // 2) * size, size), size)
        at = pl.ds(pl.multiple_of(lax.rem(n, HEADS // 2) * 2 * HEAD, 2 * HEAD), 2 * HEAD)
        q2, k2, v2, grad = q[rows, at], k[rows, at], v[rows, at], grad_mixed[rows, at]
        across = k2.T
        lane = lax.broadcasted_iota(jnp.int32, k2.shape, 1)
        parts = []
        grad_k = jnp.zeros(k2.shape, F32)
        grad_v = jnp.zeros(k2.shape, F32)
        for side in range(2):
            mine = (lane >= HEAD) if side else (lane < HEAD)
            none = jnp.zeros_like(k2)
            chances = probs[slot, 2 * i + side]
            grad_probs = dot_nt(jnp.where(mine, v2, none), grad)
            grad_v = grad_v + dot_nn(chances, jnp.where(mine, grad, none))
            full = chances.astype(F32)
            both = full * grad_probs
            scores = (both - full * jnp.sum(both, 0, keepdims=True)).astype(BF)
            grad_k = grad_k + dot_nn(scores, jnp.where(mine, q2, none))
            parts.append(dot_nn(across[side * HEAD : (side + 1) * HEAD], scores))
        grad_q = jnp.concatenate(parts, 0).T * HEAD**-0.5
        dq[rows, at] = grad_q.astype(BF)
        dk[rows, at] = grad_k.astype(BF)
        dv[rows, at] = grad_v.astype(BF)
        sums[0:1, at] += column_sum(grad_q)
        sums[1:2, at] += column_sum(grad_v)

    groups = seqs * HEADS // 4

    def pairs(n, carry):
        @pl.when(n + 1 < groups)
        def _():
            probs_copy(n + 1).start()

        probs_copy(n).wait()
        slot = lax.rem(n, 2)
        for i in range(2):
            pair(2 * n + i, slot, i)

        @pl.when(n == 2)
        def _():
            second_step(0)

        @pl.when(n == 3)
        def _():
            first_step(1)

        @pl.when(n == 5)
        def _():
            second_step(1)

        return carry

    first_step(0)
    lax.fori_loop(0, groups, pairs, 0)
    out_copies = [
        pltpu.make_async_copy(source, target, out_sem.at[5 + i])
        for i, (source, target) in enumerate(((dq, dq_out), (dk, dk_out), (dv, dv_out)))
    ]
    for copy in out_copies:
        copy.start()

    def close(n, carry):
        at = pl.ds(pl.multiple_of(n * tile, tile), tile)
        first[:, at] = (
            first[:, at]
            + dot_nt(dq[...], weights[0, at, :])
            + dot_nt(dk[...], weights[1, at, :])
            + dot_nt(dv[...], weights[2, at, :])
        )
        return carry

    lax.fori_loop(0, width // tile, close, 0)
    column_of(kinds, kind_column)
    few = 128
    lane = lax.broadcasted_iota(jnp.int32, (few, 128), 1)

    def back(at):
        unit, inverse = stats(table[at, :])
        grad = first[at, :]
        grad_emb = norm_back(grad, emb_gain[...][None], unit, inverse)
        sums[2:3, :] += column_sum(grad * unit)
        sums[3:4, :] += column_sum(grad)
        kind = kind_column[at, :]
        for t in range(2):
            sums[4 + t : 5 + t, :] += column_sum(jnp.where(kind == t, grad_emb, 0.0))
        return grad_emb

    def last(n, carry):
        at = pl.ds(pl.multiple_of(n * few, few), few)
        left = back(at)
        right = back(pl.ds(pl.multiple_of(size + n * few, few), few))
        pos[at, :] = (left + right).astype(BF)
        for t in range(width // 128):
            one, two = left[:, t * 128 : (t + 1) * 128], right[:, t * 128 : (t + 1) * 128]
            q = 2 * (t % 2)
            raw[t // 2, q, at, :] = jnp.where(lane < 64, one, pltpu.roll(two, 64, 1)).astype(BF)
            raw[t // 2, q + 1, at, :] = jnp.where(lane < 64, pltpu.roll(one, 64, 1), two).astype(BF)
        return carry

    lax.fori_loop(0, size // few, last, 0)
    raw_copy = pltpu.make_async_copy(raw, raw_out, out_sem.at[3])
    raw_copy.start()
    pos_copy = pltpu.make_async_copy(pos, pos_out, out_sem.at[8])
    pos_copy.start()
    place_step(0)
    place_step(1)
    feed_copy = pltpu.make_async_copy(kept.at[0], feed_out, out_sem.at[2])
    feed_copy.start()
    part_copy = pltpu.make_async_copy(kept.at[1], part_out, out_sem.at[0])
    part_copy.start()
    for copy in [first_copy, raw_copy, pos_copy, feed_copy, part_copy] + out_copies:
        copy.wait()
    for g in range(2):
        for copy in [core_copy(g, n) for n in range(4)] + first_copies(g) + second_copies(g) + place_copies(g):
            copy.wait_send()


def mid(
    active, upper_low, second_low, hidden_low, grad_first, embedded, q, k, v, probs, wq, wk, wv, wo, kinds, emb_gain
):
    tokens, width = grad_first.shape
    seqs, heads, size, _ = probs.shape
    units = active.shape[1]
    per = width // 8
    wide = 4 * width
    vmem = pl.BlockSpec(memory_space=pltpu.VMEM)
    hbm = pl.BlockSpec(memory_space=pl.ANY)
    low = jax.ShapeDtypeStruct((tokens, width), BF)
    small = pltpu.VMEM((tokens, width), BF)
    large = pltpu.VMEM((tokens, width), F32)
    return pl.pallas_call(
        mid_kernel,
        out_shape=[low] * 4
        + [
            jax.ShapeDtypeStruct((3, 4, size, 128), BF),
            jax.ShapeDtypeStruct((size, width), BF),
            jax.ShapeDtypeStruct((per, width), BF),
            jax.ShapeDtypeStruct((per, width), BF),
            jax.ShapeDtypeStruct((8, width), F32),
        ],
        in_specs=[hbm] * 16,
        out_specs=[hbm] * 8 + [vmem],
        scratch_shapes=[
            pltpu.VMEM((2, tokens, 768), BF),
            small,
            pltpu.VMEM((width, tokens), BF),
            pltpu.VMEM((2, 4, 2, per, wide), BF),
            pltpu.VMEM((2, 4, per, wide), BF),
            pltpu.VMEM((2, 2, per, wide // 2), BF),
            pltpu.VMEM((2, 2, per, wide // 2), BF),
            pltpu.VMEM((2, 2, per, width), BF),
            pltpu.VMEM((2, 2, per, width), BF),
            pltpu.VMEM((2, 3, per, width), BF),
            pltpu.VMEM((2, per, width), BF),
            large,
            small,
            small,
            small,
            small,
            small,
            small,
            small,
            small,
            pltpu.VMEM((4, width, width), BF),
            large,
            pltpu.VMEM((3, 4, size, 128), BF),
            pltpu.VMEM((size, width), BF),
            pltpu.VMEM((2, 4, size, size), BF),
            pltpu.VMEM((tokens, 1), jnp.int32),
            pltpu.VMEM((seqs, size), jnp.int32),
            pltpu.VMEM((width,), F32),
            pltpu.SemaphoreType.DMA((13,)),
            pltpu.SemaphoreType.DMA((2,)),
            pltpu.SemaphoreType.DMA((2,)),
            pltpu.SemaphoreType.DMA((9,)),
            pltpu.SemaphoreType.DMA((24,)),
            pltpu.SemaphoreType.DMA((24,)),
        ],
        compiler_params=pltpu.CompilerParams(
            collective_id=2, has_side_effects=True, vmem_limit_bytes=62 * MIB
        ),
        name="mid",
    )(
        active, upper_low, second_low, hidden_low, grad_first, embedded, q, k, v, probs, wq, wk, wv, wo,
        kinds, emb_gain,
    )


def flipped(index, bits):
    out = 0
    for place in range(3):
        bit = lax.rem(lax.div(index, 1 << place), 2)
        out = out + (1 << place) * (1 - bit if (bits >> place) & 1 else bit)
    return out


def exchanged(index, bits):
    out = 0
    for place in range(2):
        one = lax.rem(lax.div(index, 1 << place), 2)
        two = lax.rem(lax.div(bits, 1 << place), 2)
        out = out + (1 << place) * (one + two - 2 * one * two)
    return out


ORDER = (6, 7, 4, 5, 2, 3, 1)


def tail_kernel(
    slots, asked, pos, feed_sums, up_sums, mid_sums, raw, normed, mixed, gfirst, dq, dk, dv, feed_own, up_part,
    word, packed, feed_out, up_out, small_out,
    tok, hot, og, inc, rhs, kinds, places, total, dense, ops, turned, wbuf, wcore, w1a, w1b, w2a, w2b, wz, wown, small_by, small_in, small_dp,
    load_sem, t_send, t_recv, z_send, z_recv, d_send, d_recv, w_send, w_recv, s_send, s_recv, own_sem,
):
    chunks, owners, sources, pairs, lanes = og.shape
    half, width = pos.shape
    tokens = 2 * half
    cap = 2 * pairs
    tall = dense.shape[1]
    me = lax.axis_index("vocab")
    spot = lax.axis_index("dp")
    core, place = lax.rem(me, 2), lax.div(me, 2)
    xb, yb = lax.rem(spot, 2), lax.div(spot, 2)
    across_x = {"dp": spot + 1 - 2 * xb}
    across_y = {"dp": spot + 2 - 4 * yb}

    barrier = pltpu.get_barrier_semaphore()
    for k in ORDER:
        pl.semaphore_signal(barrier, inc=1, device_id={"vocab": flipped(me, k)}, device_id_type=MESH)
    for k in (1, 2, 3):
        pl.semaphore_signal(barrier, inc=1, device_id={"dp": flipped(spot, k)}, device_id_type=MESH)
    loads = [
        pltpu.make_async_copy(ref, ops.at[i], load_sem.at[i])
        for i, ref in enumerate((normed, dq, dk, dv, mixed, gfirst))
    ]
    for load in loads:
        load.start()
    per = width // owners
    order = ((1, 0), (1, 1), (0, 5), (0, 3), (0, 4), (1, 2), (1, 3), (0, 2), (0, 0), (0, 1), (1, 4), (1, 5))
    for v in range(owners):
        small_by[v] = jnp.zeros(small_by.shape[1:], F32)
        for i, (which, line) in enumerate(order):
            source = (feed_sums, mid_sums)[which]
            small_by[v, i : i + 1, :per] = source[line : line + 1, v * per : (v + 1) * per]
        for i in range(4):
            at = (4 * v + i) * per
            small_by[v, 12 + i : 13 + i, :per] = up_sums[:, at : at + per]
    pl.semaphore_wait(barrier, len(ORDER) + 3)

    def remote(src, dst, send, recv, peer):
        return pltpu.make_async_remote_copy(
            src_ref=src, dst_ref=dst, send_sem=send, recv_sem=recv, device_id=peer, device_id_type=MESH
        )

    def start(copies):
        for copy in copies:
            copy.start()

    def arrived(copies):
        for copy in copies:
            copy.wait_recv()

    def gone(copies):
        for copy in copies:
            copy.wait_send()

    def token_copy(c, k):
        peer = flipped(spot, k) if isinstance(k, int) else exchanged(spot, k)
        return remote(raw.at[c, peer], tok.at[c, spot], t_send.at[c, k], t_recv.at[c, k], {"dp": peer})

    def token_copies(c):
        return [token_copy(c, k) for k in (1, 2, 3)]

    def token_own(c):
        return pltpu.make_async_copy(raw.at[c, spot], tok.at[c, spot], own_sem.at[c])

    for c in range(chunks):
        start(token_copies(c))
        token_own(c).start()

    def row_copies(c, j):
        source = flipped(spot, j) if isinstance(j, int) else exchanged(spot, j)
        copies = []
        for k in ORDER:
            peer = flipped(me, k)
            copies.append(
                remote(
                    og.at[c, peer, source],
                    inc.at[c, me, source],
                    z_send.at[c, j, k],
                    z_recv.at[c, j, k],
                    {"vocab": peer},
                )
            )
        return copies

    def make_hot(d):
        def one(v, carry):
            wanted = lax.broadcasted_iota(jnp.int32, (cap, half), 0) + v * cap
            for s in range(2):
                hit = wanted == slots[d, :, s * half : (s + 1) * half]
                hot[d, s, v] = jnp.where(hit, 1.0, 0.0).astype(BF)
            return carry

        lax.fori_loop(0, owners, one, 0)

    def fill(d, first, count):
        lane = lax.broadcasted_iota(jnp.int32, (pairs, lanes), 1)
        values = jnp.concatenate([tok[first + i, d] for i in range(count)], 1)
        early = dot_nn(hot[d, 0].reshape(owners * cap, half), values)
        late = dot_nn(hot[d, 1].reshape(owners * cap, half), values)
        for v in range(owners):
            low, high = slice(v * cap, v * cap + pairs), slice(v * cap + pairs, (v + 1) * cap)
            for i in range(count):
                there = slice(i * lanes, (i + 1) * lanes)
                straight = jnp.where(lane < 64, early[low, there], late[high, there])
                crossed = jnp.where(lane < 64, early[high, there], late[low, there])
                og[first + i, v, d] = (straight + pltpu.roll(crossed, 64, 1)).astype(BF)

    def own_copy(c):
        return pltpu.make_async_copy(og.at[c, me], inc.at[c, me], own_sem.at[11 + c])

    def fill_first(j):
        d = flipped(spot, j) if isinstance(j, int) else exchanged(spot, j)
        make_hot(d)
        if isinstance(j, int) and j == 0:
            token_own(0).wait()
        else:
            token_copy(0, j).wait_recv()
        fill(d, 0, 1)
        start(row_copies(0, j))

    depth = 1024

    def sort_rows():
        for v in range(owners):
            lines = []
            for d in range(sources):
                for h in range(2):
                    ids = asked[d, v, :, h * pairs : (h + 1) * pairs]
                    kind = sum(jnp.where(ids >= n * tall, 1, 0) for n in (1, 2, 3))
                    places[h, :, pl.ds((v * sources + d) * pairs, pairs)] = ids - tall * kind
                    lines.append(kind)
            kinds[v] = jnp.concatenate(lines, 0).astype(F32).T.astype(jnp.int32)

    def prepare(c):
        def one(v, carry):
            lane = lax.broadcasted_iota(jnp.int32, (pairs, lanes), 1)
            side = jnp.where(lane < 64, 0, 1)
            for d in range(sources):
                at = pl.ds(pl.multiple_of((v * sources + d) * pairs, pairs), pairs)
                straight = inc[c, v, d].astype(F32)
                crossed = pltpu.roll(straight, 64, 1)
                for h in range(2):
                    kind = kinds[v, :, 2 * d + h : 2 * d + h + 1] - side
                    twice = jnp.where(lane < 64, crossed if h else straight, straight if h else crossed)
                    rhs[h, at, :lanes] = jnp.where(kind == 0, twice, 0.0).astype(BF)
                    rhs[h, at, lanes:] = jnp.where(kind == 2, twice, 0.0).astype(BF)
            return carry

        lax.fori_loop(0, owners, one, 0)

    def gather_rows(c, p):
        tile = tall // 2
        blocks = owners * sources * pairs // depth
        total[...] = jnp.zeros_like(total)

        def one(n, carry):
            h, b = lax.div(n, blocks), lax.rem(n, blocks)
            at = pl.ds(pl.multiple_of(b * depth, depth), depth)
            ids = places[h, :, at] - p * tile
            hit = lax.broadcasted_iota(jnp.int32, (tile, depth), 0) == ids
            total[...] += dot_nn(jnp.where(hit, 1.0, 0.0).astype(BF), rhs[h, at, :])
            return carry

        lax.fori_loop(0, 2 * blocks, one, 0, unroll=2)
        dense[c, pl.ds(pl.multiple_of(p * tile, tile), tile), :] = total[...].astype(BF)

    part = tall // 2

    def lines_of(p):
        return pl.ds(pl.multiple_of(p * part, part), part)

    def keep_copy(c, p):
        return pltpu.make_async_copy(
            dense.at[c, lines_of(p)], word.at[c, spot, lines_of(p)], own_sem.at[3 + 2 * c + p]
        )

    def near_copies(c, p):
        return [
            remote(
                dense.at[c, lines_of(p)], word.at[c, spot, lines_of(p)], d_send.at[c, 2 * p], d_recv.at[c, 2 * p], across_x
            ),
            remote(
                dense.at[c, lines_of(p)],
                word.at[c, spot, lines_of(p)],
                d_send.at[c, 2 * p + 1],
                d_recv.at[c, 2 * p + 1],
                across_y,
            ),
        ]

    def far_copy(c, p):
        source = flipped(spot, 1) if p == 0 else flipped(spot, 2)
        view = word.at[c, source, lines_of(p)]
        return remote(view, view, d_send.at[c, 4 + p], d_recv.at[c, 4 + p], across_y if p == 0 else across_x)

    corner = 256
    block = 768
    quarter = wown.shape[0]

    def turn(which):
        def one(i, carry):
            at = pl.ds(pl.multiple_of(i * corner, corner), corner)
            for j in range(width // corner):
                there = pl.ds(j * corner, corner)
                turned[there, at] = ops[which, at, there].T
            return carry

        lax.fori_loop(0, tokens // corner, one, 0)

    def weight(which, at):
        def one(n, carry):
            there = pl.ds(pl.multiple_of(n * block, block), block)
            out = dot_nn(turned[...], ops[which, :, there]).astype(BF)
            for v in range(owners):
                wbuf[v // 2, v % 2, pl.ds(at * per, per), there] = out[v * per : (v + 1) * per]
            return carry

        lax.fori_loop(0, width // block, one, 0)

    core_copy = remote(wbuf.at[:, 1 - core], wcore, w_send.at[0], w_recv.at[0], {"vocab": flipped(me, 1)})

    def wide(b):
        return pl.ds(pl.multiple_of(b * 2 * quarter, quarter), 2 * quarter)

    def narrow(b, c):
        return pl.ds(pl.multiple_of((2 * b + c) * quarter, quarter), quarter)

    def add(view, value):
        view[...] = (view[...].astype(F32) + value.astype(F32)).astype(BF)

    def core_step():
        core_copy.wait_recv()

        def one(i, carry):
            z = lax.div(i, 4)
            at = pl.ds(pl.multiple_of(lax.rem(i, 4) * quarter, quarter), quarter)
            add(wbuf.at[z, core, at, :], wcore[z, at, :])
            return carry

        lax.fori_loop(0, 16, one, 0)

    def first_weights():
        return [
            remote(wbuf.at[pl.ds(0, 2), core, wide(1 - xb), :], w1a, w_send.at[1], w_recv.at[1], across_x),
            remote(wbuf.at[pl.ds(2, 2), core, wide(1 - yb), :], w1b, w_send.at[2], w_recv.at[2], across_y),
        ]

    def second_weights():
        return [
            remote(wbuf.at[pl.ds(0, 2), core, narrow(xb, 1 - yb), :], w2a, w_send.at[3], w_recv.at[3], across_y),
            remote(wbuf.at[pl.ds(2, 2), core, narrow(yb, 1 - xb), :], w2b, w_send.at[4], w_recv.at[4], across_x),
        ]

    def first_step():
        arrived(first_weights())
        for z in range(2):
            add(wbuf.at[z, core, wide(xb), :], w1a[z])
            add(wbuf.at[2 + z, core, wide(yb), :], w1b[z])

    def second_step():
        arrived(second_weights())
        for z in range(2):
            add(wbuf.at[z, core, narrow(xb, yb), :], w2a[z])
            add(wbuf.at[2 + z, core, narrow(yb, xb), :], w2b[z])

    def owned(z):
        at = 2 * xb + yb + lax.div(z, 2) * (yb - xb)
        return wbuf.at[z, core, pl.ds(pl.multiple_of(at * quarter, quarter), quarter), :]

    def third_weights():
        copies = []
        for k in (3, 2, 1):
            to = flipped(place, k)
            copies.append(
                remote(owned(to), wz.at[k - 1], w_send.at[4 + k], w_recv.at[4 + k], {"vocab": 2 * to + core})
            )
        return copies

    def third_step():
        arrived(third_weights())
        total = owned(place)[...].astype(F32)
        for k in range(3):
            total = total + wz[k].astype(F32)
        wown[...] = total.astype(BF)

    def spread(own, target, at):
        wide_half = width // 2
        left, right = pl.ds(0, wide_half), pl.ds(wide_half, wide_half)
        kept = pltpu.make_async_copy(own, target.at[xb, yb], own_sem.at[(9, 10, 15)[at]])
        sems = [(w_send.at[8 + 4 * at + i], w_recv.at[8 + 4 * at + i]) for i in range(4)]
        near = [
            remote(own, target.at[xb, yb], *sems[0], across_x),
            remote(own, target.at[xb, yb], *sems[1], across_y),
        ]
        from_x, from_y = target.at[1 - xb, yb, :, left], target.at[xb, 1 - yb, :, right]
        far = [remote(from_x, from_x, *sems[2], across_y), remote(from_y, from_y, *sems[3], across_x)]
        return kept, near, far

    feed_kept, feed_near, feed_far = spread(feed_own, feed_out, 0)
    kept, fourth_weights, fifth_weights = spread(wown, packed, 1)
    up_kept, up_near, up_far = spread(up_part, up_out, 2)

    def small_copies():
        copies = []
        for k in ORDER:
            peer = flipped(me, k)
            copies.append(remote(small_by.at[peer], small_in.at[k], s_send.at[k], s_recv.at[k], {"vocab": peer}))
        return copies

    def small_last():
        return [
            remote(small_in.at[0], small_dp.at[k - 1], s_send.at[7 + k], s_recv.at[7 + k], {"dp": flipped(spot, k)})
            for k in (1, 2, 3)
        ]

    start(small_copies())
    fill_first(0)
    for near, kept_copy in ((feed_near, feed_kept), (up_near, up_kept)):
        start(near)
        kept_copy.start()
    loads[0].wait()
    turn(0)
    for i in range(3):
        loads[1 + i].wait()
        weight(1 + i, i)
        if i == 0:
            fill_first(1)
    loads[4].wait()
    turn(4)
    loads[5].wait()
    weight(5, 3)
    share = half // owners
    for v in range(owners):
        wbuf[v // 2, v % 2, pl.ds(4 * per, share), :] = pos[pl.ds(v * share, share), :]
    core_copy.start()

    def fill_next(j, carry):
        fill_first(j)
        return carry

    lax.fori_loop(2, sources, fill_next, 0)
    own_copy(0).start()
    for near, far, kept_copy in ((feed_near, feed_far, feed_kept), (up_near, up_far, up_kept)):
        kept_copy.wait()
        arrived(near)
        start(far)
    core_step()
    start(first_weights())
    for c in (1, 2):
        token_own(c).wait()
        arrived(token_copies(c))

    def rest(d, carry):
        fill(d, 1, 2)
        return carry

    lax.fori_loop(0, sources, rest, 0)
    for c in (1, 2):
        own_copy(c).start()
    sort_rows()
    arrived(small_copies())
    short = small_by[me]
    for k in ORDER:
        short = short + small_in[k]
    small_in[0] = short
    start(small_last())

    def close_chunk(c):
        for j in range(sources):
            arrived(row_copies(c, j))
        own_copy(c).wait()
        if c + 1 < chunks:
            for j in range(sources):
                start(row_copies(c + 1, j))
        else:
            start(third_weights())
        prepare(c)
        def half_rows(p, carry):
            gather_rows(c, p)
            start(near_copies(c, p))
            keep_copy(c, p).start()
            return carry

        lax.fori_loop(0, 2, half_rows, 0)

    def pass_on(c):
        arrived(near_copies(c, 0))
        far_copy(c, 0).start()
        arrived(near_copies(c, 1))
        far_copy(c, 1).start()

    close_chunk(0)
    first_step()
    start(second_weights())
    pass_on(0)
    close_chunk(1)
    second_step()
    arrived(small_last())
    short = small_in[0]
    for k in range(3):
        short = short + small_dp[k]
    small_out[...] = short
    pass_on(1)
    close_chunk(2)
    third_step()
    start(fourth_weights)
    kept.start()
    pass_on(2)
    kept.wait()
    arrived(fourth_weights)
    start(fifth_weights)

    for c in range(chunks):
        for p in range(2):
            keep_copy(c, p).wait()
            far_copy(c, p).wait_recv()
    arrived(feed_far)
    arrived(fifth_weights)
    arrived(up_far)
    gone(up_near)
    gone(up_far)
    core_copy.wait_send()
    gone(small_copies())
    gone(small_last())
    for c in range(chunks):
        gone(token_copies(c))
        for j in range(sources):
            gone(row_copies(c, j))
        for p in range(2):
            gone(near_copies(c, p))
            far_copy(c, p).wait_send()
    for copies in (first_weights(), second_weights(), third_weights(), fourth_weights, fifth_weights, feed_near, feed_far):
        gone(copies)


def tail(
    slots, asked, pos, feed_sums, up_sums, mid_sums, raw, normed, mixed, gfirst, dq, dk, dv, feed_own, up_part, rows_local
):
    half, width = pos.shape
    sources, owners, _, cap = asked.shape
    chunks = raw.shape[0]
    pairs = cap // 2
    tall = rows_local // 4
    lines = 4 * (width // owners) + half // owners
    vmem = pl.BlockSpec(memory_space=pltpu.VMEM)
    hbm = pl.BlockSpec(memory_space=pl.ANY)
    return pl.pallas_call(
        tail_kernel,
        out_shape=(
            jax.ShapeDtypeStruct((chunks, sources, tall, 256), BF),
            jax.ShapeDtypeStruct((2, 2, lines // 4, width), BF),
            jax.ShapeDtypeStruct((2, 2) + feed_own.shape, BF),
            jax.ShapeDtypeStruct((2, 2) + feed_own.shape, BF),
            jax.ShapeDtypeStruct((16, 128), F32),
        ),
        in_specs=[vmem] * 6 + [hbm] * 9,
        out_specs=(hbm, hbm, hbm, hbm, vmem),
        scratch_shapes=[
            pltpu.VMEM((chunks, sources, half, 128), BF),
            pltpu.VMEM((sources, 2, owners, cap, half), BF),
            pltpu.VMEM((chunks, owners, sources, pairs, 128), BF),
            pltpu.VMEM((chunks, owners, sources, pairs, 128), BF),
            pltpu.VMEM((2, owners * sources * pairs, 256), BF),
            pltpu.VMEM((owners, pairs, 2 * sources), jnp.int32),
            pltpu.VMEM((2, 1, owners * sources * pairs), jnp.int32),
            pltpu.VMEM((tall // 2, 256), F32),
            pltpu.VMEM((chunks, tall, 256), BF),
            pltpu.VMEM((6, 2 * half, width), BF),
            pltpu.VMEM((width, 2 * half), BF),
            pltpu.VMEM((4, 2, lines, width), BF),
            pltpu.VMEM((4, lines, width), BF),
            pltpu.VMEM((2, lines // 2, width), BF),
            pltpu.VMEM((2, lines // 2, width), BF),
            pltpu.VMEM((2, lines // 4, width), BF),
            pltpu.VMEM((2, lines // 4, width), BF),
            pltpu.VMEM((3, lines // 4, width), BF),
            pltpu.VMEM((lines // 4, width), BF),
            pltpu.VMEM((owners, 16, 128), F32),
            pltpu.VMEM((owners, 16, 128), F32),
            pltpu.VMEM((3, 16, 128), F32),
            pltpu.SemaphoreType.DMA((6,)),
            pltpu.SemaphoreType.DMA((chunks, 4)),
            pltpu.SemaphoreType.DMA((chunks, 4)),
            pltpu.SemaphoreType.DMA((chunks, sources, owners)),
            pltpu.SemaphoreType.DMA((chunks, sources, owners)),
            pltpu.SemaphoreType.DMA((chunks, 6)),
            pltpu.SemaphoreType.DMA((chunks, 6)),
            pltpu.SemaphoreType.DMA((20,)),
            pltpu.SemaphoreType.DMA((20,)),
            pltpu.SemaphoreType.DMA((14,)),
            pltpu.SemaphoreType.DMA((14,)),
            pltpu.SemaphoreType.DMA((16,)),
        ],
        compiler_params=pltpu.CompilerParams(collective_id=1, has_side_effects=True, vmem_limit_bytes=60 * MIB),
        name="tail",
    )(
        slots, asked, pos, feed_sums, up_sums, mid_sums,
        raw, normed, mixed, gfirst, dq, dk, dv, feed_own, up_part,
    )


def fetch_kernel(
    token_ids_in, kinds_in, pos_in, types_in, gain_in, bias_in, table_in,
    embedded_out, normed_out, slots_out, asked_out,
    token_ids, kinds, pos, types, gain, bias, table, request, asked_in, rows_out, rows_in, embedded, normed, column, kind_column,
    load_sem, q_send, q_recv, s_send, s_recv, a_send, a_recv, z_send, z_recv, out_sem,
):
    owners, cap, width = rows_out.shape
    tokens = normed.shape[0]
    rows_local = table.shape[0]
    me = lax.axis_index("vocab")
    spot = lax.axis_index("dp")
    table_copy = pltpu.make_async_copy(table_in, table, load_sem.at[0])
    loads = [
        pltpu.make_async_copy(source, target, load_sem.at[1 + i])
        for i, (source, target) in enumerate(
            (
                (token_ids_in, token_ids),
                (kinds_in, kinds),
                (pos_in, pos),
                (types_in, types),
                (gain_in, gain),
                (bias_in, bias),
            )
        )
    ]
    for load in loads:
        load.start()
    table_copy.start()
    barrier = pltpu.get_barrier_semaphore()
    for k in ORDER:
        pl.semaphore_signal(barrier, inc=1, device_id={"vocab": flipped(me, k)}, device_id_type=MESH)
    for k in (1, 2, 3):
        pl.semaphore_signal(barrier, inc=1, device_id={"dp": flipped(spot, k)}, device_id_type=MESH)

    def remote(src, dst, send, recv, peer):
        return pltpu.make_async_remote_copy(
            src_ref=src, dst_ref=dst, send_sem=send, recv_sem=recv, device_id=peer, device_id_type=MESH
        )

    loads[0].wait()
    ids = jnp.concatenate([token_ids[s : s + 1, :] for s in range(token_ids.shape[0])], 1)
    owner = jnp.zeros(ids.shape, jnp.int32)
    for v in range(1, owners):
        owner = owner + jnp.where(ids >= v * rows_local, 1, 0)
    member = jnp.where(lax.broadcasted_iota(jnp.int32, (owners, tokens), 0) == owner, 1.0, 0.0)
    block = 256
    rank = []
    for n in range(tokens // block):
        before = lax.broadcasted_iota(jnp.int32, (tokens, block), 0) < (
            lax.broadcasted_iota(jnp.int32, (tokens, block), 1) + n * block
        )
        earlier = dot_nn(member.astype(BF), jnp.where(before, 1.0, 0.0).astype(BF))
        rank.append(jnp.sum(earlier * member[:, n * block : (n + 1) * block], 0, keepdims=True))
    slot = owner * cap + jnp.concatenate(rank, 1).astype(jnp.int32)
    local = ids - owner * rows_local
    line = lax.broadcasted_iota(jnp.int32, (8, tokens), 0)
    high = lax.shift_right_logical(local, 6)
    values = jnp.where(line == 0, high, jnp.where(line == 1, local - high * 64, jnp.where(line == 2, 1, 0)))
    values = values.astype(F32).astype(BF)
    slots_out[spot] = slot

    def ask(v, carry):
        wanted = lax.broadcasted_iota(jnp.int32, (cap, tokens), 0) + v * cap
        found = dot_nt(values, jnp.where(wanted == slots_out[spot], 1.0, 0.0).astype(BF))
        number = found[0:1] * 64.0 + found[1:2]
        request[v] = jnp.where(found[2:3] > 0.5, number, -1.0).astype(jnp.int32)
        return carry

    lax.fori_loop(0, owners, ask, 0)
    pl.semaphore_wait(barrier, len(ORDER) + 3)
    asks = []
    for k in ORDER:
        peer = flipped(me, k)
        asks.append(remote(request.at[peer], asked_in.at[me], q_send.at[k], q_recv.at[k], {"vocab": peer}))
    for copy in asks:
        copy.start()
    asked_in[me] = request[me]
    lists = []
    for k in (1, 2, 3):
        peer = {"dp": flipped(spot, k)}
        lists.append(remote(slots_out.at[spot], slots_out.at[spot], s_send.at[k], s_recv.at[k], peer))
    for copy in lists:
        copy.start()
    column[...] = jnp.broadcast_to(slot.astype(F32), (8, tokens)).T[:, 0:1].astype(jnp.int32)
    for load in loads[1:]:
        load.wait()
    column_of(kinds, kind_column)
    half = tokens // 2
    for s in range(2):
        at = pl.ds(s * half, half)
        kind = jnp.where(kind_column[at, :] == 0, types[0:1, :].astype(F32), types[1:2, :].astype(F32))
        embedded[at, :] = pos[...].astype(F32) + kind
    for copy in asks:
        copy.wait_recv()
    asked_out[spot] = asked_in[...]
    for k in (1, 2, 3):
        peer = {"dp": flipped(spot, k)}
        copy = remote(asked_in, asked_out.at[spot], a_send.at[k], a_recv.at[k], peer)
        lists.append(copy)
        copy.start()
    table_copy.wait()

    def find(source):
        asked = jnp.broadcast_to(asked_in[source].astype(F32), (8, cap)).T[:, 0:1]
        depth = rows_local // 3
        total = jnp.zeros((cap, width), F32)
        for n in range(3):
            at = lax.broadcasted_iota(jnp.int32, (cap, depth), 1) + n * depth
            hit = jnp.where(at == asked.astype(jnp.int32), 1.0, 0.0).astype(BF)
            total = total + dot_nn(hit, table[pl.ds(n * depth, depth), :])
        return total.astype(BF)

    def row_copy(peer):
        return remote(rows_out.at[peer], rows_in.at[me], z_send.at[peer], z_recv.at[me], {"vocab": peer})

    def row_arrival(peer):
        return remote(rows_out.at[peer], rows_in.at[peer], z_send.at[peer], z_recv.at[peer], {"vocab": peer})

    core, spot_z = lax.rem(me, 2), lax.div(me, 2)
    side = lax.div(spot_z, 2)

    def answer(i, carry):
        j = lax.div(i, 2)
        to_end = lax.div((1 - j) * (2 - j) * (3 - j), 6)
        to_middle = lax.div(j * (2 - j) * (3 - j), 2)
        to_next = lax.div(j * (j - 1) * (3 - j), 2)
        to_core = lax.div(j * (j - 1) * (j - 2), 6)
        chip = (
            to_end * 3 * (1 - side)
            + to_middle * (2 - side)
            + to_next * (spot_z + 1 - 2 * lax.rem(spot_z, 2))
            + to_core * spot_z
        )
        peer = 2 * chip + lax.rem(i, 2) * (1 - to_core) + (1 - core) * to_core
        rows_out[peer] = find(peer)
        row_copy(peer).start()
        return carry

    lax.fori_loop(0, owners - 1, answer, 0)
    rows_in[me] = find(me)

    def place(source):
        part = 256

        def one(n, carry):
            at = pl.ds(pl.multiple_of(n * part, part), part)
            hit = lax.broadcasted_iota(jnp.int32, (part, cap), 1) + source * cap
            hit = jnp.where(hit == column[at, :], 1.0, 0.0).astype(BF)
            embedded[at, :] += dot_nn(hit, rows_in[source])
            return carry

        lax.fori_loop(0, tokens // part, one, 0)

    place(me)
    for k in (1, 2, 3, 4, 5, 6, 7):
        peer = flipped(me, k)
        row_arrival(peer).wait_recv()
        place(peer)
    part = 128

    def out_copies(n):
        at = pl.ds(n * part, part)
        return [
            pltpu.make_async_copy(embedded.at[at, :], embedded_out.at[at, :], out_sem.at[n, 0]),
            pltpu.make_async_copy(normed.at[at, :], normed_out.at[at, :], out_sem.at[n, 1]),
        ]

    for n in range(tokens // part):
        at = pl.ds(n * part, part)
        unit, _ = stats(embedded[at, :])
        normed[at, :] = unit * gain[...][None] + bias[...][None]
        for copy in out_copies(n):
            copy.start()
    for n in range(tokens // part):
        for copy in out_copies(n):
            copy.wait()
    for copy in lists:
        copy.wait_recv()
        copy.wait_send()
    for copy in asks:
        copy.wait_send()
    for k in ORDER:
        row_copy(flipped(me, k)).wait_send()


def fetch(ids, kinds, table, pos, types, gain, bias, owners):
    tokens = ids.size
    rows_local, width = table.shape
    cap = 2 * tokens // owners
    vmem = pl.BlockSpec(memory_space=pltpu.VMEM)
    hbm = pl.BlockSpec(memory_space=pl.ANY)
    full = jax.ShapeDtypeStruct((tokens, width), F32)
    dma = pltpu.SemaphoreType.DMA
    return pl.pallas_call(
        fetch_kernel,
        out_shape=(
            full,
            full,
            jax.ShapeDtypeStruct((4, 1, tokens), jnp.int32),
            jax.ShapeDtypeStruct((4, owners, 1, cap), jnp.int32),
        ),
        in_specs=[hbm] * 7,
        out_specs=(hbm, hbm, vmem, vmem),
        scratch_shapes=[
            pltpu.VMEM(ids.shape, jnp.int32),
            pltpu.VMEM(ids.shape, jnp.int32),
            pltpu.VMEM(pos.shape, BF),
            pltpu.VMEM(types.shape, BF),
            pltpu.VMEM((width,), F32),
            pltpu.VMEM((width,), F32),
            pltpu.VMEM((rows_local, width), BF),
            pltpu.VMEM((owners, 1, cap), jnp.int32),
            pltpu.VMEM((owners, 1, cap), jnp.int32),
            pltpu.VMEM((owners, cap, width), BF),
            pltpu.VMEM((owners, cap, width), BF),
            pltpu.VMEM((tokens, width), F32),
            pltpu.VMEM((tokens, width), F32),
            pltpu.VMEM((tokens, 1), jnp.int32),
            pltpu.VMEM((tokens, 1), jnp.int32),
            dma((7,)),
            dma((owners,)),
            dma((owners,)),
            dma((4,)),
            dma((4,)),
            dma((4,)),
            dma((4,)),
            dma((owners,)),
            dma((owners,)),
            dma((tokens // 128, 2)),
        ],
        compiler_params=pltpu.CompilerParams(collective_id=3, has_side_effects=True, vmem_limit_bytes=62 * MIB),
        name="fetch",
    )(ids, kinds, pos, types, gain, bias, table)


def finish_kernel(
    near, word_in, packed, feeds, ups, small,
    word, query_out, keys_out, values_out, out_out, pos_out, up_out, down_out, kinds, up_bias, *rest,
):
    vectors, (query, keys, values, out, pos, up, down, sem) = rest[:10], rest[10:]
    copies = [
        pltpu.make_async_copy(source, target, sem.at[i])
        for i, (source, target) in enumerate(
            (
                (query, query_out),
                (keys, keys_out),
                (values, values_out),
                (out, out_out),
                (pos, pos_out),
                (up, up_out),
                (down, down_out),
            )
        )
    ]
    chunks, sources, part, _ = word_in.shape
    lane = lax.broadcasted_iota(jnp.int32, (part, 128), 1)
    for c in range(chunks):
        for q in range(0, sources, 2):
            at = pl.ds((c * sources + q) * 64, 128)
            for j in range(2):
                there = pl.ds(j * 128, 128)
                one, two = word_in[c, q, :, there].astype(F32), word_in[c, q + 1, :, there].astype(F32)
                word[2 * j, :, at] = jnp.where(lane < 64, one, pltpu.roll(two, 64, 1))
                word[2 * j + 1, :, at] = jnp.where(lane < 64, pltpu.roll(one, 64, 1), two)

    @pl.when(pl.program_id(0) == 0)
    def _():
        n = near[0]
        order = ((0, 0), (1 - n, n), (n, 1 - n), (1, 1))
        per, width = query.shape
        rows = jnp.concatenate([packed[a, b] for a, b in order], 0).astype(F32)
        for i, target in enumerate((query, keys, values, out)):
            target[...] = rows[i * per : (i + 1) * per]
        pos[...] = rows[4 * per :]
        lines = []
        for i, (a, b) in enumerate(order):
            up[:, pl.ds(i * width, width)] = ups[a, b].astype(F32)
            for j in range(2):
                lines.append(feeds[a, b, :, j * 4 * per : (j + 1) * 4 * per])
        down[...] = jnp.concatenate(lines, 0).astype(F32).T
        for copy in copies:
            copy.start()
        for i, vector in enumerate(vectors):
            vector[...] = small[i, :per]
        kinds[...] = small[10:12, :per]
        up_bias[...] = jnp.concatenate([small[12 + i : 13 + i, :per] for i in range(4)], 1)[0]

    @pl.when(pl.program_id(0) == pl.num_programs(0) - 1)
    def _():
        for copy in copies:
            copy.wait()


def finish(near, word, packed, feeds, ups, small, rows_local, owners):
    chunks, sources, tall, _ = word.shape
    width = packed.shape[3]
    per = width // owners
    steps = 3
    part = tall // steps
    held = jax.ShapeDtypeStruct((per, width), F32)
    share = packed.shape[2] * 4 - 4 * per
    shapes = [held] * 4 + [
        jax.ShapeDtypeStruct((share, width), F32),
        jax.ShapeDtypeStruct((per, 4 * width), F32),
        jax.ShapeDtypeStruct((4 * per, width), F32),
        jax.ShapeDtypeStruct((2, per), F32),
        jax.ShapeDtypeStruct((4 * per,), F32),
    ] + [jax.ShapeDtypeStruct((per,), F32)] * 10
    results = pl.pallas_call(
        finish_kernel,
        grid_spec=pltpu.PrefetchScalarGridSpec(
            num_scalar_prefetch=1,
            grid=(steps,),
            in_specs=[
                pl.BlockSpec((chunks, sources, part, 256), lambda i, *_: (0, 0, i, 0)),
                fixed(packed.shape),
                fixed(feeds.shape),
                fixed(ups.shape),
                fixed(small.shape),
            ],
            out_specs=[pl.BlockSpec((4, part, width), lambda i, *_: (0, i, 0))]
            + [pl.BlockSpec(memory_space=pl.ANY)] * 7
            + [fixed(s.shape) for s in shapes[7:]],
            scratch_shapes=[pltpu.VMEM(s.shape, F32) for s in shapes[:7]] + [pltpu.SemaphoreType.DMA((7,))],
        ),
        out_shape=[jax.ShapeDtypeStruct((4, tall, width), F32)] + shapes,
        compiler_params=pltpu.CompilerParams(vmem_limit_bytes=62 * MIB),
        name="finish",
    )(near.astype(jnp.int32).reshape(1), word, packed, feeds, ups, small)
    return [results[0].reshape(rows_local, width)] + list(results[1:])


def local(
    token_ids,
    type_ids,
    lengths,
    word_table,
    pos_table,
    token_type_embeddings,
    emb_gain,
    emb_bias,
    query_weight,
    query_bias,
    key_weight,
    value_weight,
    value_bias,
    out_weight,
    out_bias,
    attn_gain,
    attn_bias,
    up_weight,
    up_bias,
    down_weight,
    down_bias,
    final_gain,
    final_bias,
    cotangent,
):
    seq_count, seq_len = token_ids.shape
    tokens = seq_count * seq_len
    width = word_table.shape[1]
    rows_local = word_table.shape[0]
    owners = lax.axis_size("vocab")
    capacity = max(2, 2 * tokens // owners)
    fast = owners == 8 and lax.axis_size("dp") == 4
    if fast:
        embedded, normed, slots, askeds = fetch(
            token_ids, type_ids, word_table, pos_table, token_type_embeddings, emb_gain, emb_bias, owners
        )
    else:
        flat_ids = token_ids.reshape(tokens)
        owner = flat_ids // rows_local
        member = (owner[:, None] == jnp.arange(owners)[None, :]).astype(jnp.int32)
        earlier = jnp.cumsum(member, 0) - member
        rank = jnp.sum(earlier * member, 1)
        slot = owner * capacity + rank
        requests = (
            jnp.full((owners * capacity,), -1, jnp.int32).at[slot].set(flat_ids - owner * rows_local)
        )
        requests = requests.reshape(owners, capacity)
        asked = lax.all_to_all(requests, "vocab", split_axis=0, concat_axis=0, tiled=True)
        valid = asked >= 0
        found = word_table[jnp.maximum(asked, 0)]
        found = jnp.where(valid[..., None], found, jnp.zeros((), jnp.bfloat16))
        returned = lax.all_to_all(found, "vocab", split_axis=0, concat_axis=0, tiled=True)
        word_rows = returned.reshape(owners * capacity, width)[slot]
        kinds = token_type_embeddings.shape[0]
        selection_matrix = (type_ids[..., None] == jnp.arange(kinds)[None, None, :]).astype(jnp.float32)
        type_rows = jnp.einsum(
            "tcr,rb->tcb",
            selection_matrix,
            token_type_embeddings.astype(jnp.float32),
            precision=lax.Precision.HIGHEST,
        )
        embedded = (
            word_rows.reshape(seq_count, seq_len, width).astype(jnp.float32)
            + pos_table.astype(jnp.float32)[None]
            + type_rows
        )
        embedded = embedded.reshape(tokens, width)
        normed = layer_norm(embedded, emb_gain, emb_bias)
    normed_low, query, keys, values, mixed_low, first, probs = attend(
        lengths, normed, query_weight, key_weight, value_weight, out_weight, query_bias, value_bias, out_bias
    )
    encoded, active_low, grad_second_low, hidden_low, grad_upper_low, grad_first, feed_sums, up_sums = feed(
        first,
        cotangent.reshape(tokens, width),
        up_weight,
        down_weight,
        up_bias,
        down_bias,
        attn_gain,
        attn_bias,
        final_gain,
        final_bias,
    )
    grad_final_gain, grad_final_bias, grad_down_bias, grad_attn_gain, grad_attn_bias, grad_out_bias = [
        feed_sums[i] for i in range(6)
    ]
    grad_up_bias = up_sums[0]
    if fast:
        (
            grad_first_low,
            grad_query_low,
            grad_keys_low,
            grad_values_low,
            raw,
            grad_pos,
            feed_own,
            up_part,
            mid_sums,
        ) = mid(
            active_low,
            grad_upper_low,
            grad_second_low,
            hidden_low,
            grad_first,
            embedded,
            query,
            keys,
            values,
            probs,
            query_weight,
            key_weight,
            value_weight,
            out_weight,
            type_ids,
            emb_gain,
        )
    else:
        grad_down = matmul_tn(active_low, grad_second_low)
        grad_up = matmul_tn(hidden_low, grad_upper_low)
        grad_first_low, grad_query_low, grad_keys_low, grad_values_low, embedding_output_gradient, mid_sums = attend_back(
            grad_first,
            embedded,
            type_ids,
            query,
            keys,
            values,
            probs,
            query_weight,
            key_weight,
            value_weight,
            out_weight,
            emb_gain,
        )
        grad_pos = jnp.sum(embedding_output_gradient.astype(jnp.float32).reshape(seq_count, seq_len, width), 0)
    grad_query_bias, grad_value_bias, grad_emb_gain, grad_emb_bias = [mid_sums[i] for i in range(4)]
    token_type_gradient = mid_sums[4:6]
    bf = jnp.bfloat16
    per = width // owners
    small = jnp.stack(
        [
            grad_query_bias,
            grad_value_bias,
            grad_out_bias,
            grad_attn_gain,
            grad_attn_bias,
            grad_emb_gain,
            grad_emb_bias,
            grad_down_bias,
            grad_final_gain,
            grad_final_bias,
            token_type_gradient[0],
            token_type_gradient[1],
        ]
    )
    if fast:
        word_pairs, packed, feeds, ups, small = tail(
            slots,
            askeds,
            grad_pos,
            feed_sums,
            up_sums,
            mid_sums,
            raw,
            normed_low,
            mixed_low,
            grad_first_low,
            grad_query_low,
            grad_keys_low,
            grad_values_low,
            feed_own,
            up_part,
            rows_local,
        )
        near = lax.axis_index("vocab") < owners // 2
        (
            grad_word,
            grad_query_weight,
            grad_key_weight,
            grad_value_weight,
            grad_out_weight,
            grad_pos,
            grad_up,
            grad_down,
            token_type_gradient,
            grad_up_bias,
            *short,
        ) = finish(near, word_pairs, packed, feeds, ups, small, rows_local, owners)
    else:
        grad_down = sum_over_all(grad_down.astype(bf))
        grad_up = sum_over_all(grad_up.astype(bf))
        places = slot[None, :] == jnp.arange(owners * capacity)[:, None]
        outgoing = matmul(
            places.astype(bf), embedding_output_gradient.reshape(tokens, width).astype(bf)
        ).astype(bf)
        hits = (jnp.arange(rows_local)[:, None] == asked.reshape(-1)[None, :]).astype(bf)
        pieces = []
        step = 256
        for start in range(0, width, step):
            incoming = lax.all_to_all(
                outgoing[:, start : start + step].reshape(owners, capacity, step),
                "vocab",
                split_axis=0,
                concat_axis=0,
                tiled=True,
            )
            dense = matmul(hits, incoming.reshape(owners * capacity, step)).astype(bf)
            pieces.append(sum_over_dp(dense))
        grad_word = jnp.concatenate(pieces, 1)
        small = small.reshape(12, owners, per).transpose(1, 0, 2).reshape(owners, 12 * per)
        small = jnp.concatenate([small, grad_up_bias.reshape(owners, 4 * per)], 1)
        wide = 4 * width
        lines = (seq_len // owners) * width // wide
        rest = per // 3 - lines
        small_lines = jnp.pad(small, ((0, 0), (0, rest * wide - 16 * per))).reshape(owners, rest, wide)
        grad_query_weight, grad_key_weight, grad_value_weight = [
            matmul_tn(normed_low, g) for g in (grad_query_low, grad_keys_low, grad_values_low)
        ]
        grad_out_weight = matmul_tn(mixed_low, grad_first_low)
        mixed_grads = jnp.concatenate(
            [grad_query_weight, grad_key_weight, grad_value_weight, grad_out_weight], 1
        ).astype(bf)
        packed = jnp.concatenate(
            [
                mixed_grads.reshape(owners, per, wide),
                grad_pos.astype(bf).reshape(owners, lines, wide),
                small_lines.astype(bf),
            ],
            1,
        )
        packed = sum_over_all(packed.reshape(-1, wide))
        weights = packed[:per]
        grad_query_weight = weights[:, :width]
        grad_key_weight = weights[:, width : 2 * width]
        grad_value_weight = weights[:, 2 * width : 3 * width]
        grad_out_weight = weights[:, 3 * width :]
        grad_pos = packed[per : per + lines].reshape(seq_len // owners, width)
        small = packed[per + lines :].reshape(-1)[: 16 * per].reshape(16, per)
        short = [small[i] for i in range(10)]
        token_type_gradient = small[10:12]
        grad_up_bias = small[12:].reshape(-1)
    (
        grad_query_bias,
        grad_value_bias,
        grad_out_bias,
        grad_attn_gain,
        grad_attn_bias,
        grad_emb_gain,
        grad_emb_bias,
        grad_down_bias,
        grad_final_gain,
        grad_final_bias,
    ) = short
    return (
        encoded.reshape(seq_count, seq_len, width),
        grad_word,
        grad_pos,
        token_type_gradient,
        grad_emb_gain,
        grad_emb_bias,
        grad_query_weight,
        grad_query_bias,
        grad_key_weight,
        grad_value_weight,
        grad_value_bias,
        grad_out_weight,
        grad_out_bias,
        grad_attn_gain,
        grad_attn_bias,
        grad_up,
        grad_up_bias,
        grad_down,
        grad_down_bias,
        grad_final_gain,
        grad_final_bias,
    )


def solution(mesh):
    placed = (
        P(("dp", "vocab"), None),
        P(("dp", "vocab"), None),
        P(("dp", "vocab")),
        P("vocab", None),
        P(),
        P(),
        P(),
        P(),
        P(),
        P(),
        P(),
        P(),
        P(),
        P(),
        P(),
        P(),
        P(),
        P(),
        P(),
        P(),
        P(),
        P(),
        P(),
        P(("dp", "vocab"), None, None),
    )
    return jax.shard_map(
        local,
        mesh=mesh,
        in_specs=placed,
        out_specs=(
            P(("dp", "vocab"), None, None),
            P("vocab", None),
            P("vocab", None),
            P(None, "vocab"),
            P("vocab"),
            P("vocab"),
            P("vocab", None),
            P("vocab"),
            P("vocab", None),
            P("vocab", None),
            P("vocab"),
            P("vocab", None),
            P("vocab"),
            P("vocab"),
            P("vocab"),
            P("vocab", None),
            P("vocab"),
            P("vocab", None),
            P("vocab"),
            P("vocab"),
            P("vocab"),
        ),
        check_vma=False,
    )
```
